32 devices in a mesh: ctx: 8 (over y, x, core), wt: 4 (over z).
Axes of the slice: x: 2, y: 2, z: 4, core: 2. Of those that a mesh axis runs over, the one named last changes fastest.
Arguments:
- words: bfloat16 [6144, 512], P(('ctx', 'wt')), may hold values from -6 to 6
- teacher: bfloat16 [6144, 512], P(('ctx', 'wt')), may hold values from -6 to 6
- valid: int32 [6144], P(('ctx', 'wt')), may hold values from 0 to 1, as said below
- lengths: int32 [4], replicated, may hold values from 384 to 3072, as said below
- deal: int32 [32], replicated, may hold values from 0 to 31, as said below
- gain_attn: bfloat16 [512], P('wt'), may hold values from 0.25 to 1.75
- shift_attn: bfloat16 [512], P('wt'), may hold values from -3 to 3
- w_qkv: bfloat16 [512, 1536], P('wt'), may hold values from -0.25 to 0.25
- w_out: bfloat16 [512, 512], P('wt'), may hold values from -2 to 2
- gain_mlp: bfloat16 [512], P('wt'), may hold values from 0.25 to 1.75
- shift_mlp: bfloat16 [512], P('wt'), may hold values from -3 to 3
- w_up: bfloat16 [512, 2048], P('wt'), may hold values from -0.25 to 0.25
- w_down: bfloat16 [2048, 512], P('wt'), may hold values from -0.125 to 0.125
Outputs:
- layer_out: bfloat16 [6144, 512], P(('ctx', 'wt'))
- loss: float32 [], replicated
- grad_words: float32 [6144, 512], P(('ctx', 'wt'))
- grad_gain_attn: float32 [512], P('wt')
- grad_shift_attn: float32 [512], P('wt')
- grad_w_qkv: float32 [512, 1536], P('wt')
- grad_w_out: float32 [512, 512], P('wt')
- grad_gain_mlp: float32 [512], P('wt')
- grad_shift_mlp: float32 [512], P('wt')
- grad_w_up: float32 [512, 2048], P('wt')
- grad_w_down: float32 [2048, 512], P('wt')
The draws below stay inside these ranges and needn't reach their ends.
Inputs may be any that keep to these rules, and one draw needn't show every extreme that they name: lengths are multiples of 192 that sum to 6144; one sequence has exactly 3072 words. `deal`: each initial block appears once; initial blocks that differ by a multiple of the number of ctx indices lie on the same ctx index. The first word of every dealt block is valid.
All inputs are finite; a program needn't handle non-finite values.
Results may differ from the reference program's by a relative error of at most 0.02.
Values may be sent and summed in bfloat16 or wider, within the bound.
No kernel may reach another device: no remote copies, remote signals or barrier semaphores. Data moves between devices by JAX's collectives and lax.ppermute only.
A program may use at most 128 MiB of HBM per device.

```python
import jax
import jax.numpy as jnp
from jax import lax

D = 512
H = 8
HEAD = 64
FF = 2048
BLK = 192
MIN_BLOCKS = 2
N_BLOCKS = 32
TOKENS = 6144
NSEQ = 4
MAX_BLOCKS = 16
N_CTX = 8
N_WT = 4


def draw_valid(key, part):
    places = jnp.arange(TOKENS, dtype=jnp.int32)
    level = 200 + 600 * places // TOKENS
    rolled = jax.random.randint(key, (TOKENS,), 0, 1000, dtype=jnp.int32)
    keep_word = (rolled < level) | (places % BLK == 0)
    return keep_word.astype(jnp.int32)


def draw_lengths(key, part):
    spare = N_BLOCKS - MAX_BLOCKS - (NSEQ - 1) * MIN_BLOCKS
    slots = spare + NSEQ - 2
    cut_key, place_key = jax.random.split(key)
    order = jax.random.permutation(cut_key, jnp.arange(slots, dtype=jnp.int32))
    bars = jnp.sort(order[:NSEQ - 2])
    edges = jnp.concatenate([jnp.array([-1], dtype=jnp.int32), bars.astype(jnp.int32), jnp.array([slots], dtype=jnp.int32)])
    pieces = edges[1:] - edges[:-1] - 1 + MIN_BLOCKS
    units = jnp.concatenate([pieces, jnp.array([MAX_BLOCKS], dtype=jnp.int32)])
    offset = jax.random.randint(place_key, (), 0, NSEQ, dtype=jnp.int32)
    return (jnp.roll(units, offset) * BLK).astype(jnp.int32)


def draw_deal(key, part):
    group_keys = jax.random.split(key, N_CTX)
    orders = jax.vmap(lambda one_key: jax.random.permutation(one_key, jnp.arange(N_WT, dtype=jnp.int32)))(group_keys)
    groups = jnp.arange(N_CTX, dtype=jnp.int32)[:, None]
    return (orders.astype(jnp.int32) * N_CTX + groups).reshape(N_BLOCKS).astype(jnp.int32)


def level_of(rng, extent, cuts, least, high):
    gain = 1.0
    for dim, shards_of in cuts:
        heights = jax.random.uniform(jax.random.fold_in(jax.random.fold_in(rng, 6), dim), (shards_of,), jnp.float32, least / len(cuts), high / len(cuts))
        gain = gain * jnp.repeat(jnp.exp(heights), extent[dim] // shards_of).reshape((-1,) + (1,) * (len(extent) - 1 - dim))
    return gain


def noise(stream_key, extent, spread, most, cuts=(), held_as=jnp.bfloat16):
    entries = spread * jax.random.normal(stream_key, extent, jnp.float32)
    if cuts:
        entries = entries * level_of(stream_key, extent, cuts, -0.22, 0.18)
    return jnp.clip(entries, -most, most).astype(held_as)


def setup_inputs(seed: int = 0) -> dict:
    keys = jax.random.split(jax.random.key(seed), 14)
    words = noise(keys[0], (TOKENS, D), 1.0, 6.0, ((0, 32),))
    teacher = noise(keys[1], (TOKENS, D), 1.0, 6.0, ((0, 32),))
    valid = draw_valid(jax.random.fold_in(keys[13], 71), 0)
    lengths = draw_lengths(jax.random.fold_in(keys[13], 71), 0)
    deal = draw_deal(jax.random.fold_in(keys[13], 71), 0)
    gain_attn = jnp.clip(1.0 + 0.15 * jax.random.normal(keys[5], (D,), jnp.float32), 0.25, 1.75).astype(jnp.bfloat16)
    shift_attn = noise(keys[6], (D,), 0.5, 3.0, ((0, 4),))
    w_qkv = noise(keys[7], (D, 3 * D), D ** -0.5, 0.25, ((0, 4),))
    w_out = noise(keys[8], (D, D), (D // 64) ** -0.5, 2.0, ((0, 4),))
    gain_mlp = jnp.clip(1.0 + 0.15 * jax.random.normal(keys[9], (D,), jnp.float32), 0.25, 1.75).astype(jnp.bfloat16)
    shift_mlp = noise(keys[10], (D,), 0.5, 3.0, ((0, 4),))
    w_up = noise(keys[11], (D, FF), D ** -0.5, 0.25, ((0, 4),))
    w_down = noise(keys[12], (FF, D), FF ** -0.5, 0.125, ((0, 4),))
    return dict(words=words, teacher=teacher, valid=valid, lengths=lengths, deal=deal, gain_attn=gain_attn, shift_attn=shift_attn, w_qkv=w_qkv, w_out=w_out, gain_mlp=gain_mlp, shift_mlp=shift_mlp, w_up=w_up, w_down=w_down)


EPS = 1e-05
LOSS_SCALE = 262144.0
HIGHEST = lax.Precision.HIGHEST

@jax.custom_vjp
def low(v):
    return lax.optimization_barrier(v.astype(jnp.bfloat16)).astype(jnp.float32)

@jax.custom_vjp
def low_back(v):
    return v

def low_keep(v):
    return (low(v), None)

def low_pass(kept, grad):
    return (grad,)

def back_keep(v):
    return (v, None)

def back_low(kept, grad):
    return (low(grad),)
low.defvjp(low_keep, low_pass)
low_back.defvjp(back_keep, back_low)

def layer_norm(values, gain_vec, shift_vec):
    center = values - lax.optimization_barrier(jnp.mean(values, axis=-1, keepdims=True))
    variance = lax.optimization_barrier(jnp.mean(center * center, axis=-1, keepdims=True))
    return center * lax.rsqrt(variance + EPS) * gain_vec + shift_vec

def word_places(lengths):
    places = jnp.arange(TOKENS, dtype=jnp.int32)
    bounds = jnp.cumsum(lengths).astype(jnp.int32)
    sequence = lax.optimization_barrier(jnp.sum((places[:, None] >= bounds[None, :]).astype(jnp.int32), axis=1))
    return (places, sequence)

def to_initial(values, deal):
    blocked = values.reshape((N_BLOCKS, BLK) + values.shape[1:])
    return jnp.zeros_like(blocked).at[deal].set(blocked).reshape(values.shape)

def to_dealt(values, deal):
    blocked = values.reshape((N_BLOCKS, BLK) + values.shape[1:])
    return blocked[deal].reshape(values.shape)

def attention(packed, places, sequence):
    heads = packed.reshape(TOKENS, H, 3, HEAD)
    queries = heads[:, :, 0]
    keys_all = heads[:, :, 1]
    values_all = heads[:, :, 2]
    query_block = min(512, TOKENS)
    window = min(MAX_BLOCKS * BLK + query_block, TOKENS)
    score_scale = HEAD ** (-0.5)

    def one_block(start):
        first = jnp.clip(start + query_block - window, 0, TOKENS - window).astype(jnp.int32)
        query_rows = lax.dynamic_slice_in_dim(queries, start, query_block, 0)
        key_rows = lax.dynamic_slice_in_dim(keys_all, first, window, 0)
        value_rows = lax.dynamic_slice_in_dim(values_all, first, window, 0)
        query_place = lax.dynamic_slice_in_dim(places, start, query_block, 0)
        query_seq = lax.dynamic_slice_in_dim(sequence, start, query_block, 0)
        key_place = lax.dynamic_slice_in_dim(places, first, window, 0)
        key_seq = lax.dynamic_slice_in_dim(sequence, first, window, 0)
        scores = low_back(jnp.einsum('qhd,khd->hqk', query_rows, key_rows, precision=HIGHEST) * score_scale)
        visible = (key_seq[None, :] == query_seq[:, None]) & (key_place[None, :] <= query_place[:, None])
        scores = jnp.where(visible[None], scores, -1e+30)
        largest = lax.optimization_barrier(jnp.max(scores, axis=-1, keepdims=True))
        weights = jnp.exp(scores - largest)
        probs = weights / lax.optimization_barrier(jnp.sum(weights, axis=-1, keepdims=True))
        return jnp.einsum('hqk,khd->qhd', low(probs), value_rows, precision=HIGHEST)
    starts = jnp.arange(0, TOKENS, query_block, dtype=jnp.int32)
    return lax.map(jax.checkpoint(one_block), starts).reshape(TOKENS, H * HEAD)

def forward(inputs, gain_attn, shift_attn, w_qkv, w_out, gain_mlp, shift_mlp, w_up, w_down, target, weight_mask, places, sequence):
    normed_one = layer_norm(inputs, gain_attn, shift_attn)
    packed = low_back(low(jnp.dot(low(normed_one), w_qkv, precision=HIGHEST)))
    attended = low_back(low(attention(packed, places, sequence)))
    residual_one = inputs + low_back(jnp.dot(attended, w_out, precision=HIGHEST))
    normed_two = layer_norm(residual_one, gain_mlp, shift_mlp)
    before_act = low_back(jnp.dot(low(normed_two), w_up, precision=HIGHEST))
    activated = low(jax.nn.gelu(before_act, approximate=False))
    residual_two = residual_one + low_back(jnp.dot(activated, w_down, precision=HIGHEST))
    distance = residual_two - target
    count_all = jnp.sum(weight_mask)
    loss_value = jnp.sum(weight_mask * lax.optimization_barrier(jnp.sum(distance * distance, axis=-1))) / (count_all * D)
    return (residual_two, loss_value)

def reference(words, teacher, valid, lengths, deal, gain_attn, shift_attn, w_qkv, w_out, gain_mlp, shift_mlp, w_up, w_down):
    places, sequence = word_places(lengths)
    inputs = to_initial(words.astype(jnp.float32), deal)
    target = to_initial(teacher.astype(jnp.float32), deal)
    weight_mask = to_initial(valid, deal).astype(jnp.float32)
    params = (inputs, gain_attn.astype(jnp.float32), shift_attn.astype(jnp.float32), w_qkv.astype(jnp.float32), w_out.astype(jnp.float32), gain_mlp.astype(jnp.float32), shift_mlp.astype(jnp.float32), w_up.astype(jnp.float32), w_down.astype(jnp.float32))

    def objective(*values):
        return forward(*values, target, weight_mask, places, sequence)
    (residual_two, loss_value), pullback = jax.vjp(objective, *params)
    grads = pullback((jnp.zeros_like(residual_two), jnp.asarray(LOSS_SCALE, dtype=loss_value.dtype)))
    layer_out = to_dealt(residual_two, deal).astype(jnp.bfloat16)
    grad_words = to_dealt(grads[0], deal)
    return (layer_out, loss_value, grad_words, grads[1], grads[2], grads[3], grads[4], grads[5], grads[6], grads[7], grads[8])
```

```python
import jax
import jax.numpy as jnp
from jax import lax
from jax.experimental import pallas as pl
from jax.experimental.pallas import tpu as pltpu
from jax.sharding import PartitionSpec as P

H = 8
HEAD = 64
EPS = 1e-05
LOSS_SCALE = 262144.0
CTX_HEADS = 4
WT_HEADS = 2
CHUNK = 512
TILE = 16
F32 = jnp.float32
BF16 = jnp.bfloat16
NEG = -1e30
NT = (((1,), (1,)), ((), ()))
TN = (((0,), (0,)), ((), ()))
NN = (((1,), (0,)), ((), ()))


def mm(a, b, dims=NN):
    return lax.dot_general(a, b, dims, preferred_element_type=F32)


def lane_iota(shape):
    return lax.broadcasted_iota(jnp.int32, shape, len(shape) - 1)


def norm_stats(values):
    center = values - jnp.mean(values, axis=-1, keepdims=True)
    inverse = lax.rsqrt(jnp.mean(center * center, axis=-1, keepdims=True) + EPS)
    return center * inverse, inverse


def norm_back(upstream, unit, inverse, gain):
    scaled = upstream * gain
    inner = jnp.mean(scaled * unit, axis=-1, keepdims=True)
    return inverse * (scaled - jnp.mean(scaled, axis=-1, keepdims=True) - unit * inner)


SMEM = pl.BlockSpec(memory_space=pltpu.SMEM)
VMEM = pl.BlockSpec(memory_space=pltpu.VMEM)
ANY = pl.BlockSpec(memory_space=pl.ANY)


def call(body, name, ins, in_specs, outs, scratch=(), flops=0, trans=0, out_specs=None):
    nbytes = sum(x.size * x.dtype.itemsize for x in list(ins) + list(outs))
    return pl.pallas_call(
        body,
        name=name,
        out_shape=list(outs),
        in_specs=in_specs,
        out_specs=out_specs or [VMEM] * len(outs),
        scratch_shapes=list(scratch),
        compiler_params=pltpu.CompilerParams(vmem_limit_bytes=58 * 1024 * 1024),
        cost_estimate=pl.CostEstimate(flops=flops, bytes_accessed=nbytes, transcendentals=trans),
    )(*ins)


def sds(shape, dtype):
    return jax.ShapeDtypeStruct(shape, dtype)


class Plan:
    def __init__(self, n_ctx, n_wt):
        self.n_ctx, self.n_wt = n_ctx, n_wt
        ac, aw = CTX_HEADS, WT_HEADS
        assert ac * aw == H and n_ctx % ac == 0 and n_wt % aw == 0
        self.peers = [(mc, mw) for mw in range(aw) for mc in range(0, ac, 2)]
        self.slots = [(mc | k, mw) for k in (0, 1) for mc, mw in self.peers]
        self.groups = [(mc, mw) for mc in range(0, n_ctx, ac) for mw in range(0, n_wt, aw)]
        self.all_slots = [(gc ^ sc, gw ^ sw) for gc, gw in self.groups for sc, sw in self.slots]

    def head(self, ctx, wt):
        return (wt % WT_HEADS) * CTX_HEADS + ctx % CTX_HEADS

    def swap(self, x, mask):
        mc, mw = mask
        n = self.n_wt
        perm = [
            (c * n + w, (c ^ mc) * n + (w ^ mw)) for c in range(self.n_ctx) for w in range(n)
        ]
        return lax.ppermute(x, ("ctx", "wt"), perm)


def project_body(plan, shard, blk):
    ns, nw = len(plan.slots), plan.n_wt

    def body(info, *refs):
        xs, wps = refs[:ns], refs[ns : ns + nw]
        q_ref, kv_ref, normed_ref, wh_ref, vec_ref = refs[ns + nw :]
        wt = info[1]
        for m in range(nw):
            row = pl.multiple_of((wt ^ m) * shard, shard)
            wh_ref[pl.ds(row, shard), :] = wps[m][...]
        weight = wh_ref[...]
        rows = lax.broadcasted_iota(jnp.int32, (8, 4 * HEAD), 0)
        pick = jnp.where(lane_iota((8, 4 * HEAD)) == rows + 3 * HEAD, 1.0, 0.0).astype(BF16)
        vecs = mm(pick, weight, NT)
        vec_ref[...] = vecs
        gain, shift = vecs[0:1], vecs[1:2]
        low = lane_iota((blk, 2 * HEAD)) < HEAD
        for s in range(ns):
            unit, _ = norm_stats(xs[s][...].astype(F32))
            normed = (unit * gain + shift).astype(BF16)
            normed_ref[s] = normed
            y = mm(normed, weight)
            q_ref[s] = (
                jnp.where(low, y[:, : 2 * HEAD], 0.0).astype(BF16).astype(F32) * HEAD**-0.5
            ).astype(BF16)
            kv_ref[s] = pltpu.roll(y, 3 * HEAD, 1)[:, : 2 * HEAD].astype(BF16)

    return body


def fill_slots(plan, info, deal, slot_of):
    for s, (mc, mw) in enumerate(plan.all_slots):
        slot_of[deal[(info[0] ^ mc) * plan.n_wt + (info[1] ^ mw)]] = s


def slot_range(plan, info, deal, lengths, codes, i, blk, nseq):
    code = codes[i]
    here = deal[(info[0] ^ (code // plan.n_wt)) * plan.n_wt + (info[1] ^ (code % plan.n_wt))]
    first = jnp.int32(0)
    total = jnp.int32(0)
    for n in range(nseq):
        total = total + lengths[n]
        bound = total // blk
        first = jnp.where(bound <= here, bound, first)
    return first, here


def load_kv(kv_refs, kvs, sem, ns):
    copies = [
        pltpu.make_async_copy(ref, kvs.at[pl.ds(b * ns, ns)], sem.at[b])
        for b, ref in enumerate(kv_refs)
    ]
    for c in copies:
        c.start()
    for c in copies:
        c.wait()


def attend_body(plan, blk, nseq):
    ns, nb = len(plan.slots), len(plan.groups)

    def body(info, deal, lengths, codes, q_ref, *refs):
        kv_refs = refs[:nb]
        o_ref, of_ref, lse_ref = refs[nb : nb + 3]
        kvs, slot_of, acc_ref, m_ref, l_ref, sem = refs[nb + 3 :]
        load_kv(kv_refs, kvs, sem, ns)
        fill_slots(plan, info, deal, slot_of)
        core = info[0] % 2
        tri = lax.broadcasted_iota(jnp.int32, (blk, blk), 0) <= lane_iota((blk, blk))

        def one_block(i, _):
            first, here = slot_range(plan, info, deal, lengths, codes, i, blk, nseq)
            q = q_ref[i]
            kv = kvs[slot_of[here]]
            s = jnp.where(tri, mm(kv, q, NT), NEG)
            m = jnp.max(s, axis=0, keepdims=True)
            p = jnp.exp(s - m)
            m_ref[...] = m
            l_ref[...] = jnp.sum(p, axis=0, keepdims=True)
            acc_ref[...] = mm(kv, p.astype(BF16), TN)

            def step(b, _):
                kv = kvs[slot_of[b]]
                s = mm(kv, q, NT)
                m_old = m_ref[...]
                m = jnp.maximum(m_old, jnp.max(s, axis=0, keepdims=True))
                p = jnp.exp(s - m)
                factor = jnp.exp(m_old - m)
                m_ref[...] = m
                l_ref[...] = l_ref[...] * factor + jnp.sum(p, axis=0, keepdims=True)
                acc_ref[...] = acc_ref[...] * factor + mm(kv, p.astype(BF16), TN)
                return 0

            lax.fori_loop(first, here, step, 0)
            total = l_ref[...]
            lse_ref[i] = m_ref[...] + jnp.log(total)
            out = acc_ref[HEAD:, :] / total
            zero = jnp.zeros_like(out)
            placed = jnp.concatenate(
                [jnp.where(core == 0, out, zero), jnp.where(core == 1, out, zero)], axis=0
            )
            wide = placed.T
            of_ref[i] = wide
            o_ref[i] = wide.astype(BF16)
            return 0

        lax.fori_loop(0, ns, one_block, 0)

    return body


def attend_back_body(plan, blk, nseq):
    ns, nb, nj = len(plan.slots), len(plan.groups), len(plan.peers)

    def body(info, deal, lengths, codes, q_ref, of_ref, lse_ref, *refs):
        g_refs, gs_ref = refs[:nj], refs[nj]
        kv_refs = refs[nj + 1 : nj + 1 + nb]
        outs = refs[nj + 1 + nb :]
        dq_ref, dkv_refs = outs[0], outs[1 : 1 + nb]
        kvs, slot_of, dkvs, dq_acc, g_ext, delta_ref, sem = outs[1 + nb :]
        load_kv(kv_refs, kvs, sem, ns)
        fill_slots(plan, info, deal, slot_of)
        core = info[0] % 2
        tri = lax.broadcasted_iota(jnp.int32, (blk, blk), 0) <= lane_iota((blk, blk))
        high = lane_iota((blk, 2 * HEAD)) >= HEAD
        own_half = (lane_iota((blk, 2 * HEAD)) // HEAD) == core
        for s in range(ns):
            g = (g_refs[s][...] if s < nj else gs_ref[s - nj]).astype(F32)
            g = jnp.where(own_half, g, 0.0)
            delta_ref[s] = jnp.sum((g * of_ref[s]).T, axis=0, keepdims=True)
            turned = pltpu.roll(g, HEAD, 1)
            g_ext[s] = jnp.where(high, jnp.where(core == 1, g, turned), 0.0).astype(BF16)
        dkvs[...] = jnp.zeros_like(dkvs)

        def one_block(i, _):
            first, here = slot_range(plan, info, deal, lengths, codes, i, blk, nseq)
            q = q_ref[i]
            g = g_ext[i]
            lse = lse_ref[i]
            delta = delta_ref[i]

            def pair(b, mask):
                slot = slot_of[b]
                kv = kvs[slot]
                p = jnp.exp(mm(kv, q, NT) - lse)
                if mask:
                    p = jnp.where(tri, p, 0.0)
                ds = (p * (mm(kv, g, NT) - delta)).astype(BF16)
                dkvs[slot] += mm(ds, q) + mm(p.astype(BF16), g)
                return mm(kv, ds, TN)

            dq_acc[...] = pair(here, True)

            def step(b, _):
                dq_acc[...] += pair(b, False)
                return 0

            lax.fori_loop(first, here, step, 0)
            wide = dq_acc[...].T * HEAD**-0.5
            dq_ref[i] = jnp.where(high, 0.0, wide).astype(BF16)
            return 0

        lax.fori_loop(0, ns, one_block, 0)
        for b in range(nb):
            dkv_refs[b][...] = dkvs[b * ns : (b + 1) * ns].astype(BF16)

    return body


def mlp_body(plan, width, ff, blk, packed, pieces):
    nj, nw, nc = len(plan.peers), plan.n_wt, plan.n_ctx
    nq = ff // CHUNK

    def body(info, *refs):
        refs = list(refs)
        x_ref, teacher_ref, valid_ref, vec_ref, count_ref = refs[:5]
        att = refs[5 : 5 + nj]
        rest = refs[5 + nj :]
        nwt_in = len(pieces) if packed else 3
        w_in, rest = rest[:nwt_in], rest[nwt_in:]
        (lo_ref, sq_ref, g1_ref, gatt_ref, act_ref, gpre_ref, n2_ref, gb_ref, ga_ref, gv_ref) = (
            rest[:10]
        )
        if packed:
            wup, wdown, wout, meta, slope_ref, acc_ref, sem = rest[10:]
            copies = []
            for n, (jc, src) in enumerate(zip(pieces, w_in)):
                c = info[0] ^ jc
                for m in range(nw):
                    w = info[1] ^ m
                    copies += [
                        pltpu.make_async_copy(
                            src.at[m, pl.ds(nq + 4, 1)], wout.at[w, pl.ds(c, 1)], sem.at[0]
                        ),
                        pltpu.make_async_copy(src.at[m, pl.ds(0, nq)], wup.at[:, w, c], sem.at[1]),
                        pltpu.make_async_copy(
                            src.at[m, pl.ds(nq, 4)], wdown.at[w, pl.ds(c * 4, 4)], sem.at[2]
                        ),
                        pltpu.make_async_copy(
                            src.at[m, pl.ds(nq + 5, 1)], meta.at[w, pl.ds(c, 1)], sem.at[3]
                        ),
                    ]
            for cp in copies:
                cp.start()
            for cp in copies:
                cp.wait()
            w_up = lambda q: wup[q].reshape(width, CHUNK)
            w_down = lambda q: wdown[q].reshape(CHUNK, width)
            out_rows = width // nw
            pair_rows = 2 * HEAD
            wout_flat = wout.reshape(width, width)
            w_out = lambda row: wout_flat[pl.ds(row, pair_rows), :]
            count = jnp.sum(meta[:, :, 0:1, 0:1].astype(F32))
        else:
            slope_ref, acc_ref = rest[10:]
            w_up = lambda q: w_in[0][q]
            w_down = lambda q: w_in[1][q]
            w_out = lambda row: w_in[2][pl.ds(row, 2 * HEAD), :]
            count = count_ref[0]
        vecs = vec_ref[...]
        gain, shift = vecs[2:3], vecs[3:4]
        rows = []
        for mc, mw in plan.peers:
            head = plan.head(info[0] ^ mc, info[1] ^ mw)
            rows.append(pl.multiple_of((head // 2) * (2 * HEAD), 2 * HEAD))
        mixed = mm(att[0][...], w_out(rows[0]))
        for j in range(1, nj):
            mixed = mixed + mm(att[j][...], w_out(rows[j]))
        res = mixed + x_ref[...].astype(F32)
        unit, inverse = norm_stats(res)
        n2 = (unit * gain + shift).astype(BF16)
        n2_ref[...] = n2
        for q in range(nq):
            pre = mm(n2, w_up(q))
            cdf = 0.5 * (1.0 + lax.erf(pre * 0.7071067811865476))
            pdf = jnp.exp(-0.5 * pre * pre) * 0.3989422804014327
            act = (pre * cdf).astype(BF16)
            slope_ref[q] = cdf + pre * pdf
            act_ref[q] = act
            if q == 0:
                acc_ref[...] = mm(act, w_down(q))
            else:
                acc_ref[...] += mm(act, w_down(q))
        two = acc_ref[...] + res
        lo_ref[...] = two.astype(BF16)
        distance = two - teacher_ref[...].astype(F32)
        valid = valid_ref[...].astype(F32)
        weighed = valid * distance
        square = jnp.sum(weighed * distance)
        first_row = lax.broadcasted_iota(jnp.int32, (8, 128), 0) == 0
        sq_ref[...] = jnp.where(first_row, square, count)
        g2 = (2.0 * LOSS_SCALE / (count * width)) * weighed
        gb = g2.astype(BF16)
        gb_ref[...] = gb
        for q in range(nq):
            gpre = (mm(gb, w_down(q), NT) * slope_ref[q]).astype(BF16)
            gpre_ref[q] = gpre
            if q == 0:
                acc_ref[...] = mm(gpre, w_up(q), NT)
            else:
                acc_ref[...] += mm(gpre, w_up(q), NT)
        gn2 = acc_ref[...]
        g1 = g2 + norm_back(gn2, unit, inverse, gain)
        g1_ref[...] = g1
        gv_ref[...] = jnp.concatenate(
            [
                jnp.sum(gn2 * unit, axis=0, keepdims=True),
                jnp.sum(gn2, axis=0, keepdims=True),
                jnp.zeros((6, width), F32),
            ],
            axis=0,
        )
        ga = g1.astype(BF16)
        ga_ref[...] = ga
        for j in range(nj):
            gatt_ref[j] = mm(ga, w_out(rows[j]), NT).astype(BF16)

    return body


def mlp_grads_body(plan, width, ff, blk, packed):
    nj, nw, nc = len(plan.peers), plan.n_wt, plan.n_ctx
    nq = ff // CHUNK

    def body(info, act_ref, gpre_ref, n2_ref, gb_ref, ga_ref, gv_ref, sq_ref, *refs):
        att, outs = refs[:nj], refs[nj:]
        n2, gb, ga = n2_ref[...], gb_ref[...], ga_ref[...]
        ctx, wt = info[0], info[1]
        if packed:
            out_ref = outs[0]
            rows_up = width // (nw * nc)

        for q in range(nq):
            up = mm(n2, gpre_ref[q], TN).astype(BF16)
            down = mm(act_ref[q], gb, TN).astype(BF16)
            if packed:
                up_t = up.reshape(nw, nc, rows_up, CHUNK)
                down_t = down.reshape(nc, 4, TILE, width)
                for w in range(nw):
                    for c in range(nc):
                        put_tile(out_ref, info, c, w, q, up_t[w, c])
                for c in range(nc):
                    for t in range(4):
                        put_tile(out_ref, info, c, q, nq + t, down_t[c, t])
            else:
                outs[0][q] = up
                outs[1][q] = down
        for j, (mc, mw) in enumerate(plan.peers):
            head = plan.head(ctx ^ mc, wt ^ mw)
            part = mm(att[j][...], ga, TN).astype(BF16)
            if packed:
                per = width // nw
                part_t = part.reshape(2 * HEAD // TILE, TILE, width)
                base = (head // 2) * (2 * HEAD // TILE)
                for t in range(2 * HEAD // TILE):
                    at = base + t
                    w, c = at // nc, at % nc
                    put_tile(out_ref, info, c, w, nq + 4, part_t[t])
            else:
                row = pl.multiple_of((head // 2) * (2 * HEAD), 2 * HEAD)
                outs[2][pl.ds(row, 2 * HEAD), :] = part
        if packed:
            dev = ctx * nw + wt
            square = sq_ref[0:1, 0:1]
            high = square.astype(BF16).astype(F32)
            lane = lane_iota((1, CHUNK))
            n_dev = nw * nc
            line = jnp.where(lane == dev, high, 0.0) + jnp.where(
                lane == dev + n_dev, square - high, 0.0
            )
            for w in range(nw):
                per = width // nw
                vec = gv_ref[0:2, per * w : per * (w + 1)]
                vec = jnp.concatenate([vec, jnp.zeros((2, CHUNK - per), F32)], axis=1)
                tile = jnp.concatenate([line, vec, jnp.zeros((TILE - 3, CHUNK), F32)], axis=0)
                tile = tile.astype(BF16)
                for c in range(nc):
                    put_tile(out_ref, info, c, w, nq + 5, tile)

    return body


def put_tile(out_ref, info, c, w, tile, value):
    jc = c ^ info[0]
    out_ref[jc, w ^ info[1], tile] = value


def head_grads_body(plan, blk, width, shard):
    ns, nb, nw, nj = len(plan.slots), len(plan.groups), plan.n_wt, len(plan.peers)

    def body(info, dq_ref, wh_ref, normed_ref, *refs):
        xs = refs[:ns]
        parts = refs[ns : ns + nb]
        outs = refs[ns + nb :]
        own_ref, sib_ref, dw_refs = outs[0], outs[1], outs[2 : 2 + nw]
        acc = outs[2 + nw]
        weight = wh_ref[...]
        gsum = jnp.zeros((1, width), F32)
        ssum = jnp.zeros((1, width), F32)
        for s in range(ns):
            dkv = parts[0][s].astype(F32)
            for b in range(1, nb):
                dkv = dkv + parts[b][s].astype(F32)
            zero = jnp.zeros((blk, 2 * HEAD), F32)
            wide = pltpu.roll(jnp.concatenate([dkv, zero], axis=1), HEAD, 1)
            wide = wide + jnp.concatenate([dq_ref[s].astype(F32), zero], axis=1)
            gh = wide.astype(BF16)
            back = mm(gh, weight, NT)
            if s < nj:
                own_ref[s] = back.astype(BF16)
            else:
                sib_ref[s - nj] = back.astype(BF16)
            unit, _ = norm_stats(xs[s][...].astype(F32))
            gsum = gsum + jnp.sum(back * unit, axis=0, keepdims=True)
            ssum = ssum + jnp.sum(back, axis=0, keepdims=True)
            dw = mm(normed_ref[s], gh, TN)
            if s == 0:
                acc[...] = dw
            else:
                acc[...] += dw
        vecs = jnp.concatenate([gsum, ssum, jnp.zeros((6, width), F32)], axis=0).astype(BF16)
        rows = lax.broadcasted_iota(jnp.int32, (8, 4 * HEAD), 0)
        pick = jnp.where(lane_iota((8, 4 * HEAD)) == rows + 3 * HEAD, 1.0, 0.0).astype(BF16)
        acc[...] += mm(vecs, pick, TN)
        for m in range(nw):
            row = pl.multiple_of((info[1] ^ m) * shard, shard)
            dw_refs[m][...] = acc[pl.ds(row, shard), :].astype(BF16)

    return body


def words_body(nj):
    def body(x_ref, vec_ref, g1_ref, *refs):
        parts, sibs, out_ref = refs[:nj], refs[nj : 2 * nj], refs[-1]
        up = parts[0][...].astype(F32)
        for p in parts[1:]:
            up = up + p[...].astype(F32)
        unit, inverse = norm_stats(x_ref[...].astype(F32))
        out_ref[...] = g1_ref[...] + norm_back(up, unit, inverse, vec_ref[0:1, :])

    return body


def unpack_body(plan, width, ff, pieces):
    nq, nw, nc = ff // CHUNK, plan.n_wt, plan.n_ctx

    def body(info, *refs):
        srcs, outs = refs[: len(pieces)], refs[len(pieces) :]
        up_ref, down_ref, out_ref, meta_ref = outs
        for jc, src in zip(pieces, srcs):
            c = info[0] ^ jc
            row = pl.multiple_of(c * TILE, TILE)
            for q in range(nq):
                up_ref[pl.ds(row, TILE), q * CHUNK : (q + 1) * CHUNK] = src[q].astype(F32)
            for t in range(4):
                down_ref[pl.ds(pl.multiple_of(c * 4 * TILE + t * TILE, TILE), TILE), :] = src[
                    nq + t
                ].astype(F32)
            out_ref[pl.ds(row, TILE), :] = src[nq + 4].astype(F32)
        meta = srcs[0][nq + 5].astype(F32)
        meta_ref[...] = meta

    return body


def head_out_body(plan, shard):
    def body(info, *refs):
        srcs, (out_ref, vec_ref) = refs[:H], refs[H:]
        core = info[0] % 2
        total = srcs[0][...].astype(F32)
        for s in srcs[1:]:
            total = total + s[...].astype(F32)
        rows = lax.broadcasted_iota(jnp.int32, (8, 4 * HEAD), 0)
        pick = jnp.where(lane_iota((8, 4 * HEAD)) == rows + 3 * HEAD, 1.0, 0.0)
        vec_ref[...] = lax.dot_general(
            pick, total, NT, precision=lax.Precision.HIGHEST, preferred_element_type=F32
        )
        nj = len(plan.peers)
        for j, (mc, mw) in enumerate(plan.peers):
            head = plan.head(info[0] ^ mc, info[1] ^ mw)
            own = srcs[j][...].astype(F32)
            sib = srcs[nj + j][...].astype(F32)
            even = jnp.where(core == 0, own, sib)
            odd = jnp.where(core == 0, sib, own)
            turned = pltpu.roll(odd, 3 * HEAD, 1)
            lane = lane_iota((shard, 2 * HEAD))
            mid = jnp.where(lane < HEAD, even[:, 2 * HEAD :], turned[:, 2 * HEAD :])
            last = turned[:, : 2 * HEAD]
            col = pl.multiple_of((head // 2) * (6 * HEAD), 2 * HEAD)
            out_ref[:, pl.ds(col, 2 * HEAD)] = even[:, : 2 * HEAD]
            out_ref[:, pl.ds(col + 2 * HEAD, 2 * HEAD)] = mid
            out_ref[:, pl.ds(col + 4 * HEAD, 2 * HEAD)] = last

    return body


def per_device(
    words,
    teacher,
    valid,
    lengths,
    deal,
    gain_attn,
    shift_attn,
    w_qkv,
    w_out,
    gain_mlp,
    shift_mlp,
    w_up,
    w_down,
):
    n_ctx, n_wt = lax.axis_size("ctx"), lax.axis_size("wt")
    plan = Plan(n_ctx, n_wt)
    ctx, wt = lax.axis_index("ctx"), lax.axis_index("wt")
    blk, width = words.shape
    shard = width // n_wt
    ff = w_up.shape[1]
    nq = ff // CHUNK
    nseq = lengths.shape[0]
    ns, nb, nj = len(plan.slots), len(plan.groups), len(plan.peers)
    packed = width == CHUNK and width % (n_wt * n_ctx * TILE) == 0 and n_wt * CHUNK == ff
    info = jnp.stack([ctx, wt]).astype(jnp.int32)
    codes = jnp.array([mc * n_wt + mw for mc, mw in plan.slots], jnp.int32)
    core = (1, 0)

    xs = [words] + [plan.swap(words, m) for m in plan.peers[1:]]
    vec_cols = jnp.stack([gain_attn, shift_attn, gain_mlp, shift_mlp], axis=1)
    vec_cols = jnp.pad(vec_cols, ((0, 0), (0, HEAD - 4)))

    def head_cols(m):
        head = plan.head(ctx, wt ^ m)
        cols = lax.dynamic_slice_in_dim(w_qkv, head * 3 * HEAD, 3 * HEAD, 1)
        return jnp.concatenate([cols, vec_cols], axis=1)

    w_parts = [plan.swap(head_cols(m), (0, m)) for m in range(1, n_wt)]
    w_parts = [head_cols(0)] + w_parts
    xs = xs + [plan.swap(x, core) for x in xs]

    q, kv, normed, w_head, vecs = call(
        project_body(plan, shard, blk),
        "project",
        [info] + xs + w_parts,
        [SMEM] + [VMEM] * (ns + n_wt),
        [
            sds((ns, blk, 2 * HEAD), BF16),
            sds((ns, blk, 2 * HEAD), BF16),
            sds((ns, blk, width), BF16),
            sds((width, 4 * HEAD), BF16),
            sds((8, width), F32),
        ],
        flops=2 * ns * blk * width * 4 * HEAD,
    )
    kvs = [kv] + [plan.swap(kv, m) for m in plan.groups[1:]]

    if packed:
        rows_up = width // (n_wt * n_ctx)
        up_piece = lax.dynamic_slice_in_dim(w_up, ctx * rows_up, rows_up, 0)
        up_piece = up_piece.reshape(rows_up, nq, CHUNK).transpose(1, 0, 2)
        down_piece = lax.dynamic_slice_in_dim(w_down, ctx * 4 * TILE, 4 * TILE, 0)
        out_piece = lax.dynamic_slice_in_dim(w_out, ctx * TILE, TILE, 0)
        count_here = jnp.sum(valid).astype(BF16)
        piece = jnp.concatenate(
            [
                up_piece,
                down_piece.reshape(4, TILE, CHUNK),
                out_piece[None],
                jnp.full((1, TILE, CHUNK), count_here, BF16),
            ],
            axis=0,
        )
        piece, _ = lax.optimization_barrier((piece, q))
        stack = jnp.stack([piece] + [plan.swap(piece, (0, m)) for m in range(1, n_wt)])
        planes = [2 * p for p in range(n_ctx // 2)]
        stacks = [stack] + [plan.swap(stack, (p, 0)) for p in planes[1:]]
        stacks = stacks + [plan.swap(s, core) for s in stacks]
        piece_ids = planes + [p + 1 for p in planes]
        weights = stacks
        count = jnp.zeros((1,), F32)
    else:
        piece_ids = []
        up_full = lax.all_gather(w_up, "wt", axis=0, tiled=True)
        down_full = lax.all_gather(w_down, "wt", axis=0, tiled=True)
        out_full = lax.all_gather(w_out, "wt", axis=0, tiled=True)
        weights = [
            up_full.reshape(width, nq, CHUNK).transpose(1, 0, 2),
            down_full.reshape(nq, CHUNK, width),
            out_full,
        ]
        count = lax.psum(jnp.sum(valid).astype(F32), ("ctx", "wt")).reshape(1)

    pairs = ns * nb * ns // 4
    o, of32, lse = call(
        attend_body(plan, blk, nseq),
        "attend",
        [info, deal, lengths, codes, q] + kvs,
        [SMEM] * 4 + [VMEM] + [ANY] * nb,
        [
            sds((ns, blk, 2 * HEAD), BF16),
            sds((ns, blk, 2 * HEAD), F32),
            sds((ns, 1, blk), F32),
        ],
        scratch=[
            pltpu.VMEM((nb * ns, blk, 2 * HEAD), BF16),
            pltpu.SMEM((n_ctx * n_wt,), jnp.int32),
            pltpu.VMEM((2 * HEAD, blk), F32),
            pltpu.VMEM((1, blk), F32),
            pltpu.VMEM((1, blk), F32),
            pltpu.SemaphoreType.DMA((nb,)),
        ],
        flops=pairs * 4 * blk * blk * 128,
        trans=pairs * blk * blk,
    )
    mixed = o[:nj] + plan.swap(o[nj:], core)
    att = [mixed[0]] + [plan.swap(mixed[j], plan.peers[j]) for j in range(1, nj)]

    mlp_in = [info, words, teacher, valid[:, None], vecs, count] + att + weights
    specs = [SMEM] + [VMEM] * 4 + [SMEM] + [VMEM] * nj
    specs += [ANY] * len(weights) if packed else [VMEM] * len(weights)
    scratch = [pltpu.VMEM((nq, blk, CHUNK), F32), pltpu.VMEM((blk, width), F32)]
    if packed:
        scratch = [
            pltpu.VMEM((nq, n_wt, n_ctx, TILE, CHUNK), BF16),
            pltpu.VMEM((n_wt, n_ctx * 4, TILE, CHUNK), BF16),
            pltpu.VMEM((n_wt, n_ctx, TILE, CHUNK), BF16),
            pltpu.VMEM((n_wt, n_ctx, TILE, CHUNK), BF16),
            *scratch,
            pltpu.SemaphoreType.DMA((4,)),
        ]
    layer_out, square, grad_one, gatt, act, gpre, n2, gb, ga, gvec = call(
        mlp_body(plan, width, ff, blk, packed, piece_ids),
        "mlp",
        mlp_in,
        specs,
        [
            sds((blk, width), BF16),
            sds((8, 128), F32),
            sds((blk, width), F32),
            sds((nj, blk, 2 * HEAD), BF16),
            sds((nq, blk, CHUNK), BF16),
            sds((nq, blk, CHUNK), BF16),
            sds((blk, width), BF16),
            sds((blk, width), BF16),
            sds((blk, width), BF16),
            sds((8, width), F32),
        ],
        scratch=scratch,
        flops=8 * blk * width * ff,
        trans=2 * blk * ff,
    )
    g_own = [gatt[0]] + [plan.swap(gatt[j], plan.peers[j]) for j in range(1, nj)]
    g_sib = plan.swap(jnp.stack(g_own), core)

    grads_in = [info, act, gpre, n2, gb, ga, gvec, square] + att
    if packed:
        grads_out = [sds((n_ctx, n_wt, nq + 6, TILE, CHUNK), BF16)]
    else:
        grads_out = [
            sds((nq, width, CHUNK), BF16),
            sds((nq, CHUNK, width), BF16),
            sds((width, width), BF16),
        ]
    weight_grads = call(
        mlp_grads_body(plan, width, ff, blk, packed),
        "mlp_grads",
        grads_in,
        [SMEM] + [VMEM] * (7 + nj),
        grads_out,
        flops=4 * blk * width * ff,
    )

    back = call(
        attend_back_body(plan, blk, nseq),
        "attend_back",
        [info, deal, lengths, codes, q, of32, lse] + g_own + [g_sib] + kvs,
        [SMEM] * 4 + [VMEM] * (3 + nj + 1) + [ANY] * nb,
        [sds((ns, blk, 2 * HEAD), BF16)] + [sds((ns, blk, 2 * HEAD), BF16)] * nb,
        scratch=[
            pltpu.VMEM((nb * ns, blk, 2 * HEAD), BF16),
            pltpu.SMEM((n_ctx * n_wt,), jnp.int32),
            pltpu.VMEM((nb * ns, blk, 2 * HEAD), F32),
            pltpu.VMEM((2 * HEAD, blk), F32),
            pltpu.VMEM((ns, blk, 2 * HEAD), BF16),
            pltpu.VMEM((ns, 1, blk), F32),
            pltpu.SemaphoreType.DMA((nb,)),
        ],
        flops=pairs * 10 * blk * blk * 128,
        trans=pairs * blk * blk,
    )
    dq, dkvs = back[0], back[1:]
    parts = [dkvs[0]] + [plan.swap(dkvs[b], plan.groups[b]) for b in range(1, nb)]

    outs = call(
        head_grads_body(plan, blk, width, shard),
        "head_grads",
        [info, dq, w_head, normed] + xs + parts,
        [SMEM] + [VMEM] * (3 + ns + nb),
        [sds((nj, blk, width), BF16)] * 2 + [sds((shard, 4 * HEAD), BF16)] * n_wt,
        scratch=[pltpu.VMEM((width, 4 * HEAD), F32)],
        flops=4 * ns * blk * width * 4 * HEAD,
    )
    own_rows, sib_rows, dw = outs[0], outs[1], outs[2:]
    rows = (own_rows.astype(F32) + plan.swap(sib_rows, core).astype(F32)).astype(BF16)
    up_rows = [rows[0]] + [plan.swap(rows[j], plan.peers[j]) for j in range(1, nj)]
    grad_words = call(
        words_body(nj),
        "words_grad",
        [words, vecs, grad_one] + up_rows,
        [VMEM] * (3 + nj),
        [sds((blk, width), F32)],
    )[0]

    dw = [dw[0]] + [plan.swap(dw[m], (0, m)) for m in range(1, n_wt)]
    merged = []
    for a in range(WT_HEADS):
        total = dw[a].astype(F32)
        for m in range(a + WT_HEADS, n_wt, WT_HEADS):
            total = total + dw[m].astype(F32)
        merged.append(total)
    heads = jnp.stack(merged).astype(BF16)
    step = CTX_HEADS
    while step < n_ctx:
        heads = (heads.astype(F32) + plan.swap(heads, (step, 0)).astype(F32)).astype(BF16)
        step *= 2
    cols = [heads]
    for mc in range(2, CTX_HEADS, 2):
        cols.append(plan.swap(heads, (mc, 0)))
    own_heads = jnp.stack(cols, axis=1)
    sib_heads = plan.swap(own_heads, core)
    srcs = [own_heads[a, p] for a in range(WT_HEADS) for p in range(CTX_HEADS // 2)]
    srcs += [sib_heads[a, p] for a in range(WT_HEADS) for p in range(CTX_HEADS // 2)]
    g_qkv, gvec_attn = call(
        head_out_body(plan, shard),
        "head_out",
        [info] + srcs,
        [SMEM] + [VMEM] * H,
        [sds((shard, 3 * width), F32), sds((8, shard), F32)],
    )

    if packed:
        g_all = weight_grads[0].reshape(n_ctx // 2, 2, n_wt, nq + 6, TILE, CHUNK)
        half = (g_all[:, 0].astype(F32) + plan.swap(g_all[:, 1], core).astype(F32)).astype(BF16)
        total = half[0].astype(F32)
        for p in range(1, n_ctx // 2):
            total = total + plan.swap(half[p], (2 * p, 0)).astype(F32)
        total = total.astype(BF16)
        final = total[0].astype(F32)
        for m in range(1, n_wt):
            final = final + plan.swap(total[m], (0, m)).astype(F32)
        final = final.astype(BF16)
        finals = [final] + [plan.swap(final, (p, 0)) for p in planes[1:]]
        finals_sib = plan.swap(jnp.stack(finals), core)
        finals = finals + [finals_sib[p] for p in range(n_ctx // 2)]
        g_up, g_down, g_out, meta = call(
            unpack_body(plan, width, ff, piece_ids),
            "unpack",
            [info] + finals,
            [SMEM] + [VMEM] * len(finals),
            [
                sds((shard, ff), F32),
                sds((ff // n_wt, width), F32),
                sds((shard, width), F32),
                sds((TILE, CHUNK), F32),
            ],
        )
        square_all = jnp.sum(meta[0])
        g_gain, g_shift = meta[1, :shard], meta[2, :shard]
        count_all = square[1, 0]
    else:
        g_up, g_down, g_out = weight_grads
        g_up = g_up.transpose(1, 0, 2).reshape(width, ff)
        g_down = g_down.reshape(ff, width)

        def reduce_rows(g):
            part = lax.psum_scatter(g.astype(BF16), "wt", scatter_dimension=0, tiled=True)
            return lax.psum(part, "ctx").astype(F32)

        g_up, g_down, g_out = reduce_rows(g_up), reduce_rows(g_down), reduce_rows(g_out)
        both = lax.psum(gvec[:2], ("ctx", "wt"))
        both = lax.dynamic_slice_in_dim(both, wt * shard, shard, 1)
        g_gain, g_shift = both[0], both[1]
        count_all = count[0]
        square_all = lax.psum(square[0, 0], ("ctx", "wt"))
    loss = square_all / (count_all * width)
    return (
        layer_out,
        loss,
        grad_words,
        gvec_attn[0],
        gvec_attn[1],
        g_qkv,
        g_out,
        g_gain,
        g_shift,
        g_up,
        g_down,
    )


def solution(mesh):
    placed = (
        P(("ctx", "wt"), None),
        P(("ctx", "wt"), None),
        P(("ctx", "wt")),
        P(),
        P(),
        P("wt"),
        P("wt"),
        P("wt", None),
        P("wt", None),
        P("wt"),
        P("wt"),
        P("wt", None),
        P("wt", None),
    )
    return jax.shard_map(
        per_device,
        mesh=mesh,
        in_specs=placed,
        out_specs=(
            P(("ctx", "wt"), None),
            P(),
            P(("ctx", "wt"), None),
            P("wt"),
            P("wt"),
            P("wt", None),
            P("wt", None),
            P("wt"),
            P("wt"),
            P("wt", None),
            P("wt", None),
        ),
        check_vma=False,
    )
```

```python
import jax
import jax.numpy as jnp
from jax import lax
from jax.experimental import pallas as pl
from jax.experimental.pallas import tpu as pltpu
from jax.sharding import PartitionSpec as P

H = 8
HEAD = 64
EPS = 1e-05
LOSS_SCALE = 262144.0
CTX_HEADS = 2
WT_HEADS = 4
CHUNK = 512
TILE = 16
F32 = jnp.float32
BF16 = jnp.bfloat16
NEG = -1e30
NT = (((1,), (1,)), ((), ()))
TN = (((0,), (0,)), ((), ()))
NN = (((1,), (0,)), ((), ()))


def mm(a, b, dims=NN):
    return lax.dot_general(a, b, dims, preferred_element_type=F32)


def lane_iota(shape):
    return lax.broadcasted_iota(jnp.int32, shape, len(shape) - 1)


def norm_stats(values):
    center = values - jnp.mean(values, axis=-1, keepdims=True)
    inverse = lax.rsqrt(jnp.mean(center * center, axis=-1, keepdims=True) + EPS)
    return center * inverse, inverse


def norm_back(upstream, unit, inverse, gain):
    scaled = upstream * gain
    inner = jnp.mean(scaled * unit, axis=-1, keepdims=True)
    return inverse * (scaled - jnp.mean(scaled, axis=-1, keepdims=True) - unit * inner)


SMEM = pl.BlockSpec(memory_space=pltpu.SMEM)
VMEM = pl.BlockSpec(memory_space=pltpu.VMEM)
ANY = pl.BlockSpec(memory_space=pl.ANY)


def call(body, name, ins, in_specs, outs, scratch=(), flops=0, trans=0, out_specs=None):
    nbytes = sum(x.size * x.dtype.itemsize for x in list(ins) + list(outs))
    return pl.pallas_call(
        body,
        name=name,
        out_shape=list(outs),
        in_specs=in_specs,
        out_specs=out_specs or [VMEM] * len(outs),
        scratch_shapes=list(scratch),
        compiler_params=pltpu.CompilerParams(vmem_limit_bytes=58 * 1024 * 1024),
        cost_estimate=pl.CostEstimate(flops=flops, bytes_accessed=nbytes, transcendentals=trans),
    )(*ins)


def sds(shape, dtype):
    return jax.ShapeDtypeStruct(shape, dtype)


class Plan:
    def __init__(self, n_ctx, n_wt):
        self.n_ctx, self.n_wt = n_ctx, n_wt
        ac, aw = CTX_HEADS, WT_HEADS
        assert ac * aw == H and n_ctx % ac == 0 and n_wt % aw == 0
        self.peers = [(mc, mw) for mw in range(aw) for mc in range(0, ac, 2)]
        self.slots = [(mc | k, mw) for k in (0, 1) for mc, mw in self.peers]
        self.groups = [(mc, mw) for mc in range(0, n_ctx, ac) for mw in range(0, n_wt, aw)]
        self.square = n_ctx == 8 and n_wt == aw

    def near(self, core):
        return [0, 2 + 2 * core, 4 - 2 * core, 6]

    def group_masks(self, core):
        return [(m, 0) for m in self.near(core)] if self.square else self.groups

    def head(self, ctx, wt):
        return (wt % WT_HEADS) * CTX_HEADS + ctx % CTX_HEADS

    def swap(self, x, mask):
        mc, mw = mask
        n = self.n_wt
        perm = [
            (c * n + w, (c ^ mc) * n + (w ^ mw)) for c in range(self.n_ctx) for w in range(n)
        ]
        return lax.ppermute(x, ("ctx", "wt"), perm)

    def turn(self, x, first):
        n = self.n_wt
        masks = (2, 4) if first else (4, 2)
        perm = [
            (c * n + w, (c ^ masks[c % 2]) * n + w) for c in range(self.n_ctx) for w in range(n)
        ]
        return lax.ppermute(x, ("ctx", "wt"), perm)

    def gather_square(self, x):
        one = self.turn(x, True)
        return [x, one, self.turn(x, False), self.turn(one, False)]

    def gather_groups(self, x):
        if self.square:
            return self.gather_square(x)
        return [x] + [self.swap(x, m) for m in self.groups[1:]]


def pack_body(plan, shard, blk):
    nw, half = plan.n_wt, shard // 2

    def body(info, words_ref, w_ref, vec_ref, *outs):
        odd = (info[0] % 2) == 1
        vec = vec_ref[...].astype(F32)
        lane = lane_iota((shard, 4 * HEAD))
        for m in range(nw):
            pair = plan.head(info[0], info[1] ^ m) // 2
            col = pl.multiple_of(pair * (6 * HEAD), 2 * HEAD)
            both = w_ref[:, pl.ds(col, 6 * HEAD)].astype(F32)
            turned = pltpu.roll(both, 3 * HEAD, 1)
            cols = jnp.where(odd, turned[:, : 4 * HEAD], both[:, : 4 * HEAD])
            cols = jnp.where(lane < 3 * HEAD, cols, vec).astype(BF16)
            outs[m][:blk, :] = words_ref[...]
            outs[m][blk:, : 4 * HEAD] = cols[:half]
            outs[m][blk:, 4 * HEAD :] = cols[half:]

    return body


def project_body(plan, shard, blk):
    ns, nw, half = len(plan.slots), plan.n_wt, shard // 2

    def body(info, *refs):
        xs, wps = refs[:ns], refs[ns : ns + nw]
        q_ref, kv_ref, normed_ref, wh_ref, vec_ref = refs[ns + nw :]
        wt = info[1]
        for m in range(nw):
            row = pl.multiple_of((wt ^ m) * shard, shard)
            wh_ref[pl.ds(row, half), :] = wps[m][blk:, : 4 * HEAD]
            wh_ref[pl.ds(row + half, half), :] = wps[m][blk:, 4 * HEAD :]
        weight = wh_ref[...]
        rows = lax.broadcasted_iota(jnp.int32, (8, 4 * HEAD), 0)
        pick = jnp.where(lane_iota((8, 4 * HEAD)) == rows + 3 * HEAD, 1.0, 0.0).astype(BF16)
        vecs = mm(pick, weight, NT)
        vec_ref[...] = vecs
        gain, shift = vecs[0:1], vecs[1:2]
        low = lane_iota((blk, 2 * HEAD)) < HEAD
        for s in range(ns):
            unit, _ = norm_stats(xs[s][:blk, :].astype(F32))
            normed = (unit * gain + shift).astype(BF16)
            normed_ref[s] = normed
            y = mm(normed, weight)
            q_ref[s] = (
                jnp.where(low, y[:, : 2 * HEAD], 0.0).astype(BF16).astype(F32) * HEAD**-0.5
            ).astype(BF16)
            kv_ref[s] = pltpu.roll(y, 3 * HEAD, 1)[:, : 2 * HEAD].astype(BF16)

    return body


def fill_slots(plan, info, deal, slot_of):
    for g, (gc, gw) in enumerate(plan.group_masks(info[0] % 2)):
        for s, (mc, mw) in enumerate(plan.slots):
            at = (info[0] ^ gc ^ mc) * plan.n_wt + (info[1] ^ gw ^ mw)
            slot_of[deal[at]] = g * len(plan.slots) + s


def slot_range(plan, info, deal, lengths, codes, i, blk, nseq):
    code = codes[i]
    here = deal[(info[0] ^ (code // plan.n_wt)) * plan.n_wt + (info[1] ^ (code % plan.n_wt))]
    first = jnp.int32(0)
    total = jnp.int32(0)
    for n in range(nseq):
        total = total + lengths[n]
        bound = total // blk
        first = jnp.where(bound <= here, bound, first)
    return first, here


def list_pairs(plan, info, deal, lengths, codes, blk, nseq, slot_of, pairs, low, high):
    fill_slots(plan, info, deal, slot_of)

    def one_block(i, n):
        first, here = slot_range(plan, info, deal, lengths, codes, i, blk, nseq)

        def one_key(b, n):
            slot = slot_of[b]
            inside = (slot >= low) & (slot < high)
            pairs[n] = i * 1024 + slot - low
            return n + inside.astype(jnp.int32)

        return lax.fori_loop(first, here, one_key, n)

    n = lax.fori_loop(0, len(plan.slots), one_block, jnp.int32(0))
    pairs[n] = pairs[jnp.maximum(n - 1, 0)]
    return n


def attend_body(plan, blk, nseq, lo, hi, last):
    ns, nb = len(plan.slots), hi - lo

    def body(info, deal, lengths, codes, q_ref, *refs):
        kv_refs, refs = refs[:nb], refs[nb:]
        if lo:
            olds, refs = refs[:3], refs[3:]
        (m_ref, l_ref, acc_ref), refs = refs[:3], refs[3:]
        if last:
            (o_ref, of_ref, lse_ref), refs = refs[:3], refs[3:]
        kvs, slot_of, pairs, sem = refs
        copies = [
            pltpu.make_async_copy(ref, kvs.at[pl.ds(b * ns, ns)], sem.at[b])
            for b, ref in enumerate(kv_refs)
        ]
        for c in copies:
            c.start()
        n = list_pairs(
            plan, info, deal, lengths, codes, blk, nseq, slot_of, pairs, lo * ns, hi * ns
        )
        if lo:
            for new, old in zip((m_ref, l_ref, acc_ref), olds):
                new[...] = old[...]
        for c in copies:
            c.wait()
        if not lo:
            tri = lax.broadcasted_iota(jnp.int32, (blk, blk), 0) <= lane_iota((blk, blk))

            def diagonal(h, _):
                scores = [mm(kvs[h * 2 + k], q_ref[h * 2 + k], NT) for k in (0, 1)]
                for k in (0, 1):
                    i = h * 2 + k
                    s = jnp.where(tri, scores[k], NEG)
                    m = jnp.max(s, axis=0, keepdims=True)
                    p = jnp.exp(s - m)
                    m_ref[i] = m
                    l_ref[i] = jnp.sum(p, axis=0, keepdims=True)
                    acc_ref[i] = mm(kvs[i], p.astype(BF16), TN)
                return 0

            lax.fori_loop(0, ns // 2, diagonal, 0)

        def step(h, _):
            codes2 = [pairs[h * 2], pairs[h * 2 + 1]]
            rows = [c // 1024 for c in codes2]
            cols = [c % 1024 for c in codes2]
            scores = [mm(kvs[cols[k]], q_ref[rows[k]], NT) for k in (0, 1)]
            scores[1] = jnp.where(h * 2 + 1 < n, scores[1], NEG)
            for k in (0, 1):
                i, s = rows[k], scores[k]
                m_old = m_ref[i]
                m = jnp.maximum(m_old, jnp.max(s, axis=0, keepdims=True))
                p = jnp.exp(s - m)
                factor = jnp.exp(m_old - m)
                m_ref[i] = m
                l_ref[i] = l_ref[i] * factor + jnp.sum(p, axis=0, keepdims=True)
                acc_ref[i] = acc_ref[i] * factor + mm(kvs[cols[k]], p.astype(BF16), TN)
            return 0

        lax.fori_loop(0, (n + 1) // 2, step, 0)
        if last:
            core = info[0] % 2

            def finish(i, _):
                total = l_ref[i]
                lse_ref[i] = m_ref[i] + jnp.log(total)
                out = acc_ref[i, HEAD:, :] / total
                zero = jnp.zeros_like(out)
                placed = jnp.concatenate(
                    [jnp.where(core == 0, out, zero), jnp.where(core == 1, out, zero)], axis=0
                )
                wide = placed.T
                of_ref[i] = wide
                o_ref[i] = wide.astype(BF16)
                return 0

            lax.fori_loop(0, ns, finish, 0)

    return body


def attend_part(plan, blk, nseq, lo, hi, last, scalars, q, kvs, olds):
    ns, nb = len(plan.slots), hi - lo
    outs = [sds((ns, 1, blk), F32), sds((ns, 1, blk), F32), sds((ns, 2 * HEAD, blk), F32)]
    if last:
        outs += [
            sds((ns, blk, 2 * HEAD), BF16),
            sds((ns, blk, 2 * HEAD), F32),
            sds((ns, 1, blk), F32),
        ]
    n_dev = plan.n_ctx * plan.n_wt
    pairs = 14 * nb
    return call(
        attend_body(plan, blk, nseq, lo, hi, last),
        "attend",
        list(scalars) + [q] + list(kvs[lo:hi]) + list(olds),
        [SMEM] * 4 + [VMEM] + [ANY] * nb + [VMEM] * len(olds),
        outs,
        scratch=[
            pltpu.VMEM((nb * ns, blk, 2 * HEAD), BF16),
            pltpu.SMEM((n_dev,), jnp.int32),
            pltpu.SMEM((ns * n_dev + 1,), jnp.int32),
            pltpu.SemaphoreType.DMA((nb,)),
        ],
        flops=pairs * 4 * blk * blk * 128 * 8,
        trans=pairs * blk * blk,
    )


def attend_back_body(plan, blk, nseq, lo, hi, first, last):
    ns, nb, nj = len(plan.slots), hi - lo, len(plan.peers)

    def body(info, deal, lengths, codes, q_ref, lse_ref, *refs):
        kv_refs, refs = refs[:nb], refs[nb:]
        if first:
            of_ref, g_refs, gs_ref, refs = refs[0], refs[1 : 1 + nj], refs[1 + nj], refs[2 + nj :]
        else:
            g_ext, delta_ref, old_dq, refs = refs[0], refs[1], refs[2], refs[3:]
        dkv_refs, refs = refs[:nb], refs[nb:]
        dq_acc, refs = refs[0], refs[1:]
        if first:
            g_ext, delta_ref, refs = refs[0], refs[1], refs[2:]
        if last:
            dq_ref, refs = refs[0], refs[1:]
        kvs, dkvs, slot_of, pairs, sem = refs
        copies = [
            pltpu.make_async_copy(ref, kvs.at[pl.ds(b * ns, ns)], sem.at[b])
            for b, ref in enumerate(kv_refs)
        ]
        for c in copies:
            c.start()
        n = list_pairs(
            plan, info, deal, lengths, codes, blk, nseq, slot_of, pairs, lo * ns, hi * ns
        )
        core = info[0] % 2
        high = lane_iota((blk, 2 * HEAD)) >= HEAD
        if first:
            own_half = (lane_iota((blk, 2 * HEAD)) // HEAD) == core
            for s in range(ns):
                g = (g_refs[s][...] if s < nj else gs_ref[s - nj]).astype(F32)
                g = jnp.where(own_half, g, 0.0)
                delta_ref[s] = jnp.sum((g * of_ref[s]).T, axis=0, keepdims=True)
                turned = pltpu.roll(g, HEAD, 1)
                g_ext[s] = jnp.where(high, jnp.where(core == 1, g, turned), 0.0).astype(BF16)
            dq_acc[...] = jnp.zeros_like(dq_acc)
        else:
            dq_acc[...] = old_dq[...]
        dkvs[...] = jnp.zeros_like(dkvs)
        for c in copies:
            c.wait()

        def pair_terms(rows, cols, mask):
            scores = [mm(kvs[c], q_ref[i], NT) for i, c in zip(rows, cols)]
            slopes = [mm(kvs[c], g_ext[i], NT) for i, c in zip(rows, cols)]
            for k, (i, c) in enumerate(zip(rows, cols)):
                p = jnp.exp(scores[k] - lse_ref[i])
                p = mask(k, p)
                ds = (p * (slopes[k] - delta_ref[i])).astype(BF16)
                dkvs[c] += mm(ds, q_ref[i]) + mm(p.astype(BF16), g_ext[i])
                dq_acc[i] += mm(kvs[c], ds, TN)

        if not lo:
            tri = lax.broadcasted_iota(jnp.int32, (blk, blk), 0) <= lane_iota((blk, blk))

            def diagonal(h, _):
                at = [h * 2, h * 2 + 1]
                pair_terms(at, at, lambda k, p: jnp.where(tri, p, 0.0))
                return 0

            lax.fori_loop(0, ns // 2, diagonal, 0)

        def step(h, _):
            codes2 = [pairs[h * 2], pairs[h * 2 + 1]]
            pair_terms(
                [c // 1024 for c in codes2],
                [c % 1024 for c in codes2],
                lambda k, p: jnp.where(h * 2 + 1 < n, p, 0.0) if k else p,
            )
            return 0

        lax.fori_loop(0, (n + 1) // 2, step, 0)
        if last:

            def finish(i, _):
                wide = dq_acc[i].T * HEAD**-0.5
                dq_ref[i] = jnp.where(high, 0.0, wide).astype(BF16)
                return 0

            lax.fori_loop(0, ns, finish, 0)
        for b in range(nb):
            dkv_refs[b][...] = dkvs[b * ns : (b + 1) * ns].astype(BF16)

    return body


def attend_back_part(plan, blk, nseq, lo, hi, first, last, scalars, q, lse, kvs, extra):
    ns, nb = len(plan.slots), hi - lo
    rows = sds((ns, blk, 2 * HEAD), BF16)
    outs = [rows] * nb + [sds((ns, 2 * HEAD, blk), F32)]
    if first:
        outs += [rows, sds((ns, 1, blk), F32)]
    if last:
        outs += [rows]
    n_dev = plan.n_ctx * plan.n_wt
    pairs = 14 * nb
    return call(
        attend_back_body(plan, blk, nseq, lo, hi, first, last),
        "attend_back",
        list(scalars) + [q, lse] + list(kvs[lo:hi]) + list(extra),
        [SMEM] * 4 + [VMEM] * 2 + [ANY] * nb + [VMEM] * len(extra),
        outs,
        scratch=[
            pltpu.VMEM((nb * ns, blk, 2 * HEAD), BF16),
            pltpu.VMEM((nb * ns, blk, 2 * HEAD), F32),
            pltpu.SMEM((n_dev,), jnp.int32),
            pltpu.SMEM((ns * n_dev + 1,), jnp.int32),
            pltpu.SemaphoreType.DMA((nb,)),
        ],
        flops=pairs * 10 * blk * blk * 128 * 8,
        trans=pairs * blk * blk,
    )


Z_ORDER = (0, 2, 1, 3)


def mlp_body(plan, width, ff, blk, packed):
    nj, nw, nc = len(plan.peers), plan.n_wt, plan.n_ctx
    nq = ff // CHUNK

    def body(info, *refs):
        refs = list(refs)
        x_ref, teacher_ref, valid_ref, vec_ref, count_ref = refs[:5]
        att = refs[5 : 5 + nj]
        rest = refs[5 + nj :]
        nwt_in = nc if packed else 3
        w_in, rest = rest[:nwt_in], rest[nwt_in:]
        (lo_ref, sq_ref, g1_ref, gatt_ref, act_ref, gpre_ref, n2_ref, gb_ref, ga_ref, gv_ref) = (
            rest[:10]
        )
        if packed:
            wup, wdown, wout, meta, slope_ref, acc_ref, sem = rest[10:]
            copies = []
            here = info[0] % 2
            owners = [info[0] ^ m for m in plan.near(here)]
            owners += [info[0] ^ 1 ^ m for m in plan.near(1 - here)]
            for c, src in zip(owners, w_in):
                for m in range(nw):
                    w = info[1] ^ Z_ORDER[m]
                    copies += [
                        pltpu.make_async_copy(
                            src.at[m, pl.ds(nq + 4, 1)], wout.at[w, pl.ds(c, 1)], sem.at[0]
                        ),
                        pltpu.make_async_copy(src.at[m, pl.ds(0, nq)], wup.at[:, w, c], sem.at[1]),
                        pltpu.make_async_copy(
                            src.at[m, pl.ds(nq, 4)], wdown.at[w, pl.ds(c * 4, 4)], sem.at[2]
                        ),
                        pltpu.make_async_copy(
                            src.at[m, pl.ds(nq + 5, 1)], meta.at[w, pl.ds(c, 1)], sem.at[3]
                        ),
                    ]
            for cp in copies:
                cp.start()
            for cp in copies:
                cp.wait()
            w_up = lambda q: wup[q].reshape(width, CHUNK)
            w_down = lambda q: wdown[q].reshape(CHUNK, width)
            out_rows = width // nw
            pair_rows = 2 * HEAD
            wout_flat = wout.reshape(width, width)
            w_out = lambda row: wout_flat[pl.ds(row, pair_rows), :]
            count = jnp.sum(meta[:, :, 0:1, 0:1].astype(F32))
        else:
            slope_ref, acc_ref = rest[10:]
            w_up = lambda q: w_in[0][q]
            w_down = lambda q: w_in[1][q]
            w_out = lambda row: w_in[2][pl.ds(row, 2 * HEAD), :]
            count = count_ref[0]
        vecs = vec_ref[...]
        gain, shift = vecs[2:3], vecs[3:4]
        rows = []
        for mc, mw in plan.peers:
            head = plan.head(info[0] ^ mc, info[1] ^ mw)
            rows.append(pl.multiple_of((head // 2) * (2 * HEAD), 2 * HEAD))
        mixed = mm(att[0][...], w_out(rows[0]))
        for j in range(1, nj):
            mixed = mixed + mm(att[j][...], w_out(rows[j]))
        res = mixed + x_ref[...].astype(F32)
        unit, inverse = norm_stats(res)
        n2 = (unit * gain + shift).astype(BF16)
        n2_ref[...] = n2
        for q in range(nq):
            pre = mm(n2, w_up(q))
            cdf = 0.5 * (1.0 + lax.erf(pre * 0.7071067811865476))
            pdf = jnp.exp(-0.5 * pre * pre) * 0.3989422804014327
            act = (pre * cdf).astype(BF16)
            slope_ref[q] = cdf + pre * pdf
            act_ref[q] = act
            if q == 0:
                acc_ref[...] = mm(act, w_down(q))
            else:
                acc_ref[...] += mm(act, w_down(q))
        two = acc_ref[...] + res
        lo_ref[...] = two.astype(BF16)
        distance = two - teacher_ref[...].astype(F32)
        valid = valid_ref[...].astype(F32)
        weighed = valid * distance
        square = jnp.sum(weighed * distance)
        first_row = lax.broadcasted_iota(jnp.int32, (8, 128), 0) == 0
        sq_ref[...] = jnp.where(first_row, square, count)
        g2 = (2.0 * LOSS_SCALE / (count * width)) * weighed
        gb = g2.astype(BF16)
        gb_ref[...] = gb
        for q in range(nq):
            gpre = (mm(gb, w_down(q), NT) * slope_ref[q]).astype(BF16)
            gpre_ref[q] = gpre
            if q == 0:
                acc_ref[...] = mm(gpre, w_up(q), NT)
            else:
                acc_ref[...] += mm(gpre, w_up(q), NT)
        gn2 = acc_ref[...]
        g1 = g2 + norm_back(gn2, unit, inverse, gain)
        g1_ref[...] = g1
        gv_ref[...] = jnp.concatenate(
            [
                jnp.sum(gn2 * unit, axis=0, keepdims=True),
                jnp.sum(gn2, axis=0, keepdims=True),
                jnp.zeros((6, width), F32),
            ],
            axis=0,
        )
        ga = g1.astype(BF16)
        ga_ref[...] = ga
        for j in range(nj):
            gatt_ref[j] = mm(ga, w_out(rows[j]), NT).astype(BF16)

    return body


def mlp_grads_body(plan, width, ff, blk, packed):
    nj, nw, nc = len(plan.peers), plan.n_wt, plan.n_ctx
    nq = ff // CHUNK

    def body(info, act_ref, gpre_ref, n2_ref, gb_ref, ga_ref, gv_ref, sq_ref, *refs):
        att, outs = refs[:nj], refs[nj:]
        n2, gb, ga = n2_ref[...], gb_ref[...], ga_ref[...]
        ctx, wt = info[0], info[1]
        rows_up = width // (nw * nc)
        for q in range(nq):
            up = mm(n2, gpre_ref[q], TN).astype(BF16)
            down = mm(act_ref[q], gb, TN).astype(BF16)
            if packed:
                up_t = up.reshape(nw, nc, rows_up, CHUNK)
                down_t = down.reshape(nc, 4, TILE, width)
                for w in range(nw):
                    for c in range(nc):
                        put_tile(outs, info, c, w, q, up_t[w, c])
                for c in range(nc):
                    for t in range(4):
                        put_tile(outs, info, c, q, nq + t, down_t[c, t])
            else:
                outs[0][q] = up
                outs[1][q] = down
        for j, (mc, mw) in enumerate(plan.peers):
            head = plan.head(ctx ^ mc, wt ^ mw)
            part = mm(att[j][...], ga, TN).astype(BF16)
            if packed:
                per = width // nw
                part_t = part.reshape(2 * HEAD // TILE, TILE, width)
                base = (head // 2) * (2 * HEAD // TILE)
                for t in range(2 * HEAD // TILE):
                    at = base + t
                    w, c = at // nc, at % nc
                    put_tile(outs, info, c, w, nq + 4, part_t[t])
            else:
                row = pl.multiple_of((head // 2) * (2 * HEAD), 2 * HEAD)
                outs[2][pl.ds(row, 2 * HEAD), :] = part
        if packed:
            dev = ctx * nw + wt
            square = sq_ref[0:1, 0:1]
            high = square.astype(BF16).astype(F32)
            lane = lane_iota((1, CHUNK))
            n_dev = nw * nc
            line = jnp.where(lane == dev, high, 0.0) + jnp.where(
                lane == dev + n_dev, square - high, 0.0
            )
            for w in range(nw):
                per = width // nw
                vec = gv_ref[0:2, per * w : per * (w + 1)]
                vec = jnp.concatenate([vec, jnp.zeros((2, CHUNK - per), F32)], axis=1)
                tile = jnp.concatenate([line, vec, jnp.zeros((TILE - 3, CHUNK), F32)], axis=0)
                tile = tile.astype(BF16)
                for c in range(nc):
                    put_tile(outs, info, c, w, nq + 5, tile)

    return body


def put_tile(outs, info, c, w, tile, value):
    plane = (c ^ info[0]) // 2
    core = c % 2
    middle = (plane == 1) | (plane == 2)
    place = jnp.where(middle & (core == 1), 3 - plane, plane)
    zed = w ^ info[1]
    zed = jnp.where((zed == 1) | (zed == 2), 3 - zed, zed)
    outs[0][core ^ (info[0] % 2), place, zed, tile] = value


def head_grads_body(plan, blk, width, shard, nb):
    ns, nw, nj = len(plan.slots), plan.n_wt, len(plan.peers)

    def body(info, dq_ref, wh_ref, normed_ref, *refs):
        xs = refs[:ns]
        parts = refs[ns : ns + nb]
        outs = refs[ns + nb :]
        own_ref, sib_ref, dw_refs = outs[0], outs[1], outs[2 : 2 + nw]
        acc = outs[2 + nw]
        weight = wh_ref[...]
        gsum = jnp.zeros((1, width), F32)
        ssum = jnp.zeros((1, width), F32)
        for s in range(ns):
            dkv = parts[0][s].astype(F32)
            for b in range(1, nb):
                dkv = dkv + parts[b][s].astype(F32)
            zero = jnp.zeros((blk, 2 * HEAD), F32)
            wide = pltpu.roll(jnp.concatenate([dkv, zero], axis=1), HEAD, 1)
            wide = wide + jnp.concatenate([dq_ref[s].astype(F32), zero], axis=1)
            gh = wide.astype(BF16)
            back = mm(gh, weight, NT)
            if s < nj:
                own_ref[s] = back.astype(BF16)
            else:
                sib_ref[s - nj] = back.astype(BF16)
            unit, _ = norm_stats(xs[s][:blk, :].astype(F32))
            gsum = gsum + jnp.sum(back * unit, axis=0, keepdims=True)
            ssum = ssum + jnp.sum(back, axis=0, keepdims=True)
            dw = mm(normed_ref[s], gh, TN)
            if s == 0:
                acc[...] = dw
            else:
                acc[...] += dw
        vecs = jnp.concatenate([gsum, ssum, jnp.zeros((6, width), F32)], axis=0).astype(BF16)
        rows = lax.broadcasted_iota(jnp.int32, (8, 4 * HEAD), 0)
        pick = jnp.where(lane_iota((8, 4 * HEAD)) == rows + 3 * HEAD, 1.0, 0.0).astype(BF16)
        acc[...] += mm(vecs, pick, TN)
        for m in range(nw):
            row = pl.multiple_of((info[1] ^ m) * shard, shard)
            dw_refs[m][...] = acc[pl.ds(row, shard), :].astype(BF16)

    return body


def words_body(nj):
    def body(x_ref, vec_ref, g1_ref, *refs):
        parts, sibs, out_ref = refs[:nj], refs[nj : 2 * nj], refs[-1]
        up = parts[0][...].astype(F32)
        for p in parts[1:]:
            up = up + p[...].astype(F32)
        unit, inverse = norm_stats(x_ref[...].astype(F32))
        out_ref[...] = g1_ref[...] + norm_back(up, unit, inverse, vec_ref[0:1, :])

    return body


def unpack_body(plan, width, ff):
    nq, nw, nc = ff // CHUNK, plan.n_wt, plan.n_ctx

    def body(info, *refs):
        srcs, outs = refs[:nc], refs[nc:]
        up_ref, down_ref, out_ref, meta_ref = outs
        here = info[0] % 2
        owners = [info[0] ^ m for m in plan.near(here)]
        owners += [info[0] ^ 1 ^ m for m in plan.near(1 - here)]
        for c, src in zip(owners, srcs):
            row = pl.multiple_of(c * TILE, TILE)
            for q in range(nq):
                up_ref[pl.ds(row, TILE), q * CHUNK : (q + 1) * CHUNK] = src[q].astype(F32)
            for t in range(4):
                down_ref[pl.ds(pl.multiple_of(c * 4 * TILE + t * TILE, TILE), TILE), :] = src[
                    nq + t
                ].astype(F32)
            out_ref[pl.ds(row, TILE), :] = src[nq + 4].astype(F32)
        meta = srcs[0][nq + 5].astype(F32)
        meta_ref[...] = meta

    return body


def head_out_body(plan, shard):
    def body(info, *refs):
        srcs, (out_ref, vec_ref) = refs[:H], refs[H:]
        core = info[0] % 2
        total = srcs[0][...].astype(F32)
        for s in srcs[1:]:
            total = total + s[...].astype(F32)
        rows = lax.broadcasted_iota(jnp.int32, (8, 4 * HEAD), 0)
        pick = jnp.where(lane_iota((8, 4 * HEAD)) == rows + 3 * HEAD, 1.0, 0.0)
        vec_ref[...] = lax.dot_general(
            pick, total, NT, precision=lax.Precision.HIGHEST, preferred_element_type=F32
        )
        nj = len(plan.peers)
        for j, (mc, mw) in enumerate(plan.peers):
            head = plan.head(info[0] ^ mc, info[1] ^ mw)
            own = srcs[j][...].astype(F32)
            sib = srcs[nj + j][...].astype(F32)
            even = jnp.where(core == 0, own, sib)
            odd = jnp.where(core == 0, sib, own)
            turned = pltpu.roll(odd, 3 * HEAD, 1)
            lane = lane_iota((shard, 2 * HEAD))
            mid = jnp.where(lane < HEAD, even[:, 2 * HEAD :], turned[:, 2 * HEAD :])
            last = turned[:, : 2 * HEAD]
            col = pl.multiple_of((head // 2) * (6 * HEAD), 2 * HEAD)
            out_ref[:, pl.ds(col, 2 * HEAD)] = even[:, : 2 * HEAD]
            out_ref[:, pl.ds(col + 2 * HEAD, 2 * HEAD)] = mid
            out_ref[:, pl.ds(col + 4 * HEAD, 2 * HEAD)] = last

    return body


def per_device(
    words,
    teacher,
    valid,
    lengths,
    deal,
    gain_attn,
    shift_attn,
    w_qkv,
    w_out,
    gain_mlp,
    shift_mlp,
    w_up,
    w_down,
):
    n_ctx, n_wt = lax.axis_size("ctx"), lax.axis_size("wt")
    plan = Plan(n_ctx, n_wt)
    ctx, wt = lax.axis_index("ctx"), lax.axis_index("wt")
    blk, width = words.shape
    shard = width // n_wt
    ff = w_up.shape[1]
    nq = ff // CHUNK
    nseq = lengths.shape[0]
    ns, nb, nj = len(plan.slots), len(plan.groups), len(plan.peers)
    packed = plan.square and width == CHUNK and width % (n_wt * n_ctx * TILE) == 0 and n_wt * CHUNK == ff
    info = jnp.stack([ctx, wt]).astype(jnp.int32)
    codes = jnp.array([mc * n_wt + mw for mc, mw in plan.slots], jnp.int32)
    core = (1, 0)

    vec_cols = jnp.stack([gain_attn, shift_attn, gain_mlp, shift_mlp], axis=1)
    vec_cols = jnp.pad(vec_cols, ((0, 0), (3 * HEAD, HEAD - 4)))
    load = call(
        pack_body(plan, shard, blk),
        "pack",
        [info, words, w_qkv, vec_cols],
        [SMEM] + [VMEM] * 3,
        [sds((blk + shard // 2, width), BF16)] * n_wt,
    )
    loads = [load[0]] + [plan.swap(load[m], (0, m)) for m in range(1, n_wt)]
    xs = loads[:nj] + [plan.swap(x, core) for x in loads[:nj]]

    q, kv, normed, w_head, vecs = call(
        project_body(plan, shard, blk),
        "project",
        [info] + xs + loads,
        [SMEM] + [VMEM] * (ns + n_wt),
        [
            sds((ns, blk, 2 * HEAD), BF16),
            sds((ns, blk, 2 * HEAD), BF16),
            sds((ns, blk, width), BF16),
            sds((width, 4 * HEAD), BF16),
            sds((8, width), F32),
        ],
        flops=2 * ns * blk * width * 4 * HEAD,
    )
    kvs = plan.gather_groups(kv)

    if packed:
        rows_up = width // (n_wt * n_ctx)
        up_piece = lax.dynamic_slice_in_dim(w_up, ctx * rows_up, rows_up, 0)
        up_piece = up_piece.reshape(rows_up, nq, CHUNK).transpose(1, 0, 2)
        down_piece = lax.dynamic_slice_in_dim(w_down, ctx * 4 * TILE, 4 * TILE, 0)
        out_piece = lax.dynamic_slice_in_dim(w_out, ctx * TILE, TILE, 0)
        count_here = jnp.sum(valid).astype(BF16)
        piece = jnp.concatenate(
            [
                up_piece,
                down_piece.reshape(4, TILE, CHUNK),
                out_piece[None],
                jnp.full((1, TILE, CHUNK), count_here, BF16),
            ],
            axis=0,
        )
        piece, _ = lax.optimization_barrier((piece, q))
        two = jnp.stack([piece, plan.swap(piece, (0, 2))])
        two, _ = lax.optimization_barrier((two, kvs[1]))
        stack = jnp.concatenate([two, plan.swap(two, (0, 1))])
        stack, _ = lax.optimization_barrier((stack, kvs[3]))
        stacks = plan.gather_square(stack)
        stacks = stacks + [plan.swap(s, core) for s in stacks]
        weights = stacks
        count = jnp.zeros((1,), F32)
    else:
        up_full = lax.all_gather(w_up, "wt", axis=0, tiled=True)
        down_full = lax.all_gather(w_down, "wt", axis=0, tiled=True)
        out_full = lax.all_gather(w_out, "wt", axis=0, tiled=True)
        weights = [
            up_full.reshape(width, nq, CHUNK).transpose(1, 0, 2),
            down_full.reshape(nq, CHUNK, width),
            out_full,
        ]
        count = lax.psum(jnp.sum(valid).astype(F32), ("ctx", "wt")).reshape(1)

    scalars = [info, deal, lengths, codes]
    state = []
    cuts = [(0, 1), (1, 3), (3, 4)] if plan.square else [(0, nb)]
    for lo, hi in cuts:
        state = attend_part(plan, blk, nseq, lo, hi, hi == nb, scalars, q, kvs, state)
    o, of32, lse = state[3:]
    mixed = o[:nj] + plan.swap(o[nj:], core)
    att = [mixed[0]] + [plan.swap(mixed[j], plan.peers[j]) for j in range(1, nj)]

    mlp_in = [info, words, teacher, valid[:, None], vecs, count] + att + weights
    specs = [SMEM] + [VMEM] * 4 + [SMEM] + [VMEM] * nj
    specs += [ANY] * len(weights) if packed else [VMEM] * len(weights)
    scratch = [pltpu.VMEM((nq, blk, CHUNK), F32), pltpu.VMEM((blk, width), F32)]
    if packed:
        scratch = [
            pltpu.VMEM((nq, n_wt, n_ctx, TILE, CHUNK), BF16),
            pltpu.VMEM((n_wt, n_ctx * 4, TILE, CHUNK), BF16),
            pltpu.VMEM((n_wt, n_ctx, TILE, CHUNK), BF16),
            pltpu.VMEM((n_wt, n_ctx, TILE, CHUNK), BF16),
            *scratch,
            pltpu.SemaphoreType.DMA((4,)),
        ]
    layer_out, square, grad_one, gatt, act, gpre, n2, gb, ga, gvec = call(
        mlp_body(plan, width, ff, blk, packed),
        "mlp",
        mlp_in,
        specs,
        [
            sds((blk, width), BF16),
            sds((8, 128), F32),
            sds((blk, width), F32),
            sds((nj, blk, 2 * HEAD), BF16),
            sds((nq, blk, CHUNK), BF16),
            sds((nq, blk, CHUNK), BF16),
            sds((blk, width), BF16),
            sds((blk, width), BF16),
            sds((blk, width), BF16),
            sds((8, width), F32),
        ],
        scratch=scratch,
        flops=8 * blk * width * ff,
        trans=2 * blk * ff,
    )
    g_own = [gatt[0]] + [plan.swap(gatt[j], plan.peers[j]) for j in range(1, nj)]
    g_sib = plan.swap(jnp.stack(g_own), core)

    grads_in = [info, act, gpre, n2, gb, ga, gvec, square] + att
    if packed:
        grads_out = [sds((2, n_ctx // 2, n_wt, nq + 6, TILE, CHUNK), BF16)]
    else:
        grads_out = [
            sds((nq, width, CHUNK), BF16),
            sds((nq, CHUNK, width), BF16),
            sds((width, width), BF16),
        ]
    weight_grads = call(
        mlp_grads_body(plan, width, ff, blk, packed),
        "mlp_grads",
        grads_in,
        [SMEM] + [VMEM] * (7 + nj),
        grads_out,
        flops=4 * blk * width * ff,
    )

    extra = [of32] + g_own + [g_sib]
    if plan.square:
        part = attend_back_part(plan, blk, nseq, 2, 4, True, False, scalars, q, lse, kvs, extra)
        dkv2, dkv3, dq_part, g_ext, delta = part
        far = [plan.turn(d, False) for d in (dkv3, dkv2)]
        dkv1, dq_part = attend_back_part(
            plan, blk, nseq, 1, 2, False, False, scalars, q, lse, kvs, [g_ext, delta, dq_part]
        )
        mid = plan.turn((dkv1.astype(F32) + far[0].astype(F32)).astype(BF16), True)
        dkv0, _, dq = attend_back_part(
            plan, blk, nseq, 0, 1, False, True, scalars, q, lse, kvs, [g_ext, delta, dq_part]
        )
        parts = [dkv0, far[1], mid]
    else:
        part = attend_back_part(plan, blk, nseq, 0, nb, True, True, scalars, q, lse, kvs, extra)
        dq = part[-1]
        parts = [part[0]] + [plan.swap(part[b], plan.groups[b]) for b in range(1, nb)]

    outs = call(
        head_grads_body(plan, blk, width, shard, len(parts)),
        "head_grads",
        [info, dq, w_head, normed] + xs + parts,
        [SMEM] + [VMEM] * (3 + ns + len(parts)),
        [sds((nj, blk, width), BF16)] * 2 + [sds((shard, 4 * HEAD), BF16)] * n_wt,
        scratch=[pltpu.VMEM((width, 4 * HEAD), F32)],
        flops=4 * ns * blk * width * 4 * HEAD,
    )
    own_rows, sib_rows, dw = outs[0], outs[1], outs[2:]
    rows = (own_rows.astype(F32) + plan.swap(sib_rows, core).astype(F32)).astype(BF16)
    up_rows = [rows[0]] + [plan.swap(rows[j], plan.peers[j]) for j in range(1, nj)]
    grad_words = call(
        words_body(nj),
        "words_grad",
        [words, vecs, grad_one] + up_rows,
        [VMEM] * (3 + nj),
        [sds((blk, width), F32)],
    )[0]

    dw = [dw[0]] + [plan.swap(dw[m], (0, m)) for m in range(1, n_wt)]
    merged = []
    for a in range(WT_HEADS):
        total = dw[a].astype(F32)
        for m in range(a + WT_HEADS, n_wt, WT_HEADS):
            total = total + dw[m].astype(F32)
        merged.append(total)
    heads = jnp.stack(merged).astype(BF16)
    step = CTX_HEADS
    while step < n_ctx:
        heads = (heads.astype(F32) + plan.swap(heads, (step, 0)).astype(F32)).astype(BF16)
        step *= 2
    cols = [heads]
    own_heads = jnp.stack(cols, axis=1)
    sib_heads = plan.swap(own_heads, core)
    srcs = [own_heads[a, p] for a in range(WT_HEADS) for p in range(CTX_HEADS // 2)]
    srcs += [sib_heads[a, p] for a in range(WT_HEADS) for p in range(CTX_HEADS // 2)]
    g_qkv, gvec_attn = call(
        head_out_body(plan, shard),
        "head_out",
        [info] + srcs,
        [SMEM] + [VMEM] * H,
        [sds((shard, 3 * width), F32), sds((8, shard), F32)],
    )

    if packed:
        g_all = weight_grads[0]
        g_core = plan.swap(g_all[1], core)
        far = (g_all[0, 2:].astype(F32) + g_core[2:].astype(F32)).astype(BF16)
        far = plan.turn(far, False)
        mid = g_all[0, 1].astype(F32) + g_core[1].astype(F32) + far[1].astype(F32)
        mid = plan.turn(mid.astype(BF16), True)
        near = g_all[0, 0].astype(F32) + g_core[0].astype(F32) + far[0].astype(F32)
        near = (near + mid.astype(F32)).astype(BF16)
        far = plan.swap(near[2:], (0, 1))
        two = (near[:2].astype(F32) + far.astype(F32)).astype(BF16)
        final = (two[0].astype(F32) + plan.swap(two[1], (0, 2)).astype(F32)).astype(BF16)
        finals = plan.gather_square(final)
        finals = finals + [plan.swap(f, core) for f in finals]
        g_up, g_down, g_out, meta = call(
            unpack_body(plan, width, ff),
            "unpack",
            [info] + finals,
            [SMEM] + [VMEM] * len(finals),
            [
                sds((shard, ff), F32),
                sds((ff // n_wt, width), F32),
                sds((shard, width), F32),
                sds((TILE, CHUNK), F32),
            ],
        )
        square_all = jnp.sum(meta[0])
        g_gain, g_shift = meta[1, :shard], meta[2, :shard]
        count_all = square[1, 0]
    else:
        g_up, g_down, g_out = weight_grads
        g_up = g_up.transpose(1, 0, 2).reshape(width, ff)
        g_down = g_down.reshape(ff, width)

        def reduce_rows(g):
            part = lax.psum_scatter(g.astype(BF16), "wt", scatter_dimension=0, tiled=True)
            return lax.psum(part, "ctx").astype(F32)

        g_up, g_down, g_out = reduce_rows(g_up), reduce_rows(g_down), reduce_rows(g_out)
        both = lax.psum(gvec[:2], ("ctx", "wt"))
        both = lax.dynamic_slice_in_dim(both, wt * shard, shard, 1)
        g_gain, g_shift = both[0], both[1]
        count_all = count[0]
        square_all = lax.psum(square[0, 0], ("ctx", "wt"))
    loss = square_all / (count_all * width)
    return (
        layer_out,
        loss,
        grad_words,
        gvec_attn[0],
        gvec_attn[1],
        g_qkv,
        g_out,
        g_gain,
        g_shift,
        g_up,
        g_down,
    )


def solution(mesh):
    placed = (
        P(("ctx", "wt"), None),
        P(("ctx", "wt"), None),
        P(("ctx", "wt")),
        P(),
        P(),
        P("wt"),
        P("wt"),
        P("wt", None),
        P("wt", None),
        P("wt"),
        P("wt"),
        P("wt", None),
        P("wt", None),
    )
    return jax.shard_map(
        per_device,
        mesh=mesh,
        in_specs=placed,
        out_specs=(
            P(("ctx", "wt"), None),
            P(),
            P(("ctx", "wt"), None),
            P("wt"),
            P("wt"),
            P("wt", None),
            P("wt", None),
            P("wt"),
            P("wt"),
            P("wt", None),
            P("wt", None),
        ),
        check_vma=False,
    )
```

```python
import jax
import jax.numpy as jnp
from jax import lax
from jax.experimental import pallas as pl
from jax.experimental.pallas import tpu as pltpu
from jax.sharding import PartitionSpec as P

H = 8
HEAD = 64
EPS = 1e-05
LOSS_SCALE = 262144.0
CTX_HEADS = 2
WT_HEADS = 4
CHUNK = 512
TILE = 16
F32 = jnp.float32
BF16 = jnp.bfloat16
NEG = -1e30
NT = (((1,), (1,)), ((), ()))
TN = (((0,), (0,)), ((), ()))
NN = (((1,), (0,)), ((), ()))


def mm(a, b, dims=NN):
    return lax.dot_general(a, b, dims, preferred_element_type=F32)


def lane_iota(shape):
    return lax.broadcasted_iota(jnp.int32, shape, len(shape) - 1)


def norm_stats(values):
    center = values - jnp.mean(values, axis=-1, keepdims=True)
    inverse = lax.rsqrt(jnp.mean(center * center, axis=-1, keepdims=True) + EPS)
    return center * inverse, inverse


def norm_back(upstream, unit, inverse, gain):
    scaled = upstream * gain
    inner = jnp.mean(scaled * unit, axis=-1, keepdims=True)
    return inverse * (scaled - jnp.mean(scaled, axis=-1, keepdims=True) - unit * inner)


SMEM = pl.BlockSpec(memory_space=pltpu.SMEM)
VMEM = pl.BlockSpec(memory_space=pltpu.VMEM)
ANY = pl.BlockSpec(memory_space=pl.ANY)


def call(body, name, ins, in_specs, outs, scratch=(), flops=0, trans=0, out_specs=None):
    nbytes = sum(x.size * x.dtype.itemsize for x in list(ins) + list(outs))
    return pl.pallas_call(
        body,
        name=name,
        out_shape=list(outs),
        in_specs=in_specs,
        out_specs=out_specs or [VMEM] * len(outs),
        scratch_shapes=list(scratch),
        compiler_params=pltpu.CompilerParams(vmem_limit_bytes=58 * 1024 * 1024),
        cost_estimate=pl.CostEstimate(flops=flops, bytes_accessed=nbytes, transcendentals=trans),
    )(*ins)


def after(value, *earlier):
    return lax.optimization_barrier((value, *earlier))[0]


def sds(shape, dtype):
    return jax.ShapeDtypeStruct(shape, dtype)


class Plan:
    def __init__(self, n_ctx, n_wt):
        self.n_ctx, self.n_wt = n_ctx, n_wt
        ac, aw = CTX_HEADS, WT_HEADS
        assert ac * aw == H and n_ctx % ac == 0 and n_wt % aw == 0
        self.peers = [(mc, mw) for mw in range(aw) for mc in range(0, ac, 2)]
        self.slots = [(mc | k, mw) for k in (0, 1) for mc, mw in self.peers]
        self.groups = [(mc, mw) for mc in range(0, n_ctx, ac) for mw in range(0, n_wt, aw)]
        self.square = n_ctx == 8 and n_wt == aw

    def near(self, core):
        return [0, 2 + 2 * core, 4 - 2 * core, 6]

    def group_masks(self, core):
        return [(m, 0) for m in self.near(core)] if self.square else self.groups

    def head(self, ctx, wt):
        return (wt % WT_HEADS) * CTX_HEADS + ctx % CTX_HEADS

    def swap(self, x, mask):
        mc, mw = mask
        n = self.n_wt
        perm = [
            (c * n + w, (c ^ mc) * n + (w ^ mw)) for c in range(self.n_ctx) for w in range(n)
        ]
        return lax.ppermute(x, ("ctx", "wt"), perm)

    def turn(self, x, first):
        n = self.n_wt
        masks = (2, 4) if first else (4, 2)
        perm = [
            (c * n + w, (c ^ masks[c % 2]) * n + w) for c in range(self.n_ctx) for w in range(n)
        ]
        return lax.ppermute(x, ("ctx", "wt"), perm)

    def gather_square(self, x):
        one = self.turn(x, True)
        return [x, one, self.turn(x, False), self.turn(one, False)]

    def gather_groups(self, x):
        if self.square:
            return self.gather_square(x)
        return [x] + [self.swap(x, m) for m in self.groups[1:]]


def pack_body(plan, shard, blk):
    nw, half = plan.n_wt, shard // 2

    def body(info, words_ref, w_ref, vec_ref, *outs):
        odd = (info[0] % 2) == 1
        rows = lax.broadcasted_iota(jnp.int32, (4, 4 * HEAD), 0)
        pick = jnp.where(lane_iota((4, 4 * HEAD)) == rows + 3 * HEAD, 1.0, 0.0).astype(BF16)
        vec = mm(vec_ref[...], pick, TN)
        lane = lane_iota((shard, 4 * HEAD))
        for m in range(nw):
            pair = plan.head(info[0], info[1] ^ m) // 2
            col = pl.multiple_of(pair * (6 * HEAD), 2 * HEAD)
            both = w_ref[:, pl.ds(col, 6 * HEAD)].astype(F32)
            turned = pltpu.roll(both, 3 * HEAD, 1)
            cols = jnp.where(odd, turned[:, : 4 * HEAD], both[:, : 4 * HEAD])
            cols = jnp.where(lane < 3 * HEAD, cols, vec).astype(BF16)
            outs[m][:blk, :] = words_ref[...]
            outs[m][blk:, : 4 * HEAD] = cols[:half]
            outs[m][blk:, 4 * HEAD :] = cols[half:]

    return body


def project_body(plan, shard, blk):
    ns, nw, half = len(plan.slots), plan.n_wt, shard // 2

    def body(info, *refs):
        xs, wps = refs[:ns], refs[ns : ns + nw]
        q_ref, kv_ref, normed_ref, wh_ref, vec_ref = refs[ns + nw :]
        wt = info[1]
        for m in range(nw):
            row = pl.multiple_of((wt ^ m) * shard, shard)
            wh_ref[pl.ds(row, half), :] = wps[m][blk:, : 4 * HEAD]
            wh_ref[pl.ds(row + half, half), :] = wps[m][blk:, 4 * HEAD :]
        weight = wh_ref[...]
        rows = lax.broadcasted_iota(jnp.int32, (8, 4 * HEAD), 0)
        pick = jnp.where(lane_iota((8, 4 * HEAD)) == rows + 3 * HEAD, 1.0, 0.0).astype(BF16)
        vecs = mm(pick, weight, NT)
        vec_ref[...] = vecs
        gain, shift = vecs[0:1], vecs[1:2]
        low = lane_iota((blk, 2 * HEAD)) < HEAD
        for s in range(ns):
            unit, _ = norm_stats(xs[s][:blk, :].astype(F32))
            normed = (unit * gain + shift).astype(BF16)
            normed_ref[s] = normed
            y = mm(normed, weight)
            q_ref[s] = (
                jnp.where(low, y[:, : 2 * HEAD], 0.0).astype(BF16).astype(F32) * HEAD**-0.5
            ).astype(BF16)
            kv_ref[s] = pltpu.roll(y, 3 * HEAD, 1)[:, : 2 * HEAD].astype(BF16)

    return body


def fill_slots(plan, info, deal, slot_of):
    for g, (gc, gw) in enumerate(plan.group_masks(info[0] % 2)):
        for s, (mc, mw) in enumerate(plan.slots):
            at = (info[0] ^ gc ^ mc) * plan.n_wt + (info[1] ^ gw ^ mw)
            slot_of[deal[at]] = g * len(plan.slots) + s


def slot_range(plan, info, deal, lengths, codes, i, blk, nseq):
    code = codes[i]
    here = deal[(info[0] ^ (code // plan.n_wt)) * plan.n_wt + (info[1] ^ (code % plan.n_wt))]
    first = jnp.int32(0)
    total = jnp.int32(0)
    for n in range(nseq):
        total = total + lengths[n]
        bound = total // blk
        first = jnp.where(bound <= here, bound, first)
    return first, here


def list_pairs(plan, info, deal, lengths, codes, blk, nseq, slot_of, pairs, low, high):
    fill_slots(plan, info, deal, slot_of)

    def one_block(i, n):
        first, here = slot_range(plan, info, deal, lengths, codes, i, blk, nseq)

        def one_key(b, n):
            slot = slot_of[b]
            inside = (slot >= low) & (slot < high)
            pairs[n] = i * 1024 + slot - low
            return n + inside.astype(jnp.int32)

        return lax.fori_loop(first, here, one_key, n)

    n = lax.fori_loop(0, len(plan.slots), one_block, jnp.int32(0))
    pairs[n] = pairs[jnp.maximum(n - 1, 0)]
    return n


def attend_body(plan, blk, nseq, lo, hi, last):
    ns, nb = len(plan.slots), hi - lo

    def body(info, deal, lengths, codes, q_ref, *refs):
        kv_refs, refs = refs[:nb], refs[nb:]
        if lo:
            olds, refs = refs[:3], refs[3:]
        (m_ref, l_ref, acc_ref), refs = refs[:3], refs[3:]
        if last:
            (o_ref, o_sib_ref, of_ref, lse_ref), refs = refs[:4], refs[4:]
        kvs, slot_of, pairs, sem = refs
        copies = [
            pltpu.make_async_copy(ref, kvs.at[pl.ds(b * ns, ns)], sem.at[b])
            for b, ref in enumerate(kv_refs)
        ]
        for c in copies:
            c.start()
        n = list_pairs(
            plan, info, deal, lengths, codes, blk, nseq, slot_of, pairs, lo * ns, hi * ns
        )
        if lo:
            for new, old in zip((m_ref, l_ref, acc_ref), olds):
                new[...] = old[...]
        for c in copies:
            c.wait()
        if not lo:
            tri = lax.broadcasted_iota(jnp.int32, (blk, blk), 0) <= lane_iota((blk, blk))

            def diagonal(h, _):
                scores = [mm(kvs[h * 2 + k], q_ref[h * 2 + k], NT) for k in (0, 1)]
                for k in (0, 1):
                    i = h * 2 + k
                    s = jnp.where(tri, scores[k], NEG)
                    m = jnp.max(s, axis=0, keepdims=True)
                    p = jnp.exp(s - m)
                    m_ref[i] = m
                    l_ref[i] = jnp.sum(p, axis=0, keepdims=True)
                    acc_ref[i] = mm(kvs[i], p.astype(BF16), TN)
                return 0

            lax.fori_loop(0, ns // 2, diagonal, 0)

        def step(h, _):
            codes2 = [pairs[h * 2], pairs[h * 2 + 1]]
            rows = [c // 1024 for c in codes2]
            cols = [c % 1024 for c in codes2]
            scores = [mm(kvs[cols[k]], q_ref[rows[k]], NT) for k in (0, 1)]
            scores[1] = jnp.where(h * 2 + 1 < n, scores[1], NEG)
            for k in (0, 1):
                i, s = rows[k], scores[k]
                m_old = m_ref[i]
                m = jnp.maximum(m_old, jnp.max(s, axis=0, keepdims=True))
                p = jnp.exp(s - m)
                factor = jnp.exp(m_old - m)
                m_ref[i] = m
                l_ref[i] = l_ref[i] * factor + jnp.sum(p, axis=0, keepdims=True)
                acc_ref[i] = acc_ref[i] * factor + mm(kvs[cols[k]], p.astype(BF16), TN)
            return 0

        lax.fori_loop(0, (n + 1) // 2, step, 0)
        if last:
            core = info[0] % 2

            def finish(i, _):
                total = l_ref[i]
                lse_ref[i] = m_ref[i] + jnp.log(total)
                out = acc_ref[i, HEAD:, :] / total
                zero = jnp.zeros_like(out)
                placed = jnp.concatenate(
                    [jnp.where(core == 0, out, zero), jnp.where(core == 1, out, zero)], axis=0
                )
                wide = placed.T
                of_ref[i] = wide

                @pl.when(i < ns // 2)
                def _():
                    o_ref[i] = wide.astype(BF16)

                @pl.when(i >= ns // 2)
                def _():
                    o_sib_ref[i - ns // 2] = wide.astype(BF16)

                return 0

            lax.fori_loop(0, ns, finish, 0)

    return body


def attend_part(plan, blk, nseq, lo, hi, last, scalars, q, kvs, olds):
    ns, nb = len(plan.slots), hi - lo
    outs = [sds((ns, 1, blk), F32), sds((ns, 1, blk), F32), sds((ns, 2 * HEAD, blk), F32)]
    if last:
        outs += [
            sds((ns // 2, blk, 2 * HEAD), BF16),
            sds((ns // 2, blk, 2 * HEAD), BF16),
            sds((ns, blk, 2 * HEAD), F32),
            sds((ns, 1, blk), F32),
        ]
    n_dev = plan.n_ctx * plan.n_wt
    pairs = 14 * nb
    return call(
        attend_body(plan, blk, nseq, lo, hi, last),
        "attend",
        list(scalars) + [q] + list(kvs[lo:hi]) + list(olds),
        [SMEM] * 4 + [VMEM] + [ANY] * nb + [VMEM] * len(olds),
        outs,
        scratch=[
            pltpu.VMEM((nb * ns, blk, 2 * HEAD), BF16),
            pltpu.SMEM((n_dev,), jnp.int32),
            pltpu.SMEM((ns * n_dev + 1,), jnp.int32),
            pltpu.SemaphoreType.DMA((nb,)),
        ],
        flops=pairs * 4 * blk * blk * 128 * 8,
        trans=pairs * blk * blk,
    )


def attend_back_body(plan, blk, nseq, lo, hi, first, last):
    ns, nb, nj = len(plan.slots), hi - lo, len(plan.peers)

    def body(info, deal, lengths, codes, q_ref, lse_ref, *refs):
        kv_refs, refs = refs[:nb], refs[nb:]
        if first:
            of_ref, g_refs, gs_ref, refs = refs[0], refs[1 : 1 + nj], refs[1 + nj], refs[2 + nj :]
        else:
            g_ext, delta_ref, old_dq, refs = refs[0], refs[1], refs[2], refs[3:]
        dkv_refs, refs = refs[:nb], refs[nb:]
        dq_acc, refs = refs[0], refs[1:]
        if first:
            g_ext, delta_ref, refs = refs[0], refs[1], refs[2:]
        if last:
            dq_ref, refs = refs[0], refs[1:]
        kvs, dkvs, slot_of, pairs, sem = refs
        copies = [
            pltpu.make_async_copy(ref, kvs.at[pl.ds(b * ns, ns)], sem.at[b])
            for b, ref in enumerate(kv_refs)
        ]
        for c in copies:
            c.start()
        n = list_pairs(
            plan, info, deal, lengths, codes, blk, nseq, slot_of, pairs, lo * ns, hi * ns
        )
        core = info[0] % 2
        high = lane_iota((blk, 2 * HEAD)) >= HEAD
        if first:
            own_half = (lane_iota((blk, 2 * HEAD)) // HEAD) == core
            for s in range(ns):
                g = (g_refs[s][...] if s < nj else gs_ref[s - nj]).astype(F32)
                g = jnp.where(own_half, g, 0.0)
                delta_ref[s] = jnp.sum((g * of_ref[s]).T, axis=0, keepdims=True)
                turned = pltpu.roll(g, HEAD, 1)
                g_ext[s] = jnp.where(high, jnp.where(core == 1, g, turned), 0.0).astype(BF16)
            dq_acc[...] = jnp.zeros_like(dq_acc)
        else:
            dq_acc[...] = old_dq[...]
        dkvs[...] = jnp.zeros_like(dkvs)
        for c in copies:
            c.wait()

        def pair_terms(rows, cols, mask):
            scores = [mm(kvs[c], q_ref[i], NT) for i, c in zip(rows, cols)]
            slopes = [mm(kvs[c], g_ext[i], NT) for i, c in zip(rows, cols)]
            for k, (i, c) in enumerate(zip(rows, cols)):
                p = jnp.exp(scores[k] - lse_ref[i])
                p = mask(k, p)
                ds = (p * (slopes[k] - delta_ref[i])).astype(BF16)
                dkvs[c] += mm(ds, q_ref[i]) + mm(p.astype(BF16), g_ext[i])
                dq_acc[i] += mm(kvs[c], ds, TN)

        if not lo:
            tri = lax.broadcasted_iota(jnp.int32, (blk, blk), 0) <= lane_iota((blk, blk))

            def diagonal(h, _):
                at = [h * 2, h * 2 + 1]
                pair_terms(at, at, lambda k, p: jnp.where(tri, p, 0.0))
                return 0

            lax.fori_loop(0, ns // 2, diagonal, 0)

        def step(h, _):
            codes2 = [pairs[h * 2], pairs[h * 2 + 1]]
            pair_terms(
                [c // 1024 for c in codes2],
                [c % 1024 for c in codes2],
                lambda k, p: jnp.where(h * 2 + 1 < n, p, 0.0) if k else p,
            )
            return 0

        lax.fori_loop(0, (n + 1) // 2, step, 0)
        if last:

            def finish(i, _):
                wide = dq_acc[i].T * HEAD**-0.5
                dq_ref[i] = jnp.where(high, 0.0, wide).astype(BF16)
                return 0

            lax.fori_loop(0, ns, finish, 0)
        for b in range(nb):
            dkv_refs[b][...] = dkvs[b * ns : (b + 1) * ns].astype(BF16)

    return body


def attend_back_part(plan, blk, nseq, lo, hi, first, last, scalars, q, lse, kvs, extra):
    ns, nb = len(plan.slots), hi - lo
    rows = sds((ns, blk, 2 * HEAD), BF16)
    outs = [rows] * nb + [sds((ns, 2 * HEAD, blk), F32)]
    if first:
        outs += [rows, sds((ns, 1, blk), F32)]
    if last:
        outs += [rows]
    n_dev = plan.n_ctx * plan.n_wt
    pairs = 14 * nb
    return call(
        attend_back_body(plan, blk, nseq, lo, hi, first, last),
        "attend_back",
        list(scalars) + [q, lse] + list(kvs[lo:hi]) + list(extra),
        [SMEM] * 4 + [VMEM] * 2 + [ANY] * nb + [VMEM] * len(extra),
        outs,
        scratch=[
            pltpu.VMEM((nb * ns, blk, 2 * HEAD), BF16),
            pltpu.VMEM((nb * ns, blk, 2 * HEAD), F32),
            pltpu.SMEM((n_dev,), jnp.int32),
            pltpu.SMEM((ns * n_dev + 1,), jnp.int32),
            pltpu.SemaphoreType.DMA((nb,)),
        ],
        flops=pairs * 10 * blk * blk * 128 * 8,
        trans=pairs * blk * blk,
    )


Z_ORDER = (0, 2, 1, 3)


def mlp_body(plan, width, ff, blk, packed):
    nj, nw, nc = len(plan.peers), plan.n_wt, plan.n_ctx
    nq = ff // CHUNK

    def body(info, *refs):
        refs = list(refs)
        x_ref, teacher_ref, valid_ref, vec_ref, count_ref = refs[:5]
        att = refs[5 : 5 + nj]
        rest = refs[5 + nj :]
        nwt_in = 6 if packed else 3
        w_in, rest = rest[:nwt_in], rest[nwt_in:]
        lo_ref, sq_ref, g1_ref = rest[:3]
        gatt_refs, rest = rest[3 : 3 + nj], rest[3 + nj :]
        act_ref, gpre_ref, n2_ref, gb_ref, ga_ref, gv_ref = rest[:6]
        rest = rest[6:]
        if packed:
            wup, wdown, wout, meta, slope_ref, acc_ref, sem = rest
            copies = []
            here = info[0] % 2
            owners = [info[0] ^ m for m in plan.near(here)]
            owners += [info[0] ^ 1 ^ m for m in plan.near(1 - here)]
            sources = []
            for head, pair, tail in (w_in[:3], w_in[3:]):
                sources += [head, pair.at[0], pair.at[1], tail]
            for c, src in zip(owners, sources):
                for m in range(nw):
                    w = info[1] ^ Z_ORDER[m]
                    copies += [
                        pltpu.make_async_copy(
                            src.at[m, pl.ds(nq + 4, 1)], wout.at[w, pl.ds(c, 1)], sem.at[0]
                        ),
                        pltpu.make_async_copy(src.at[m, pl.ds(0, nq)], wup.at[:, w, c], sem.at[1]),
                        pltpu.make_async_copy(
                            src.at[m, pl.ds(nq, 4)], wdown.at[w, pl.ds(c * 4, 4)], sem.at[2]
                        ),
                        pltpu.make_async_copy(
                            src.at[m, pl.ds(nq + 5, 1)], meta.at[w, pl.ds(c, 1)], sem.at[3]
                        ),
                    ]
            for cp in copies:
                cp.start()
            for cp in copies:
                cp.wait()
            w_up = lambda q: wup[q].reshape(width, CHUNK)
            w_down = lambda q: wdown[q].reshape(CHUNK, width)
            out_rows = width // nw
            pair_rows = 2 * HEAD
            wout_flat = wout.reshape(width, width)
            w_out = lambda row: wout_flat[pl.ds(row, pair_rows), :]
            count = jnp.sum(meta[:, :, 0:1, 0:1].astype(F32))
        else:
            slope_ref, acc_ref = rest
            w_up = lambda q: w_in[0][q]
            w_down = lambda q: w_in[1][q]
            w_out = lambda row: w_in[2][pl.ds(row, 2 * HEAD), :]
            count = count_ref[0]
        vecs = vec_ref[...]
        gain, shift = vecs[2:3], vecs[3:4]
        rows = []
        for mc, mw in plan.peers:
            head = plan.head(info[0] ^ mc, info[1] ^ mw)
            rows.append(pl.multiple_of((head // 2) * (2 * HEAD), 2 * HEAD))
        mixed = mm(att[0][...], w_out(rows[0]))
        for j in range(1, nj):
            mixed = mixed + mm(att[j][...], w_out(rows[j]))
        res = mixed + x_ref[...].astype(F32)
        unit, inverse = norm_stats(res)
        n2 = (unit * gain + shift).astype(BF16)
        n2_ref[...] = n2
        for q in range(nq):
            pre = mm(n2, w_up(q))
            cdf = 0.5 * (1.0 + lax.erf(pre * 0.7071067811865476))
            pdf = jnp.exp(-0.5 * pre * pre) * 0.3989422804014327
            act = (pre * cdf).astype(BF16)
            slope_ref[q] = cdf + pre * pdf
            act_ref[q] = act
            if q == 0:
                acc_ref[...] = mm(act, w_down(q))
            else:
                acc_ref[...] += mm(act, w_down(q))
        two = acc_ref[...] + res
        lo_ref[...] = two.astype(BF16)
        distance = two - teacher_ref[...].astype(F32)
        valid = valid_ref[...].astype(F32)
        weighed = valid * distance
        square = jnp.sum(weighed * distance)
        first_row = lax.broadcasted_iota(jnp.int32, (8, 128), 0) == 0
        sq_ref[...] = jnp.where(first_row, square, count)
        g2 = (2.0 * LOSS_SCALE / (count * width)) * weighed
        gb = g2.astype(BF16)
        gb_ref[...] = gb
        for q in range(nq):
            gpre = (mm(gb, w_down(q), NT) * slope_ref[q]).astype(BF16)
            gpre_ref[q] = gpre
            if q == 0:
                acc_ref[...] = mm(gpre, w_up(q), NT)
            else:
                acc_ref[...] += mm(gpre, w_up(q), NT)
        gn2 = acc_ref[...]
        g1 = g2 + norm_back(gn2, unit, inverse, gain)
        g1_ref[...] = g1
        gv_ref[...] = jnp.concatenate(
            [
                jnp.sum(gn2 * unit, axis=0, keepdims=True),
                jnp.sum(gn2, axis=0, keepdims=True),
                jnp.zeros((6, width), F32),
            ],
            axis=0,
        )
        ga = g1.astype(BF16)
        ga_ref[...] = ga
        for j in range(nj):
            gatt_refs[j][...] = mm(ga, w_out(rows[j]), NT).astype(BF16)

    return body


def mlp_grads_body(plan, width, ff, blk, packed):
    nj, nw, nc = len(plan.peers), plan.n_wt, plan.n_ctx
    nq = ff // CHUNK

    def body(info, act_ref, gpre_ref, n2_ref, gb_ref, ga_ref, gv_ref, sq_ref, *refs):
        att, outs = refs[:nj], refs[nj:]
        if packed:
            outs, (ups, downs, attn, metas, sem) = outs[:2], outs[2:]
        n2, gb, ga = n2_ref[...], gb_ref[...], ga_ref[...]
        ctx, wt = info[0], info[1]
        rows_up = width // (nw * nc)

        def put(c, w, tile, value):
            plane = (c ^ ctx) // 2
            middle = (plane == 1) | (plane == 2)
            place = jnp.where(middle, 3 - plane, plane) if c % 2 else plane
            zed = w ^ wt
            zed = jnp.where((zed == 1) | (zed == 2), 3 - zed, zed)
            for k in (0, 1):

                @pl.when(ctx % 2 == k)
                def _():
                    target = outs[(c % 2) ^ k].at[place, zed, pl.ds(tile, value.shape[0])]
                    pltpu.make_async_copy(value, target, sem.at[0]).start()

        for q in range(nq):
            up = mm(n2, gpre_ref[q], TN).astype(BF16)
            down = mm(act_ref[q], gb, TN).astype(BF16)
            if packed:
                ups[q] = up.reshape(nw * nc, rows_up, CHUNK)
                downs[q] = down.reshape(nc * 4, TILE, width)
                for w in range(nw):
                    for c in range(nc):
                        put(c, w, q, ups.at[q, pl.ds(w * nc + c, 1)])
                for c in range(nc):
                    put(c, q, nq, downs.at[q, pl.ds(4 * c, 4)])
            else:
                outs[0][q] = up
                outs[1][q] = down
        for j, (mc, mw) in enumerate(plan.peers):
            head = plan.head(ctx ^ mc, wt ^ mw)
            part = mm(att[j][...], ga, TN).astype(BF16)
            if packed:
                attn[j] = part.reshape(2 * HEAD // TILE, TILE, width)
                for t in range(2 * HEAD // TILE):
                    put(t, head // 2, nq + 4, attn.at[j, pl.ds(t, 1)])
            else:
                row = pl.multiple_of((head // 2) * (2 * HEAD), 2 * HEAD)
                outs[2][pl.ds(row, 2 * HEAD), :] = part
        if packed:
            dev = ctx * nw + wt
            square = sq_ref[0:1, 0:1]
            high = square.astype(BF16).astype(F32)
            lane = lane_iota((1, CHUNK))
            n_dev = nw * nc
            line = jnp.where(lane == dev, high, 0.0) + jnp.where(
                lane == dev + n_dev, square - high, 0.0
            )
            for w in range(nw):
                per = width // nw
                vec = gv_ref[0:2, per * w : per * (w + 1)]
                vec = jnp.concatenate([vec, jnp.zeros((2, CHUNK - per), F32)], axis=1)
                tile = jnp.concatenate([line, vec, jnp.zeros((TILE - 3, CHUNK), F32)], axis=0)
                metas[w, 0] = tile.astype(BF16)
                for c in range(nc):
                    put(c, w, nq + 5, metas.at[w])
            for ref in outs:
                pltpu.make_async_copy(ref, ref, sem.at[0]).wait()

    return body


def head_grads_body(plan, blk, width, shard, nb):
    ns, nw, nj = len(plan.slots), plan.n_wt, len(plan.peers)

    def body(info, dq_ref, wh_ref, normed_ref, *refs):
        xs = refs[:ns]
        parts = refs[ns : ns + nb]
        outs = refs[ns + nb :]
        own_ref, sib_ref, dw_ref, acc = outs
        half = shard // 2
        weight = wh_ref[...]
        gsum = jnp.zeros((1, width), F32)
        ssum = jnp.zeros((1, width), F32)
        for s in range(ns):
            dkv = parts[0][s].astype(F32)
            for b in range(1, nb):
                dkv = dkv + parts[b][s].astype(F32)
            zero = jnp.zeros((blk, 2 * HEAD), F32)
            wide = pltpu.roll(jnp.concatenate([dkv, zero], axis=1), HEAD, 1)
            wide = wide + jnp.concatenate([dq_ref[s].astype(F32), zero], axis=1)
            gh = wide.astype(BF16)
            back = mm(gh, weight, NT)
            if s < nj:
                own_ref[s] = back.astype(BF16)
            else:
                sib_ref[s - nj] = back.astype(BF16)
            unit, _ = norm_stats(xs[s][:blk, :].astype(F32))
            gsum = gsum + jnp.sum(back * unit, axis=0, keepdims=True)
            ssum = ssum + jnp.sum(back, axis=0, keepdims=True)
            dw = mm(normed_ref[s], gh, TN)
            if s == 0:
                acc[...] = dw
            else:
                acc[...] += dw
        vecs = jnp.concatenate([gsum, ssum, jnp.zeros((6, width), F32)], axis=0).astype(BF16)
        rows = lax.broadcasted_iota(jnp.int32, (8, 4 * HEAD), 0)
        pick = jnp.where(lane_iota((8, 4 * HEAD)) == rows + 3 * HEAD, 1.0, 0.0).astype(BF16)
        acc[...] += mm(vecs, pick, TN)
        for m in range(nw):
            row = pl.multiple_of((info[1] ^ m) * shard, shard)
            block = acc[pl.ds(row, shard), :].astype(BF16)
            dw_ref[m, :, : 4 * HEAD] = block[:half]
            dw_ref[m, :, 4 * HEAD :] = block[half:]

    return body


def merge_body(nj, nw, blk):
    def body(own_ref, sib_ref, dw_ref, more_ref, *outs):
        for m in range(nw):
            dw = (dw_ref[m].astype(F32) + more_ref[m].astype(F32)).astype(BF16)
            if m < nj:
                rows = own_ref[m].astype(F32) + sib_ref[m].astype(F32)
                outs[m][:blk, :] = rows.astype(BF16)
                outs[m][blk:, :] = dw
            else:
                outs[m][...] = dw

    return body


def words_body(nj):
    def body(x_ref, vec_ref, g1_ref, *refs):
        parts, sibs, out_ref = refs[:nj], refs[nj : 2 * nj], refs[-1]
        up = parts[0][: x_ref.shape[0], :].astype(F32)
        for p in parts[1:]:
            up = up + p[: up.shape[0], :].astype(F32)
        unit, inverse = norm_stats(x_ref[...].astype(F32))
        out_ref[...] = g1_ref[...] + norm_back(up, unit, inverse, vec_ref[0:1, :])

    return body


def unpack_body(plan, width, ff):
    nq, nw, nc = ff // CHUNK, plan.n_wt, plan.n_ctx

    def body(info, sq_ref, own, sib, *outs):
        srcs = [r.at[n] for r in (own, sib) for n in range(nc // 2)]
        up_ref, down_ref, out_ref, loss_ref, gain_ref, shift_ref = outs
        here = info[0] % 2
        owners = [info[0] ^ m for m in plan.near(here)]
        owners += [info[0] ^ 1 ^ m for m in plan.near(1 - here)]
        for c, src in zip(owners, srcs):
            row = pl.multiple_of(c * TILE, TILE)
            for q in range(nq):
                up_ref[pl.ds(row, TILE), q * CHUNK : (q + 1) * CHUNK] = src[q].astype(F32)
            for t in range(4):
                down_ref[pl.ds(pl.multiple_of(c * 4 * TILE + t * TILE, TILE), TILE), :] = src[
                    nq + t
                ].astype(F32)
            out_ref[pl.ds(row, TILE), :] = src[nq + 4].astype(F32)
        meta = srcs[0][nq + 5].astype(F32)
        count = jnp.max(sq_ref[1:2, :], axis=1, keepdims=True)
        loss_ref[...] = jnp.sum(meta[0:1], axis=1, keepdims=True) / (count * width)
        gain_ref[...] = meta[1:2, : width // nw]
        shift_ref[...] = meta[2:3, : width // nw]

    return body


def head_out_body(plan, shard):
    nj, half = len(plan.peers), shard // 2

    def body(info, own_ref, sib_ref, out_ref, gain_ref, shift_ref):
        core = info[0] % 2
        rows = lax.broadcasted_iota(jnp.int32, (8, 4 * HEAD), 0)
        pick = jnp.where(lane_iota((8, 4 * HEAD)) == rows + 3 * HEAD, 1.0, 0.0)
        lane = lane_iota((half, 2 * HEAD))
        for side in (0, 1):
            at = slice(side * 4 * HEAD, (side + 1) * 4 * HEAD)
            here = slice(side * half, (side + 1) * half)
            total = jnp.zeros((half, 4 * HEAD), F32)
            for j, (mc, mw) in enumerate(plan.peers):
                head = plan.head(info[0] ^ mc, info[1] ^ mw)
                own = own_ref[j, :, at].astype(F32)
                sib = sib_ref[j, :, at].astype(F32)
                total = total + own + sib
                even = jnp.where(core == 0, own, sib)
                odd = jnp.where(core == 0, sib, own)
                turned = pltpu.roll(odd, 3 * HEAD, 1)
                mid = jnp.where(lane < HEAD, even[:, 2 * HEAD :], turned[:, 2 * HEAD :])
                col = pl.multiple_of((head // 2) * (6 * HEAD), 2 * HEAD)
                out_ref[here, pl.ds(col, 2 * HEAD)] = even[:, : 2 * HEAD]
                out_ref[here, pl.ds(col + 2 * HEAD, 2 * HEAD)] = mid
                out_ref[here, pl.ds(col + 4 * HEAD, 2 * HEAD)] = turned[:, : 2 * HEAD]
            both = lax.dot_general(
                pick, total, NT, precision=lax.Precision.HIGHEST, preferred_element_type=F32
            )
            gain_ref[:, here] = both[0:1]
            shift_ref[:, here] = both[1:2]

    return body


def per_device(
    words,
    teacher,
    valid,
    lengths,
    deal,
    gain_attn,
    shift_attn,
    w_qkv,
    w_out,
    gain_mlp,
    shift_mlp,
    w_up,
    w_down,
):
    n_ctx, n_wt = lax.axis_size("ctx"), lax.axis_size("wt")
    plan = Plan(n_ctx, n_wt)
    ctx, wt = lax.axis_index("ctx"), lax.axis_index("wt")
    blk, width = words.shape
    shard = width // n_wt
    ff = w_up.shape[1]
    nq = ff // CHUNK
    nseq = lengths.shape[0]
    ns, nb, nj = len(plan.slots), len(plan.groups), len(plan.peers)
    packed = plan.square and width == CHUNK and width % (n_wt * n_ctx * TILE) == 0
    packed = packed and n_wt * CHUNK == ff and 2 * HEAD // TILE == n_ctx
    info = jnp.stack([ctx, wt]).astype(jnp.int32)
    codes = jnp.array([mc * n_wt + mw for mc, mw in plan.slots], jnp.int32)
    core = (1, 0)

    vecs_here = jnp.stack([gain_attn, shift_attn, gain_mlp, shift_mlp])
    load = call(
        pack_body(plan, shard, blk),
        "pack",
        [info, words, w_qkv, vecs_here],
        [SMEM] + [VMEM] * 3,
        [sds((blk + shard // 2, width), BF16)] * n_wt,
    )
    loads = [load[0]] + [plan.swap(load[m], (0, m)) for m in range(1, n_wt)]
    xs = loads[:nj] + [plan.swap(x, core) for x in loads[:nj]]

    q, kv, normed, w_head, vecs = call(
        project_body(plan, shard, blk),
        "project",
        [info] + xs + loads,
        [SMEM] + [VMEM] * (ns + n_wt),
        [
            sds((ns, blk, 2 * HEAD), BF16),
            sds((ns, blk, 2 * HEAD), BF16),
            sds((ns, blk, width), BF16),
            sds((width, 4 * HEAD), BF16),
            sds((8, width), F32),
        ],
        flops=2 * ns * blk * width * 4 * HEAD,
    )
    kvs = plan.gather_groups(kv)

    if packed:
        rows_up = width // (n_wt * n_ctx)
        up_piece = lax.dynamic_slice_in_dim(w_up, ctx * rows_up, rows_up, 0)
        up_piece = up_piece.reshape(rows_up, nq, CHUNK).transpose(1, 0, 2)
        down_piece = lax.dynamic_slice_in_dim(w_down, ctx * 4 * TILE, 4 * TILE, 0)
        out_piece = lax.dynamic_slice_in_dim(w_out, ctx * TILE, TILE, 0)
        count_here = jnp.sum(valid).astype(BF16)
        piece = jnp.concatenate(
            [
                up_piece,
                down_piece.reshape(4, TILE, CHUNK),
                out_piece[None],
                jnp.full((1, TILE, CHUNK), count_here, BF16),
            ],
            axis=0,
        )
        piece = after(piece, kvs[1])
        count = jnp.zeros((1,), F32)
    else:
        up_full = lax.all_gather(w_up, "wt", axis=0, tiled=True)
        down_full = lax.all_gather(w_down, "wt", axis=0, tiled=True)
        out_full = lax.all_gather(w_out, "wt", axis=0, tiled=True)
        weights = [
            up_full.reshape(width, nq, CHUNK).transpose(1, 0, 2),
            down_full.reshape(nq, CHUNK, width),
            out_full,
        ]
        count = lax.psum(jnp.sum(valid).astype(F32), ("ctx", "wt")).reshape(1)

    scalars = [info, deal, lengths, codes]
    state = []
    if not plan.square:
        state = attend_part(plan, blk, nseq, 0, nb, True, scalars, q, kvs, state)
    else:
        state = attend_part(plan, blk, nseq, 0, 1, False, scalars, q, kvs, state)
        if packed:
            two = jnp.stack([piece, plan.swap(piece, (0, 2))])
            two = after(two, state[0])
            other = plan.swap(two, (0, 1))
        state = [after(state[0], kvs[3]), *state[1:]]
        state = attend_part(plan, blk, nseq, 1, 3, False, scalars, q, kvs, state)
        if packed:
            stack = jnp.concatenate([two, other])
            stack = after(stack, state[0])
            one, side = plan.turn(stack, True), plan.turn(stack, False)
            stack_sib = plan.swap(stack, core)
        state = attend_part(plan, blk, nseq, 3, 4, True, scalars, q, kvs, state)
    o, o_sib, of32, lse = state[3:]
    o_sib = plan.swap(o_sib, core)
    if packed:
        one = after(one, o_sib)
        last = plan.turn(one, False)
        pair = jnp.stack([one, side])
        weights = [stack, pair, last, stack_sib, plan.swap(pair, core)]
    mixed = o + o_sib
    att = [mixed[0]] + [plan.swap(mixed[j], plan.peers[j]) for j in range(1, nj)]
    if packed:
        weights += [plan.swap(after(last, *att[1:]), core)]

    mlp_in = [info, words, teacher, valid[:, None], vecs, count] + att + weights
    specs = [SMEM] + [VMEM] * 4 + [SMEM] + [VMEM] * nj
    specs += [ANY] * len(weights) if packed else [VMEM] * len(weights)
    scratch = [pltpu.VMEM((nq, blk, CHUNK), F32), pltpu.VMEM((blk, width), F32)]
    if packed:
        scratch = [
            pltpu.VMEM((nq, n_wt, n_ctx, TILE, CHUNK), BF16),
            pltpu.VMEM((n_wt, n_ctx * 4, TILE, CHUNK), BF16),
            pltpu.VMEM((n_wt, n_ctx, TILE, CHUNK), BF16),
            pltpu.VMEM((n_wt, n_ctx, TILE, CHUNK), BF16),
            *scratch,
            pltpu.SemaphoreType.DMA((4,)),
        ]
    layer_out, square, grad_one, *rest = call(
        mlp_body(plan, width, ff, blk, packed),
        "mlp",
        mlp_in,
        specs,
        [
            sds((blk, width), BF16),
            sds((8, 128), F32),
            sds((blk, width), F32),
            *[sds((blk, 2 * HEAD), BF16)] * nj,
            sds((nq, blk, CHUNK), BF16),
            sds((nq, blk, CHUNK), BF16),
            sds((blk, width), BF16),
            sds((blk, width), BF16),
            sds((blk, width), BF16),
            sds((8, width), F32),
        ],
        scratch=scratch,
        flops=8 * blk * width * ff,
        trans=2 * blk * ff,
    )
    gatt, (act, gpre, n2, gb, ga, gvec) = rest[:nj], rest[nj:]
    g_own = [gatt[0]] + [plan.swap(gatt[j], plan.peers[j]) for j in range(1, nj)]
    g_sib = plan.swap(jnp.stack(g_own), core)

    grads_in = [info, act, gpre, n2, gb, ga, gvec, square] + att
    if packed:
        grads_out = [sds((n_ctx // 2, n_wt, nq + 6, TILE, CHUNK), BF16)] * 2
        grads_scratch = [
            pltpu.VMEM((nq, n_wt * n_ctx, TILE, CHUNK), BF16),
            pltpu.VMEM((nq, n_ctx * 4, TILE, CHUNK), BF16),
            pltpu.VMEM((nj, n_ctx, TILE, CHUNK), BF16),
            pltpu.VMEM((n_wt, 1, TILE, CHUNK), BF16),
            pltpu.SemaphoreType.DMA((1,)),
        ]
    else:
        grads_out = [
            sds((nq, width, CHUNK), BF16),
            sds((nq, CHUNK, width), BF16),
            sds((width, width), BF16),
        ]
        grads_scratch = []
    weight_grads = call(
        mlp_grads_body(plan, width, ff, blk, packed),
        "mlp_grads",
        grads_in,
        [SMEM] + [VMEM] * (7 + nj),
        grads_out,
        scratch=grads_scratch,
        out_specs=[ANY if packed else VMEM] * len(grads_out),
        flops=4 * blk * width * ff,
    )

    extra = [of32] + g_own + [g_sib]
    if plan.square:
        if packed:
            g_all, g_core = weight_grads[0], plan.swap(weight_grads[1], core)
            g_far = (g_all[2:].astype(F32) + g_core[2:].astype(F32)).astype(BF16)
            extra = [after(of32, g_far)] + extra[1:]
            g_far = plan.turn(g_far, False)
        part = attend_back_part(plan, blk, nseq, 2, 4, True, False, scalars, q, lse, kvs, extra)
        dkv2, dkv3, dq_part, g_ext, delta = part
        far = [plan.turn(d, False) for d in (dkv3, dkv2)]
        dkv1, dq_part = attend_back_part(
            plan, blk, nseq, 1, 2, False, False, scalars, q, lse, kvs, [g_ext, delta, dq_part]
        )
        mid = plan.turn((dkv1.astype(F32) + far[0].astype(F32)).astype(BF16), True)
        if packed:
            g_far = after(g_far, dkv1)
            g_mid = g_all[1].astype(F32) + g_core[1].astype(F32) + g_far[1].astype(F32)
            g_mid = g_mid.astype(BF16)
            dq_part = after(dq_part, g_mid)
            g_mid = plan.turn(g_mid, True)
        dkv0, _, dq = attend_back_part(
            plan, blk, nseq, 0, 1, False, True, scalars, q, lse, kvs, [g_ext, delta, dq_part]
        )
        if packed:
            g_mid = after(g_mid, dkv0)
            g_near = g_all[0].astype(F32) + g_core[0].astype(F32) + g_far[0].astype(F32)
            g_near = (g_near + g_mid.astype(F32)).astype(BF16)
            dq = after(dq, g_near)
            g_other = plan.swap(g_near[2:], (0, 1))
        parts = [dkv0, far[1], mid]
    else:
        part = attend_back_part(plan, blk, nseq, 0, nb, True, True, scalars, q, lse, kvs, extra)
        dq = part[-1]
        parts = [part[0]] + [plan.swap(part[b], plan.groups[b]) for b in range(1, nb)]

    head_outs = call(
        head_grads_body(plan, blk, width, shard, len(parts)),
        "head_grads",
        [info, dq, w_head, normed] + xs + parts,
        [SMEM] + [VMEM] * (3 + ns + len(parts)),
        [sds((nj, blk, width), BF16)] * 2 + [sds((n_wt, shard // 2, width), BF16)],
        scratch=[pltpu.VMEM((width, 4 * HEAD), F32)],
        flops=4 * ns * blk * width * 4 * HEAD,
    )
    own_rows, sib_rows, dw = head_outs
    if packed:
        g_two = (g_near[:2].astype(F32) + g_other.astype(F32)).astype(BF16)
        g_last = plan.swap(g_two[1], (0, 2))
    sib_rows = plan.swap(sib_rows, core)

    if plan.square:
        dw = (dw.astype(F32) + plan.turn(dw, True).astype(F32)).astype(BF16)
        dw_more = plan.turn(dw, False)
    else:
        step = CTX_HEADS
        while step < n_ctx:
            dw_more = plan.swap(dw, (step, 0))
            step *= 2
            if step < n_ctx:
                dw = (dw.astype(F32) + dw_more.astype(F32)).astype(BF16)
    load = call(
        merge_body(nj, n_wt, blk),
        "merge",
        [own_rows, sib_rows, dw, dw_more],
        [VMEM] * 4,
        [sds((blk + shard // 2, width), BF16)] * nj
        + [sds((shard // 2, width), BF16)] * (n_wt - nj),
    )
    loads = [load[0]] + [plan.swap(load[m], (0, m)) for m in range(1, n_wt)]
    if packed:
        g_last = after(g_last, load[0])
        final = (g_two[0].astype(F32) + g_last.astype(F32)).astype(BF16)
        finals = plan.gather_square(final)
        finals = jnp.stack(finals)
        finals = [finals, plan.swap(finals, core)]
        g_up, g_down, g_out, loss, g_gain, g_shift = call(
            unpack_body(plan, width, ff),
            "unpack",
            [info, square] + finals,
            [SMEM] + [VMEM] * 3,
            [
                sds((shard, ff), F32),
                sds((ff // n_wt, width), F32),
                sds((shard, width), F32),
                sds((1, 1), F32),
                sds((1, shard), F32),
                sds((1, shard), F32),
            ],
        )
        loss, g_gain, g_shift = loss[0, 0], g_gain.reshape(shard), g_shift.reshape(shard)
    else:
        g_up, g_down, g_out = weight_grads
        g_up = g_up.transpose(1, 0, 2).reshape(width, ff)
        g_down = g_down.reshape(ff, width)

        def reduce_rows(g):
            part = lax.psum_scatter(g.astype(BF16), "wt", scatter_dimension=0, tiled=True)
            return lax.psum(part, "ctx").astype(F32)

        g_up, g_down, g_out = reduce_rows(g_up), reduce_rows(g_down), reduce_rows(g_out)
        both = lax.psum(gvec[:2], ("ctx", "wt"))
        both = lax.dynamic_slice_in_dim(both, wt * shard, shard, 1)
        g_gain, g_shift = both[0], both[1]
        loss = lax.psum(square[0, 0], ("ctx", "wt")) / (count[0] * width)
    if packed:
        loads = loads[:3] + [after(loads[3], g_up)]
    own_heads = jnp.stack([x[blk:] for x in loads[:nj]])
    if n_wt > nj:
        own_heads = (own_heads.astype(F32) + jnp.stack(loads[nj:]).astype(F32)).astype(BF16)
    sib_heads = plan.swap(own_heads, core)
    grad_words = call(
        words_body(nj),
        "words_grad",
        [words, vecs, grad_one] + loads[:nj],
        [VMEM] * (3 + nj),
        [sds((blk, width), F32)],
    )[0]
    g_qkv, gain_one, shift_one = call(
        head_out_body(plan, shard),
        "head_out",
        [info, own_heads, sib_heads],
        [SMEM] + [VMEM] * 2,
        [sds((shard, 3 * width), F32), sds((1, shard), F32), sds((1, shard), F32)],
    )

    return (
        layer_out,
        loss,
        grad_words,
        gain_one.reshape(shard),
        shift_one.reshape(shard),
        g_qkv,
        g_out,
        g_gain,
        g_shift,
        g_up,
        g_down,
    )


def solution(mesh):
    placed = (
        P(("ctx", "wt"), None),
        P(("ctx", "wt"), None),
        P(("ctx", "wt")),
        P(),
        P(),
        P("wt"),
        P("wt"),
        P("wt", None),
        P("wt", None),
        P("wt"),
        P("wt"),
        P("wt", None),
        P("wt", None),
    )
    return jax.shard_map(
        per_device,
        mesh=mesh,
        in_specs=placed,
        out_specs=(
            P(("ctx", "wt"), None),
            P(),
            P(("ctx", "wt"), None),
            P("wt"),
            P("wt"),
            P("wt", None),
            P("wt", None),
            P("wt"),
            P("wt"),
            P("wt", None),
            P("wt", None),
        ),
        check_vma=False,
    )
```

```python
import jax
import jax.numpy as jnp
from jax import lax
from jax.experimental import pallas as pl
from jax.experimental.pallas import tpu as pltpu
from jax.sharding import PartitionSpec as P

H = 8
HEAD = 64
EPS = 1e-05
LOSS_SCALE = 262144.0
CTX_HEADS = 2
WT_HEADS = 4
CHUNK = 512
TILE = 16
WIDE = 4
WIDE_BACK = 4
F32 = jnp.float32
BF16 = jnp.bfloat16
NEG = -1e30
NT = (((1,), (1,)), ((), ()))
TN = (((0,), (0,)), ((), ()))
NN = (((1,), (0,)), ((), ()))


def mm(a, b, dims=NN):
    return lax.dot_general(a, b, dims, preferred_element_type=F32)


def lane_iota(shape):
    return lax.broadcasted_iota(jnp.int32, shape, len(shape) - 1)


def norm_stats(values):
    center = values - jnp.mean(values, axis=-1, keepdims=True)
    inverse = lax.rsqrt(jnp.mean(center * center, axis=-1, keepdims=True) + EPS)
    return center * inverse, inverse


def norm_back(upstream, unit, inverse, gain):
    scaled = upstream * gain
    inner = jnp.mean(scaled * unit, axis=-1, keepdims=True)
    return inverse * (scaled - jnp.mean(scaled, axis=-1, keepdims=True) - unit * inner)


SMEM = pl.BlockSpec(memory_space=pltpu.SMEM)
VMEM = pl.BlockSpec(memory_space=pltpu.VMEM)
ANY = pl.BlockSpec(memory_space=pl.ANY)


def call(body, name, ins, in_specs, outs, scratch=(), flops=0, trans=0, out_specs=None):
    nbytes = sum(x.size * x.dtype.itemsize for x in list(ins) + list(outs))
    return pl.pallas_call(
        body,
        name=name,
        out_shape=list(outs),
        in_specs=in_specs,
        out_specs=out_specs or [VMEM] * len(outs),
        scratch_shapes=list(scratch),
        compiler_params=pltpu.CompilerParams(vmem_limit_bytes=58 * 1024 * 1024),
        cost_estimate=pl.CostEstimate(flops=flops, bytes_accessed=nbytes, transcendentals=trans),
    )(*ins)


def after(value, *earlier):
    return lax.optimization_barrier((value, *earlier))[0]


def sds(shape, dtype):
    return jax.ShapeDtypeStruct(shape, dtype)


class Plan:
    def __init__(self, n_ctx, n_wt):
        self.n_ctx, self.n_wt = n_ctx, n_wt
        ac, aw = CTX_HEADS, WT_HEADS
        assert ac * aw == H and n_ctx % ac == 0 and n_wt % aw == 0
        self.peers = [(mc, mw) for mw in range(aw) for mc in range(0, ac, 2)]
        self.slots = [(mc | k, mw) for k in (0, 1) for mc, mw in self.peers]
        self.groups = [(mc, mw) for mc in range(0, n_ctx, ac) for mw in range(0, n_wt, aw)]
        self.square = n_ctx == 8 and n_wt == aw

    def near(self, core):
        return [0, 2 + 2 * core, 4 - 2 * core, 6]

    def group_masks(self, core):
        return [(m, 0) for m in self.near(core)] if self.square else self.groups

    def head(self, ctx, wt):
        return (wt % WT_HEADS) * CTX_HEADS + ctx % CTX_HEADS

    def swap(self, x, mask):
        mc, mw = mask
        n = self.n_wt
        perm = [
            (c * n + w, (c ^ mc) * n + (w ^ mw)) for c in range(self.n_ctx) for w in range(n)
        ]
        return lax.ppermute(x, ("ctx", "wt"), perm)

    def turn(self, x, first):
        n = self.n_wt
        masks = (2, 4) if first else (4, 2)
        perm = [
            (c * n + w, (c ^ masks[c % 2]) * n + w) for c in range(self.n_ctx) for w in range(n)
        ]
        return lax.ppermute(x, ("ctx", "wt"), perm)

    def gather_square(self, x):
        one = self.turn(x, True)
        return [x, one, self.turn(x, False), self.turn(one, False)]

    def gather_groups(self, x):
        if self.square:
            return self.gather_square(x)
        return [x] + [self.swap(x, m) for m in self.groups[1:]]


def pack_body(plan, shard, blk):
    nw, half = plan.n_wt, shard // 2

    def body(info, words_ref, w_ref, vec_ref, *outs):
        odd = (info[0] % 2) == 1
        rows = lax.broadcasted_iota(jnp.int32, (4, 4 * HEAD), 0)
        pick = jnp.where(lane_iota((4, 4 * HEAD)) == rows + 3 * HEAD, 1.0, 0.0).astype(BF16)
        vec = mm(vec_ref[...], pick, TN)
        lane = lane_iota((shard, 4 * HEAD))
        for m in range(nw):
            pair = plan.head(info[0], info[1] ^ m) // 2
            col = pl.multiple_of(pair * (6 * HEAD), 2 * HEAD)
            both = w_ref[:, pl.ds(col, 6 * HEAD)].astype(F32)
            turned = pltpu.roll(both, 3 * HEAD, 1)
            cols = jnp.where(odd, turned[:, : 4 * HEAD], both[:, : 4 * HEAD])
            cols = jnp.where(lane < 3 * HEAD, cols, vec).astype(BF16)
            outs[m][:blk, :] = words_ref[...]
            outs[m][blk:, : 4 * HEAD] = cols[:half]
            outs[m][blk:, 4 * HEAD :] = cols[half:]

    return body


def project_body(plan, shard, blk):
    ns, nw, half = len(plan.slots), plan.n_wt, shard // 2

    def body(info, *refs):
        xs, wps = refs[:ns], refs[ns : ns + nw]
        q_ref, kv_ref, normed_ref, wh_ref, vec_ref = refs[ns + nw :]
        wt = info[1]
        for m in range(nw):
            row = pl.multiple_of((wt ^ m) * shard, shard)
            wh_ref[pl.ds(row, half), :] = wps[m][blk:, : 4 * HEAD]
            wh_ref[pl.ds(row + half, half), :] = wps[m][blk:, 4 * HEAD :]
        weight = wh_ref[...]
        rows = lax.broadcasted_iota(jnp.int32, (8, 4 * HEAD), 0)
        pick = jnp.where(lane_iota((8, 4 * HEAD)) == rows + 3 * HEAD, 1.0, 0.0).astype(BF16)
        vecs = mm(pick, weight, NT)
        vec_ref[...] = vecs
        gain, shift = vecs[0:1], vecs[1:2]
        low = lane_iota((blk, 2 * HEAD)) < HEAD
        for s in range(ns):
            unit, _ = norm_stats(xs[s][:blk, :].astype(F32))
            normed = (unit * gain + shift).astype(BF16)
            normed_ref[s] = normed
            y = mm(normed, weight)
            q_ref[s] = (
                jnp.where(low, y[:, : 2 * HEAD], 0.0).astype(BF16).astype(F32) * HEAD**-0.5
            ).astype(BF16)
            kv_ref[s] = pltpu.roll(y, 3 * HEAD, 1)[:, : 2 * HEAD].astype(BF16)

    return body


def fill_slots(plan, info, deal, slot_of):
    for g, (gc, gw) in enumerate(plan.group_masks(info[0] % 2)):
        for s, (mc, mw) in enumerate(plan.slots):
            at = (info[0] ^ gc ^ mc) * plan.n_wt + (info[1] ^ gw ^ mw)
            slot_of[deal[at]] = g * len(plan.slots) + s


def slot_range(plan, info, deal, lengths, codes, i, blk, nseq):
    code = codes[i]
    here = deal[(info[0] ^ (code // plan.n_wt)) * plan.n_wt + (info[1] ^ (code % plan.n_wt))]
    first = jnp.int32(0)
    total = jnp.int32(0)
    for n in range(nseq):
        total = total + lengths[n]
        bound = total // blk
        first = jnp.where(bound <= here, bound, first)
    return first, here


def lists_body(plan, blk, nseq, sets):
    ns = len(plan.slots)

    def body(info, deal, lengths, codes, *refs):
        outs, slot_of = refs[:-1], refs[-1]
        fill_slots(plan, info, deal, slot_of)

        def one_block(i, counts):
            first, here = slot_range(plan, info, deal, lengths, codes, i, blk, nseq)

            def one_key(b, counts):
                slot = slot_of[b]
                more = []
                for out, n, (lo, hi) in zip(outs, counts, sets):
                    inside = (slot >= lo * ns) & (slot < hi * ns)
                    out[n] = i * 1024 + slot - lo * ns
                    more.append(n + inside.astype(jnp.int32))
                return tuple(more)

            return lax.fori_loop(first, here, one_key, counts)

        start = tuple(jnp.int32(1) for _ in sets)
        counts = lax.fori_loop(0, ns, one_block, start)
        for out, n in zip(outs, counts):
            spare = jnp.where(n > 1, out[jnp.maximum(n - 1, 1)], 0)
            for t in range(max(WIDE, WIDE_BACK) - 1):
                out[n + t] = spare
            out[0] = n - 1

    return body


def attend_body(plan, blk, lo, hi, last):
    ns, nb = len(plan.slots), hi - lo

    def body(info, pairs, q_ref, *refs):
        kv_refs, refs = refs[:nb], refs[nb:]
        if lo:
            olds, refs = refs[:3], refs[3:]
        (m_ref, l_ref, acc_ref), refs = refs[:3], refs[3:]
        if last:
            (o_ref, o_sib_ref, of_ref, lse_ref), refs = refs[:4], refs[4:]
        kvs, sem = refs
        copies = [
            pltpu.make_async_copy(ref, kvs.at[pl.ds(b * ns, ns)], sem.at[b])
            for b, ref in enumerate(kv_refs)
        ]
        for c in copies:
            c.start()
        n = pairs[0]
        if lo:
            for new, old in zip((m_ref, l_ref, acc_ref), olds):
                new[...] = old[...]
        for c in copies:
            c.wait()
        if not lo:
            tri = lax.broadcasted_iota(jnp.int32, (blk, blk), 0) <= lane_iota((blk, blk))

            def diagonal(h, _):
                scores = [mm(kvs[h * WIDE + k], q_ref[h * WIDE + k], NT) for k in range(WIDE)]
                for k in range(WIDE):
                    i = h * WIDE + k
                    s = jnp.where(tri, scores[k], NEG)
                    m = jnp.max(s, axis=0, keepdims=True)
                    p = jnp.exp(s - m)
                    m_ref[i] = m
                    l_ref[i] = jnp.sum(p, axis=0, keepdims=True)
                    acc_ref[i] = mm(kvs[i], p.astype(BF16), TN)
                return 0

            lax.fori_loop(0, ns // WIDE, diagonal, 0)

        def step(h, _):
            codes2 = [pairs[h * WIDE + 1 + k] for k in range(WIDE)]
            rows = [c // 1024 for c in codes2]
            cols = [c % 1024 for c in codes2]
            scores = [mm(kvs[cols[k]], q_ref[rows[k]], NT) for k in range(WIDE)]
            for k in range(1, WIDE):
                scores[k] = jnp.where(h * WIDE + k < n, scores[k], NEG)
            for k in range(WIDE):
                i, s = rows[k], scores[k]
                m_old = m_ref[i]
                m = jnp.maximum(m_old, jnp.max(s, axis=0, keepdims=True))
                p = jnp.exp(s - m)
                factor = jnp.exp(m_old - m)
                m_ref[i] = m
                l_ref[i] = l_ref[i] * factor + jnp.sum(p, axis=0, keepdims=True)
                acc_ref[i] = acc_ref[i] * factor + mm(kvs[cols[k]], p.astype(BF16), TN)
            return 0

        lax.fori_loop(0, (n + WIDE - 1) // WIDE, step, 0)
        if last:
            core = info[0] % 2

            def finish(i, _):
                total = l_ref[i]
                lse_ref[i] = m_ref[i] + jnp.log(total)
                out = acc_ref[i, HEAD:, :] / total
                zero = jnp.zeros_like(out)
                placed = jnp.concatenate(
                    [jnp.where(core == 0, out, zero), jnp.where(core == 1, out, zero)], axis=0
                )
                wide = placed.T
                of_ref[i] = wide

                @pl.when(i < ns // 2)
                def _():
                    o_ref[i] = wide.astype(BF16)

                @pl.when(i >= ns // 2)
                def _():
                    o_sib_ref[i - ns // 2] = wide.astype(BF16)

                return 0

            lax.fori_loop(0, ns, finish, 0)

    return body


def attend_part(plan, blk, lo, hi, last, info, lists, q, kvs, olds):
    ns, nb = len(plan.slots), hi - lo
    outs = [sds((ns, 1, blk), F32), sds((ns, 1, blk), F32), sds((ns, 2 * HEAD, blk), F32)]
    if last:
        outs += [
            sds((ns // 2, blk, 2 * HEAD), BF16),
            sds((ns // 2, blk, 2 * HEAD), BF16),
            sds((ns, blk, 2 * HEAD), F32),
            sds((ns, 1, blk), F32),
        ]
    pairs = 14 * nb
    return call(
        attend_body(plan, blk, lo, hi, last),
        "attend",
        [info, lists[lo, hi], q] + list(kvs[lo:hi]) + list(olds),
        [SMEM] * 2 + [VMEM] + [ANY] * nb + [VMEM] * len(olds),
        outs,
        scratch=[
            pltpu.VMEM((nb * ns, blk, 2 * HEAD), BF16),
            pltpu.SemaphoreType.DMA((nb,)),
        ],
        flops=pairs * 4 * blk * blk * 128 * 8,
        trans=pairs * blk * blk,
    )


def attend_back_body(plan, blk, lo, hi, first, last):
    ns, nb, nj = len(plan.slots), hi - lo, len(plan.peers)

    def body(info, pairs, q_ref, lse_ref, *refs):
        kv_refs, refs = refs[:nb], refs[nb:]
        if first:
            of_ref, g_refs, gs_ref, refs = refs[0], refs[1 : 1 + nj], refs[1 + nj], refs[2 + nj :]
        else:
            g_ext, delta_ref, old_dq, refs = refs[0], refs[1], refs[2], refs[3:]
        dkv_refs, refs = refs[:nb], refs[nb:]
        dq_acc, refs = refs[0], refs[1:]
        if first:
            g_ext, delta_ref, refs = refs[0], refs[1], refs[2:]
        if last:
            dq_ref, refs = refs[0], refs[1:]
        kvs, dkvs, sem = refs
        copies = [
            pltpu.make_async_copy(ref, kvs.at[pl.ds(b * ns, ns)], sem.at[b])
            for b, ref in enumerate(kv_refs)
        ]
        for c in copies:
            c.start()
        n = pairs[0]
        core = info[0] % 2
        high = lane_iota((blk, 2 * HEAD)) >= HEAD
        if first:
            own_half = (lane_iota((blk, 2 * HEAD)) // HEAD) == core
            for s in range(ns):
                g = (g_refs[s][...] if s < nj else gs_ref[s - nj]).astype(F32)
                g = jnp.where(own_half, g, 0.0)
                delta_ref[s] = jnp.sum((g * of_ref[s]).T, axis=0, keepdims=True)
                turned = pltpu.roll(g, HEAD, 1)
                g_ext[s] = jnp.where(high, jnp.where(core == 1, g, turned), 0.0).astype(BF16)
            dq_acc[...] = jnp.zeros_like(dq_acc)
        else:
            dq_acc[...] = old_dq[...]
        dkvs[...] = jnp.zeros_like(dkvs)
        for c in copies:
            c.wait()

        def pair_terms(rows, cols, mask):
            scores = [mm(kvs[c], q_ref[i], NT) for i, c in zip(rows, cols)]
            slopes = [mm(kvs[c], g_ext[i], NT) for i, c in zip(rows, cols)]
            for k, (i, c) in enumerate(zip(rows, cols)):
                p = jnp.exp(scores[k] - lse_ref[i])
                p = mask(k, p)
                ds = (p * (slopes[k] - delta_ref[i])).astype(BF16)
                dkvs[c] += mm(ds, q_ref[i]) + mm(p.astype(BF16), g_ext[i])
                dq_acc[i] += mm(kvs[c], ds, TN)

        if not lo:
            tri = lax.broadcasted_iota(jnp.int32, (blk, blk), 0) <= lane_iota((blk, blk))

            def diagonal(h, _):
                at = [h * WIDE_BACK + k for k in range(WIDE_BACK)]
                pair_terms(at, at, lambda k, p: jnp.where(tri, p, 0.0))
                return 0

            lax.fori_loop(0, ns // WIDE_BACK, diagonal, 0)

        def step(h, _):
            codes2 = [pairs[h * WIDE_BACK + 1 + k] for k in range(WIDE_BACK)]
            pair_terms(
                [c // 1024 for c in codes2],
                [c % 1024 for c in codes2],
                lambda k, p: jnp.where(h * WIDE_BACK + k < n, p, 0.0) if k else p,
            )
            return 0

        lax.fori_loop(0, (n + WIDE_BACK - 1) // WIDE_BACK, step, 0)
        if last:

            def finish(i, _):
                wide = dq_acc[i].T * HEAD**-0.5
                dq_ref[i] = jnp.where(high, 0.0, wide).astype(BF16)
                return 0

            lax.fori_loop(0, ns, finish, 0)
        for b in range(nb):
            dkv_refs[b][...] = dkvs[b * ns : (b + 1) * ns].astype(BF16)

    return body


def attend_back_part(plan, blk, lo, hi, first, last, info, lists, q, lse, kvs, extra):
    ns, nb = len(plan.slots), hi - lo
    rows = sds((ns, blk, 2 * HEAD), BF16)
    outs = [rows] * nb + [sds((ns, 2 * HEAD, blk), F32)]
    if first:
        outs += [rows, sds((ns, 1, blk), F32)]
    if last:
        outs += [rows]
    pairs = 14 * nb
    return call(
        attend_back_body(plan, blk, lo, hi, first, last),
        "attend_back",
        [info, lists[lo, hi], q, lse] + list(kvs[lo:hi]) + list(extra),
        [SMEM] * 2 + [VMEM] * 2 + [ANY] * nb + [VMEM] * len(extra),
        outs,
        scratch=[
            pltpu.VMEM((nb * ns, blk, 2 * HEAD), BF16),
            pltpu.VMEM((nb * ns, blk, 2 * HEAD), F32),
            pltpu.SemaphoreType.DMA((nb,)),
        ],
        flops=pairs * 10 * blk * blk * 128 * 8,
        trans=pairs * blk * blk,
    )


Z_ORDER = (0, 2, 1, 3)


def mlp_body(plan, width, ff, blk, packed):
    nj, nw, nc = len(plan.peers), plan.n_wt, plan.n_ctx
    nq = ff // CHUNK

    def body(info, *refs):
        refs = list(refs)
        x_ref, teacher_ref, valid_ref, vec_ref, count_ref = refs[:5]
        att = refs[5 : 5 + nj]
        rest = refs[5 + nj :]
        nwt_in = 6 if packed else 3
        w_in, rest = rest[:nwt_in], rest[nwt_in:]
        lo_ref, sq_ref, g1_ref = rest[:3]
        gatt_refs, rest = rest[3 : 3 + nj], rest[3 + nj :]
        act_ref, gpre_ref, n2_ref, gb_ref, ga_ref, gv_ref = rest[:6]
        rest = rest[6:]
        if packed:
            wup, wdown, wout, meta, slope_ref, acc_ref, sem = rest
            copies = []
            here = info[0] % 2
            owners = [info[0] ^ m for m in plan.near(here)]
            owners += [info[0] ^ 1 ^ m for m in plan.near(1 - here)]
            sources = []
            for head, pair, tail in (w_in[:3], w_in[3:]):
                sources += [head, pair.at[0], pair.at[1], tail]
            for c, src in zip(owners, sources):
                for m in range(nw):
                    w = info[1] ^ Z_ORDER[m]
                    copies += [
                        pltpu.make_async_copy(
                            src.at[m, pl.ds(nq + 4, 1)], wout.at[w, pl.ds(c, 1)], sem.at[0]
                        ),
                        pltpu.make_async_copy(src.at[m, pl.ds(0, nq)], wup.at[:, w, c], sem.at[1]),
                        pltpu.make_async_copy(
                            src.at[m, pl.ds(nq, 4)], wdown.at[w, pl.ds(c * 4, 4)], sem.at[2]
                        ),
                        pltpu.make_async_copy(
                            src.at[m, pl.ds(nq + 5, 1)], meta.at[w, pl.ds(c, 1)], sem.at[3]
                        ),
                    ]
            for cp in copies:
                cp.start()
            for cp in copies:
                cp.wait()
            w_up = lambda q: wup[q].reshape(width, CHUNK)
            w_down = lambda q: wdown[q].reshape(CHUNK, width)
            out_rows = width // nw
            pair_rows = 2 * HEAD
            wout_flat = wout.reshape(width, width)
            w_out = lambda row: wout_flat[pl.ds(row, pair_rows), :]
            count = jnp.sum(meta[:, :, 0:1, 0:1].astype(F32))
        else:
            slope_ref, acc_ref = rest
            w_up = lambda q: w_in[0][q]
            w_down = lambda q: w_in[1][q]
            w_out = lambda row: w_in[2][pl.ds(row, 2 * HEAD), :]
            count = count_ref[0]
        vecs = vec_ref[...]
        gain, shift = vecs[2:3], vecs[3:4]
        rows = []
        for mc, mw in plan.peers:
            head = plan.head(info[0] ^ mc, info[1] ^ mw)
            rows.append(pl.multiple_of((head // 2) * (2 * HEAD), 2 * HEAD))
        mixed = mm(att[0][...], w_out(rows[0]))
        for j in range(1, nj):
            mixed = mixed + mm(att[j][...], w_out(rows[j]))
        res = mixed + x_ref[...].astype(F32)
        unit, inverse = norm_stats(res)
        n2 = (unit * gain + shift).astype(BF16)
        n2_ref[...] = n2
        for q in range(nq):
            pre = mm(n2, w_up(q))
            cdf = 0.5 * (1.0 + lax.erf(pre * 0.7071067811865476))
            pdf = jnp.exp(-0.5 * pre * pre) * 0.3989422804014327
            act = (pre * cdf).astype(BF16)
            slope_ref[q] = cdf + pre * pdf
            act_ref[q] = act
            if q == 0:
                acc_ref[...] = mm(act, w_down(q))
            else:
                acc_ref[...] += mm(act, w_down(q))
        two = acc_ref[...] + res
        lo_ref[...] = two.astype(BF16)
        distance = two - teacher_ref[...].astype(F32)
        valid = valid_ref[...].astype(F32)
        weighed = valid * distance
        square = jnp.sum(weighed * distance)
        first_row = lax.broadcasted_iota(jnp.int32, (8, 128), 0) == 0
        sq_ref[...] = jnp.where(first_row, square, count)
        g2 = (2.0 * LOSS_SCALE / (count * width)) * weighed
        gb = g2.astype(BF16)
        gb_ref[...] = gb
        for q in range(nq):
            gpre = (mm(gb, w_down(q), NT) * slope_ref[q]).astype(BF16)
            gpre_ref[q] = gpre
            if q == 0:
                acc_ref[...] = mm(gpre, w_up(q), NT)
            else:
                acc_ref[...] += mm(gpre, w_up(q), NT)
        gn2 = acc_ref[...]
        g1 = g2 + norm_back(gn2, unit, inverse, gain)
        g1_ref[...] = g1
        gv_ref[...] = jnp.concatenate(
            [
                jnp.sum(gn2 * unit, axis=0, keepdims=True),
                jnp.sum(gn2, axis=0, keepdims=True),
                jnp.zeros((6, width), F32),
            ],
            axis=0,
        )
        ga = g1.astype(BF16)
        ga_ref[...] = ga
        for j in range(nj):
            gatt_refs[j][...] = mm(ga, w_out(rows[j]), NT).astype(BF16)

    return body


def mlp_grads_body(plan, width, ff, blk, packed):
    nj, nw, nc = len(plan.peers), plan.n_wt, plan.n_ctx
    nq = ff // CHUNK

    def body(info, act_ref, gpre_ref, n2_ref, gb_ref, ga_ref, gv_ref, sq_ref, *refs):
        att, outs = refs[:nj], refs[nj:]
        if packed:
            outs, (ups, downs, attn, metas, sem) = outs[:2], outs[2:]
        n2, gb, ga = n2_ref[...], gb_ref[...], ga_ref[...]
        ctx, wt = info[0], info[1]
        rows_up = width // (nw * nc)

        def put(c, w, tile, value):
            plane = (c ^ ctx) // 2
            middle = (plane == 1) | (plane == 2)
            place = jnp.where(middle, 3 - plane, plane) if c % 2 else plane
            zed = w ^ wt
            zed = jnp.where((zed == 1) | (zed == 2), 3 - zed, zed)
            for k in (0, 1):

                @pl.when(ctx % 2 == k)
                def _():
                    target = outs[(c % 2) ^ k].at[place, zed, pl.ds(tile, value.shape[0])]
                    pltpu.make_async_copy(value, target, sem.at[0]).start()

        for q in range(nq):
            up = mm(n2, gpre_ref[q], TN).astype(BF16)
            down = mm(act_ref[q], gb, TN).astype(BF16)
            if packed:
                ups[q] = up.reshape(nw * nc, rows_up, CHUNK)
                downs[q] = down.reshape(nc * 4, TILE, width)
                for w in range(nw):
                    for c in range(nc):
                        put(c, w, q, ups.at[q, pl.ds(w * nc + c, 1)])
                for c in range(nc):
                    put(c, q, nq, downs.at[q, pl.ds(4 * c, 4)])
            else:
                outs[0][q] = up
                outs[1][q] = down
        for j, (mc, mw) in enumerate(plan.peers):
            head = plan.head(ctx ^ mc, wt ^ mw)
            part = mm(att[j][...], ga, TN).astype(BF16)
            if packed:
                attn[j] = part.reshape(2 * HEAD // TILE, TILE, width)
                for t in range(2 * HEAD // TILE):
                    put(t, head // 2, nq + 4, attn.at[j, pl.ds(t, 1)])
            else:
                row = pl.multiple_of((head // 2) * (2 * HEAD), 2 * HEAD)
                outs[2][pl.ds(row, 2 * HEAD), :] = part
        if packed:
            dev = ctx * nw + wt
            square = sq_ref[0:1, 0:1]
            high = square.astype(BF16).astype(F32)
            lane = lane_iota((1, CHUNK))
            n_dev = nw * nc
            line = jnp.where(lane == dev, high, 0.0) + jnp.where(
                lane == dev + n_dev, square - high, 0.0
            )
            for w in range(nw):
                per = width // nw
                vec = gv_ref[0:2, per * w : per * (w + 1)]
                vec = jnp.concatenate([vec, jnp.zeros((2, CHUNK - per), F32)], axis=1)
                tile = jnp.concatenate([line, vec, jnp.zeros((TILE - 3, CHUNK), F32)], axis=0)
                metas[w, 0] = tile.astype(BF16)
                for c in range(nc):
                    put(c, w, nq + 5, metas.at[w])
            for ref in outs:
                pltpu.make_async_copy(ref, ref, sem.at[0]).wait()

    return body


def head_grads_body(plan, blk, width, shard, nb):
    ns, nw, nj = len(plan.slots), plan.n_wt, len(plan.peers)

    def body(info, dq_ref, wh_ref, normed_ref, *refs):
        xs = refs[:ns]
        parts = refs[ns : ns + nb]
        outs = refs[ns + nb :]
        own_ref, sib_ref, dw_ref, acc = outs
        half = shard // 2
        weight = wh_ref[...]
        gsum = jnp.zeros((1, width), F32)
        ssum = jnp.zeros((1, width), F32)
        for s in range(ns):
            dkv = parts[0][s].astype(F32)
            for b in range(1, nb):
                dkv = dkv + parts[b][s].astype(F32)
            zero = jnp.zeros((blk, 2 * HEAD), F32)
            wide = pltpu.roll(jnp.concatenate([dkv, zero], axis=1), HEAD, 1)
            wide = wide + jnp.concatenate([dq_ref[s].astype(F32), zero], axis=1)
            gh = wide.astype(BF16)
            back = mm(gh, weight, NT)
            if s < nj:
                own_ref[s] = back.astype(BF16)
            else:
                sib_ref[s - nj] = back.astype(BF16)
            unit, _ = norm_stats(xs[s][:blk, :].astype(F32))
            gsum = gsum + jnp.sum(back * unit, axis=0, keepdims=True)
            ssum = ssum + jnp.sum(back, axis=0, keepdims=True)
            dw = mm(normed_ref[s], gh, TN)
            if s == 0:
                acc[...] = dw
            else:
                acc[...] += dw
        vecs = jnp.concatenate([gsum, ssum, jnp.zeros((6, width), F32)], axis=0).astype(BF16)
        rows = lax.broadcasted_iota(jnp.int32, (8, 4 * HEAD), 0)
        pick = jnp.where(lane_iota((8, 4 * HEAD)) == rows + 3 * HEAD, 1.0, 0.0).astype(BF16)
        acc[...] += mm(vecs, pick, TN)
        for m in range(nw):
            row = pl.multiple_of((info[1] ^ m) * shard, shard)
            block = acc[pl.ds(row, shard), :].astype(BF16)
            dw_ref[m, :, : 4 * HEAD] = block[:half]
            dw_ref[m, :, 4 * HEAD :] = block[half:]

    return body


def merge_body(nj, nw, blk):
    def body(own_ref, sib_ref, dw_ref, more_ref, *outs):
        for m in range(nw):
            dw = (dw_ref[m].astype(F32) + more_ref[m].astype(F32)).astype(BF16)
            if m < nj:
                rows = own_ref[m].astype(F32) + sib_ref[m].astype(F32)
                outs[m][:blk, :] = rows.astype(BF16)
                outs[m][blk:, :] = dw
            else:
                outs[m][...] = dw

    return body


def words_body(nj):
    def body(x_ref, vec_ref, g1_ref, *refs):
        parts, sibs, out_ref = refs[:nj], refs[nj : 2 * nj], refs[-1]
        up = parts[0][: x_ref.shape[0], :].astype(F32)
        for p in parts[1:]:
            up = up + p[: up.shape[0], :].astype(F32)
        unit, inverse = norm_stats(x_ref[...].astype(F32))
        out_ref[...] = g1_ref[...] + norm_back(up, unit, inverse, vec_ref[0:1, :])

    return body


def unpack_body(plan, width, ff):
    nq, nw, nc = ff // CHUNK, plan.n_wt, plan.n_ctx

    def body(info, sq_ref, own, sib, *outs):
        srcs = [r.at[n] for r in (own, sib) for n in range(nc // 2)]
        up_ref, down_ref, out_ref, loss_ref, gain_ref, shift_ref = outs
        here = info[0] % 2
        owners = [info[0] ^ m for m in plan.near(here)]
        owners += [info[0] ^ 1 ^ m for m in plan.near(1 - here)]
        for c, src in zip(owners, srcs):
            row = pl.multiple_of(c * TILE, TILE)
            for q in range(nq):
                up_ref[pl.ds(row, TILE), q * CHUNK : (q + 1) * CHUNK] = src[q].astype(F32)
            for t in range(4):
                down_ref[pl.ds(pl.multiple_of(c * 4 * TILE + t * TILE, TILE), TILE), :] = src[
                    nq + t
                ].astype(F32)
            out_ref[pl.ds(row, TILE), :] = src[nq + 4].astype(F32)
        meta = srcs[0][nq + 5].astype(F32)
        count = jnp.max(sq_ref[1:2, :], axis=1, keepdims=True)
        loss_ref[...] = jnp.sum(meta[0:1], axis=1, keepdims=True) / (count * width)
        gain_ref[...] = meta[1:2, : width // nw]
        shift_ref[...] = meta[2:3, : width // nw]

    return body


def head_out_body(plan, shard):
    nj, half = len(plan.peers), shard // 2

    def body(info, own_ref, sib_ref, out_ref, gain_ref, shift_ref):
        core = info[0] % 2
        rows = lax.broadcasted_iota(jnp.int32, (8, 4 * HEAD), 0)
        pick = jnp.where(lane_iota((8, 4 * HEAD)) == rows + 3 * HEAD, 1.0, 0.0)
        lane = lane_iota((half, 2 * HEAD))
        for side in (0, 1):
            at = slice(side * 4 * HEAD, (side + 1) * 4 * HEAD)
            here = slice(side * half, (side + 1) * half)
            total = jnp.zeros((half, 4 * HEAD), F32)
            for j, (mc, mw) in enumerate(plan.peers):
                head = plan.head(info[0] ^ mc, info[1] ^ mw)
                own = own_ref[j, :, at].astype(F32)
                sib = sib_ref[j, :, at].astype(F32)
                total = total + own + sib
                even = jnp.where(core == 0, own, sib)
                odd = jnp.where(core == 0, sib, own)
                turned = pltpu.roll(odd, 3 * HEAD, 1)
                mid = jnp.where(lane < HEAD, even[:, 2 * HEAD :], turned[:, 2 * HEAD :])
                col = pl.multiple_of((head // 2) * (6 * HEAD), 2 * HEAD)
                out_ref[here, pl.ds(col, 2 * HEAD)] = even[:, : 2 * HEAD]
                out_ref[here, pl.ds(col + 2 * HEAD, 2 * HEAD)] = mid
                out_ref[here, pl.ds(col + 4 * HEAD, 2 * HEAD)] = turned[:, : 2 * HEAD]
            both = lax.dot_general(
                pick, total, NT, precision=lax.Precision.HIGHEST, preferred_element_type=F32
            )
            gain_ref[:, here] = both[0:1]
            shift_ref[:, here] = both[1:2]

    return body


def per_device(
    words,
    teacher,
    valid,
    lengths,
    deal,
    gain_attn,
    shift_attn,
    w_qkv,
    w_out,
    gain_mlp,
    shift_mlp,
    w_up,
    w_down,
):
    n_ctx, n_wt = lax.axis_size("ctx"), lax.axis_size("wt")
    plan = Plan(n_ctx, n_wt)
    ctx, wt = lax.axis_index("ctx"), lax.axis_index("wt")
    blk, width = words.shape
    shard = width // n_wt
    ff = w_up.shape[1]
    nq = ff // CHUNK
    nseq = lengths.shape[0]
    ns, nb, nj = len(plan.slots), len(plan.groups), len(plan.peers)
    packed = plan.square and width == CHUNK and width % (n_wt * n_ctx * TILE) == 0
    packed = packed and n_wt * CHUNK == ff and 2 * HEAD // TILE == n_ctx
    info = jnp.stack([ctx, wt]).astype(jnp.int32)
    codes = jnp.array([mc * n_wt + mw for mc, mw in plan.slots], jnp.int32)
    core = (1, 0)

    vecs_here = jnp.stack([gain_attn, shift_attn, gain_mlp, shift_mlp])
    load = call(
        pack_body(plan, shard, blk),
        "pack",
        [info, words, w_qkv, vecs_here],
        [SMEM] + [VMEM] * 3,
        [sds((blk + shard // 2, width), BF16)] * n_wt,
    )
    loads = [load[0]] + [plan.swap(load[m], (0, m)) for m in range(1, n_wt)]
    sets = [(0, 1), (1, 3), (3, 4), (2, 4), (1, 2)] if plan.square else [(0, nb)]
    lists = call(
        lists_body(plan, blk, nseq, sets),
        "lists",
        [after(info, load[1]), deal, lengths, codes],
        [SMEM] * 4,
        [sds((ns * n_ctx * n_wt + WIDE + WIDE_BACK,), jnp.int32)] * len(sets),
        scratch=[pltpu.SMEM((n_ctx * n_wt,), jnp.int32)],
        out_specs=[SMEM] * len(sets),
    )
    lists = dict(zip(sets, lists))
    late = [loads[0], after(loads[1], lists[sets[0]])] + loads[2:]
    xs = loads[:nj] + [plan.swap(x, core) for x in late[:nj]]

    q, kv, normed, w_head, vecs = call(
        project_body(plan, shard, blk),
        "project",
        [info] + xs + loads,
        [SMEM] + [VMEM] * (ns + n_wt),
        [
            sds((ns, blk, 2 * HEAD), BF16),
            sds((ns, blk, 2 * HEAD), BF16),
            sds((ns, blk, width), BF16),
            sds((width, 4 * HEAD), BF16),
            sds((8, width), F32),
        ],
        flops=2 * ns * blk * width * 4 * HEAD,
    )
    kvs = plan.gather_groups(kv)

    if packed:
        rows_up = width // (n_wt * n_ctx)
        up_piece = lax.dynamic_slice_in_dim(w_up, ctx * rows_up, rows_up, 0)
        up_piece = up_piece.reshape(rows_up, nq, CHUNK).transpose(1, 0, 2)
        down_piece = lax.dynamic_slice_in_dim(w_down, ctx * 4 * TILE, 4 * TILE, 0)
        out_piece = lax.dynamic_slice_in_dim(w_out, ctx * TILE, TILE, 0)
        count_here = jnp.sum(valid).astype(BF16)
        piece = jnp.concatenate(
            [
                up_piece,
                down_piece.reshape(4, TILE, CHUNK),
                out_piece[None],
                jnp.full((1, TILE, CHUNK), count_here, BF16),
            ],
            axis=0,
        )
        piece = after(piece, loads[2])
        two = jnp.stack([piece, plan.swap(piece, (0, 2))])
        two = after(two, kvs[1])
        near = plan.swap(two, (0, 1))
        count = jnp.zeros((1,), F32)
    else:
        up_full = lax.all_gather(w_up, "wt", axis=0, tiled=True)
        down_full = lax.all_gather(w_down, "wt", axis=0, tiled=True)
        out_full = lax.all_gather(w_out, "wt", axis=0, tiled=True)
        weights = [
            up_full.reshape(width, nq, CHUNK).transpose(1, 0, 2),
            down_full.reshape(nq, CHUNK, width),
            out_full,
        ]
        count = lax.psum(jnp.sum(valid).astype(F32), ("ctx", "wt")).reshape(1)

    state = []
    if not plan.square:
        state = attend_part(plan, blk, 0, nb, True, info, lists, q, kvs, state)
    else:
        state = attend_part(plan, blk, 0, 1, False, info, lists, q, kvs, state)
        if packed:
            stack = jnp.concatenate([two, near])
            stack = after(stack, kvs[3])
            kvs = kvs[:3] + [after(kvs[3], stack)]
        state = [after(state[0], kvs[3]), *state[1:]]
        state = attend_part(plan, blk, 1, 3, False, info, lists, q, kvs, state)
        if packed:
            one, side = plan.turn(stack, True), plan.turn(stack, False)
            stack_sib = plan.swap(stack, core)
        state = attend_part(plan, blk, 3, 4, True, info, lists, q, kvs, state)
    o, o_sib, of32, lse = state[3:]
    o_sib = plan.swap(o_sib, core)
    if packed:
        one = after(one, o_sib)
        last = plan.turn(one, False)
        pair = jnp.stack([one, side])
        weights = [stack, pair, last, stack_sib, plan.swap(pair, core)]
    mixed = o + o_sib
    att = [mixed[0]] + [plan.swap(mixed[j], plan.peers[j]) for j in range(1, nj)]
    if packed:
        weights += [plan.swap(after(last, *att[1:]), core)]

    mlp_in = [info, words, teacher, valid[:, None], vecs, count] + att + weights
    specs = [SMEM] + [VMEM] * 4 + [SMEM] + [VMEM] * nj
    specs += [ANY] * len(weights) if packed else [VMEM] * len(weights)
    scratch = [pltpu.VMEM((nq, blk, CHUNK), F32), pltpu.VMEM((blk, width), F32)]
    if packed:
        scratch = [
            pltpu.VMEM((nq, n_wt, n_ctx, TILE, CHUNK), BF16),
            pltpu.VMEM((n_wt, n_ctx * 4, TILE, CHUNK), BF16),
            pltpu.VMEM((n_wt, n_ctx, TILE, CHUNK), BF16),
            pltpu.VMEM((n_wt, n_ctx, TILE, CHUNK), BF16),
            *scratch,
            pltpu.SemaphoreType.DMA((4,)),
        ]
    layer_out, square, grad_one, *rest = call(
        mlp_body(plan, width, ff, blk, packed),
        "mlp",
        mlp_in,
        specs,
        [
            sds((blk, width), BF16),
            sds((8, 128), F32),
            sds((blk, width), F32),
            *[sds((blk, 2 * HEAD), BF16)] * nj,
            sds((nq, blk, CHUNK), BF16),
            sds((nq, blk, CHUNK), BF16),
            sds((blk, width), BF16),
            sds((blk, width), BF16),
            sds((blk, width), BF16),
            sds((8, width), F32),
        ],
        scratch=scratch,
        flops=8 * blk * width * ff,
        trans=2 * blk * ff,
    )
    gatt, (act, gpre, n2, gb, ga, gvec) = rest[:nj], rest[nj:]
    g_own = [gatt[0]] + [plan.swap(gatt[j], plan.peers[j]) for j in range(1, nj)]
    g_sib = plan.swap(jnp.stack(g_own), core)

    grads_in = [info, act, gpre, n2, gb, ga, gvec, square] + att
    if packed:
        grads_out = [sds((n_ctx // 2, n_wt, nq + 6, TILE, CHUNK), BF16)] * 2
        grads_scratch = [
            pltpu.VMEM((nq, n_wt * n_ctx, TILE, CHUNK), BF16),
            pltpu.VMEM((nq, n_ctx * 4, TILE, CHUNK), BF16),
            pltpu.VMEM((nj, n_ctx, TILE, CHUNK), BF16),
            pltpu.VMEM((n_wt, 1, TILE, CHUNK), BF16),
            pltpu.SemaphoreType.DMA((1,)),
        ]
    else:
        grads_out = [
            sds((nq, width, CHUNK), BF16),
            sds((nq, CHUNK, width), BF16),
            sds((width, width), BF16),
        ]
        grads_scratch = []
    weight_grads = call(
        mlp_grads_body(plan, width, ff, blk, packed),
        "mlp_grads",
        grads_in,
        [SMEM] + [VMEM] * (7 + nj),
        grads_out,
        scratch=grads_scratch,
        out_specs=[ANY if packed else VMEM] * len(grads_out),
        flops=4 * blk * width * ff,
    )

    extra = [of32] + g_own + [g_sib]
    if plan.square:
        if packed:
            g_all, g_core = weight_grads[0], plan.swap(weight_grads[1], core)
            g_far = (g_all[2:].astype(F32) + g_core[2:].astype(F32)).astype(BF16)
            extra = [after(of32, g_far)] + extra[1:]
            g_far = plan.turn(g_far, False)
        part = attend_back_part(plan, blk, 2, 4, True, False, info, lists, q, lse, kvs, extra)
        dkv2, dkv3, dq_part, g_ext, delta = part
        far = [plan.turn(d, False) for d in (dkv3, dkv2)]
        dkv1, dq_part = attend_back_part(
            plan, blk, 1, 2, False, False, info, lists, q, lse, kvs, [g_ext, delta, dq_part]
        )
        mid = plan.turn((dkv1.astype(F32) + far[0].astype(F32)).astype(BF16), True)
        if packed:
            g_far = after(g_far, dkv1)
            g_mid = g_all[1].astype(F32) + g_core[1].astype(F32) + g_far[1].astype(F32)
            g_mid = g_mid.astype(BF16)
            dq_part = after(dq_part, g_mid)
            g_mid = plan.turn(g_mid, True)
        dkv0, _, dq = attend_back_part(
            plan, blk, 0, 1, False, True, info, lists, q, lse, kvs, [g_ext, delta, dq_part]
        )
        if packed:
            g_mid = after(g_mid, dkv0)
            g_near = g_all[0].astype(F32) + g_core[0].astype(F32) + g_far[0].astype(F32)
            g_near = (g_near + g_mid.astype(F32)).astype(BF16)
            dq = after(dq, g_near)
            g_other = plan.swap(g_near[2:], (0, 1))
        parts = [dkv0, far[1], mid]
    else:
        part = attend_back_part(plan, blk, 0, nb, True, True, info, lists, q, lse, kvs, extra)
        dq = part[-1]
        parts = [part[0]] + [plan.swap(part[b], plan.groups[b]) for b in range(1, nb)]

    head_outs = call(
        head_grads_body(plan, blk, width, shard, len(parts)),
        "head_grads",
        [info, dq, w_head, normed] + xs + parts,
        [SMEM] + [VMEM] * (3 + ns + len(parts)),
        [sds((nj, blk, width), BF16)] * 2 + [sds((n_wt, shard // 2, width), BF16)],
        scratch=[pltpu.VMEM((width, 4 * HEAD), F32)],
        flops=4 * ns * blk * width * 4 * HEAD,
    )
    own_rows, sib_rows, dw = head_outs
    if packed:
        g_two = (g_near[:2].astype(F32) + g_other.astype(F32)).astype(BF16)
        g_last = plan.swap(g_two[1], (0, 2))
    sib_rows = plan.swap(sib_rows, core)

    if plan.square:
        dw = (dw.astype(F32) + plan.turn(dw, True).astype(F32)).astype(BF16)
        dw_more = plan.turn(dw, False)
    else:
        step = CTX_HEADS
        while step < n_ctx:
            dw_more = plan.swap(dw, (step, 0))
            step *= 2
            if step < n_ctx:
                dw = (dw.astype(F32) + dw_more.astype(F32)).astype(BF16)
    load = call(
        merge_body(nj, n_wt, blk),
        "merge",
        [own_rows, sib_rows, dw, dw_more],
        [VMEM] * 4,
        [sds((blk + shard // 2, width), BF16)] * nj
        + [sds((shard // 2, width), BF16)] * (n_wt - nj),
    )
    loads = [load[0]] + [plan.swap(load[m], (0, m)) for m in range(1, n_wt)]
    if packed:
        g_last = after(g_last, load[0])
        final = (g_two[0].astype(F32) + g_last.astype(F32)).astype(BF16)
        finals = plan.gather_square(final)
        finals = jnp.stack(finals)
        finals = [finals, plan.swap(finals, core)]
        g_up, g_down, g_out, loss, g_gain, g_shift = call(
            unpack_body(plan, width, ff),
            "unpack",
            [info, square] + finals,
            [SMEM] + [VMEM] * 3,
            [
                sds((shard, ff), F32),
                sds((ff // n_wt, width), F32),
                sds((shard, width), F32),
                sds((1, 1), F32),
                sds((1, shard), F32),
                sds((1, shard), F32),
            ],
        )
        loss, g_gain, g_shift = loss[0, 0], g_gain.reshape(shard), g_shift.reshape(shard)
    else:
        g_up, g_down, g_out = weight_grads
        g_up = g_up.transpose(1, 0, 2).reshape(width, ff)
        g_down = g_down.reshape(ff, width)

        def reduce_rows(g):
            part = lax.psum_scatter(g.astype(BF16), "wt", scatter_dimension=0, tiled=True)
            return lax.psum(part, "ctx").astype(F32)

        g_up, g_down, g_out = reduce_rows(g_up), reduce_rows(g_down), reduce_rows(g_out)
        both = lax.psum(gvec[:2], ("ctx", "wt"))
        both = lax.dynamic_slice_in_dim(both, wt * shard, shard, 1)
        g_gain, g_shift = both[0], both[1]
        loss = lax.psum(square[0, 0], ("ctx", "wt")) / (count[0] * width)
    own_heads = jnp.stack([x[blk:] for x in loads[:nj]])
    if n_wt > nj:
        own_heads = (own_heads.astype(F32) + jnp.stack(loads[nj:]).astype(F32)).astype(BF16)
    sib_heads = plan.swap(own_heads, core)
    grad_words = call(
        words_body(nj),
        "words_grad",
        [words, vecs, grad_one] + loads[:nj],
        [VMEM] * (3 + nj),
        [sds((blk, width), F32)],
    )[0]
    g_qkv, gain_one, shift_one = call(
        head_out_body(plan, shard),
        "head_out",
        [info, own_heads, sib_heads],
        [SMEM] + [VMEM] * 2,
        [sds((shard, 3 * width), F32), sds((1, shard), F32), sds((1, shard), F32)],
    )

    return (
        layer_out,
        loss,
        grad_words,
        gain_one.reshape(shard),
        shift_one.reshape(shard),
        g_qkv,
        g_out,
        g_gain,
        g_shift,
        g_up,
        g_down,
    )


def solution(mesh):
    placed = (
        P(("ctx", "wt"), None),
        P(("ctx", "wt"), None),
        P(("ctx", "wt")),
        P(),
        P(),
        P("wt"),
        P("wt"),
        P("wt", None),
        P("wt", None),
        P("wt"),
        P("wt"),
        P("wt", None),
        P("wt", None),
    )
    return jax.shard_map(
        per_device,
        mesh=mesh,
        in_specs=placed,
        out_specs=(
            P(("ctx", "wt"), None),
            P(),
            P(("ctx", "wt"), None),
            P("wt"),
            P("wt"),
            P("wt", None),
            P("wt", None),
            P("wt"),
            P("wt"),
            P("wt", None),
            P("wt", None),
        ),
        check_vma=False,
    )
```

```python
import jax
import jax.numpy as jnp
from jax import lax
from jax.experimental import pallas as pl
from jax.experimental.pallas import tpu as pltpu
from jax.sharding import PartitionSpec as P

H = 8
HEAD = 64
EPS = 1e-05
LOSS_SCALE = 262144.0
CTX_HEADS = 2
WT_HEADS = 4
CHUNK = 512
TILE = 16
WIDE = 4
WIDE_BACK = 4
F32 = jnp.float32
BF16 = jnp.bfloat16
NEG = -1e30
NT = (((1,), (1,)), ((), ()))
TN = (((0,), (0,)), ((), ()))
NN = (((1,), (0,)), ((), ()))


def mm(a, b, dims=NN):
    return lax.dot_general(a, b, dims, preferred_element_type=F32)


def lane_iota(shape):
    return lax.broadcasted_iota(jnp.int32, shape, len(shape) - 1)


def norm_stats(values):
    center = values - jnp.mean(values, axis=-1, keepdims=True)
    inverse = lax.rsqrt(jnp.mean(center * center, axis=-1, keepdims=True) + EPS)
    return center * inverse, inverse


def norm_back(upstream, unit, inverse, gain):
    scaled = upstream * gain
    inner = jnp.mean(scaled * unit, axis=-1, keepdims=True)
    return inverse * (scaled - jnp.mean(scaled, axis=-1, keepdims=True) - unit * inner)


SMEM = pl.BlockSpec(memory_space=pltpu.SMEM)
VMEM = pl.BlockSpec(memory_space=pltpu.VMEM)
ANY = pl.BlockSpec(memory_space=pl.ANY)


def call(body, name, ins, in_specs, outs, scratch=(), flops=0, trans=0, out_specs=None):
    nbytes = sum(x.size * x.dtype.itemsize for x in list(ins) + list(outs))
    return pl.pallas_call(
        body,
        name=name,
        out_shape=list(outs),
        in_specs=in_specs,
        out_specs=out_specs or [VMEM] * len(outs),
        scratch_shapes=list(scratch),
        compiler_params=pltpu.CompilerParams(vmem_limit_bytes=58 * 1024 * 1024),
        cost_estimate=pl.CostEstimate(flops=flops, bytes_accessed=nbytes, transcendentals=trans),
    )(*ins)


def after(value, *earlier):
    return lax.optimization_barrier((value, *earlier))[0]


def sds(shape, dtype):
    return jax.ShapeDtypeStruct(shape, dtype)


class Plan:
    def __init__(self, n_ctx, n_wt):
        self.n_ctx, self.n_wt = n_ctx, n_wt
        ac, aw = CTX_HEADS, WT_HEADS
        assert ac * aw == H and n_ctx % ac == 0 and n_wt % aw == 0
        self.peers = [(mc, mw) for mw in range(aw) for mc in range(0, ac, 2)]
        self.slots = [(mc | k, mw) for k in (0, 1) for mc, mw in self.peers]
        self.groups = [(mc, mw) for mc in range(0, n_ctx, ac) for mw in range(0, n_wt, aw)]
        self.square = n_ctx == 8 and n_wt == aw

    def near(self, core):
        return [0, 2 + 2 * core, 4 - 2 * core, 6]

    def group_masks(self, core):
        return [(m, 0) for m in self.near(core)] if self.square else self.groups

    def head(self, ctx, wt):
        return (wt % WT_HEADS) * CTX_HEADS + ctx % CTX_HEADS

    def swap(self, x, mask):
        mc, mw = mask
        n = self.n_wt
        perm = [
            (c * n + w, (c ^ mc) * n + (w ^ mw)) for c in range(self.n_ctx) for w in range(n)
        ]
        return lax.ppermute(x, ("ctx", "wt"), perm)

    def turn(self, x, first):
        n = self.n_wt
        masks = (2, 4) if first else (4, 2)
        perm = [
            (c * n + w, (c ^ masks[c % 2]) * n + w) for c in range(self.n_ctx) for w in range(n)
        ]
        return lax.ppermute(x, ("ctx", "wt"), perm)

    def gather_square(self, x):
        one = self.turn(x, True)
        return [x, one, self.turn(x, False), self.turn(one, False)]

    def gather_groups(self, x):
        if self.square:
            return self.gather_square(x)
        return [x] + [self.swap(x, m) for m in self.groups[1:]]


def pack_body(plan, shard, blk):
    nw, half = plan.n_wt, shard // 2

    def body(info, words_ref, w_ref, vec_ref, *outs):
        odd = (info[0] % 2) == 1
        rows = lax.broadcasted_iota(jnp.int32, (4, 4 * HEAD), 0)
        pick = jnp.where(lane_iota((4, 4 * HEAD)) == rows + 3 * HEAD, 1.0, 0.0).astype(BF16)
        vec = mm(vec_ref[...], pick, TN)
        lane = lane_iota((shard, 4 * HEAD))
        for m in range(nw):
            pair = plan.head(info[0], info[1] ^ m) // 2
            col = pl.multiple_of(pair * (6 * HEAD), 2 * HEAD)
            both = w_ref[:, pl.ds(col, 6 * HEAD)].astype(F32)
            turned = pltpu.roll(both, 3 * HEAD, 1)
            cols = jnp.where(odd, turned[:, : 4 * HEAD], both[:, : 4 * HEAD])
            cols = jnp.where(lane < 3 * HEAD, cols, vec).astype(BF16)
            outs[m][:blk, :] = words_ref[...]
            outs[m][blk:, : 4 * HEAD] = cols[:half]
            outs[m][blk:, 4 * HEAD :] = cols[half:]

    return body


def project_body(plan, shard, blk):
    ns, nw, half = len(plan.slots), plan.n_wt, shard // 2

    def body(info, *refs):
        xs, wps = refs[:ns], refs[ns : ns + nw]
        q_ref, kv_ref, normed_ref, wh_ref, vec_ref = refs[ns + nw :]
        wt = info[1]
        for m in range(nw):
            row = pl.multiple_of((wt ^ m) * shard, shard)
            wh_ref[pl.ds(row, half), :] = wps[m][blk:, : 4 * HEAD]
            wh_ref[pl.ds(row + half, half), :] = wps[m][blk:, 4 * HEAD :]
        weight = wh_ref[...]
        rows = lax.broadcasted_iota(jnp.int32, (8, 4 * HEAD), 0)
        pick = jnp.where(lane_iota((8, 4 * HEAD)) == rows + 3 * HEAD, 1.0, 0.0).astype(BF16)
        vecs = mm(pick, weight, NT)
        vec_ref[...] = vecs
        gain, shift = vecs[0:1], vecs[1:2]
        low = lane_iota((blk, 2 * HEAD)) < HEAD
        for s in range(ns):
            unit, _ = norm_stats(xs[s][:blk, :].astype(F32))
            normed = (unit * gain + shift).astype(BF16)
            normed_ref[s] = normed
            y = mm(normed, weight)
            q_ref[s] = (
                jnp.where(low, y[:, : 2 * HEAD], 0.0).astype(BF16).astype(F32) * HEAD**-0.5
            ).astype(BF16)
            kv_ref[s] = pltpu.roll(y, 3 * HEAD, 1)[:, : 2 * HEAD].astype(BF16)

    return body


def fill_slots(plan, info, deal, slot_of):
    for g, (gc, gw) in enumerate(plan.group_masks(info[0] % 2)):
        for s, (mc, mw) in enumerate(plan.slots):
            at = (info[0] ^ gc ^ mc) * plan.n_wt + (info[1] ^ gw ^ mw)
            slot_of[deal[at]] = g * len(plan.slots) + s


def slot_range(plan, info, deal, lengths, codes, i, blk, nseq):
    code = codes[i]
    here = deal[(info[0] ^ (code // plan.n_wt)) * plan.n_wt + (info[1] ^ (code % plan.n_wt))]
    first = jnp.int32(0)
    total = jnp.int32(0)
    for n in range(nseq):
        total = total + lengths[n]
        bound = total // blk
        first = jnp.where(bound <= here, bound, first)
    return first, here


def lists_body(plan, blk, nseq, sets):
    ns = len(plan.slots)

    def body(info, deal, lengths, codes, *refs):
        outs, slot_of = refs[:-1], refs[-1]
        fill_slots(plan, info, deal, slot_of)

        def one_block(i, counts):
            first, here = slot_range(plan, info, deal, lengths, codes, i, blk, nseq)

            def one_key(b, counts):
                slot = slot_of[b]
                more = []
                for out, n, (lo, hi) in zip(outs, counts, sets):
                    inside = (slot >= lo * ns) & (slot < hi * ns)
                    out[n] = i * 1024 + slot - lo * ns
                    more.append(n + inside.astype(jnp.int32))
                return tuple(more)

            return lax.fori_loop(first, here, one_key, counts)

        start = tuple(jnp.int32(1) for _ in sets)
        counts = lax.fori_loop(0, ns, one_block, start)
        for out, n in zip(outs, counts):
            spare = jnp.where(n > 1, out[jnp.maximum(n - 1, 1)], 0)
            for t in range(max(WIDE, WIDE_BACK) - 1):
                out[n + t] = spare
            out[0] = n - 1

    return body


def attend_body(plan, blk, lo, hi, last):
    ns, nb = len(plan.slots), hi - lo

    def body(info, pairs, q_ref, *refs):
        kv_refs, refs = refs[:nb], refs[nb:]
        if lo:
            olds, refs = refs[:3], refs[3:]
        (m_ref, l_ref, acc_ref), refs = refs[:3], refs[3:]
        if last:
            (o_ref, o_sib_ref, of_ref, lse_ref), refs = refs[:4], refs[4:]
        kvs, sem = refs
        copies = [
            pltpu.make_async_copy(ref, kvs.at[pl.ds(b * ns, ns)], sem.at[b])
            for b, ref in enumerate(kv_refs)
        ]
        for c in copies:
            c.start()
        n = pairs[0]
        if lo:
            for new, old in zip((m_ref, l_ref, acc_ref), olds):
                new[...] = old[...]
        for c in copies:
            c.wait()
        if not lo:
            tri = lax.broadcasted_iota(jnp.int32, (blk, blk), 0) <= lane_iota((blk, blk))

            def diagonal(h, _):
                scores = [mm(kvs[h * WIDE + k], q_ref[h * WIDE + k], NT) for k in range(WIDE)]
                for k in range(WIDE):
                    i = h * WIDE + k
                    s = jnp.where(tri, scores[k], NEG)
                    m = jnp.max(s, axis=0, keepdims=True)
                    p = jnp.exp(s - m)
                    m_ref[i] = m
                    l_ref[i] = jnp.sum(p, axis=0, keepdims=True)
                    acc_ref[i] = mm(kvs[i], p.astype(BF16), TN)
                return 0

            lax.fori_loop(0, ns // WIDE, diagonal, 0)

        def step(h, _):
            codes2 = [pairs[h * WIDE + 1 + k] for k in range(WIDE)]
            rows = [c // 1024 for c in codes2]
            cols = [c % 1024 for c in codes2]
            scores = [mm(kvs[cols[k]], q_ref[rows[k]], NT) for k in range(WIDE)]
            for k in range(1, WIDE):
                scores[k] = jnp.where(h * WIDE + k < n, scores[k], NEG)
            for k in range(WIDE):
                i, s = rows[k], scores[k]
                m_old = m_ref[i]
                m = jnp.maximum(m_old, jnp.max(s, axis=0, keepdims=True))
                p = jnp.exp(s - m)
                factor = jnp.exp(m_old - m)
                m_ref[i] = m
                l_ref[i] = l_ref[i] * factor + jnp.sum(p, axis=0, keepdims=True)
                acc_ref[i] = acc_ref[i] * factor + mm(kvs[cols[k]], p.astype(BF16), TN)
            return 0

        lax.fori_loop(0, (n + WIDE - 1) // WIDE, step, 0)
        if last:
            core = info[0] % 2

            def finish(i, _):
                total = l_ref[i]
                lse_ref[i] = m_ref[i] + jnp.log(total)
                out = acc_ref[i, HEAD:, :] / total
                zero = jnp.zeros_like(out)
                placed = jnp.concatenate(
                    [jnp.where(core == 0, out, zero), jnp.where(core == 1, out, zero)], axis=0
                )
                wide = placed.T
                of_ref[i] = wide

                @pl.when(i < ns // 2)
                def _():
                    o_ref[i] = wide.astype(BF16)

                @pl.when(i >= ns // 2)
                def _():
                    o_sib_ref[i - ns // 2] = wide.astype(BF16)

                return 0

            lax.fori_loop(0, ns, finish, 0)

    return body


def attend_part(plan, blk, lo, hi, last, info, lists, q, kvs, olds):
    ns, nb = len(plan.slots), hi - lo
    outs = [sds((ns, 1, blk), F32), sds((ns, 1, blk), F32), sds((ns, 2 * HEAD, blk), F32)]
    if last:
        outs += [
            sds((ns // 2, blk, 2 * HEAD), BF16),
            sds((ns // 2, blk, 2 * HEAD), BF16),
            sds((ns, blk, 2 * HEAD), F32),
            sds((ns, 1, blk), F32),
        ]
    pairs = 14 * nb
    return call(
        attend_body(plan, blk, lo, hi, last),
        "attend",
        [info, lists[lo, hi], q] + list(kvs[lo:hi]) + list(olds),
        [SMEM] * 2 + [VMEM] + [ANY] * nb + [VMEM] * len(olds),
        outs,
        scratch=[
            pltpu.VMEM((nb * ns, blk, 2 * HEAD), BF16),
            pltpu.SemaphoreType.DMA((nb,)),
        ],
        flops=pairs * 4 * blk * blk * 128 * 8,
        trans=pairs * blk * blk,
    )


def attend_back_body(plan, blk, lo, hi, first, last):
    ns, nb, nj = len(plan.slots), hi - lo, len(plan.peers)

    def body(info, pairs, q_ref, lse_ref, *refs):
        kv_refs, refs = refs[:nb], refs[nb:]
        if first:
            of_ref, g_refs, gs_ref, refs = refs[0], refs[1 : 1 + nj], refs[1 + nj], refs[2 + nj :]
        else:
            g_ext, delta_ref, old_dq, refs = refs[0], refs[1], refs[2], refs[3:]
        dkv_refs, refs = refs[:nb], refs[nb:]
        dq_acc, refs = refs[0], refs[1:]
        if first:
            g_ext, delta_ref, refs = refs[0], refs[1], refs[2:]
        if last:
            dq_ref, refs = refs[0], refs[1:]
        kvs, dkvs, sem = refs
        copies = [
            pltpu.make_async_copy(ref, kvs.at[pl.ds(b * ns, ns)], sem.at[b])
            for b, ref in enumerate(kv_refs)
        ]
        for c in copies:
            c.start()
        n = pairs[0]
        core = info[0] % 2
        high = lane_iota((blk, 2 * HEAD)) >= HEAD
        if first:
            own_half = (lane_iota((blk, 2 * HEAD)) // HEAD) == core
            for s in range(ns):
                g = (g_refs[s][...] if s < nj else gs_ref[s - nj]).astype(F32)
                g = jnp.where(own_half, g, 0.0)
                delta_ref[s] = jnp.sum((g * of_ref[s]).T, axis=0, keepdims=True)
                turned = pltpu.roll(g, HEAD, 1)
                g_ext[s] = jnp.where(high, jnp.where(core == 1, g, turned), 0.0).astype(BF16)
            dq_acc[...] = jnp.zeros_like(dq_acc)
        else:
            dq_acc[...] = old_dq[...]
        dkvs[...] = jnp.zeros_like(dkvs)
        for c in copies:
            c.wait()

        def pair_terms(rows, cols, mask):
            scores = [mm(kvs[c], q_ref[i], NT) for i, c in zip(rows, cols)]
            slopes = [mm(kvs[c], g_ext[i], NT) for i, c in zip(rows, cols)]
            for k, (i, c) in enumerate(zip(rows, cols)):
                p = jnp.exp(scores[k] - lse_ref[i])
                p = mask(k, p)
                ds = (p * (slopes[k] - delta_ref[i])).astype(BF16)
                dkvs[c] += mm(ds, q_ref[i]) + mm(p.astype(BF16), g_ext[i])
                dq_acc[i] += mm(kvs[c][:, :HEAD], ds, TN)

        if not lo:
            tri = lax.broadcasted_iota(jnp.int32, (blk, blk), 0) <= lane_iota((blk, blk))

            def diagonal(h, _):
                at = [h * WIDE_BACK + k for k in range(WIDE_BACK)]
                pair_terms(at, at, lambda k, p: jnp.where(tri, p, 0.0))
                return 0

            lax.fori_loop(0, ns // WIDE_BACK, diagonal, 0)

        def step(h, _):
            codes2 = [pairs[h * WIDE_BACK + 1 + k] for k in range(WIDE_BACK)]
            pair_terms(
                [c // 1024 for c in codes2],
                [c % 1024 for c in codes2],
                lambda k, p: jnp.where(h * WIDE_BACK + k < n, p, 0.0) if k else p,
            )
            return 0

        lax.fori_loop(0, (n + WIDE_BACK - 1) // WIDE_BACK, step, 0)
        if last:

            def finish(i, _):
                thin = dq_acc[i] * HEAD**-0.5
                wide = jnp.concatenate([thin, jnp.zeros_like(thin)], axis=0).T
                dq_ref[i] = wide.astype(BF16)
                return 0

            lax.fori_loop(0, ns, finish, 0)
        for b in range(nb):
            dkv_refs[b][...] = dkvs[b * ns : (b + 1) * ns].astype(BF16)

    return body


def attend_back_part(plan, blk, lo, hi, first, last, info, lists, q, lse, kvs, extra):
    ns, nb = len(plan.slots), hi - lo
    rows = sds((ns, blk, 2 * HEAD), BF16)
    outs = [rows] * nb + [sds((ns, HEAD, blk), F32)]
    if first:
        outs += [rows, sds((ns, 1, blk), F32)]
    if last:
        outs += [rows]
    pairs = 14 * nb
    return call(
        attend_back_body(plan, blk, lo, hi, first, last),
        "attend_back",
        [info, lists[lo, hi], q, lse] + list(kvs[lo:hi]) + list(extra),
        [SMEM] * 2 + [VMEM] * 2 + [ANY] * nb + [VMEM] * len(extra),
        outs,
        scratch=[
            pltpu.VMEM((nb * ns, blk, 2 * HEAD), BF16),
            pltpu.VMEM((nb * ns, blk, 2 * HEAD), F32),
            pltpu.SemaphoreType.DMA((nb,)),
        ],
        flops=pairs * 10 * blk * blk * 128 * 8,
        trans=pairs * blk * blk,
    )


Z_ORDER = (0, 2, 1, 3)


def mlp_body(plan, width, ff, blk, packed):
    nj, nw, nc = len(plan.peers), plan.n_wt, plan.n_ctx
    nq = ff // CHUNK

    def body(info, *refs):
        refs = list(refs)
        x_ref, teacher_ref, valid_ref, vec_ref, count_ref = refs[:5]
        att = refs[5 : 5 + nj]
        rest = refs[5 + nj :]
        nwt_in = 6 if packed else 3
        w_in, rest = rest[:nwt_in], rest[nwt_in:]
        lo_ref, sq_ref, g1_ref = rest[:3]
        gatt_refs, rest = rest[3 : 3 + nj], rest[3 + nj :]
        act_ref, gpre_ref, n2_ref, gb_ref, ga_ref, gv_ref = rest[:6]
        rest = rest[6:]
        if packed:
            wup, wdown, wout, meta, slope_ref, acc_ref, sem = rest
            copies = []
            here = info[0] % 2
            owners = [info[0] ^ m for m in plan.near(here)]
            owners += [info[0] ^ 1 ^ m for m in plan.near(1 - here)]
            sources = []
            for head, pair, tail in (w_in[:3], w_in[3:]):
                sources += [head, pair.at[0], pair.at[1], tail]
            for c, src in zip(owners, sources):
                for m in range(nw):
                    w = info[1] ^ Z_ORDER[m]
                    copies += [
                        pltpu.make_async_copy(
                            src.at[m, pl.ds(nq + 4, 1)], wout.at[w, pl.ds(c, 1)], sem.at[0]
                        ),
                        pltpu.make_async_copy(src.at[m, pl.ds(0, nq)], wup.at[:, w, c], sem.at[1]),
                        pltpu.make_async_copy(
                            src.at[m, pl.ds(nq, 4)], wdown.at[w, pl.ds(c * 4, 4)], sem.at[2]
                        ),
                        pltpu.make_async_copy(
                            src.at[m, pl.ds(nq + 5, 1)], meta.at[w, pl.ds(c, 1)], sem.at[3]
                        ),
                    ]
            for part in (0, 3, 1, 2):
                for cp in copies[part::4]:
                    cp.start()

            def arrived(*parts):
                for part in parts:
                    for cp in copies[part::4]:
                        cp.wait()

            arrived(0, 3)
            w_up = lambda q: wup[q].reshape(width, CHUNK)
            w_down = lambda q: wdown[q].reshape(CHUNK, width)
            out_rows = width // nw
            pair_rows = 2 * HEAD
            wout_flat = wout.reshape(width, width)
            w_out = lambda row: wout_flat[pl.ds(row, pair_rows), :]
            count = jnp.sum(meta[:, :, 0:1, 0:1].astype(F32))
        else:
            slope_ref, acc_ref = rest
            arrived = lambda *parts: None
            w_up = lambda q: w_in[0][q]
            w_down = lambda q: w_in[1][q]
            w_out = lambda row: w_in[2][pl.ds(row, 2 * HEAD), :]
            count = count_ref[0]
        vecs = vec_ref[...]
        gain, shift = vecs[2:3], vecs[3:4]
        rows = []
        for mc, mw in plan.peers:
            head = plan.head(info[0] ^ mc, info[1] ^ mw)
            rows.append(pl.multiple_of((head // 2) * (2 * HEAD), 2 * HEAD))
        mixed = mm(att[0][...], w_out(rows[0]))
        for j in range(1, nj):
            mixed = mixed + mm(att[j][...], w_out(rows[j]))
        res = mixed + x_ref[...].astype(F32)
        unit, inverse = norm_stats(res)
        n2 = (unit * gain + shift).astype(BF16)
        n2_ref[...] = n2
        arrived(1)
        for q in range(nq):
            if q == 0:
                first = mm(n2, w_up(q))
                arrived(2)
            pre = first if q == 0 else mm(n2, w_up(q))
            cdf = 0.5 * (1.0 + lax.erf(pre * 0.7071067811865476))
            pdf = jnp.exp(-0.5 * pre * pre) * 0.3989422804014327
            act = (pre * cdf).astype(BF16)
            slope_ref[q] = cdf + pre * pdf
            act_ref[q] = act
            if q == 0:
                acc_ref[...] = mm(act, w_down(q))
            else:
                acc_ref[...] += mm(act, w_down(q))
        two = acc_ref[...] + res
        lo_ref[...] = two.astype(BF16)
        distance = two - teacher_ref[...].astype(F32)
        valid = valid_ref[...].astype(F32)
        weighed = valid * distance
        square = jnp.sum(weighed * distance)
        first_row = lax.broadcasted_iota(jnp.int32, (8, 128), 0) == 0
        sq_ref[...] = jnp.where(first_row, square, count)
        g2 = (2.0 * LOSS_SCALE / (count * width)) * weighed
        gb = g2.astype(BF16)
        gb_ref[...] = gb
        for q in range(nq):
            gpre = (mm(gb, w_down(q), NT) * slope_ref[q]).astype(BF16)
            gpre_ref[q] = gpre
            if q == 0:
                acc_ref[...] = mm(gpre, w_up(q), NT)
            else:
                acc_ref[...] += mm(gpre, w_up(q), NT)
        gn2 = acc_ref[...]
        g1 = g2 + norm_back(gn2, unit, inverse, gain)
        g1_ref[...] = g1
        gv_ref[...] = jnp.concatenate(
            [
                jnp.sum(gn2 * unit, axis=0, keepdims=True),
                jnp.sum(gn2, axis=0, keepdims=True),
                jnp.zeros((6, width), F32),
            ],
            axis=0,
        )
        ga = g1.astype(BF16)
        ga_ref[...] = ga
        for j in range(nj):
            gatt_refs[j][...] = mm(ga, w_out(rows[j]), NT).astype(BF16)

    return body


def mlp_grads_body(plan, width, ff, blk, packed):
    nj, nw, nc = len(plan.peers), plan.n_wt, plan.n_ctx
    nq = ff // CHUNK

    def body(info, act_ref, gpre_ref, n2_ref, gb_ref, ga_ref, gv_ref, sq_ref, *refs):
        att, outs = refs[:nj], refs[nj:]
        if packed:
            outs, (ups, downs, attn, metas, sem) = outs[:2], outs[2:]
        n2, gb, ga = n2_ref[...], gb_ref[...], ga_ref[...]
        ctx, wt = info[0], info[1]
        rows_up = width // (nw * nc)

        def put(c, w, tile, value):
            plane = (c ^ ctx) // 2
            middle = (plane == 1) | (plane == 2)
            place = jnp.where(middle, 3 - plane, plane) if c % 2 else plane
            zed = w ^ wt
            zed = jnp.where((zed == 1) | (zed == 2), 3 - zed, zed)
            for k in (0, 1):

                @pl.when(ctx % 2 == k)
                def _():
                    target = outs[(c % 2) ^ k].at[place, zed, pl.ds(tile, value.shape[0])]
                    pltpu.make_async_copy(value, target, sem.at[0]).start()

        for q in range(nq):
            up = mm(n2, gpre_ref[q], TN).astype(BF16)
            down = mm(act_ref[q], gb, TN).astype(BF16)
            if packed:
                ups[q] = up.reshape(nw * nc, rows_up, CHUNK)
                downs[q] = down.reshape(nc * 4, TILE, width)
                for w in range(nw):
                    for c in range(nc):
                        put(c, w, q, ups.at[q, pl.ds(w * nc + c, 1)])
                for c in range(nc):
                    put(c, q, nq, downs.at[q, pl.ds(4 * c, 4)])
            else:
                outs[0][q] = up
                outs[1][q] = down
        for j, (mc, mw) in enumerate(plan.peers):
            head = plan.head(ctx ^ mc, wt ^ mw)
            part = mm(att[j][...], ga, TN).astype(BF16)
            if packed:
                attn[j] = part.reshape(2 * HEAD // TILE, TILE, width)
                for t in range(2 * HEAD // TILE):
                    put(t, head // 2, nq + 4, attn.at[j, pl.ds(t, 1)])
            else:
                row = pl.multiple_of((head // 2) * (2 * HEAD), 2 * HEAD)
                outs[2][pl.ds(row, 2 * HEAD), :] = part
        if packed:
            dev = ctx * nw + wt
            square = sq_ref[0:1, 0:1]
            high = square.astype(BF16).astype(F32)
            lane = lane_iota((1, CHUNK))
            n_dev = nw * nc
            line = jnp.where(lane == dev, high, 0.0) + jnp.where(
                lane == dev + n_dev, square - high, 0.0
            )
            for w in range(nw):
                per = width // nw
                vec = gv_ref[0:2, per * w : per * (w + 1)]
                vec = jnp.concatenate([vec, jnp.zeros((2, CHUNK - per), F32)], axis=1)
                tile = jnp.concatenate([line, vec, jnp.zeros((TILE - 3, CHUNK), F32)], axis=0)
                metas[w, 0] = tile.astype(BF16)
                for c in range(nc):
                    put(c, w, nq + 5, metas.at[w])
            for ref in outs:
                pltpu.make_async_copy(ref, ref, sem.at[0]).wait()

    return body


def head_grads_body(plan, blk, width, shard, nb):
    ns, nw, nj = len(plan.slots), plan.n_wt, len(plan.peers)

    def body(info, dq_ref, wh_ref, normed_ref, *refs):
        xs = refs[:ns]
        parts = refs[ns : ns + nb]
        outs = refs[ns + nb :]
        own_ref, sib_ref, dw_ref, acc = outs
        half = shard // 2
        weight = wh_ref[...]
        gsum = jnp.zeros((1, width), F32)
        ssum = jnp.zeros((1, width), F32)
        for s in range(ns):
            dkv = parts[0][s].astype(F32)
            for b in range(1, nb):
                dkv = dkv + parts[b][s].astype(F32)
            zero = jnp.zeros((blk, 2 * HEAD), F32)
            wide = pltpu.roll(jnp.concatenate([dkv, zero], axis=1), HEAD, 1)
            wide = wide + jnp.concatenate([dq_ref[s].astype(F32), zero], axis=1)
            gh = wide.astype(BF16)
            back = mm(gh, weight, NT)
            if s < nj:
                own_ref[s] = back.astype(BF16)
            else:
                sib_ref[s - nj] = back.astype(BF16)
            unit, _ = norm_stats(xs[s][:blk, :].astype(F32))
            gsum = gsum + jnp.sum(back * unit, axis=0, keepdims=True)
            ssum = ssum + jnp.sum(back, axis=0, keepdims=True)
            dw = mm(normed_ref[s], gh, TN)
            if s == 0:
                acc[...] = dw
            else:
                acc[...] += dw
        vecs = jnp.concatenate([gsum, ssum, jnp.zeros((6, width), F32)], axis=0).astype(BF16)
        rows = lax.broadcasted_iota(jnp.int32, (8, 4 * HEAD), 0)
        pick = jnp.where(lane_iota((8, 4 * HEAD)) == rows + 3 * HEAD, 1.0, 0.0).astype(BF16)
        acc[...] += mm(vecs, pick, TN)
        for m in range(nw):
            row = pl.multiple_of((info[1] ^ m) * shard, shard)
            block = acc[pl.ds(row, shard), :].astype(BF16)
            dw_ref[m, :, : 4 * HEAD] = block[:half]
            dw_ref[m, :, 4 * HEAD :] = block[half:]

    return body


def merge_body(nj, nw, blk):
    def body(own_ref, sib_ref, dw_ref, more_ref, *outs):
        for m in range(nw):
            dw = (dw_ref[m].astype(F32) + more_ref[m].astype(F32)).astype(BF16)
            if m < nj:
                rows = own_ref[m].astype(F32) + sib_ref[m].astype(F32)
                outs[m][:blk, :] = rows.astype(BF16)
                outs[m][blk:, :] = dw
            else:
                outs[m][...] = dw

    return body


def words_body(nj):
    def body(x_ref, vec_ref, g1_ref, *refs):
        parts, sibs, out_ref = refs[:nj], refs[nj : 2 * nj], refs[-1]
        up = parts[0][: x_ref.shape[0], :].astype(F32)
        for p in parts[1:]:
            up = up + p[: up.shape[0], :].astype(F32)
        unit, inverse = norm_stats(x_ref[...].astype(F32))
        out_ref[...] = g1_ref[...] + norm_back(up, unit, inverse, vec_ref[0:1, :])

    return body


def unpack_body(plan, width, ff):
    nq, nw, nc = ff // CHUNK, plan.n_wt, plan.n_ctx

    def body(info, sq_ref, own, sib, *outs):
        srcs = [r.at[n] for r in (own, sib) for n in range(nc // 2)]
        up_ref, down_ref, out_ref, loss_ref, gain_ref, shift_ref = outs
        here = info[0] % 2
        owners = [info[0] ^ m for m in plan.near(here)]
        owners += [info[0] ^ 1 ^ m for m in plan.near(1 - here)]
        for c, src in zip(owners, srcs):
            row = pl.multiple_of(c * TILE, TILE)
            for q in range(nq):
                up_ref[pl.ds(row, TILE), q * CHUNK : (q + 1) * CHUNK] = src[q].astype(F32)
            for t in range(4):
                down_ref[pl.ds(pl.multiple_of(c * 4 * TILE + t * TILE, TILE), TILE), :] = src[
                    nq + t
                ].astype(F32)
            out_ref[pl.ds(row, TILE), :] = src[nq + 4].astype(F32)
        meta = srcs[0][nq + 5].astype(F32)
        count = jnp.max(sq_ref[1:2, :], axis=1, keepdims=True)
        loss_ref[...] = jnp.sum(meta[0:1], axis=1, keepdims=True) / (count * width)
        gain_ref[...] = meta[1:2, : width // nw]
        shift_ref[...] = meta[2:3, : width // nw]

    return body


def head_out_body(plan, shard):
    nj, half = len(plan.peers), shard // 2

    def body(info, own_ref, sib_ref, out_ref, gain_ref, shift_ref):
        core = info[0] % 2
        rows = lax.broadcasted_iota(jnp.int32, (8, 4 * HEAD), 0)
        pick = jnp.where(lane_iota((8, 4 * HEAD)) == rows + 3 * HEAD, 1.0, 0.0)
        lane = lane_iota((half, 2 * HEAD))
        for side in (0, 1):
            at = slice(side * 4 * HEAD, (side + 1) * 4 * HEAD)
            here = slice(side * half, (side + 1) * half)
            total = jnp.zeros((half, 4 * HEAD), F32)
            for j, (mc, mw) in enumerate(plan.peers):
                head = plan.head(info[0] ^ mc, info[1] ^ mw)
                own = own_ref[j, :, at].astype(F32)
                sib = sib_ref[j, :, at].astype(F32)
                total = total + own + sib
                even = jnp.where(core == 0, own, sib)
                odd = jnp.where(core == 0, sib, own)
                turned = pltpu.roll(odd, 3 * HEAD, 1)
                mid = jnp.where(lane < HEAD, even[:, 2 * HEAD :], turned[:, 2 * HEAD :])
                col = pl.multiple_of((head // 2) * (6 * HEAD), 2 * HEAD)
                out_ref[here, pl.ds(col, 2 * HEAD)] = even[:, : 2 * HEAD]
                out_ref[here, pl.ds(col + 2 * HEAD, 2 * HEAD)] = mid
                out_ref[here, pl.ds(col + 4 * HEAD, 2 * HEAD)] = turned[:, : 2 * HEAD]
            both = lax.dot_general(
                pick, total, NT, precision=lax.Precision.HIGHEST, preferred_element_type=F32
            )
            gain_ref[:, here] = both[0:1]
            shift_ref[:, here] = both[1:2]

    return body


def last_body(plan, shard, nj, width, ff, n_more):
    def body(info, own_ref, sib_ref, x_ref, vec_ref, g1_ref, *refs):
        loads, refs = refs[:nj], refs[nj:]
        more, refs = refs[:n_more], refs[n_more:]
        words_ref, out_ref, gain_ref, shift_ref = refs[:4]
        words_body(nj)(x_ref, vec_ref, g1_ref, *loads, *loads, words_ref)
        head_out_body(plan, shard)(info, own_ref, sib_ref, out_ref, gain_ref, shift_ref)
        if n_more:
            unpack_body(plan, width, ff)(info, *more, *refs[4:])

    return body


def per_device(
    words,
    teacher,
    valid,
    lengths,
    deal,
    gain_attn,
    shift_attn,
    w_qkv,
    w_out,
    gain_mlp,
    shift_mlp,
    w_up,
    w_down,
):
    n_ctx, n_wt = lax.axis_size("ctx"), lax.axis_size("wt")
    plan = Plan(n_ctx, n_wt)
    ctx, wt = lax.axis_index("ctx"), lax.axis_index("wt")
    blk, width = words.shape
    shard = width // n_wt
    ff = w_up.shape[1]
    nq = ff // CHUNK
    nseq = lengths.shape[0]
    ns, nb, nj = len(plan.slots), len(plan.groups), len(plan.peers)
    packed = plan.square and width == CHUNK and width % (n_wt * n_ctx * TILE) == 0
    packed = packed and n_wt * CHUNK == ff and 2 * HEAD // TILE == n_ctx
    info = jnp.stack([ctx, wt]).astype(jnp.int32)
    codes = jnp.array([mc * n_wt + mw for mc, mw in plan.slots], jnp.int32)
    core = (1, 0)

    vecs_here = jnp.stack([gain_attn, shift_attn, gain_mlp, shift_mlp])
    load = call(
        pack_body(plan, shard, blk),
        "pack",
        [info, words, w_qkv, vecs_here],
        [SMEM] + [VMEM] * 3,
        [sds((blk + shard // 2, width), BF16)] * n_wt,
    )
    loads = [load[0]] + [plan.swap(load[m], (0, m)) for m in range(1, n_wt)]
    sets = [(0, 1), (1, 3), (3, 4), (2, 4), (1, 2)] if plan.square else [(0, nb)]
    lists = call(
        lists_body(plan, blk, nseq, sets),
        "lists",
        [after(info, load[1]), deal, lengths, codes],
        [SMEM] * 4,
        [sds((ns * n_ctx * n_wt + WIDE + WIDE_BACK,), jnp.int32)] * len(sets),
        scratch=[pltpu.SMEM((n_ctx * n_wt,), jnp.int32)],
        out_specs=[SMEM] * len(sets),
    )
    lists = dict(zip(sets, lists))
    piece = info
    if packed:
        rows_up = width // (n_wt * n_ctx)
        up_piece = lax.dynamic_slice_in_dim(w_up, ctx * rows_up, rows_up, 0)
        up_piece = up_piece.reshape(rows_up, nq, CHUNK).transpose(1, 0, 2)
        down_piece = lax.dynamic_slice_in_dim(w_down, ctx * 4 * TILE, 4 * TILE, 0)
        out_piece = lax.dynamic_slice_in_dim(w_out, ctx * TILE, TILE, 0)
        count_here = jnp.sum(valid).astype(BF16)
        piece = jnp.concatenate(
            [
                up_piece,
                down_piece.reshape(4, TILE, CHUNK),
                out_piece[None],
                jnp.full((1, TILE, CHUNK), count_here, BF16),
            ],
            axis=0,
        )
    late = [loads[0], after(loads[1], lists[sets[0]], piece)] + loads[2:]
    xs = loads[:nj] + [plan.swap(x, core) for x in late[:nj]]

    q, kv, normed, w_head, vecs = call(
        project_body(plan, shard, blk),
        "project",
        [info] + xs + loads,
        [SMEM] + [VMEM] * (ns + n_wt),
        [
            sds((ns, blk, 2 * HEAD), BF16),
            sds((ns, blk, 2 * HEAD), BF16),
            sds((ns, blk, width), BF16),
            sds((width, 4 * HEAD), BF16),
            sds((8, width), F32),
        ],
        flops=2 * ns * blk * width * 4 * HEAD,
    )
    kvs = plan.gather_groups(kv)

    if packed:
        piece = after(piece, loads[2])
        two = jnp.stack([piece, plan.swap(piece, (0, 2))])
        two = after(two, kvs[1])
        near = plan.swap(two, (0, 1))
        count = jnp.zeros((1,), F32)
    else:
        up_full = lax.all_gather(w_up, "wt", axis=0, tiled=True)
        down_full = lax.all_gather(w_down, "wt", axis=0, tiled=True)
        out_full = lax.all_gather(w_out, "wt", axis=0, tiled=True)
        weights = [
            up_full.reshape(width, nq, CHUNK).transpose(1, 0, 2),
            down_full.reshape(nq, CHUNK, width),
            out_full,
        ]
        count = lax.psum(jnp.sum(valid).astype(F32), ("ctx", "wt")).reshape(1)

    state = []
    if not plan.square:
        state = attend_part(plan, blk, 0, nb, True, info, lists, q, kvs, state)
    else:
        state = attend_part(plan, blk, 0, 1, False, info, lists, q, kvs, state)
        if packed:
            stack = jnp.concatenate([two, near])
            stack = after(stack, kvs[3])
            kvs = kvs[:3] + [after(kvs[3], stack)]
        state = [after(state[0], kvs[3]), *state[1:]]
        state = attend_part(plan, blk, 1, 3, False, info, lists, q, kvs, state)
        if packed:
            one, side = plan.turn(stack, True), plan.turn(stack, False)
            stack_sib = plan.swap(stack, core)
        state = attend_part(plan, blk, 3, 4, True, info, lists, q, kvs, state)
    o, o_sib, of32, lse = state[3:]
    o_sib = plan.swap(o_sib, core)
    if packed:
        one = after(one, o_sib)
        last = plan.turn(one, False)
        pair = jnp.stack([one, side])
        weights = [stack, pair, last, stack_sib, plan.swap(pair, core)]
    mixed = o + o_sib
    att = [mixed[0]] + [plan.swap(mixed[j], plan.peers[j]) for j in range(1, nj)]
    if packed:
        weights += [plan.swap(after(last, *att[1:]), core)]

    mlp_in = [info, words, teacher, valid[:, None], vecs, count] + att + weights
    specs = [SMEM] + [VMEM] * 4 + [SMEM] + [VMEM] * nj
    specs += [ANY] * len(weights) if packed else [VMEM] * len(weights)
    scratch = [pltpu.VMEM((nq, blk, CHUNK), F32), pltpu.VMEM((blk, width), F32)]
    if packed:
        scratch = [
            pltpu.VMEM((nq, n_wt, n_ctx, TILE, CHUNK), BF16),
            pltpu.VMEM((n_wt, n_ctx * 4, TILE, CHUNK), BF16),
            pltpu.VMEM((n_wt, n_ctx, TILE, CHUNK), BF16),
            pltpu.VMEM((n_wt, n_ctx, TILE, CHUNK), BF16),
            *scratch,
            pltpu.SemaphoreType.DMA((4,)),
        ]
    layer_out, square, grad_one, *rest = call(
        mlp_body(plan, width, ff, blk, packed),
        "mlp",
        mlp_in,
        specs,
        [
            sds((blk, width), BF16),
            sds((8, 128), F32),
            sds((blk, width), F32),
            *[sds((blk, 2 * HEAD), BF16)] * nj,
            sds((nq, blk, CHUNK), BF16),
            sds((nq, blk, CHUNK), BF16),
            sds((blk, width), BF16),
            sds((blk, width), BF16),
            sds((blk, width), BF16),
            sds((8, width), F32),
        ],
        scratch=scratch,
        flops=8 * blk * width * ff,
        trans=2 * blk * ff,
    )
    gatt, (act, gpre, n2, gb, ga, gvec) = rest[:nj], rest[nj:]
    g_own = [gatt[0]] + [plan.swap(gatt[j], plan.peers[j]) for j in range(1, nj)]
    g_sib = plan.swap(jnp.stack(g_own), core)

    grads_in = [info, act, gpre, n2, gb, ga, gvec, square] + att
    if packed:
        grads_out = [sds((n_ctx // 2, n_wt, nq + 6, TILE, CHUNK), BF16)] * 2
        grads_scratch = [
            pltpu.VMEM((nq, n_wt * n_ctx, TILE, CHUNK), BF16),
            pltpu.VMEM((nq, n_ctx * 4, TILE, CHUNK), BF16),
            pltpu.VMEM((nj, n_ctx, TILE, CHUNK), BF16),
            pltpu.VMEM((n_wt, 1, TILE, CHUNK), BF16),
            pltpu.SemaphoreType.DMA((1,)),
        ]
    else:
        grads_out = [
            sds((nq, width, CHUNK), BF16),
            sds((nq, CHUNK, width), BF16),
            sds((width, width), BF16),
        ]
        grads_scratch = []
    weight_grads = call(
        mlp_grads_body(plan, width, ff, blk, packed),
        "mlp_grads",
        grads_in,
        [SMEM] + [VMEM] * (7 + nj),
        grads_out,
        scratch=grads_scratch,
        out_specs=[ANY if packed else VMEM] * len(grads_out),
        flops=4 * blk * width * ff,
    )

    extra = [of32] + g_own + [g_sib]
    if plan.square:
        if packed:
            g_all, g_core = weight_grads[0], plan.swap(weight_grads[1], core)
            g_far = (g_all[2:].astype(F32) + g_core[2:].astype(F32)).astype(BF16)
            extra = [after(of32, g_far)] + extra[1:]
            g_far = plan.turn(g_far, False)
        part = attend_back_part(plan, blk, 2, 4, True, False, info, lists, q, lse, kvs, extra)
        dkv2, dkv3, dq_part, g_ext, delta = part
        far = [plan.turn(d, False) for d in (dkv3, dkv2)]
        dkv1, dq_part = attend_back_part(
            plan, blk, 1, 2, False, False, info, lists, q, lse, kvs, [g_ext, delta, dq_part]
        )
        mid = plan.turn((dkv1.astype(F32) + far[0].astype(F32)).astype(BF16), True)
        if packed:
            g_far = after(g_far, dkv1)
            g_mid = g_all[1].astype(F32) + g_core[1].astype(F32) + g_far[1].astype(F32)
            g_mid = g_mid.astype(BF16)
            dq_part = after(dq_part, g_mid)
            g_mid = plan.turn(g_mid, True)
        dkv0, _, dq = attend_back_part(
            plan, blk, 0, 1, False, True, info, lists, q, lse, kvs, [g_ext, delta, dq_part]
        )
        if packed:
            g_mid = after(g_mid, dkv0)
            g_near = g_all[0].astype(F32) + g_core[0].astype(F32) + g_far[0].astype(F32)
            g_near = (g_near + g_mid.astype(F32)).astype(BF16)
            dq = after(dq, g_near)
            g_other = plan.swap(g_near[2:], (0, 1))
        parts = [dkv0, far[1], mid]
    else:
        part = attend_back_part(plan, blk, 0, nb, True, True, info, lists, q, lse, kvs, extra)
        dq = part[-1]
        parts = [part[0]] + [plan.swap(part[b], plan.groups[b]) for b in range(1, nb)]

    head_outs = call(
        head_grads_body(plan, blk, width, shard, len(parts)),
        "head_grads",
        [info, dq, w_head, normed] + xs + parts,
        [SMEM] + [VMEM] * (3 + ns + len(parts)),
        [sds((nj, blk, width), BF16)] * 2 + [sds((n_wt, shard // 2, width), BF16)],
        scratch=[pltpu.VMEM((width, 4 * HEAD), F32)],
        flops=4 * ns * blk * width * 4 * HEAD,
    )
    own_rows, sib_rows, dw = head_outs
    if packed:
        g_two = (g_near[:2].astype(F32) + g_other.astype(F32)).astype(BF16)
        g_last = plan.swap(g_two[1], (0, 2))
    sib_rows = plan.swap(sib_rows, core)

    if plan.square:
        dw = (dw.astype(F32) + plan.turn(dw, True).astype(F32)).astype(BF16)
        dw_more = plan.turn(dw, False)
    else:
        step = CTX_HEADS
        while step < n_ctx:
            dw_more = plan.swap(dw, (step, 0))
            step *= 2
            if step < n_ctx:
                dw = (dw.astype(F32) + dw_more.astype(F32)).astype(BF16)
    load = call(
        merge_body(nj, n_wt, blk),
        "merge",
        [own_rows, sib_rows, dw, dw_more],
        [VMEM] * 4,
        [sds((blk + shard // 2, width), BF16)] * nj
        + [sds((shard // 2, width), BF16)] * (n_wt - nj),
    )
    loads = [load[0]] + [plan.swap(load[m], (0, m)) for m in range(1, n_wt)]
    if packed:
        g_last = after(g_last, load[0])
        final = (g_two[0].astype(F32) + g_last.astype(F32)).astype(BF16)
        finals = plan.gather_square(final)
        finals = jnp.stack(finals)
        finals = [finals, plan.swap(finals, core)]
    else:
        g_up, g_down, g_out = weight_grads
        g_up = g_up.transpose(1, 0, 2).reshape(width, ff)
        g_down = g_down.reshape(ff, width)

        def reduce_rows(g):
            part = lax.psum_scatter(g.astype(BF16), "wt", scatter_dimension=0, tiled=True)
            return lax.psum(part, "ctx").astype(F32)

        g_up, g_down, g_out = reduce_rows(g_up), reduce_rows(g_down), reduce_rows(g_out)
        both = lax.psum(gvec[:2], ("ctx", "wt"))
        both = lax.dynamic_slice_in_dim(both, wt * shard, shard, 1)
        g_gain, g_shift = both[0], both[1]
        loss = lax.psum(square[0, 0], ("ctx", "wt")) / (count[0] * width)
    own_heads = jnp.stack([x[blk:] for x in loads[:nj]])
    if n_wt > nj:
        own_heads = (own_heads.astype(F32) + jnp.stack(loads[nj:]).astype(F32)).astype(BF16)
    sib_heads = plan.swap(own_heads, core)
    more_in = [square, *finals] if packed else []
    more_out = []
    if packed:
        more_out = [
            sds((shard, ff), F32),
            sds((ff // n_wt, width), F32),
            sds((shard, width), F32),
            sds((1, 1), F32),
            sds((1, shard), F32),
            sds((1, shard), F32),
        ]
    grad_words, g_qkv, gain_one, shift_one, *more = call(
        last_body(plan, shard, nj, width, ff, len(more_in)),
        "last",
        [info, own_heads, sib_heads, words, vecs, grad_one] + loads[:nj] + more_in,
        [SMEM] + [VMEM] * (5 + nj + len(more_in)),
        [
            sds((blk, width), F32),
            sds((shard, 3 * width), F32),
            sds((1, shard), F32),
            sds((1, shard), F32),
        ]
        + more_out,
    )
    if packed:
        g_up, g_down, g_out, loss, g_gain, g_shift = more
        loss, g_gain, g_shift = loss[0, 0], g_gain.reshape(shard), g_shift.reshape(shard)
    return (
        layer_out,
        loss,
        grad_words,
        gain_one.reshape(shard),
        shift_one.reshape(shard),
        g_qkv,
        g_out,
        g_gain,
        g_shift,
        g_up,
        g_down,
    )


def solution(mesh):
    placed = (
        P(("ctx", "wt"), None),
        P(("ctx", "wt"), None),
        P(("ctx", "wt")),
        P(),
        P(),
        P("wt"),
        P("wt"),
        P("wt", None),
        P("wt", None),
        P("wt"),
        P("wt"),
        P("wt", None),
        P("wt", None),
    )
    return jax.shard_map(
        per_device,
        mesh=mesh,
        in_specs=placed,
        out_specs=(
            P(("ctx", "wt"), None),
            P(),
            P(("ctx", "wt"), None),
            P("wt"),
            P("wt"),
            P("wt", None),
            P("wt", None),
            P("wt"),
            P("wt"),
            P("wt", None),
            P("wt", None),
        ),
        check_vma=False,
    )
```

```python
import jax
import jax.numpy as jnp
from jax import lax
from jax.experimental import pallas as pl
from jax.experimental.pallas import tpu as pltpu
from jax.sharding import PartitionSpec as P

H = 8
HEAD = 64
EPS = 1e-05
LOSS_SCALE = 262144.0
CTX_HEADS = 2
WT_HEADS = 4
CHUNK = 512
TILE = 16
WIDE = 4
WIDE_BACK = 4
F32 = jnp.float32
BF16 = jnp.bfloat16
NEG = -1e30
NT = (((1,), (1,)), ((), ()))
TN = (((0,), (0,)), ((), ()))
NN = (((1,), (0,)), ((), ()))


def mm(a, b, dims=NN):
    return lax.dot_general(a, b, dims, preferred_element_type=F32)


def lane_iota(shape):
    return lax.broadcasted_iota(jnp.int32, shape, len(shape) - 1)


def norm_stats(values):
    center = values - jnp.mean(values, axis=-1, keepdims=True)
    inverse = lax.rsqrt(jnp.mean(center * center, axis=-1, keepdims=True) + EPS)
    return center * inverse, inverse


def norm_back(upstream, unit, inverse, gain):
    scaled = upstream * gain
    inner = jnp.mean(scaled * unit, axis=-1, keepdims=True)
    return inverse * (scaled - jnp.mean(scaled, axis=-1, keepdims=True) - unit * inner)


SMEM = pl.BlockSpec(memory_space=pltpu.SMEM)
VMEM = pl.BlockSpec(memory_space=pltpu.VMEM)
ANY = pl.BlockSpec(memory_space=pl.ANY)


def call(body, name, ins, in_specs, outs, scratch=(), flops=0, trans=0, out_specs=None):
    nbytes = sum(x.size * x.dtype.itemsize for x in list(ins) + list(outs))
    return pl.pallas_call(
        body,
        name=name,
        out_shape=list(outs),
        in_specs=in_specs,
        out_specs=out_specs or [VMEM] * len(outs),
        scratch_shapes=list(scratch),
        compiler_params=pltpu.CompilerParams(vmem_limit_bytes=58 * 1024 * 1024),
        cost_estimate=pl.CostEstimate(flops=flops, bytes_accessed=nbytes, transcendentals=trans),
    )(*ins)


def after(value, *earlier):
    return lax.optimization_barrier((value, *earlier))[0]


def sds(shape, dtype):
    return jax.ShapeDtypeStruct(shape, dtype)


class Plan:
    def __init__(self, n_ctx, n_wt):
        self.n_ctx, self.n_wt = n_ctx, n_wt
        ac, aw = CTX_HEADS, WT_HEADS
        assert ac * aw == H and n_ctx % ac == 0 and n_wt % aw == 0
        self.peers = [(mc, mw) for mw in range(aw) for mc in range(0, ac, 2)]
        self.slots = [(mc | k, mw) for k in (0, 1) for mc, mw in self.peers]
        self.groups = [(mc, mw) for mc in range(0, n_ctx, ac) for mw in range(0, n_wt, aw)]
        self.square = n_ctx == 8 and n_wt == aw

    def near(self, core):
        return [0, 2 + 2 * core, 4 - 2 * core, 6]

    def group_masks(self, core):
        return [(m, 0) for m in self.near(core)] if self.square else self.groups

    def head(self, ctx, wt):
        return (wt % WT_HEADS) * CTX_HEADS + ctx % CTX_HEADS

    def swap(self, x, mask):
        mc, mw = mask
        n = self.n_wt
        perm = [
            (c * n + w, (c ^ mc) * n + (w ^ mw)) for c in range(self.n_ctx) for w in range(n)
        ]
        return lax.ppermute(x, ("ctx", "wt"), perm)

    def turn(self, x, first):
        n = self.n_wt
        masks = (2, 4) if first else (4, 2)
        perm = [
            (c * n + w, (c ^ masks[c % 2]) * n + w) for c in range(self.n_ctx) for w in range(n)
        ]
        return lax.ppermute(x, ("ctx", "wt"), perm)

    def gather_square(self, x):
        one = self.turn(x, True)
        return [x, one, self.turn(x, False), self.turn(one, False)]

    def gather_groups(self, x):
        if self.square:
            return self.gather_square(x)
        return [x] + [self.swap(x, m) for m in self.groups[1:]]


def pack_body(plan, shard, blk):
    nw, half = plan.n_wt, shard // 2

    def body(info, words_ref, w_ref, vec_ref, *outs):
        odd = (info[0] % 2) == 1
        rows = lax.broadcasted_iota(jnp.int32, (4, 4 * HEAD), 0)
        pick = jnp.where(lane_iota((4, 4 * HEAD)) == rows + 3 * HEAD, 1.0, 0.0).astype(BF16)
        vec = mm(vec_ref[...], pick, TN)
        lane = lane_iota((shard, 4 * HEAD))
        for m in range(nw):
            pair = plan.head(info[0], info[1] ^ m) // 2
            col = pl.multiple_of(pair * (6 * HEAD), 2 * HEAD)
            both = w_ref[:, pl.ds(col, 6 * HEAD)].astype(F32)
            turned = pltpu.roll(both, 3 * HEAD, 1)
            cols = jnp.where(odd, turned[:, : 4 * HEAD], both[:, : 4 * HEAD])
            cols = jnp.where(lane < 3 * HEAD, cols, vec).astype(BF16)
            outs[m][:blk, :] = words_ref[...]
            outs[m][blk:, : 4 * HEAD] = cols[:half]
            outs[m][blk:, 4 * HEAD :] = cols[half:]

    return body


def project_body(plan, shard, blk):
    ns, nw, half = len(plan.slots), plan.n_wt, shard // 2

    def body(info, *refs):
        xs, wps = refs[:ns], refs[ns : ns + nw]
        q_ref, kv_ref, normed_ref, wh_ref, vec_ref = refs[ns + nw :]
        wt = info[1]
        for m in range(nw):
            row = pl.multiple_of((wt ^ m) * shard, shard)
            wh_ref[pl.ds(row, half), :] = wps[m][blk:, : 4 * HEAD]
            wh_ref[pl.ds(row + half, half), :] = wps[m][blk:, 4 * HEAD :]
        weight = wh_ref[...]
        rows = lax.broadcasted_iota(jnp.int32, (8, 4 * HEAD), 0)
        pick = jnp.where(lane_iota((8, 4 * HEAD)) == rows + 3 * HEAD, 1.0, 0.0).astype(BF16)
        vecs = mm(pick, weight, NT)
        vec_ref[...] = vecs
        gain, shift = vecs[0:1], vecs[1:2]
        low = lane_iota((blk, 2 * HEAD)) < HEAD
        for s in range(ns):
            unit, _ = norm_stats(xs[s][:blk, :].astype(F32))
            normed = (unit * gain + shift).astype(BF16)
            normed_ref[s] = normed
            y = mm(normed, weight)
            q_ref[s] = (
                jnp.where(low, y[:, : 2 * HEAD], 0.0).astype(BF16).astype(F32) * HEAD**-0.5
            ).astype(BF16)
            kv_ref[s] = pltpu.roll(y, 3 * HEAD, 1)[:, : 2 * HEAD].astype(BF16)

    return body


def fill_slots(plan, info, deal, slot_of):
    for g, (gc, gw) in enumerate(plan.group_masks(info[0] % 2)):
        for s, (mc, mw) in enumerate(plan.slots):
            at = (info[0] ^ gc ^ mc) * plan.n_wt + (info[1] ^ gw ^ mw)
            slot_of[deal[at]] = g * len(plan.slots) + s


def slot_range(plan, info, deal, lengths, codes, i, blk, nseq):
    code = codes[i]
    here = deal[(info[0] ^ (code // plan.n_wt)) * plan.n_wt + (info[1] ^ (code % plan.n_wt))]
    first = jnp.int32(0)
    total = jnp.int32(0)
    for n in range(nseq):
        total = total + lengths[n]
        bound = total // blk
        first = jnp.where(bound <= here, bound, first)
    return first, here


def lists_body(plan, blk, nseq, sets):
    ns = len(plan.slots)

    def body(info, deal, lengths, codes, *refs):
        outs, slot_of = refs[:-1], refs[-1]
        fill_slots(plan, info, deal, slot_of)

        def one_block(i, counts):
            first, here = slot_range(plan, info, deal, lengths, codes, i, blk, nseq)

            def one_key(b, counts):
                slot = slot_of[b]
                more = []
                for out, n, (lo, hi) in zip(outs, counts, sets):
                    inside = (slot >= lo * ns) & (slot < hi * ns)
                    out[n] = i * 1024 + slot - lo * ns
                    more.append(n + inside.astype(jnp.int32))
                return tuple(more)

            return lax.fori_loop(first, here, one_key, counts)

        start = tuple(jnp.int32(1) for _ in sets)
        counts = lax.fori_loop(0, ns, one_block, start)
        for out, n in zip(outs, counts):
            spare = jnp.where(n > 1, out[jnp.maximum(n - 1, 1)], 0)
            for t in range(max(WIDE, WIDE_BACK) - 1):
                out[n + t] = spare
            out[0] = n - 1

    return body


def attend_body(plan, blk, lo, hi, last):
    ns, nb = len(plan.slots), hi - lo

    def body(info, pairs, q_ref, *refs):
        kv_refs, refs = refs[:nb], refs[nb:]
        if lo:
            olds, refs = refs[:3], refs[3:]
        (m_ref, l_ref, acc_ref), refs = refs[:3], refs[3:]
        if last:
            (o_ref, o_sib_ref, of_ref, lse_ref), refs = refs[:4], refs[4:]
        kvs, sem = refs
        copies = [
            pltpu.make_async_copy(ref, kvs.at[pl.ds(b * ns, ns)], sem.at[b])
            for b, ref in enumerate(kv_refs)
        ]
        for c in copies:
            c.start()
        n = pairs[0]
        if lo:
            for new, old in zip((m_ref, l_ref, acc_ref), olds):
                new[...] = old[...]
        for c in copies:
            c.wait()
        if not lo:
            tri = lax.broadcasted_iota(jnp.int32, (blk, blk), 0) <= lane_iota((blk, blk))

            def diagonal(h, _):
                scores = [mm(kvs[h * WIDE + k], q_ref[h * WIDE + k], NT) for k in range(WIDE)]
                for k in range(WIDE):
                    i = h * WIDE + k
                    s = jnp.where(tri, scores[k], NEG)
                    m = jnp.max(s, axis=0, keepdims=True)
                    p = jnp.exp(s - m)
                    m_ref[i] = m
                    l_ref[i] = jnp.sum(p, axis=0, keepdims=True)
                    acc_ref[i] = mm(kvs[i], p.astype(BF16), TN)
                return 0

            lax.fori_loop(0, ns // WIDE, diagonal, 0)

        def step(h, _):
            codes2 = [pairs[h * WIDE + 1 + k] for k in range(WIDE)]
            rows = [c // 1024 for c in codes2]
            cols = [c % 1024 for c in codes2]
            scores = [mm(kvs[cols[k]], q_ref[rows[k]], NT) for k in range(WIDE)]
            for k in range(1, WIDE):
                scores[k] = jnp.where(h * WIDE + k < n, scores[k], NEG)
            for k in range(WIDE):
                i, s = rows[k], scores[k]
                m_old = m_ref[i]
                m = jnp.maximum(m_old, jnp.max(s, axis=0, keepdims=True))
                p = jnp.exp(s - m)
                factor = jnp.exp(m_old - m)
                m_ref[i] = m
                l_ref[i] = l_ref[i] * factor + jnp.sum(p, axis=0, keepdims=True)
                acc_ref[i] = acc_ref[i] * factor + mm(kvs[cols[k]], p.astype(BF16), TN)
            return 0

        lax.fori_loop(0, (n + WIDE - 1) // WIDE, step, 0)
        if last:
            core = info[0] % 2

            def finish(i, _):
                total = l_ref[i]
                lse_ref[i] = m_ref[i] + jnp.log(total)
                out = acc_ref[i, HEAD:, :] / total
                zero = jnp.zeros_like(out)
                placed = jnp.concatenate(
                    [jnp.where(core == 0, out, zero), jnp.where(core == 1, out, zero)], axis=0
                )
                wide = placed.T
                of_ref[i] = wide

                @pl.when(i < ns // 2)
                def _():
                    o_ref[i] = wide.astype(BF16)

                @pl.when(i >= ns // 2)
                def _():
                    o_sib_ref[i - ns // 2] = wide.astype(BF16)

                return 0

            lax.fori_loop(0, ns, finish, 0)

    return body


def attend_part(plan, blk, lo, hi, last, info, lists, q, kvs, olds):
    ns, nb = len(plan.slots), hi - lo
    outs = [sds((ns, 1, blk), F32), sds((ns, 1, blk), F32), sds((ns, 2 * HEAD, blk), F32)]
    if last:
        outs += [
            sds((ns // 2, blk, 2 * HEAD), BF16),
            sds((ns // 2, blk, 2 * HEAD), BF16),
            sds((ns, blk, 2 * HEAD), F32),
            sds((ns, 1, blk), F32),
        ]
    pairs = 14 * nb
    return call(
        attend_body(plan, blk, lo, hi, last),
        "attend",
        [info, lists[lo, hi], q] + list(kvs[lo:hi]) + list(olds),
        [SMEM] * 2 + [VMEM] + [ANY] * nb + [VMEM] * len(olds),
        outs,
        scratch=[
            pltpu.VMEM((nb * ns, blk, 2 * HEAD), BF16),
            pltpu.SemaphoreType.DMA((nb,)),
        ],
        flops=pairs * 4 * blk * blk * 128 * 8,
        trans=pairs * blk * blk,
    )


def attend_back_body(plan, blk, lo, hi, first, last):
    ns, nb, nj = len(plan.slots), hi - lo, len(plan.peers)

    def body(info, pairs, q_ref, lse_ref, *refs):
        kv_refs, refs = refs[:nb], refs[nb:]
        if first:
            of_ref, g_refs, gs_ref, refs = refs[0], refs[1 : 1 + nj], refs[1 + nj], refs[2 + nj :]
        else:
            g_ext, delta_ref, old_dq, refs = refs[0], refs[1], refs[2], refs[3:]
        dkv_refs, refs = refs[:nb], refs[nb:]
        dq_acc, refs = refs[0], refs[1:]
        if first:
            g_ext, delta_ref, refs = refs[0], refs[1], refs[2:]
        if last:
            dq_ref, refs = refs[0], refs[1:]
        kvs, dkvs, sem = refs
        copies = [
            pltpu.make_async_copy(ref, kvs.at[pl.ds(b * ns, ns)], sem.at[b])
            for b, ref in enumerate(kv_refs)
        ]
        for c in copies:
            c.start()
        n = pairs[0]
        core = info[0] % 2
        high = lane_iota((blk, 2 * HEAD)) >= HEAD
        if first:
            own_half = (lane_iota((blk, 2 * HEAD)) // HEAD) == core
            for s in range(ns):
                g = (g_refs[s][...] if s < nj else gs_ref[s - nj]).astype(F32)
                g = jnp.where(own_half, g, 0.0)
                delta_ref[s] = jnp.sum((g * of_ref[s]).T, axis=0, keepdims=True)
                turned = pltpu.roll(g, HEAD, 1)
                g_ext[s] = jnp.where(high, jnp.where(core == 1, g, turned), 0.0).astype(BF16)
            dq_acc[...] = jnp.zeros_like(dq_acc)
        else:
            dq_acc[...] = old_dq[...]
        dkvs[...] = jnp.zeros_like(dkvs)
        for c in copies:
            c.wait()

        def pair_terms(rows, cols, mask):
            scores = [mm(kvs[c], q_ref[i], NT) for i, c in zip(rows, cols)]
            slopes = [mm(kvs[c], g_ext[i], NT) for i, c in zip(rows, cols)]
            for k, (i, c) in enumerate(zip(rows, cols)):
                p = jnp.exp(scores[k] - lse_ref[i])
                p = mask(k, p)
                ds = (p * (slopes[k] - delta_ref[i])).astype(BF16)
                dkvs[c] += mm(ds, q_ref[i]) + mm(p.astype(BF16), g_ext[i])
                dq_acc[i] += mm(kvs[c][:, :HEAD], ds, TN)

        if not lo:
            tri = lax.broadcasted_iota(jnp.int32, (blk, blk), 0) <= lane_iota((blk, blk))

            def diagonal(h, _):
                at = [h * WIDE_BACK + k for k in range(WIDE_BACK)]
                pair_terms(at, at, lambda k, p: jnp.where(tri, p, 0.0))
                return 0

            lax.fori_loop(0, ns // WIDE_BACK, diagonal, 0)

        def step(h, _):
            codes2 = [pairs[h * WIDE_BACK + 1 + k] for k in range(WIDE_BACK)]
            pair_terms(
                [c // 1024 for c in codes2],
                [c % 1024 for c in codes2],
                lambda k, p: jnp.where(h * WIDE_BACK + k < n, p, 0.0) if k else p,
            )
            return 0

        lax.fori_loop(0, (n + WIDE_BACK - 1) // WIDE_BACK, step, 0)
        if last:

            def finish(i, _):
                thin = dq_acc[i] * HEAD**-0.5
                wide = jnp.concatenate([thin, jnp.zeros_like(thin)], axis=0).T
                dq_ref[i] = wide.astype(BF16)
                return 0

            lax.fori_loop(0, ns, finish, 0)
        for b in range(nb):
            dkv_refs[b][...] = dkvs[b * ns : (b + 1) * ns].astype(BF16)

    return body


def attend_back_part(plan, blk, lo, hi, first, last, info, lists, q, lse, kvs, extra):
    ns, nb = len(plan.slots), hi - lo
    rows = sds((ns, blk, 2 * HEAD), BF16)
    outs = [rows] * nb + [sds((ns, HEAD, blk), F32)]
    if first:
        outs += [rows, sds((ns, 1, blk), F32)]
    if last:
        outs += [rows]
    pairs = 14 * nb
    return call(
        attend_back_body(plan, blk, lo, hi, first, last),
        "attend_back",
        [info, lists[lo, hi], q, lse] + list(kvs[lo:hi]) + list(extra),
        [SMEM] * 2 + [VMEM] * 2 + [ANY] * nb + [VMEM] * len(extra),
        outs,
        scratch=[
            pltpu.VMEM((nb * ns, blk, 2 * HEAD), BF16),
            pltpu.VMEM((nb * ns, blk, 2 * HEAD), F32),
            pltpu.SemaphoreType.DMA((nb,)),
        ],
        flops=pairs * 10 * blk * blk * 128 * 8,
        trans=pairs * blk * blk,
    )


Z_ORDER = (0, 2, 1, 3)


def mlp_body(plan, width, ff, blk, packed):
    nj, nw, nc = len(plan.peers), plan.n_wt, plan.n_ctx
    nq = ff // CHUNK

    def body(info, *refs):
        refs = list(refs)
        x_ref, teacher_ref, valid_ref, vec_ref, count_ref = refs[:5]
        att = refs[5 : 5 + nj]
        rest = refs[5 + nj :]
        nwt_in = 6 if packed else 3
        w_in, rest = rest[:nwt_in], rest[nwt_in:]
        lo_ref, sq_ref, g1_ref = rest[:3]
        gatt_refs, rest = rest[3 : 3 + nj], rest[3 + nj :]
        act_ref, gpre_ref, n2_ref, gb_ref, ga_ref, gv_ref = rest[:6]
        rest = rest[6:]
        if packed:
            wup, wdown, wout, meta, slope_ref, acc_ref, sem = rest
            copies = []
            here = info[0] % 2
            owners = [info[0] ^ m for m in plan.near(here)]
            owners += [info[0] ^ 1 ^ m for m in plan.near(1 - here)]
            sources = []
            for head, pair, tail in (w_in[:3], w_in[3:]):
                sources += [head, pair.at[0], pair.at[1], tail]
            for c, src in zip(owners, sources):
                for m in range(nw):
                    w = info[1] ^ Z_ORDER[m]
                    copies += [
                        pltpu.make_async_copy(
                            src.at[m, pl.ds(nq + 4, 1)], wout.at[w, pl.ds(c, 1)], sem.at[0]
                        ),
                        pltpu.make_async_copy(src.at[m, pl.ds(0, nq)], wup.at[:, w, c], sem.at[1]),
                        pltpu.make_async_copy(
                            src.at[m, pl.ds(nq, 4)], wdown.at[w, pl.ds(c * 4, 4)], sem.at[2]
                        ),
                        pltpu.make_async_copy(
                            src.at[m, pl.ds(nq + 5, 1)], meta.at[w, pl.ds(c, 1)], sem.at[3]
                        ),
                    ]
            for part in (0, 3, 1, 2):
                for cp in copies[part::4]:
                    cp.start()

            def arrived(*parts):
                for part in parts:
                    for cp in copies[part::4]:
                        cp.wait()

            arrived(0, 3)
            w_up = lambda q: wup[q].reshape(width, CHUNK)
            w_down = lambda q: wdown[q].reshape(CHUNK, width)
            out_rows = width // nw
            pair_rows = 2 * HEAD
            wout_flat = wout.reshape(width, width)
            w_out = lambda row: wout_flat[pl.ds(row, pair_rows), :]
            count = jnp.sum(meta[:, :, 0:1, 0:1].astype(F32))
        else:
            slope_ref, acc_ref = rest
            arrived = lambda *parts: None
            w_up = lambda q: w_in[0][q]
            w_down = lambda q: w_in[1][q]
            w_out = lambda row: w_in[2][pl.ds(row, 2 * HEAD), :]
            count = count_ref[0]
        vecs = vec_ref[...]
        gain, shift = vecs[2:3], vecs[3:4]
        rows = []
        for mc, mw in plan.peers:
            head = plan.head(info[0] ^ mc, info[1] ^ mw)
            rows.append(pl.multiple_of((head // 2) * (2 * HEAD), 2 * HEAD))
        mixed = mm(att[0][...], w_out(rows[0]))
        for j in range(1, nj):
            mixed = mixed + mm(att[j][...], w_out(rows[j]))
        res = mixed + x_ref[...].astype(F32)
        unit, inverse = norm_stats(res)
        n2 = (unit * gain + shift).astype(BF16)
        n2_ref[...] = n2
        arrived(1)
        for q in range(nq):
            if q == 0:
                first = mm(n2, w_up(q))
                arrived(2)
            pre = first if q == 0 else mm(n2, w_up(q))
            cdf = 0.5 * (1.0 + lax.erf(pre * 0.7071067811865476))
            pdf = jnp.exp(-0.5 * pre * pre) * 0.3989422804014327
            act = (pre * cdf).astype(BF16)
            slope_ref[q] = cdf + pre * pdf
            act_ref[q] = act
            if q == 0:
                acc_ref[...] = mm(act, w_down(q))
            else:
                acc_ref[...] += mm(act, w_down(q))
        two = acc_ref[...] + res
        lo_ref[...] = two.astype(BF16)
        distance = two - teacher_ref[...].astype(F32)
        valid = valid_ref[...].astype(F32)
        weighed = valid * distance
        square = jnp.sum(weighed * distance)
        first_row = lax.broadcasted_iota(jnp.int32, (8, 128), 0) == 0
        sq_ref[...] = jnp.where(first_row, square, count)
        g2 = (2.0 * LOSS_SCALE / (count * width)) * weighed
        gb = g2.astype(BF16)
        gb_ref[...] = gb
        for q in range(nq):
            gpre = (mm(gb, w_down(q), NT) * slope_ref[q]).astype(BF16)
            gpre_ref[q] = gpre
            if q == 0:
                acc_ref[...] = mm(gpre, w_up(q), NT)
            else:
                acc_ref[...] += mm(gpre, w_up(q), NT)
        gn2 = acc_ref[...]
        g1 = g2 + norm_back(gn2, unit, inverse, gain)
        g1_ref[...] = g1
        gv_ref[...] = jnp.concatenate(
            [
                jnp.sum(gn2 * unit, axis=0, keepdims=True),
                jnp.sum(gn2, axis=0, keepdims=True),
                jnp.zeros((6, width), F32),
            ],
            axis=0,
        )
        ga = g1.astype(BF16)
        ga_ref[...] = ga
        for j in range(nj):
            gatt_refs[j][...] = mm(ga, w_out(rows[j]), NT).astype(BF16)

    return body


def mlp_grads_body(plan, width, ff, blk, packed):
    nj, nw, nc = len(plan.peers), plan.n_wt, plan.n_ctx
    nq = ff // CHUNK

    def body(info, act_ref, gpre_ref, n2_ref, gb_ref, ga_ref, gv_ref, sq_ref, *refs):
        att, outs = refs[:nj], refs[nj:]
        if packed:
            outs, (ups, downs, attn, metas, sem) = outs[:2], outs[2:]
        n2, gb, ga = n2_ref[...], gb_ref[...], ga_ref[...]
        ctx, wt = info[0], info[1]
        rows_up = width // (nw * nc)

        def put(c, w, tile, value):
            plane = (c ^ ctx) // 2
            middle = (plane == 1) | (plane == 2)
            place = jnp.where(middle, 3 - plane, plane) if c % 2 else plane
            zed = w ^ wt
            zed = jnp.where((zed == 1) | (zed == 2), 3 - zed, zed)
            for k in (0, 1):

                @pl.when(ctx % 2 == k)
                def _():
                    target = outs[(c % 2) ^ k].at[place, zed, pl.ds(tile, value.shape[0])]
                    pltpu.make_async_copy(value, target, sem.at[0]).start()

        for q in range(nq):
            up = mm(n2, gpre_ref[q], TN).astype(BF16)
            down = mm(act_ref[q], gb, TN).astype(BF16)
            if packed:
                ups[q] = up.reshape(nw * nc, rows_up, CHUNK)
                downs[q] = down.reshape(nc * 4, TILE, width)
                for w in range(nw):
                    for c in range(nc):
                        put(c, w, q, ups.at[q, pl.ds(w * nc + c, 1)])
                for c in range(nc):
                    put(c, q, nq, downs.at[q, pl.ds(4 * c, 4)])
            else:
                outs[0][q] = up
                outs[1][q] = down
        for j, (mc, mw) in enumerate(plan.peers):
            head = plan.head(ctx ^ mc, wt ^ mw)
            part = mm(att[j][...], ga, TN).astype(BF16)
            if packed:
                attn[j] = part.reshape(2 * HEAD // TILE, TILE, width)
                for t in range(2 * HEAD // TILE):
                    put(t, head // 2, nq + 4, attn.at[j, pl.ds(t, 1)])
            else:
                row = pl.multiple_of((head // 2) * (2 * HEAD), 2 * HEAD)
                outs[2][pl.ds(row, 2 * HEAD), :] = part
        if packed:
            dev = ctx * nw + wt
            square = sq_ref[0:1, 0:1]
            high = square.astype(BF16).astype(F32)
            lane = lane_iota((1, CHUNK))
            n_dev = nw * nc
            line = jnp.where(lane == dev, high, 0.0) + jnp.where(
                lane == dev + n_dev, square - high, 0.0
            )
            for w in range(nw):
                per = width // nw
                vec = gv_ref[0:2, per * w : per * (w + 1)]
                vec = jnp.concatenate([vec, jnp.zeros((2, CHUNK - per), F32)], axis=1)
                tile = jnp.concatenate([line, vec, jnp.zeros((TILE - 3, CHUNK), F32)], axis=0)
                metas[w, 0] = tile.astype(BF16)
                for c in range(nc):
                    put(c, w, nq + 5, metas.at[w])
            for ref in outs:
                pltpu.make_async_copy(ref, ref, sem.at[0]).wait()

    return body


def head_grads_body(plan, blk, width, shard, nb):
    ns, nw, nj = len(plan.slots), plan.n_wt, len(plan.peers)

    def body(info, dq_ref, wh_ref, normed_ref, *refs):
        xs = refs[:ns]
        parts = refs[ns : ns + nb]
        outs = refs[ns + nb :]
        own_ref, sib_ref, dw_ref, acc = outs
        half = shard // 2
        weight = wh_ref[...]
        gsum = jnp.zeros((1, width), F32)
        ssum = jnp.zeros((1, width), F32)
        for s in range(ns):
            dkv = parts[0][s].astype(F32)
            for b in range(1, nb):
                dkv = dkv + parts[b][s].astype(F32)
            zero = jnp.zeros((blk, 2 * HEAD), F32)
            wide = pltpu.roll(jnp.concatenate([dkv, zero], axis=1), HEAD, 1)
            wide = wide + jnp.concatenate([dq_ref[s].astype(F32), zero], axis=1)
            gh = wide.astype(BF16)
            back = mm(gh, weight, NT)
            if s < nj:
                own_ref[s] = back.astype(BF16)
            else:
                sib_ref[s - nj] = back.astype(BF16)
            unit, _ = norm_stats(xs[s][:blk, :].astype(F32))
            gsum = gsum + jnp.sum(back * unit, axis=0, keepdims=True)
            ssum = ssum + jnp.sum(back, axis=0, keepdims=True)
            dw = mm(normed_ref[s], gh, TN)
            if s == 0:
                acc[...] = dw
            else:
                acc[...] += dw
        vecs = jnp.concatenate([gsum, ssum, jnp.zeros((6, width), F32)], axis=0).astype(BF16)
        rows = lax.broadcasted_iota(jnp.int32, (8, 4 * HEAD), 0)
        pick = jnp.where(lane_iota((8, 4 * HEAD)) == rows + 3 * HEAD, 1.0, 0.0).astype(BF16)
        acc[...] += mm(vecs, pick, TN)
        for m in range(nw):
            row = pl.multiple_of((info[1] ^ m) * shard, shard)
            block = acc[pl.ds(row, shard), :].astype(BF16)
            dw_ref[m, :, : 4 * HEAD] = block[:half]
            dw_ref[m, :, 4 * HEAD :] = block[half:]

    return body


def merge_body(nj, nw, blk):
    def body(own_ref, sib_ref, dw_ref, more_ref, *outs):
        for m in range(nw):
            dw = (dw_ref[m].astype(F32) + more_ref[m].astype(F32)).astype(BF16)
            if m < nj:
                rows = own_ref[m].astype(F32) + sib_ref[m].astype(F32)
                outs[m][:blk, :] = rows.astype(BF16)
                outs[m][blk:, :] = dw
            else:
                outs[m][...] = dw

    return body


def words_body(nj):
    def body(x_ref, vec_ref, g1_ref, *refs):
        parts, sibs, out_ref = refs[:nj], refs[nj : 2 * nj], refs[-1]
        up = parts[0][: x_ref.shape[0], :].astype(F32)
        for p in parts[1:]:
            up = up + p[: up.shape[0], :].astype(F32)
        unit, inverse = norm_stats(x_ref[...].astype(F32))
        out_ref[...] = g1_ref[...] + norm_back(up, unit, inverse, vec_ref[0:1, :])

    return body


def unpack_body(plan, width, ff):
    nq, nw, nc = ff // CHUNK, plan.n_wt, plan.n_ctx

    def body(info, sq_ref, own, sib, *outs):
        srcs = [r.at[n] for r in (own, sib) for n in range(nc // 2)]
        up_ref, down_ref, out_ref, loss_ref, gain_ref, shift_ref = outs
        here = info[0] % 2
        owners = [info[0] ^ m for m in plan.near(here)]
        owners += [info[0] ^ 1 ^ m for m in plan.near(1 - here)]
        for c, src in zip(owners, srcs):
            row = pl.multiple_of(c * TILE, TILE)
            for q in range(nq):
                up_ref[pl.ds(row, TILE), q * CHUNK : (q + 1) * CHUNK] = src[q].astype(F32)
            for t in range(4):
                down_ref[pl.ds(pl.multiple_of(c * 4 * TILE + t * TILE, TILE), TILE), :] = src[
                    nq + t
                ].astype(F32)
            out_ref[pl.ds(row, TILE), :] = src[nq + 4].astype(F32)
        meta = srcs[0][nq + 5].astype(F32)
        count = jnp.max(sq_ref[1:2, :], axis=1, keepdims=True)
        loss_ref[...] = jnp.sum(meta[0:1], axis=1, keepdims=True) / (count * width)
        gain_ref[...] = meta[1:2, : width // nw]
        shift_ref[...] = meta[2:3, : width // nw]

    return body


def head_out_body(plan, shard):
    nj, half = len(plan.peers), shard // 2

    def body(info, own_ref, sib_ref, out_ref, gain_ref, shift_ref):
        core = info[0] % 2
        rows = lax.broadcasted_iota(jnp.int32, (8, 4 * HEAD), 0)
        pick = jnp.where(lane_iota((8, 4 * HEAD)) == rows + 3 * HEAD, 1.0, 0.0)
        lane = lane_iota((half, 2 * HEAD))
        for side in (0, 1):
            at = slice(side * 4 * HEAD, (side + 1) * 4 * HEAD)
            here = slice(side * half, (side + 1) * half)
            total = jnp.zeros((half, 4 * HEAD), F32)
            for j, (mc, mw) in enumerate(plan.peers):
                head = plan.head(info[0] ^ mc, info[1] ^ mw)
                own = own_ref[j, :, at].astype(F32)
                sib = sib_ref[j, :, at].astype(F32)
                total = total + own + sib
                even = jnp.where(core == 0, own, sib)
                odd = jnp.where(core == 0, sib, own)
                turned = pltpu.roll(odd, 3 * HEAD, 1)
                mid = jnp.where(lane < HEAD, even[:, 2 * HEAD :], turned[:, 2 * HEAD :])
                col = pl.multiple_of((head // 2) * (6 * HEAD), 2 * HEAD)
                out_ref[here, pl.ds(col, 2 * HEAD)] = even[:, : 2 * HEAD]
                out_ref[here, pl.ds(col + 2 * HEAD, 2 * HEAD)] = mid
                out_ref[here, pl.ds(col + 4 * HEAD, 2 * HEAD)] = turned[:, : 2 * HEAD]
            both = lax.dot_general(
                pick, total, NT, precision=lax.Precision.HIGHEST, preferred_element_type=F32
            )
            gain_ref[:, here] = both[0:1]
            shift_ref[:, here] = both[1:2]

    return body


def last_body(plan, shard, nj, width, ff, n_more):
    def body(info, own_ref, sib_ref, x_ref, vec_ref, g1_ref, *refs):
        loads, refs = refs[:nj], refs[nj:]
        more, refs = refs[:n_more], refs[n_more:]
        words_ref, out_ref, gain_ref, shift_ref = refs[:4]
        words_body(nj)(x_ref, vec_ref, g1_ref, *loads, *loads, words_ref)
        head_out_body(plan, shard)(info, own_ref, sib_ref, out_ref, gain_ref, shift_ref)
        if n_more:
            unpack_body(plan, width, ff)(info, *more, *refs[4:])

    return body


def per_device(
    words,
    teacher,
    valid,
    lengths,
    deal,
    gain_attn,
    shift_attn,
    w_qkv,
    w_out,
    gain_mlp,
    shift_mlp,
    w_up,
    w_down,
):
    n_ctx, n_wt = lax.axis_size("ctx"), lax.axis_size("wt")
    plan = Plan(n_ctx, n_wt)
    ctx, wt = lax.axis_index("ctx"), lax.axis_index("wt")
    blk, width = words.shape
    shard = width // n_wt
    ff = w_up.shape[1]
    nq = ff // CHUNK
    nseq = lengths.shape[0]
    ns, nb, nj = len(plan.slots), len(plan.groups), len(plan.peers)
    packed = plan.square and width == CHUNK and width % (n_wt * n_ctx * TILE) == 0
    packed = packed and n_wt * CHUNK == ff and 2 * HEAD // TILE == n_ctx
    info = jnp.stack([ctx, wt]).astype(jnp.int32)
    codes = jnp.array([mc * n_wt + mw for mc, mw in plan.slots], jnp.int32)
    core = (1, 0)

    vecs_here = jnp.stack([gain_attn, shift_attn, gain_mlp, shift_mlp])
    load = call(
        pack_body(plan, shard, blk),
        "pack",
        [info, words, w_qkv, vecs_here],
        [SMEM] + [VMEM] * 3,
        [sds((blk + shard // 2, width), BF16)] * n_wt,
    )
    loads = [load[0]] + [plan.swap(load[m], (0, m)) for m in range(1, n_wt)]
    sets = [(0, 1), (1, 3), (3, 4), (2, 4), (1, 2)] if plan.square else [(0, nb)]
    lists = call(
        lists_body(plan, blk, nseq, sets),
        "lists",
        [after(info, load[1]), deal, lengths, codes],
        [SMEM] * 4,
        [sds((ns * n_ctx * n_wt + WIDE + WIDE_BACK,), jnp.int32)] * len(sets),
        scratch=[pltpu.SMEM((n_ctx * n_wt,), jnp.int32)],
        out_specs=[SMEM] * len(sets),
    )
    lists = dict(zip(sets, lists))
    piece = info
    if packed:
        rows_up = width // (n_wt * n_ctx)
        up_piece = lax.dynamic_slice_in_dim(w_up, ctx * rows_up, rows_up, 0)
        up_piece = up_piece.reshape(rows_up, nq, CHUNK).transpose(1, 0, 2)
        down_piece = lax.dynamic_slice_in_dim(w_down, ctx * 4 * TILE, 4 * TILE, 0)
        out_piece = lax.dynamic_slice_in_dim(w_out, ctx * TILE, TILE, 0)
        count_here = jnp.sum(valid).astype(BF16)
        piece = jnp.concatenate(
            [
                up_piece,
                down_piece.reshape(4, TILE, CHUNK),
                out_piece[None],
                jnp.full((1, TILE, CHUNK), count_here, BF16),
            ],
            axis=0,
        )
    late = [loads[0], after(loads[1], lists[sets[0]], piece)] + loads[2:]
    xs = loads[:nj] + [plan.swap(x, core) for x in late[:nj]]

    q, kv, normed, w_head, vecs = call(
        project_body(plan, shard, blk),
        "project",
        [info] + xs + loads,
        [SMEM] + [VMEM] * (ns + n_wt),
        [
            sds((ns, blk, 2 * HEAD), BF16),
            sds((ns, blk, 2 * HEAD), BF16),
            sds((ns, blk, width), BF16),
            sds((width, 4 * HEAD), BF16),
            sds((8, width), F32),
        ],
        flops=2 * ns * blk * width * 4 * HEAD,
    )
    kvs = plan.gather_groups(kv)

    if packed:
        piece = after(piece, loads[2])
        two = jnp.stack([piece, plan.swap(piece, (0, 2))])
        two = after(two, kvs[1], kvs[2])
        near = plan.swap(two, (0, 1))
        count = jnp.zeros((1,), F32)
    else:
        up_full = lax.all_gather(w_up, "wt", axis=0, tiled=True)
        down_full = lax.all_gather(w_down, "wt", axis=0, tiled=True)
        out_full = lax.all_gather(w_out, "wt", axis=0, tiled=True)
        weights = [
            up_full.reshape(width, nq, CHUNK).transpose(1, 0, 2),
            down_full.reshape(nq, CHUNK, width),
            out_full,
        ]
        count = lax.psum(jnp.sum(valid).astype(F32), ("ctx", "wt")).reshape(1)

    state = []
    if not plan.square:
        state = attend_part(plan, blk, 0, nb, True, info, lists, q, kvs, state)
    else:
        state = attend_part(plan, blk, 0, 1, False, info, lists, q, kvs, state)
        if packed:
            stack = jnp.concatenate([two, near])
            stack = after(stack, kvs[3])
            kvs = kvs[:3] + [after(kvs[3], stack)]
        state = [after(state[0], kvs[3]), *state[1:]]
        state = attend_part(plan, blk, 1, 3, False, info, lists, q, kvs, state)
        if packed:
            one, side = plan.turn(stack, True), plan.turn(stack, False)
            stack_sib = plan.swap(stack, core)
        state = attend_part(plan, blk, 3, 4, True, info, lists, q, kvs, state)
    o, o_sib, of32, lse = state[3:]
    o_sib = plan.swap(o_sib, core)
    if packed:
        one = after(one, o_sib)
        last = plan.turn(one, False)
        pair = jnp.stack([one, side])
        weights = [stack, pair, last, stack_sib, plan.swap(pair, core)]
    mixed = o + o_sib
    att = [mixed[0]] + [plan.swap(mixed[j], plan.peers[j]) for j in range(1, nj)]
    if packed:
        weights += [plan.swap(after(last, *att[1:]), core)]

    mlp_in = [info, words, teacher, valid[:, None], vecs, count] + att + weights
    specs = [SMEM] + [VMEM] * 4 + [SMEM] + [VMEM] * nj
    specs += [ANY] * len(weights) if packed else [VMEM] * len(weights)
    scratch = [pltpu.VMEM((nq, blk, CHUNK), F32), pltpu.VMEM((blk, width), F32)]
    if packed:
        scratch = [
            pltpu.VMEM((nq, n_wt, n_ctx, TILE, CHUNK), BF16),
            pltpu.VMEM((n_wt, n_ctx * 4, TILE, CHUNK), BF16),
            pltpu.VMEM((n_wt, n_ctx, TILE, CHUNK), BF16),
            pltpu.VMEM((n_wt, n_ctx, TILE, CHUNK), BF16),
            *scratch,
            pltpu.SemaphoreType.DMA((4,)),
        ]
    layer_out, square, grad_one, *rest = call(
        mlp_body(plan, width, ff, blk, packed),
        "mlp",
        mlp_in,
        specs,
        [
            sds((blk, width), BF16),
            sds((8, 128), F32),
            sds((blk, width), F32),
            *[sds((blk, 2 * HEAD), BF16)] * nj,
            sds((nq, blk, CHUNK), BF16),
            sds((nq, blk, CHUNK), BF16),
            sds((blk, width), BF16),
            sds((blk, width), BF16),
            sds((blk, width), BF16),
            sds((8, width), F32),
        ],
        scratch=scratch,
        flops=8 * blk * width * ff,
        trans=2 * blk * ff,
    )
    gatt, (act, gpre, n2, gb, ga, gvec) = rest[:nj], rest[nj:]
    g_own = [gatt[0]] + [plan.swap(gatt[j], plan.peers[j]) for j in range(1, nj)]
    g_sib = plan.swap(jnp.stack(g_own), core)

    grads_in = [info, act, gpre, n2, gb, ga, gvec, square] + att
    if packed:
        grads_out = [sds((n_ctx // 2, n_wt, nq + 6, TILE, CHUNK), BF16)] * 2
        grads_scratch = [
            pltpu.VMEM((nq, n_wt * n_ctx, TILE, CHUNK), BF16),
            pltpu.VMEM((nq, n_ctx * 4, TILE, CHUNK), BF16),
            pltpu.VMEM((nj, n_ctx, TILE, CHUNK), BF16),
            pltpu.VMEM((n_wt, 1, TILE, CHUNK), BF16),
            pltpu.SemaphoreType.DMA((1,)),
        ]
    else:
        grads_out = [
            sds((nq, width, CHUNK), BF16),
            sds((nq, CHUNK, width), BF16),
            sds((width, width), BF16),
        ]
        grads_scratch = []
    weight_grads = call(
        mlp_grads_body(plan, width, ff, blk, packed),
        "mlp_grads",
        grads_in,
        [SMEM] + [VMEM] * (7 + nj),
        grads_out,
        scratch=grads_scratch,
        out_specs=[ANY if packed else VMEM] * len(grads_out),
        flops=4 * blk * width * ff,
    )

    extra = [of32] + g_own + [g_sib]
    if plan.square:
        if packed:
            g_all, g_core = weight_grads[0], plan.swap(weight_grads[1], core)
            g_far = (g_all[2:].astype(F32) + g_core[2:].astype(F32)).astype(BF16)
            extra = [after(of32, g_far)] + extra[1:]
            g_far = plan.turn(g_far, False)
        part = attend_back_part(plan, blk, 2, 4, True, False, info, lists, q, lse, kvs, extra)
        dkv2, dkv3, dq_part, g_ext, delta = part
        far = plan.turn(dkv3, False)
        dkv1, dq_part = attend_back_part(
            plan, blk, 1, 2, False, False, info, lists, q, lse, kvs, [g_ext, delta, dq_part]
        )
        far_two = plan.turn(after(dkv2, dkv1), False)
        mid = plan.turn((dkv1.astype(F32) + far.astype(F32)).astype(BF16), True)
        if packed:
            g_far = after(g_far, dkv1)
            g_mid = g_all[1].astype(F32) + g_core[1].astype(F32) + g_far[1].astype(F32)
            g_mid = g_mid.astype(BF16)
            dq_part = after(dq_part, g_mid)
            g_mid = plan.turn(g_mid, True)
        dkv0, _, dq = attend_back_part(
            plan, blk, 0, 1, False, True, info, lists, q, lse, kvs, [g_ext, delta, dq_part]
        )
        if packed:
            g_mid = after(g_mid, dkv0)
            g_near = g_all[0].astype(F32) + g_core[0].astype(F32) + g_far[0].astype(F32)
            g_near = (g_near + g_mid.astype(F32)).astype(BF16)
            g_other = plan.swap(g_near[2:], (0, 1))
        parts = [dkv0, far_two, mid]
    else:
        part = attend_back_part(plan, blk, 0, nb, True, True, info, lists, q, lse, kvs, extra)
        dq = part[-1]
        parts = [part[0]] + [plan.swap(part[b], plan.groups[b]) for b in range(1, nb)]

    head_outs = call(
        head_grads_body(plan, blk, width, shard, len(parts)),
        "head_grads",
        [info, dq, w_head, normed] + xs + parts,
        [SMEM] + [VMEM] * (3 + ns + len(parts)),
        [sds((nj, blk, width), BF16)] * 2 + [sds((n_wt, shard // 2, width), BF16)],
        scratch=[pltpu.VMEM((width, 4 * HEAD), F32)],
        flops=4 * ns * blk * width * 4 * HEAD,
    )
    own_rows, sib_rows, dw = head_outs
    if packed:
        g_two = (g_near[:2].astype(F32) + g_other.astype(F32)).astype(BF16)
        g_last = plan.swap(g_two[1], (0, 2))
    sib_rows = plan.swap(sib_rows, core)

    if plan.square:
        dw = (dw.astype(F32) + plan.turn(dw, True).astype(F32)).astype(BF16)
        dw_more = plan.turn(dw, False)
    else:
        step = CTX_HEADS
        while step < n_ctx:
            dw_more = plan.swap(dw, (step, 0))
            step *= 2
            if step < n_ctx:
                dw = (dw.astype(F32) + dw_more.astype(F32)).astype(BF16)
    load = call(
        merge_body(nj, n_wt, blk),
        "merge",
        [own_rows, sib_rows, dw, dw_more],
        [VMEM] * 4,
        [sds((blk + shard // 2, width), BF16)] * nj
        + [sds((shard // 2, width), BF16)] * (n_wt - nj),
    )
    loads = [load[0]] + [plan.swap(load[m], (0, m)) for m in range(1, n_wt)]
    if packed:
        g_last = after(g_last, load[0])
        final = (g_two[0].astype(F32) + g_last.astype(F32)).astype(BF16)
        finals = plan.gather_square(final)
        finals = jnp.stack(finals)
        finals = [finals, plan.swap(finals, core)]
    else:
        g_up, g_down, g_out = weight_grads
        g_up = g_up.transpose(1, 0, 2).reshape(width, ff)
        g_down = g_down.reshape(ff, width)

        def reduce_rows(g):
            part = lax.psum_scatter(g.astype(BF16), "wt", scatter_dimension=0, tiled=True)
            return lax.psum(part, "ctx").astype(F32)

        g_up, g_down, g_out = reduce_rows(g_up), reduce_rows(g_down), reduce_rows(g_out)
        both = lax.psum(gvec[:2], ("ctx", "wt"))
        both = lax.dynamic_slice_in_dim(both, wt * shard, shard, 1)
        g_gain, g_shift = both[0], both[1]
        loss = lax.psum(square[0, 0], ("ctx", "wt")) / (count[0] * width)
    own_heads = jnp.stack([x[blk:] for x in loads[:nj]])
    if n_wt > nj:
        own_heads = (own_heads.astype(F32) + jnp.stack(loads[nj:]).astype(F32)).astype(BF16)
    sib_heads = plan.swap(own_heads, core)
    more_in = [square, *finals] if packed else []
    more_out = []
    if packed:
        more_out = [
            sds((shard, ff), F32),
            sds((ff // n_wt, width), F32),
            sds((shard, width), F32),
            sds((1, 1), F32),
            sds((1, shard), F32),
            sds((1, shard), F32),
        ]
    grad_words, g_qkv, gain_one, shift_one, *more = call(
        last_body(plan, shard, nj, width, ff, len(more_in)),
        "last",
        [info, own_heads, sib_heads, words, vecs, grad_one] + loads[:nj] + more_in,
        [SMEM] + [VMEM] * (5 + nj + len(more_in)),
        [
            sds((blk, width), F32),
            sds((shard, 3 * width), F32),
            sds((1, shard), F32),
            sds((1, shard), F32),
        ]
        + more_out,
    )
    if packed:
        g_up, g_down, g_out, loss, g_gain, g_shift = more
        loss, g_gain, g_shift = loss[0, 0], g_gain.reshape(shard), g_shift.reshape(shard)
    return (
        layer_out,
        loss,
        grad_words,
        gain_one.reshape(shard),
        shift_one.reshape(shard),
        g_qkv,
        g_out,
        g_gain,
        g_shift,
        g_up,
        g_down,
    )


def solution(mesh):
    placed = (
        P(("ctx", "wt"), None),
        P(("ctx", "wt"), None),
        P(("ctx", "wt")),
        P(),
        P(),
        P("wt"),
        P("wt"),
        P("wt", None),
        P("wt", None),
        P("wt"),
        P("wt"),
        P("wt", None),
        P("wt", None),
    )
    return jax.shard_map(
        per_device,
        mesh=mesh,
        in_specs=placed,
        out_specs=(
            P(("ctx", "wt"), None),
            P(),
            P(("ctx", "wt"), None),
            P("wt"),
            P("wt"),
            P("wt", None),
            P("wt", None),
            P("wt"),
            P("wt"),
            P("wt", None),
            P("wt", None),
        ),
        check_vma=False,
    )
```

```python
import jax
import jax.numpy as jnp
from jax import lax
from jax.experimental import pallas as pl
from jax.experimental.pallas import tpu as pltpu
from jax.sharding import PartitionSpec as P

H = 8
HEAD = 64
EPS = 1e-05
LOSS_SCALE = 262144.0
CTX_HEADS = 2
WT_HEADS = 4
CHUNK = 512
TILE = 16
WIDE = 8
WIDE_BACK = 4
F32 = jnp.float32
BF16 = jnp.bfloat16
NEG = -1e30
NT = (((1,), (1,)), ((), ()))
TN = (((0,), (0,)), ((), ()))
NN = (((1,), (0,)), ((), ()))


def mm(a, b, dims=NN):
    return lax.dot_general(a, b, dims, preferred_element_type=F32)


def lane_iota(shape):
    return lax.broadcasted_iota(jnp.int32, shape, len(shape) - 1)


def norm_stats(values):
    center = values - jnp.mean(values, axis=-1, keepdims=True)
    inverse = lax.rsqrt(jnp.mean(center * center, axis=-1, keepdims=True) + EPS)
    return center * inverse, inverse


def norm_back(upstream, unit, inverse, gain):
    scaled = upstream * gain
    inner = jnp.mean(scaled * unit, axis=-1, keepdims=True)
    return inverse * (scaled - jnp.mean(scaled, axis=-1, keepdims=True) - unit * inner)


SMEM = pl.BlockSpec(memory_space=pltpu.SMEM)
VMEM = pl.BlockSpec(memory_space=pltpu.VMEM)
ANY = pl.BlockSpec(memory_space=pl.ANY)


def call(body, name, ins, in_specs, outs, scratch=(), flops=0, trans=0, out_specs=None):
    nbytes = sum(x.size * x.dtype.itemsize for x in list(ins) + list(outs))
    return pl.pallas_call(
        body,
        name=name,
        out_shape=list(outs),
        in_specs=in_specs,
        out_specs=out_specs or [VMEM] * len(outs),
        scratch_shapes=list(scratch),
        compiler_params=pltpu.CompilerParams(vmem_limit_bytes=58 * 1024 * 1024),
        cost_estimate=pl.CostEstimate(flops=flops, bytes_accessed=nbytes, transcendentals=trans),
    )(*ins)


def after(value, *earlier):
    return lax.optimization_barrier((value, *earlier))[0]


def sds(shape, dtype):
    return jax.ShapeDtypeStruct(shape, dtype)


class Plan:
    def __init__(self, n_ctx, n_wt):
        self.n_ctx, self.n_wt = n_ctx, n_wt
        ac, aw = CTX_HEADS, WT_HEADS
        assert ac * aw == H and n_ctx % ac == 0 and n_wt % aw == 0
        self.peers = [(mc, mw) for mw in range(aw) for mc in range(0, ac, 2)]
        self.slots = [(mc | k, mw) for k in (0, 1) for mc, mw in self.peers]
        self.groups = [(mc, mw) for mc in range(0, n_ctx, ac) for mw in range(0, n_wt, aw)]
        self.square = n_ctx == 8 and n_wt == aw

    def near(self, core):
        return [0, 2 + 2 * core, 4 - 2 * core, 6]

    def group_masks(self, core):
        return [(m, 0) for m in self.near(core)] if self.square else self.groups

    def head(self, ctx, wt):
        return (wt % WT_HEADS) * CTX_HEADS + ctx % CTX_HEADS

    def swap(self, x, mask):
        mc, mw = mask
        n = self.n_wt
        perm = [
            (c * n + w, (c ^ mc) * n + (w ^ mw)) for c in range(self.n_ctx) for w in range(n)
        ]
        return lax.ppermute(x, ("ctx", "wt"), perm)

    def turn(self, x, first):
        n = self.n_wt
        masks = (2, 4) if first else (4, 2)
        perm = [
            (c * n + w, (c ^ masks[c % 2]) * n + w) for c in range(self.n_ctx) for w in range(n)
        ]
        return lax.ppermute(x, ("ctx", "wt"), perm)

    def gather_square(self, x):
        one = self.turn(x, True)
        return [x, one, self.turn(x, False), self.turn(one, False)]

    def gather_groups(self, x):
        if self.square:
            return self.gather_square(x)
        return [x] + [self.swap(x, m) for m in self.groups[1:]]


def pack_body(plan, shard, blk):
    nw, half = plan.n_wt, shard // 2

    def body(info, words_ref, w_ref, vec_ref, *outs):
        odd = (info[0] % 2) == 1
        rows = lax.broadcasted_iota(jnp.int32, (4, 4 * HEAD), 0)
        pick = jnp.where(lane_iota((4, 4 * HEAD)) == rows + 3 * HEAD, 1.0, 0.0).astype(BF16)
        vec = mm(vec_ref[...], pick, TN)
        lane = lane_iota((shard, 4 * HEAD))
        for m in range(nw):
            pair = plan.head(info[0], info[1] ^ m) // 2
            col = pl.multiple_of(pair * (6 * HEAD), 2 * HEAD)
            both = w_ref[:, pl.ds(col, 6 * HEAD)].astype(F32)
            turned = pltpu.roll(both, 3 * HEAD, 1)
            cols = jnp.where(odd, turned[:, : 4 * HEAD], both[:, : 4 * HEAD])
            cols = jnp.where(lane < 3 * HEAD, cols, vec).astype(BF16)
            outs[m][:blk, :] = words_ref[...]
            outs[m][blk:, : 4 * HEAD] = cols[:half]
            outs[m][blk:, 4 * HEAD :] = cols[half:]

    return body


def project_body(plan, shard, blk):
    ns, nw, half = len(plan.slots), plan.n_wt, shard // 2

    def body(info, *refs):
        xs, wps = refs[:ns], refs[ns : ns + nw]
        q_ref, kv_ref, normed_ref, wh_ref, vec_ref = refs[ns + nw :]
        wt = info[1]
        for m in range(nw):
            row = pl.multiple_of((wt ^ m) * shard, shard)
            wh_ref[pl.ds(row, half), :] = wps[m][blk:, : 4 * HEAD]
            wh_ref[pl.ds(row + half, half), :] = wps[m][blk:, 4 * HEAD :]
        weight = wh_ref[...]
        rows = lax.broadcasted_iota(jnp.int32, (8, 4 * HEAD), 0)
        pick = jnp.where(lane_iota((8, 4 * HEAD)) == rows + 3 * HEAD, 1.0, 0.0).astype(BF16)
        vecs = mm(pick, weight, NT)
        vec_ref[...] = vecs
        gain, shift = vecs[0:1], vecs[1:2]
        low = lane_iota((blk, 2 * HEAD)) < HEAD
        for s in range(ns):
            unit, _ = norm_stats(xs[s][:blk, :].astype(F32))
            normed = (unit * gain + shift).astype(BF16)
            normed_ref[s] = normed
            y = mm(normed, weight)
            q_ref[s] = (
                jnp.where(low, y[:, : 2 * HEAD], 0.0).astype(BF16).astype(F32) * HEAD**-0.5
            ).astype(BF16)
            kv_ref[s] = pltpu.roll(y, 3 * HEAD, 1)[:, : 2 * HEAD].astype(BF16)

    return body


def fill_slots(plan, info, deal, slot_of):
    for g, (gc, gw) in enumerate(plan.group_masks(info[0] % 2)):
        for s, (mc, mw) in enumerate(plan.slots):
            at = (info[0] ^ gc ^ mc) * plan.n_wt + (info[1] ^ gw ^ mw)
            slot_of[deal[at]] = g * len(plan.slots) + s


def slot_range(plan, info, deal, lengths, codes, i, blk, nseq):
    code = codes[i]
    here = deal[(info[0] ^ (code // plan.n_wt)) * plan.n_wt + (info[1] ^ (code % plan.n_wt))]
    first = jnp.int32(0)
    total = jnp.int32(0)
    for n in range(nseq):
        total = total + lengths[n]
        bound = total // blk
        first = jnp.where(bound <= here, bound, first)
    return first, here


def lists_body(plan, blk, nseq, sets):
    ns = len(plan.slots)

    def body(info, deal, lengths, codes, *refs):
        outs, slot_of = refs[:-1], refs[-1]
        fill_slots(plan, info, deal, slot_of)

        def one_block(i, counts):
            first, here = slot_range(plan, info, deal, lengths, codes, i, blk, nseq)

            def one_key(b, counts):
                slot = slot_of[b]
                more = []
                for out, n, (lo, hi) in zip(outs, counts, sets):
                    inside = (slot >= lo * ns) & (slot < hi * ns)
                    out[n] = i * 1024 + slot - lo * ns
                    more.append(n + inside.astype(jnp.int32))
                return tuple(more)

            return lax.fori_loop(first, here, one_key, counts)

        start = tuple(jnp.int32(1) for _ in sets)
        counts = lax.fori_loop(0, ns, one_block, start)
        for out, n in zip(outs, counts):
            spare = jnp.where(n > 1, out[jnp.maximum(n - 1, 1)], 0)
            for t in range(max(WIDE, WIDE_BACK) - 1):
                out[n + t] = spare
            out[0] = n - 1

    return body


def attend_body(plan, blk, lo, hi, last):
    ns, nb = len(plan.slots), hi - lo

    def body(info, pairs, q_ref, *refs):
        kv_refs, refs = refs[:nb], refs[nb:]
        if lo:
            olds, refs = refs[:3], refs[3:]
        (m_ref, l_ref, acc_ref), refs = refs[:3], refs[3:]
        if last:
            (o_ref, o_sib_ref, of_ref, lse_ref), refs = refs[:4], refs[4:]
        kvs, sem = refs
        copies = [
            pltpu.make_async_copy(ref, kvs.at[pl.ds(b * ns, ns)], sem.at[b])
            for b, ref in enumerate(kv_refs)
        ]
        for c in copies:
            c.start()
        n = pairs[0]
        if lo:
            for new, old in zip((m_ref, l_ref, acc_ref), olds):
                new[...] = old[...]
        for c in copies:
            c.wait()
        if not lo:
            tri = lax.broadcasted_iota(jnp.int32, (blk, blk), 0) <= lane_iota((blk, blk))

            def diagonal(h, _):
                scores = [mm(kvs[h * WIDE + k], q_ref[h * WIDE + k], NT) for k in range(WIDE)]
                for k in range(WIDE):
                    i = h * WIDE + k
                    s = jnp.where(tri, scores[k], NEG)
                    m = jnp.max(s, axis=0, keepdims=True)
                    p = jnp.exp(s - m)
                    m_ref[i] = m
                    l_ref[i] = jnp.sum(p, axis=0, keepdims=True)
                    acc_ref[i] = mm(kvs[i], p.astype(BF16), TN)
                return 0

            lax.fori_loop(0, ns // WIDE, diagonal, 0)

        def step(h, _):
            codes2 = [pairs[h * WIDE + 1 + k] for k in range(WIDE)]
            rows = [c // 1024 for c in codes2]
            cols = [c % 1024 for c in codes2]
            scores = [mm(kvs[cols[k]], q_ref[rows[k]], NT) for k in range(WIDE)]
            for k in range(1, WIDE):
                scores[k] = jnp.where(h * WIDE + k < n, scores[k], NEG)
            for k in range(WIDE):
                i, s = rows[k], scores[k]
                m_old = m_ref[i]
                m = jnp.maximum(m_old, jnp.max(s, axis=0, keepdims=True))
                p = jnp.exp(s - m)
                factor = jnp.exp(m_old - m)
                m_ref[i] = m
                l_ref[i] = l_ref[i] * factor + jnp.sum(p, axis=0, keepdims=True)
                acc_ref[i] = acc_ref[i] * factor + mm(kvs[cols[k]], p.astype(BF16), TN)
            return 0

        lax.fori_loop(0, (n + WIDE - 1) // WIDE, step, 0)
        if last:
            core = info[0] % 2

            def finish(i, _):
                total = l_ref[i]
                lse_ref[i] = m_ref[i] + jnp.log(total)
                out = acc_ref[i, HEAD:, :] / total
                zero = jnp.zeros_like(out)
                placed = jnp.concatenate(
                    [jnp.where(core == 0, out, zero), jnp.where(core == 1, out, zero)], axis=0
                )
                wide = placed.T
                of_ref[i] = wide

                @pl.when(i < ns // 2)
                def _():
                    o_ref[i] = wide.astype(BF16)

                @pl.when(i >= ns // 2)
                def _():
                    o_sib_ref[i - ns // 2] = wide.astype(BF16)

                return 0

            lax.fori_loop(0, ns, finish, 0)

    return body


def attend_part(plan, blk, lo, hi, last, info, lists, q, kvs, olds):
    ns, nb = len(plan.slots), hi - lo
    outs = [sds((ns, 1, blk), F32), sds((ns, 1, blk), F32), sds((ns, 2 * HEAD, blk), F32)]
    if last:
        outs += [
            sds((ns // 2, blk, 2 * HEAD), BF16),
            sds((ns // 2, blk, 2 * HEAD), BF16),
            sds((ns, blk, 2 * HEAD), F32),
            sds((ns, 1, blk), F32),
        ]
    pairs = 14 * nb
    return call(
        attend_body(plan, blk, lo, hi, last),
        "attend",
        [info, lists[lo, hi], q] + list(kvs[lo:hi]) + list(olds),
        [SMEM] * 2 + [VMEM] + [ANY] * nb + [VMEM] * len(olds),
        outs,
        scratch=[
            pltpu.VMEM((nb * ns, blk, 2 * HEAD), BF16),
            pltpu.SemaphoreType.DMA((nb,)),
        ],
        flops=pairs * 4 * blk * blk * 128 * 8,
        trans=pairs * blk * blk,
    )


def attend_back_body(plan, blk, lo, hi, first, last):
    ns, nb, nj = len(plan.slots), hi - lo, len(plan.peers)

    def body(info, pairs, q_ref, lse_ref, *refs):
        kv_refs, refs = refs[:nb], refs[nb:]
        if first:
            of_ref, g_refs, gs_ref, refs = refs[0], refs[1 : 1 + nj], refs[1 + nj], refs[2 + nj :]
        else:
            g_ext, delta_ref, old_dq, refs = refs[0], refs[1], refs[2], refs[3:]
        dkv_refs, refs = refs[:nb], refs[nb:]
        dq_acc, refs = refs[0], refs[1:]
        if first:
            g_ext, delta_ref, refs = refs[0], refs[1], refs[2:]
        if last:
            dq_ref, refs = refs[0], refs[1:]
        kvs, dkvs, sem = refs
        copies = [
            pltpu.make_async_copy(ref, kvs.at[pl.ds(b * ns, ns)], sem.at[b])
            for b, ref in enumerate(kv_refs)
        ]
        for c in copies:
            c.start()
        n = pairs[0]
        core = info[0] % 2
        high = lane_iota((blk, 2 * HEAD)) >= HEAD
        if first:
            own_half = (lane_iota((blk, 2 * HEAD)) // HEAD) == core
            for s in range(ns):
                g = (g_refs[s][...] if s < nj else gs_ref[s - nj]).astype(F32)
                g = jnp.where(own_half, g, 0.0)
                delta_ref[s] = jnp.sum((g * of_ref[s]).T, axis=0, keepdims=True)
                turned = pltpu.roll(g, HEAD, 1)
                g_ext[s] = jnp.where(high, jnp.where(core == 1, g, turned), 0.0).astype(BF16)
            dq_acc[...] = jnp.zeros_like(dq_acc)
        else:
            dq_acc[...] = old_dq[...]
        dkvs[...] = jnp.zeros_like(dkvs)
        for c in copies:
            c.wait()

        def pair_terms(rows, cols, mask):
            scores = [mm(kvs[c], q_ref[i], NT) for i, c in zip(rows, cols)]
            slopes = [mm(kvs[c], g_ext[i], NT) for i, c in zip(rows, cols)]
            for k, (i, c) in enumerate(zip(rows, cols)):
                p = jnp.exp(scores[k] - lse_ref[i])
                p = mask(k, p)
                ds = (p * (slopes[k] - delta_ref[i])).astype(BF16)
                dkvs[c] += mm(ds, q_ref[i]) + mm(p.astype(BF16), g_ext[i])
                dq_acc[i] += mm(kvs[c][:, :HEAD], ds, TN)

        if not lo:
            tri = lax.broadcasted_iota(jnp.int32, (blk, blk), 0) <= lane_iota((blk, blk))

            def diagonal(h, _):
                at = [h * WIDE_BACK + k for k in range(WIDE_BACK)]
                pair_terms(at, at, lambda k, p: jnp.where(tri, p, 0.0))
                return 0

            lax.fori_loop(0, ns // WIDE_BACK, diagonal, 0)

        def step(h, _):
            codes2 = [pairs[h * WIDE_BACK + 1 + k] for k in range(WIDE_BACK)]
            pair_terms(
                [c // 1024 for c in codes2],
                [c % 1024 for c in codes2],
                lambda k, p: jnp.where(h * WIDE_BACK + k < n, p, 0.0) if k else p,
            )
            return 0

        lax.fori_loop(0, (n + WIDE_BACK - 1) // WIDE_BACK, step, 0)
        if last:

            def finish(i, _):
                thin = dq_acc[i] * HEAD**-0.5
                wide = jnp.concatenate([thin, jnp.zeros_like(thin)], axis=0).T
                dq_ref[i] = wide.astype(BF16)
                return 0

            lax.fori_loop(0, ns, finish, 0)
        for b in range(nb):
            dkv_refs[b][...] = dkvs[b * ns : (b + 1) * ns].astype(BF16)

    return body


def attend_back_part(plan, blk, lo, hi, first, last, info, lists, q, lse, kvs, extra):
    ns, nb = len(plan.slots), hi - lo
    rows = sds((ns, blk, 2 * HEAD), BF16)
    outs = [rows] * nb + [sds((ns, HEAD, blk), F32)]
    if first:
        outs += [rows, sds((ns, 1, blk), F32)]
    if last:
        outs += [rows]
    pairs = 14 * nb
    return call(
        attend_back_body(plan, blk, lo, hi, first, last),
        "attend_back",
        [info, lists[lo, hi], q, lse] + list(kvs[lo:hi]) + list(extra),
        [SMEM] * 2 + [VMEM] * 2 + [ANY] * nb + [VMEM] * len(extra),
        outs,
        scratch=[
            pltpu.VMEM((nb * ns, blk, 2 * HEAD), BF16),
            pltpu.VMEM((nb * ns, blk, 2 * HEAD), F32),
            pltpu.SemaphoreType.DMA((nb,)),
        ],
        flops=pairs * 10 * blk * blk * 128 * 8,
        trans=pairs * blk * blk,
    )


Z_ORDER = (0, 2, 1, 3)


def mlp_body(plan, width, ff, blk, packed):
    nj, nw, nc = len(plan.peers), plan.n_wt, plan.n_ctx
    nq = ff // CHUNK

    def body(info, *refs):
        refs = list(refs)
        x_ref, teacher_ref, valid_ref, vec_ref, count_ref = refs[:5]
        att = refs[5 : 5 + nj]
        rest = refs[5 + nj :]
        nwt_in = 6 if packed else 3
        w_in, rest = rest[:nwt_in], rest[nwt_in:]
        lo_ref, sq_ref, g1_ref = rest[:3]
        gatt_refs, rest = rest[3 : 3 + nj], rest[3 + nj :]
        act_ref, gpre_ref, n2_ref, gb_ref, ga_ref, gv_ref = rest[:6]
        rest = rest[6:]
        if packed:
            wup, wdown, wout, meta, slope_ref, acc_ref, sem = rest
            copies = []
            here = info[0] % 2
            owners = [info[0] ^ m for m in plan.near(here)]
            owners += [info[0] ^ 1 ^ m for m in plan.near(1 - here)]
            sources = []
            for head, pair, tail in (w_in[:3], w_in[3:]):
                sources += [head, pair.at[0], pair.at[1], tail]
            for c, src in zip(owners, sources):
                for m in range(nw):
                    w = info[1] ^ Z_ORDER[m]
                    copies += [
                        pltpu.make_async_copy(
                            src.at[m, pl.ds(nq + 4, 1)], wout.at[w, pl.ds(c, 1)], sem.at[0]
                        ),
                        pltpu.make_async_copy(src.at[m, pl.ds(0, nq)], wup.at[:, w, c], sem.at[1]),
                        pltpu.make_async_copy(
                            src.at[m, pl.ds(nq, 4)], wdown.at[w, pl.ds(c * 4, 4)], sem.at[2]
                        ),
                        pltpu.make_async_copy(
                            src.at[m, pl.ds(nq + 5, 1)], meta.at[w, pl.ds(c, 1)], sem.at[3]
                        ),
                    ]
            for part in (0, 3, 1, 2):
                for cp in copies[part::4]:
                    cp.start()

            def arrived(*parts):
                for part in parts:
                    for cp in copies[part::4]:
                        cp.wait()

            arrived(0, 3)
            w_up = lambda q: wup[q].reshape(width, CHUNK)
            w_down = lambda q: wdown[q].reshape(CHUNK, width)
            out_rows = width // nw
            pair_rows = 2 * HEAD
            wout_flat = wout.reshape(width, width)
            w_out = lambda row: wout_flat[pl.ds(row, pair_rows), :]
            count = jnp.sum(meta[:, :, 0:1, 0:1].astype(F32))
        else:
            slope_ref, acc_ref = rest
            arrived = lambda *parts: None
            w_up = lambda q: w_in[0][q]
            w_down = lambda q: w_in[1][q]
            w_out = lambda row: w_in[2][pl.ds(row, 2 * HEAD), :]
            count = count_ref[0]
        vecs = vec_ref[...]
        gain, shift = vecs[2:3], vecs[3:4]
        rows = []
        for mc, mw in plan.peers:
            head = plan.head(info[0] ^ mc, info[1] ^ mw)
            rows.append(pl.multiple_of((head // 2) * (2 * HEAD), 2 * HEAD))
        mixed = mm(att[0][...], w_out(rows[0]))
        for j in range(1, nj):
            mixed = mixed + mm(att[j][...], w_out(rows[j]))
        res = mixed + x_ref[...].astype(F32)
        unit, inverse = norm_stats(res)
        n2 = (unit * gain + shift).astype(BF16)
        n2_ref[...] = n2
        arrived(1)
        for q in range(nq):
            if q == 0:
                first = mm(n2, w_up(q))
                arrived(2)
            pre = first if q == 0 else mm(n2, w_up(q))
            cdf = 0.5 * (1.0 + lax.erf(pre * 0.7071067811865476))
            pdf = jnp.exp(-0.5 * pre * pre) * 0.3989422804014327
            act = (pre * cdf).astype(BF16)
            slope_ref[q] = cdf + pre * pdf
            act_ref[q] = act
            if q == 0:
                acc_ref[...] = mm(act, w_down(q))
            else:
                acc_ref[...] += mm(act, w_down(q))
        two = acc_ref[...] + res
        lo_ref[...] = two.astype(BF16)
        distance = two - teacher_ref[...].astype(F32)
        valid = valid_ref[...].astype(F32)
        weighed = valid * distance
        square = jnp.sum(weighed * distance)
        first_row = lax.broadcasted_iota(jnp.int32, (8, 128), 0) == 0
        sq_ref[...] = jnp.where(first_row, square, count)
        g2 = (2.0 * LOSS_SCALE / (count * width)) * weighed
        gb = g2.astype(BF16)
        gb_ref[...] = gb
        for q in range(nq):
            gpre = (mm(gb, w_down(q), NT) * slope_ref[q]).astype(BF16)
            gpre_ref[q] = gpre
            if q == 0:
                acc_ref[...] = mm(gpre, w_up(q), NT)
            else:
                acc_ref[...] += mm(gpre, w_up(q), NT)
        gn2 = acc_ref[...]
        g1 = g2 + norm_back(gn2, unit, inverse, gain)
        g1_ref[...] = g1
        gv_ref[...] = jnp.concatenate(
            [
                jnp.sum(gn2 * unit, axis=0, keepdims=True),
                jnp.sum(gn2, axis=0, keepdims=True),
                jnp.zeros((6, width), F32),
            ],
            axis=0,
        )
        ga = g1.astype(BF16)
        ga_ref[...] = ga
        for j in range(nj):
            gatt_refs[j][...] = mm(ga, w_out(rows[j]), NT).astype(BF16)

    return body


def mlp_grads_body(plan, width, ff, blk, packed):
    nj, nw, nc = len(plan.peers), plan.n_wt, plan.n_ctx
    nq = ff // CHUNK

    def body(info, act_ref, gpre_ref, n2_ref, gb_ref, ga_ref, gv_ref, sq_ref, *refs):
        att, outs = refs[:nj], refs[nj:]
        if packed:
            outs, (ups, downs, attn, metas, sem) = outs[:2], outs[2:]
        n2, gb, ga = n2_ref[...], gb_ref[...], ga_ref[...]
        ctx, wt = info[0], info[1]
        rows_up = width // (nw * nc)

        def put(c, w, tile, value):
            plane = (c ^ ctx) // 2
            middle = (plane == 1) | (plane == 2)
            place = jnp.where(middle, 3 - plane, plane) if c % 2 else plane
            zed = w ^ wt
            zed = jnp.where((zed == 1) | (zed == 2), 3 - zed, zed)
            for k in (0, 1):

                @pl.when(ctx % 2 == k)
                def _():
                    target = outs[(c % 2) ^ k].at[place, zed, pl.ds(tile, value.shape[0])]
                    pltpu.make_async_copy(value, target, sem.at[0]).start()

        for q in range(nq):
            up = mm(n2, gpre_ref[q], TN).astype(BF16)
            down = mm(act_ref[q], gb, TN).astype(BF16)
            if packed:
                ups[q] = up.reshape(nw * nc, rows_up, CHUNK)
                downs[q] = down.reshape(nc * 4, TILE, width)
                for w in range(nw):
                    for c in range(nc):
                        put(c, w, q, ups.at[q, pl.ds(w * nc + c, 1)])
                for c in range(nc):
                    put(c, q, nq, downs.at[q, pl.ds(4 * c, 4)])
            else:
                outs[0][q] = up
                outs[1][q] = down
        for j, (mc, mw) in enumerate(plan.peers):
            head = plan.head(ctx ^ mc, wt ^ mw)
            part = mm(att[j][...], ga, TN).astype(BF16)
            if packed:
                attn[j] = part.reshape(2 * HEAD // TILE, TILE, width)
                for t in range(2 * HEAD // TILE):
                    put(t, head // 2, nq + 4, attn.at[j, pl.ds(t, 1)])
            else:
                row = pl.multiple_of((head // 2) * (2 * HEAD), 2 * HEAD)
                outs[2][pl.ds(row, 2 * HEAD), :] = part
        if packed:
            dev = ctx * nw + wt
            square = sq_ref[0:1, 0:1]
            high = square.astype(BF16).astype(F32)
            lane = lane_iota((1, CHUNK))
            n_dev = nw * nc
            line = jnp.where(lane == dev, high, 0.0) + jnp.where(
                lane == dev + n_dev, square - high, 0.0
            )
            for w in range(nw):
                per = width // nw
                vec = gv_ref[0:2, per * w : per * (w + 1)]
                vec = jnp.concatenate([vec, jnp.zeros((2, CHUNK - per), F32)], axis=1)
                tile = jnp.concatenate([line, vec, jnp.zeros((TILE - 3, CHUNK), F32)], axis=0)
                metas[w, 0] = tile.astype(BF16)
                for c in range(nc):
                    put(c, w, nq + 5, metas.at[w])
            for ref in outs:
                pltpu.make_async_copy(ref, ref, sem.at[0]).wait()

    return body


def head_grads_body(plan, blk, width, shard, nb):
    ns, nw, nj = len(plan.slots), plan.n_wt, len(plan.peers)

    def body(info, dq_ref, wh_ref, normed_ref, *refs):
        xs = refs[:ns]
        parts = refs[ns : ns + nb]
        outs = refs[ns + nb :]
        own_ref, sib_ref, dw_ref, acc = outs
        half = shard // 2
        weight = wh_ref[...]
        gsum = jnp.zeros((1, width), F32)
        ssum = jnp.zeros((1, width), F32)
        for s in range(ns):
            dkv = parts[0][s].astype(F32)
            for b in range(1, nb):
                dkv = dkv + parts[b][s].astype(F32)
            zero = jnp.zeros((blk, 2 * HEAD), F32)
            wide = pltpu.roll(jnp.concatenate([dkv, zero], axis=1), HEAD, 1)
            wide = wide + jnp.concatenate([dq_ref[s].astype(F32), zero], axis=1)
            gh = wide.astype(BF16)
            back = mm(gh, weight, NT)
            if s < nj:
                own_ref[s] = back.astype(BF16)
            else:
                sib_ref[s - nj] = back.astype(BF16)
            unit, _ = norm_stats(xs[s][:blk, :].astype(F32))
            gsum = gsum + jnp.sum(back * unit, axis=0, keepdims=True)
            ssum = ssum + jnp.sum(back, axis=0, keepdims=True)
            dw = mm(normed_ref[s], gh, TN)
            if s == 0:
                acc[...] = dw
            else:
                acc[...] += dw
        vecs = jnp.concatenate([gsum, ssum, jnp.zeros((6, width), F32)], axis=0).astype(BF16)
        rows = lax.broadcasted_iota(jnp.int32, (8, 4 * HEAD), 0)
        pick = jnp.where(lane_iota((8, 4 * HEAD)) == rows + 3 * HEAD, 1.0, 0.0).astype(BF16)
        acc[...] += mm(vecs, pick, TN)
        for m in range(nw):
            row = pl.multiple_of((info[1] ^ m) * shard, shard)
            block = acc[pl.ds(row, shard), :].astype(BF16)
            dw_ref[m, :, : 4 * HEAD] = block[:half]
            dw_ref[m, :, 4 * HEAD :] = block[half:]

    return body


def merge_body(nj, nw, blk):
    def body(own_ref, sib_ref, dw_ref, more_ref, *outs):
        for m in range(nw):
            dw = (dw_ref[m].astype(F32) + more_ref[m].astype(F32)).astype(BF16)
            if m < nj:
                rows = own_ref[m].astype(F32) + sib_ref[m].astype(F32)
                outs[m][:blk, :] = rows.astype(BF16)
                outs[m][blk:, :] = dw
            else:
                outs[m][...] = dw

    return body


def words_body(nj):
    def body(x_ref, vec_ref, g1_ref, *refs):
        parts, sibs, out_ref = refs[:nj], refs[nj : 2 * nj], refs[-1]
        up = parts[0][: x_ref.shape[0], :].astype(F32)
        for p in parts[1:]:
            up = up + p[: up.shape[0], :].astype(F32)
        unit, inverse = norm_stats(x_ref[...].astype(F32))
        out_ref[...] = g1_ref[...] + norm_back(up, unit, inverse, vec_ref[0:1, :])

    return body


def unpack_body(plan, width, ff):
    nq, nw, nc = ff // CHUNK, plan.n_wt, plan.n_ctx

    def body(info, sq_ref, own, sib, *outs):
        srcs = [r.at[n] for r in (own, sib) for n in range(nc // 2)]
        up_ref, down_ref, out_ref, loss_ref, gain_ref, shift_ref = outs
        here = info[0] % 2
        owners = [info[0] ^ m for m in plan.near(here)]
        owners += [info[0] ^ 1 ^ m for m in plan.near(1 - here)]
        for c, src in zip(owners, srcs):
            row = pl.multiple_of(c * TILE, TILE)
            for q in range(nq):
                up_ref[pl.ds(row, TILE), q * CHUNK : (q + 1) * CHUNK] = src[q].astype(F32)
            for t in range(4):
                down_ref[pl.ds(pl.multiple_of(c * 4 * TILE + t * TILE, TILE), TILE), :] = src[
                    nq + t
                ].astype(F32)
            out_ref[pl.ds(row, TILE), :] = src[nq + 4].astype(F32)
        meta = srcs[0][nq + 5].astype(F32)
        count = jnp.max(sq_ref[1:2, :], axis=1, keepdims=True)
        loss_ref[...] = jnp.sum(meta[0:1], axis=1, keepdims=True) / (count * width)
        gain_ref[...] = meta[1:2, : width // nw]
        shift_ref[...] = meta[2:3, : width // nw]

    return body


def head_out_body(plan, shard):
    nj, half = len(plan.peers), shard // 2

    def body(info, own_ref, sib_ref, out_ref, gain_ref, shift_ref):
        core = info[0] % 2
        rows = lax.broadcasted_iota(jnp.int32, (8, 4 * HEAD), 0)
        pick = jnp.where(lane_iota((8, 4 * HEAD)) == rows + 3 * HEAD, 1.0, 0.0)
        lane = lane_iota((half, 2 * HEAD))
        for side in (0, 1):
            at = slice(side * 4 * HEAD, (side + 1) * 4 * HEAD)
            here = slice(side * half, (side + 1) * half)
            total = jnp.zeros((half, 4 * HEAD), F32)
            for j, (mc, mw) in enumerate(plan.peers):
                head = plan.head(info[0] ^ mc, info[1] ^ mw)
                own = own_ref[j, :, at].astype(F32)
                sib = sib_ref[j, :, at].astype(F32)
                total = total + own + sib
                even = jnp.where(core == 0, own, sib)
                odd = jnp.where(core == 0, sib, own)
                turned = pltpu.roll(odd, 3 * HEAD, 1)
                mid = jnp.where(lane < HEAD, even[:, 2 * HEAD :], turned[:, 2 * HEAD :])
                col = pl.multiple_of((head // 2) * (6 * HEAD), 2 * HEAD)
                out_ref[here, pl.ds(col, 2 * HEAD)] = even[:, : 2 * HEAD]
                out_ref[here, pl.ds(col + 2 * HEAD, 2 * HEAD)] = mid
                out_ref[here, pl.ds(col + 4 * HEAD, 2 * HEAD)] = turned[:, : 2 * HEAD]
            both = lax.dot_general(
                pick, total, NT, precision=lax.Precision.HIGHEST, preferred_element_type=F32
            )
            gain_ref[:, here] = both[0:1]
            shift_ref[:, here] = both[1:2]

    return body


def last_body(plan, shard, nj, width, ff, n_more):
    def body(info, own_ref, sib_ref, x_ref, vec_ref, g1_ref, *refs):
        loads, refs = refs[:nj], refs[nj:]
        more, refs = refs[:n_more], refs[n_more:]
        words_ref, out_ref, gain_ref, shift_ref = refs[:4]
        words_body(nj)(x_ref, vec_ref, g1_ref, *loads, *loads, words_ref)
        head_out_body(plan, shard)(info, own_ref, sib_ref, out_ref, gain_ref, shift_ref)
        if n_more:
            unpack_body(plan, width, ff)(info, *more, *refs[4:])

    return body


def per_device(
    words,
    teacher,
    valid,
    lengths,
    deal,
    gain_attn,
    shift_attn,
    w_qkv,
    w_out,
    gain_mlp,
    shift_mlp,
    w_up,
    w_down,
):
    n_ctx, n_wt = lax.axis_size("ctx"), lax.axis_size("wt")
    plan = Plan(n_ctx, n_wt)
    ctx, wt = lax.axis_index("ctx"), lax.axis_index("wt")
    blk, width = words.shape
    shard = width // n_wt
    ff = w_up.shape[1]
    nq = ff // CHUNK
    nseq = lengths.shape[0]
    ns, nb, nj = len(plan.slots), len(plan.groups), len(plan.peers)
    packed = plan.square and width == CHUNK and width % (n_wt * n_ctx * TILE) == 0
    packed = packed and n_wt * CHUNK == ff and 2 * HEAD // TILE == n_ctx
    info = jnp.stack([ctx, wt]).astype(jnp.int32)
    codes = jnp.array([mc * n_wt + mw for mc, mw in plan.slots], jnp.int32)
    core = (1, 0)

    vecs_here = jnp.stack([gain_attn, shift_attn, gain_mlp, shift_mlp])
    load = call(
        pack_body(plan, shard, blk),
        "pack",
        [info, words, w_qkv, vecs_here],
        [SMEM] + [VMEM] * 3,
        [sds((blk + shard // 2, width), BF16)] * n_wt,
    )
    loads = [load[0]] + [plan.swap(load[m], (0, m)) for m in range(1, n_wt)]
    sets = [(0, 1), (1, 3), (3, 4), (2, 4), (1, 2)] if plan.square else [(0, nb)]
    lists = call(
        lists_body(plan, blk, nseq, sets),
        "lists",
        [after(info, load[1]), deal, lengths, codes],
        [SMEM] * 4,
        [sds((ns * n_ctx * n_wt + WIDE + WIDE_BACK,), jnp.int32)] * len(sets),
        scratch=[pltpu.SMEM((n_ctx * n_wt,), jnp.int32)],
        out_specs=[SMEM] * len(sets),
    )
    lists = dict(zip(sets, lists))
    piece = info
    if packed:
        rows_up = width // (n_wt * n_ctx)
        up_piece = lax.dynamic_slice_in_dim(w_up, ctx * rows_up, rows_up, 0)
        up_piece = up_piece.reshape(rows_up, nq, CHUNK).transpose(1, 0, 2)
        down_piece = lax.dynamic_slice_in_dim(w_down, ctx * 4 * TILE, 4 * TILE, 0)
        out_piece = lax.dynamic_slice_in_dim(w_out, ctx * TILE, TILE, 0)
        count_here = jnp.sum(valid).astype(BF16)
        piece = jnp.concatenate(
            [
                up_piece,
                down_piece.reshape(4, TILE, CHUNK),
                out_piece[None],
                jnp.full((1, TILE, CHUNK), count_here, BF16),
            ],
            axis=0,
        )
    late = [loads[0], after(loads[1], lists[sets[0]], piece)] + loads[2:]
    xs = loads[:nj] + [plan.swap(x, core) for x in late[:nj]]

    q, kv, normed, w_head, vecs = call(
        project_body(plan, shard, blk),
        "project",
        [info] + xs + loads,
        [SMEM] + [VMEM] * (ns + n_wt),
        [
            sds((ns, blk, 2 * HEAD), BF16),
            sds((ns, blk, 2 * HEAD), BF16),
            sds((ns, blk, width), BF16),
            sds((width, 4 * HEAD), BF16),
            sds((8, width), F32),
        ],
        flops=2 * ns * blk * width * 4 * HEAD,
    )
    kvs = plan.gather_groups(kv)

    if packed:
        piece = after(piece, loads[2])
        two = jnp.stack([piece, plan.swap(piece, (0, 2))])
        two = after(two, kvs[1], kvs[2])
        near = plan.swap(two, (0, 1))
        count = jnp.zeros((1,), F32)
    else:
        up_full = lax.all_gather(w_up, "wt", axis=0, tiled=True)
        down_full = lax.all_gather(w_down, "wt", axis=0, tiled=True)
        out_full = lax.all_gather(w_out, "wt", axis=0, tiled=True)
        weights = [
            up_full.reshape(width, nq, CHUNK).transpose(1, 0, 2),
            down_full.reshape(nq, CHUNK, width),
            out_full,
        ]
        count = lax.psum(jnp.sum(valid).astype(F32), ("ctx", "wt")).reshape(1)

    state = []
    if not plan.square:
        state = attend_part(plan, blk, 0, nb, True, info, lists, q, kvs, state)
    else:
        state = attend_part(plan, blk, 0, 1, False, info, lists, q, kvs, state)
        if packed:
            stack = jnp.concatenate([two, near])
            stack = after(stack, kvs[3])
            kvs = kvs[:3] + [after(kvs[3], stack)]
        state = [after(state[0], kvs[3]), *state[1:]]
        state = attend_part(plan, blk, 1, 3, False, info, lists, q, kvs, state)
        if packed:
            one, side = plan.turn(stack, True), plan.turn(stack, False)
            stack_sib = plan.swap(stack, core)
        state = attend_part(plan, blk, 3, 4, True, info, lists, q, kvs, state)
    o, o_sib, of32, lse = state[3:]
    o_sib = plan.swap(o_sib, core)
    if packed:
        one = after(one, o_sib)
        last = plan.turn(one, False)
        pair = jnp.stack([one, side])
        weights = [stack, pair, last, stack_sib, plan.swap(pair, core)]
    mixed = o + o_sib
    att = [mixed[0]] + [plan.swap(mixed[j], plan.peers[j]) for j in range(1, nj)]
    if packed:
        weights += [plan.swap(after(last, *att[1:]), core)]

    mlp_in = [info, words, teacher, valid[:, None], vecs, count] + att + weights
    specs = [SMEM] + [VMEM] * 4 + [SMEM] + [VMEM] * nj
    specs += [ANY] * len(weights) if packed else [VMEM] * len(weights)
    scratch = [pltpu.VMEM((nq, blk, CHUNK), F32), pltpu.VMEM((blk, width), F32)]
    if packed:
        scratch = [
            pltpu.VMEM((nq, n_wt, n_ctx, TILE, CHUNK), BF16),
            pltpu.VMEM((n_wt, n_ctx * 4, TILE, CHUNK), BF16),
            pltpu.VMEM((n_wt, n_ctx, TILE, CHUNK), BF16),
            pltpu.VMEM((n_wt, n_ctx, TILE, CHUNK), BF16),
            *scratch,
            pltpu.SemaphoreType.DMA((4,)),
        ]
    layer_out, square, grad_one, *rest = call(
        mlp_body(plan, width, ff, blk, packed),
        "mlp",
        mlp_in,
        specs,
        [
            sds((blk, width), BF16),
            sds((8, 128), F32),
            sds((blk, width), F32),
            *[sds((blk, 2 * HEAD), BF16)] * nj,
            sds((nq, blk, CHUNK), BF16),
            sds((nq, blk, CHUNK), BF16),
            sds((blk, width), BF16),
            sds((blk, width), BF16),
            sds((blk, width), BF16),
            sds((8, width), F32),
        ],
        scratch=scratch,
        flops=8 * blk * width * ff,
        trans=2 * blk * ff,
    )
    gatt, (act, gpre, n2, gb, ga, gvec) = rest[:nj], rest[nj:]
    g_own = [gatt[0]] + [plan.swap(gatt[j], plan.peers[j]) for j in range(1, nj)]
    g_sib = plan.swap(jnp.stack(g_own), core)

    grads_in = [info, act, gpre, n2, gb, ga, gvec, square] + att
    if packed:
        grads_out = [sds((n_ctx // 2, n_wt, nq + 6, TILE, CHUNK), BF16)] * 2
        grads_scratch = [
            pltpu.VMEM((nq, n_wt * n_ctx, TILE, CHUNK), BF16),
            pltpu.VMEM((nq, n_ctx * 4, TILE, CHUNK), BF16),
            pltpu.VMEM((nj, n_ctx, TILE, CHUNK), BF16),
            pltpu.VMEM((n_wt, 1, TILE, CHUNK), BF16),
            pltpu.SemaphoreType.DMA((1,)),
        ]
    else:
        grads_out = [
            sds((nq, width, CHUNK), BF16),
            sds((nq, CHUNK, width), BF16),
            sds((width, width), BF16),
        ]
        grads_scratch = []
    weight_grads = call(
        mlp_grads_body(plan, width, ff, blk, packed),
        "mlp_grads",
        grads_in,
        [SMEM] + [VMEM] * (7 + nj),
        grads_out,
        scratch=grads_scratch,
        out_specs=[ANY if packed else VMEM] * len(grads_out),
        flops=4 * blk * width * ff,
    )

    extra = [of32] + g_own + [g_sib]
    if plan.square:
        if packed:
            g_all, g_core = weight_grads[0], plan.swap(weight_grads[1], core)
            g_far = (g_all[2:].astype(F32) + g_core[2:].astype(F32)).astype(BF16)
            extra = [after(of32, g_far)] + extra[1:]
            g_far = plan.turn(g_far, False)
        part = attend_back_part(plan, blk, 2, 4, True, False, info, lists, q, lse, kvs, extra)
        dkv2, dkv3, dq_part, g_ext, delta = part
        far = plan.turn(dkv3, False)
        dkv1, dq_part = attend_back_part(
            plan, blk, 1, 2, False, False, info, lists, q, lse, kvs, [g_ext, delta, dq_part]
        )
        far_two = plan.turn(after(dkv2, dkv1), False)
        mid = plan.turn((dkv1.astype(F32) + far.astype(F32)).astype(BF16), True)
        if packed:
            g_far = after(g_far, dkv1)
            g_mid = g_all[1].astype(F32) + g_core[1].astype(F32) + g_far[1].astype(F32)
            g_mid = g_mid.astype(BF16)
            dq_part = after(dq_part, g_mid)
            g_mid = plan.turn(g_mid, True)
        dkv0, _, dq = attend_back_part(
            plan, blk, 0, 1, False, True, info, lists, q, lse, kvs, [g_ext, delta, dq_part]
        )
        if packed:
            g_mid = after(g_mid, dkv0)
            g_near = g_all[0].astype(F32) + g_core[0].astype(F32) + g_far[0].astype(F32)
            g_near = (g_near + g_mid.astype(F32)).astype(BF16)
            g_other = plan.swap(g_near[2:], (0, 1))
        parts = [dkv0, far_two, mid]
    else:
        part = attend_back_part(plan, blk, 0, nb, True, True, info, lists, q, lse, kvs, extra)
        dq = part[-1]
        parts = [part[0]] + [plan.swap(part[b], plan.groups[b]) for b in range(1, nb)]

    head_outs = call(
        head_grads_body(plan, blk, width, shard, len(parts)),
        "head_grads",
        [info, dq, w_head, normed] + xs + parts,
        [SMEM] + [VMEM] * (3 + ns + len(parts)),
        [sds((nj, blk, width), BF16)] * 2 + [sds((n_wt, shard // 2, width), BF16)],
        scratch=[pltpu.VMEM((width, 4 * HEAD), F32)],
        flops=4 * ns * blk * width * 4 * HEAD,
    )
    own_rows, sib_rows, dw = head_outs
    if packed:
        g_two = (g_near[:2].astype(F32) + g_other.astype(F32)).astype(BF16)
        g_last = plan.swap(g_two[1], (0, 2))
    sib_rows = plan.swap(sib_rows, core)

    if plan.square:
        dw = (dw.astype(F32) + plan.turn(dw, True).astype(F32)).astype(BF16)
        dw_more = plan.turn(dw, False)
    else:
        step = CTX_HEADS
        while step < n_ctx:
            dw_more = plan.swap(dw, (step, 0))
            step *= 2
            if step < n_ctx:
                dw = (dw.astype(F32) + dw_more.astype(F32)).astype(BF16)
    load = call(
        merge_body(nj, n_wt, blk),
        "merge",
        [own_rows, sib_rows, dw, dw_more],
        [VMEM] * 4,
        [sds((blk + shard // 2, width), BF16)] * nj
        + [sds((shard // 2, width), BF16)] * (n_wt - nj),
    )
    loads = [load[0]] + [plan.swap(load[m], (0, m)) for m in range(1, n_wt)]
    if packed:
        g_last = after(g_last, load[0])
        final = (g_two[0].astype(F32) + g_last.astype(F32)).astype(BF16)
        finals = plan.gather_square(final)
        finals = jnp.stack(finals)
        finals = [finals, plan.swap(finals, core)]
    else:
        g_up, g_down, g_out = weight_grads
        g_up = g_up.transpose(1, 0, 2).reshape(width, ff)
        g_down = g_down.reshape(ff, width)

        def reduce_rows(g):
            part = lax.psum_scatter(g.astype(BF16), "wt", scatter_dimension=0, tiled=True)
            return lax.psum(part, "ctx").astype(F32)

        g_up, g_down, g_out = reduce_rows(g_up), reduce_rows(g_down), reduce_rows(g_out)
        both = lax.psum(gvec[:2], ("ctx", "wt"))
        both = lax.dynamic_slice_in_dim(both, wt * shard, shard, 1)
        g_gain, g_shift = both[0], both[1]
        loss = lax.psum(square[0, 0], ("ctx", "wt")) / (count[0] * width)
    own_heads = jnp.stack([x[blk:] for x in loads[:nj]])
    if n_wt > nj:
        own_heads = (own_heads.astype(F32) + jnp.stack(loads[nj:]).astype(F32)).astype(BF16)
    sib_heads = plan.swap(own_heads, core)
    more_in = [square, *finals] if packed else []
    more_out = []
    if packed:
        more_out = [
            sds((shard, ff), F32),
            sds((ff // n_wt, width), F32),
            sds((shard, width), F32),
            sds((1, 1), F32),
            sds((1, shard), F32),
            sds((1, shard), F32),
        ]
    grad_words, g_qkv, gain_one, shift_one, *more = call(
        last_body(plan, shard, nj, width, ff, len(more_in)),
        "last",
        [info, own_heads, sib_heads, words, vecs, grad_one] + loads[:nj] + more_in,
        [SMEM] + [VMEM] * (5 + nj + len(more_in)),
        [
            sds((blk, width), F32),
            sds((shard, 3 * width), F32),
            sds((1, shard), F32),
            sds((1, shard), F32),
        ]
        + more_out,
    )
    if packed:
        g_up, g_down, g_out, loss, g_gain, g_shift = more
        loss, g_gain, g_shift = loss[0, 0], g_gain.reshape(shard), g_shift.reshape(shard)
    return (
        layer_out,
        loss,
        grad_words,
        gain_one.reshape(shard),
        shift_one.reshape(shard),
        g_qkv,
        g_out,
        g_gain,
        g_shift,
        g_up,
        g_down,
    )


def solution(mesh):
    placed = (
        P(("ctx", "wt"), None),
        P(("ctx", "wt"), None),
        P(("ctx", "wt")),
        P(),
        P(),
        P("wt"),
        P("wt"),
        P("wt", None),
        P("wt", None),
        P("wt"),
        P("wt"),
        P("wt", None),
        P("wt", None),
    )
    return jax.shard_map(
        per_device,
        mesh=mesh,
        in_specs=placed,
        out_specs=(
            P(("ctx", "wt"), None),
            P(),
            P(("ctx", "wt"), None),
            P("wt"),
            P("wt"),
            P("wt", None),
            P("wt", None),
            P("wt"),
            P("wt"),
            P("wt", None),
            P("wt", None),
        ),
        check_vma=False,
    )
```

```python
import jax
import jax.numpy as jnp
from jax import lax
from jax.experimental import pallas as pl
from jax.experimental.pallas import tpu as pltpu
from jax.sharding import PartitionSpec as P

H = 8
HEAD = 64
EPS = 1e-05
LOSS_SCALE = 262144.0
CTX_HEADS = 2
WT_HEADS = 4
CHUNK = 512
TILE = 16
WIDE = 8
WIDE_BACK = 4
F32 = jnp.float32
BF16 = jnp.bfloat16
NEG = -1e30
NT = (((1,), (1,)), ((), ()))
TN = (((0,), (0,)), ((), ()))
NN = (((1,), (0,)), ((), ()))


def mm(a, b, dims=NN):
    return lax.dot_general(a, b, dims, preferred_element_type=F32)


def lane_iota(shape):
    return lax.broadcasted_iota(jnp.int32, shape, len(shape) - 1)


def norm_stats(values):
    center = values - jnp.mean(values, axis=-1, keepdims=True)
    inverse = lax.rsqrt(jnp.mean(center * center, axis=-1, keepdims=True) + EPS)
    return center * inverse, inverse


def norm_back(upstream, unit, inverse, gain):
    scaled = upstream * gain
    inner = jnp.mean(scaled * unit, axis=-1, keepdims=True)
    return inverse * (scaled - jnp.mean(scaled, axis=-1, keepdims=True) - unit * inner)


SMEM = pl.BlockSpec(memory_space=pltpu.SMEM)
VMEM = pl.BlockSpec(memory_space=pltpu.VMEM)
ANY = pl.BlockSpec(memory_space=pl.ANY)


def call(body, name, ins, in_specs, outs, scratch=(), flops=0, trans=0, out_specs=None):
    nbytes = sum(x.size * x.dtype.itemsize for x in list(ins) + list(outs))
    return pl.pallas_call(
        body,
        name=name,
        out_shape=list(outs),
        in_specs=in_specs,
        out_specs=out_specs or [VMEM] * len(outs),
        scratch_shapes=list(scratch),
        compiler_params=pltpu.CompilerParams(vmem_limit_bytes=58 * 1024 * 1024),
        cost_estimate=pl.CostEstimate(flops=flops, bytes_accessed=nbytes, transcendentals=trans),
    )(*ins)


def after(value, *earlier):
    return lax.optimization_barrier((value, *earlier))[0]


def sds(shape, dtype):
    return jax.ShapeDtypeStruct(shape, dtype)


class Plan:
    def __init__(self, n_ctx, n_wt):
        self.n_ctx, self.n_wt = n_ctx, n_wt
        ac, aw = CTX_HEADS, WT_HEADS
        assert ac * aw == H and n_ctx % ac == 0 and n_wt % aw == 0
        self.peers = [(mc, mw) for mw in range(aw) for mc in range(0, ac, 2)]
        self.slots = [(mc | k, mw) for k in (0, 1) for mc, mw in self.peers]
        self.groups = [(mc, mw) for mc in range(0, n_ctx, ac) for mw in range(0, n_wt, aw)]
        self.square = n_ctx == 8 and n_wt == aw

    def near(self, core):
        return [0, 2 + 2 * core, 4 - 2 * core, 6]

    def group_masks(self, core):
        return [(m, 0) for m in self.near(core)] if self.square else self.groups

    def head(self, ctx, wt):
        return (wt % WT_HEADS) * CTX_HEADS + ctx % CTX_HEADS

    def swap(self, x, mask):
        mc, mw = mask
        n = self.n_wt
        perm = [
            (c * n + w, (c ^ mc) * n + (w ^ mw)) for c in range(self.n_ctx) for w in range(n)
        ]
        return lax.ppermute(x, ("ctx", "wt"), perm)

    def turn(self, x, first):
        n = self.n_wt
        masks = (2, 4) if first else (4, 2)
        perm = [
            (c * n + w, (c ^ masks[c % 2]) * n + w) for c in range(self.n_ctx) for w in range(n)
        ]
        return lax.ppermute(x, ("ctx", "wt"), perm)

    def gather_square(self, x):
        one = self.turn(x, True)
        return [x, one, self.turn(x, False), self.turn(one, False)]

    def gather_groups(self, x):
        if self.square:
            return self.gather_square(x)
        return [x] + [self.swap(x, m) for m in self.groups[1:]]


def pack_body(plan, shard, blk):
    nw, half = plan.n_wt, shard // 2

    def body(info, words_ref, w_ref, *refs):
        vecs, outs = refs[:4], refs[4:]
        odd = (info[0] % 2) == 1
        rows = lax.broadcasted_iota(jnp.int32, (4, 4 * HEAD), 0)
        pick = jnp.where(lane_iota((4, 4 * HEAD)) == rows + 3 * HEAD, 1.0, 0.0).astype(BF16)
        stacked = jnp.concatenate([v[...].astype(F32) for v in vecs], axis=0).astype(BF16)
        vec = mm(stacked, pick, TN)
        lane = lane_iota((shard, 4 * HEAD))
        for m in range(nw):
            pair = plan.head(info[0], info[1] ^ m) // 2
            col = pl.multiple_of(pair * (6 * HEAD), 2 * HEAD)
            both = w_ref[:, pl.ds(col, 6 * HEAD)].astype(F32)
            turned = pltpu.roll(both, 3 * HEAD, 1)
            cols = jnp.where(odd, turned[:, : 4 * HEAD], both[:, : 4 * HEAD])
            cols = jnp.where(lane < 3 * HEAD, cols, vec).astype(BF16)
            outs[m][:blk, :] = words_ref[...]
            outs[m][blk:, : 4 * HEAD] = cols[:half]
            outs[m][blk:, 4 * HEAD :] = cols[half:]

    return body


def project_body(plan, shard, blk):
    ns, nw, half = len(plan.slots), plan.n_wt, shard // 2

    def body(info, *refs):
        xs, wps = refs[:ns], refs[ns : ns + nw]
        q_ref, kv_ref, normed_ref, wh_ref, vec_ref = refs[ns + nw :]
        wt = info[1]
        for m in range(nw):
            row = pl.multiple_of((wt ^ m) * shard, shard)
            wh_ref[pl.ds(row, half), :] = wps[m][blk:, : 4 * HEAD]
            wh_ref[pl.ds(row + half, half), :] = wps[m][blk:, 4 * HEAD :]
        weight = wh_ref[...]
        rows = lax.broadcasted_iota(jnp.int32, (8, 4 * HEAD), 0)
        pick = jnp.where(lane_iota((8, 4 * HEAD)) == rows + 3 * HEAD, 1.0, 0.0).astype(BF16)
        vecs = mm(pick, weight, NT)
        vec_ref[...] = vecs
        gain, shift = vecs[0:1], vecs[1:2]
        low = lane_iota((blk, 2 * HEAD)) < HEAD
        for s in range(ns):
            unit, _ = norm_stats(xs[s][:blk, :].astype(F32))
            normed = (unit * gain + shift).astype(BF16)
            normed_ref[s] = normed
            y = mm(normed, weight)
            q_ref[s] = (
                jnp.where(low, y[:, : 2 * HEAD], 0.0).astype(BF16).astype(F32) * HEAD**-0.5
            ).astype(BF16)
            kv_ref[s] = pltpu.roll(y, 3 * HEAD, 1)[:, : 2 * HEAD].astype(BF16)

    return body


def fill_slots(plan, info, deal, slot_of):
    for g, (gc, gw) in enumerate(plan.group_masks(info[0] % 2)):
        for s, (mc, mw) in enumerate(plan.slots):
            at = (info[0] ^ gc ^ mc) * plan.n_wt + (info[1] ^ gw ^ mw)
            slot_of[deal[at]] = g * len(plan.slots) + s


def slot_range(plan, info, deal, lengths, codes, i, blk, nseq):
    code = codes[i]
    here = deal[(info[0] ^ (code // plan.n_wt)) * plan.n_wt + (info[1] ^ (code % plan.n_wt))]
    first = jnp.int32(0)
    total = jnp.int32(0)
    for n in range(nseq):
        total = total + lengths[n]
        bound = total // blk
        first = jnp.where(bound <= here, bound, first)
    return first, here


def lists_body(plan, blk, nseq, sets):
    ns = len(plan.slots)

    def body(info, deal, lengths, codes, *refs):
        outs, slot_of = refs[:-1], refs[-1]
        fill_slots(plan, info, deal, slot_of)

        def one_block(i, counts):
            first, here = slot_range(plan, info, deal, lengths, codes, i, blk, nseq)

            def one_key(b, counts):
                slot = slot_of[b]
                more = []
                for out, n, (lo, hi) in zip(outs, counts, sets):
                    inside = (slot >= lo * ns) & (slot < hi * ns)
                    out[n] = i * 1024 + slot - lo * ns
                    more.append(n + inside.astype(jnp.int32))
                return tuple(more)

            return lax.fori_loop(first, here, one_key, counts)

        start = tuple(jnp.int32(1) for _ in sets)
        counts = lax.fori_loop(0, ns, one_block, start)
        for out, n in zip(outs, counts):
            spare = jnp.where(n > 1, out[jnp.maximum(n - 1, 1)], 0)
            for t in range(max(WIDE, WIDE_BACK) - 1):
                out[n + t] = spare
            out[0] = n - 1

    return body


def attend_body(plan, blk, lo, hi, last):
    ns, nb = len(plan.slots), hi - lo

    def body(info, pairs, q_ref, *refs):
        kv_refs, refs = refs[:nb], refs[nb:]
        if lo:
            olds, refs = refs[:3], refs[3:]
        (m_ref, l_ref, acc_ref), refs = refs[:3], refs[3:]
        if last:
            (o_ref, o_sib_ref, of_ref, lse_ref), refs = refs[:4], refs[4:]
        kvs, sem = refs
        copies = [
            pltpu.make_async_copy(ref, kvs.at[pl.ds(b * ns, ns)], sem.at[b])
            for b, ref in enumerate(kv_refs)
        ]
        for c in copies:
            c.start()
        n = pairs[0]
        if lo:
            for new, old in zip((m_ref, l_ref, acc_ref), olds):
                new[...] = old[...]
        for c in copies:
            c.wait()
        if not lo:
            tri = lax.broadcasted_iota(jnp.int32, (blk, blk), 0) <= lane_iota((blk, blk))

            def diagonal(h, _):
                scores = [mm(kvs[h * WIDE + k], q_ref[h * WIDE + k], NT) for k in range(WIDE)]
                for k in range(WIDE):
                    i = h * WIDE + k
                    s = jnp.where(tri, scores[k], NEG)
                    m = jnp.max(s, axis=0, keepdims=True)
                    p = jnp.exp(s - m)
                    m_ref[i] = m
                    l_ref[i] = jnp.sum(p, axis=0, keepdims=True)
                    acc_ref[i] = mm(kvs[i], p.astype(BF16), TN)
                return 0

            lax.fori_loop(0, ns // WIDE, diagonal, 0)

        def step(h, _):
            codes2 = [pairs[h * WIDE + 1 + k] for k in range(WIDE)]
            rows = [c // 1024 for c in codes2]
            cols = [c % 1024 for c in codes2]
            scores = [mm(kvs[cols[k]], q_ref[rows[k]], NT) for k in range(WIDE)]
            for k in range(1, WIDE):
                scores[k] = jnp.where(h * WIDE + k < n, scores[k], NEG)
            for k in range(WIDE):
                i, s = rows[k], scores[k]
                m_old = m_ref[i]
                m = jnp.maximum(m_old, jnp.max(s, axis=0, keepdims=True))
                p = jnp.exp(s - m)
                factor = jnp.exp(m_old - m)
                m_ref[i] = m
                l_ref[i] = l_ref[i] * factor + jnp.sum(p, axis=0, keepdims=True)
                acc_ref[i] = acc_ref[i] * factor + mm(kvs[cols[k]], p.astype(BF16), TN)
            return 0

        lax.fori_loop(0, (n + WIDE - 1) // WIDE, step, 0)
        if last:
            core = info[0] % 2

            def finish(i, _):
                total = l_ref[i]
                lse_ref[i] = m_ref[i] + jnp.log(total)
                out = acc_ref[i, HEAD:, :] / total
                zero = jnp.zeros_like(out)
                placed = jnp.concatenate(
                    [jnp.where(core == 0, out, zero), jnp.where(core == 1, out, zero)], axis=0
                )
                wide = placed.T
                of_ref[i] = wide

                @pl.when(i < ns // 2)
                def _():
                    o_ref[i] = wide.astype(BF16)

                @pl.when(i >= ns // 2)
                def _():
                    o_sib_ref[i - ns // 2] = wide.astype(BF16)

                return 0

            lax.fori_loop(0, ns, finish, 0)

    return body


def attend_part(plan, blk, lo, hi, last, info, lists, q, kvs, olds):
    ns, nb = len(plan.slots), hi - lo
    outs = [sds((ns, 1, blk), F32), sds((ns, 1, blk), F32), sds((ns, 2 * HEAD, blk), F32)]
    if last:
        outs += [
            sds((ns // 2, blk, 2 * HEAD), BF16),
            sds((ns // 2, blk, 2 * HEAD), BF16),
            sds((ns, blk, 2 * HEAD), F32),
            sds((ns, 1, blk), F32),
        ]
    pairs = 14 * nb
    return call(
        attend_body(plan, blk, lo, hi, last),
        "attend",
        [info, lists[lo, hi], q] + list(kvs[lo:hi]) + list(olds),
        [SMEM] * 2 + [VMEM] + [ANY] * nb + [VMEM] * len(olds),
        outs,
        scratch=[
            pltpu.VMEM((nb * ns, blk, 2 * HEAD), BF16),
            pltpu.SemaphoreType.DMA((nb,)),
        ],
        flops=pairs * 4 * blk * blk * 128 * 8,
        trans=pairs * blk * blk,
    )


def attend_back_body(plan, blk, lo, hi, first, last):
    ns, nb, nj = len(plan.slots), hi - lo, len(plan.peers)

    def body(info, pairs, q_ref, lse_ref, *refs):
        kv_refs, refs = refs[:nb], refs[nb:]
        if first:
            of_ref, g_refs, gs_ref, refs = refs[0], refs[1 : 1 + nj], refs[1 + nj], refs[2 + nj :]
        else:
            g_ext, delta_ref, old_dq, refs = refs[0], refs[1], refs[2], refs[3:]
        dkv_refs, refs = refs[:nb], refs[nb:]
        dq_acc, refs = refs[0], refs[1:]
        if first:
            g_ext, delta_ref, refs = refs[0], refs[1], refs[2:]
        if last:
            dq_ref, refs = refs[0], refs[1:]
        kvs, dkvs, sem = refs
        copies = [
            pltpu.make_async_copy(ref, kvs.at[pl.ds(b * ns, ns)], sem.at[b])
            for b, ref in enumerate(kv_refs)
        ]
        for c in copies:
            c.start()
        n = pairs[0]
        core = info[0] % 2
        high = lane_iota((blk, 2 * HEAD)) >= HEAD
        if first:
            own_half = (lane_iota((blk, 2 * HEAD)) // HEAD) == core
            for s in range(ns):
                g = (g_refs[s][...] if s < nj else gs_ref[s - nj]).astype(F32)
                g = jnp.where(own_half, g, 0.0)
                delta_ref[s] = jnp.sum((g * of_ref[s]).T, axis=0, keepdims=True)
                turned = pltpu.roll(g, HEAD, 1)
                g_ext[s] = jnp.where(high, jnp.where(core == 1, g, turned), 0.0).astype(BF16)
            dq_acc[...] = jnp.zeros_like(dq_acc)
        else:
            dq_acc[...] = old_dq[...]
        dkvs[...] = jnp.zeros_like(dkvs)
        for c in copies:
            c.wait()

        def pair_terms(rows, cols, mask):
            scores = [mm(kvs[c], q_ref[i], NT) for i, c in zip(rows, cols)]
            slopes = [mm(kvs[c], g_ext[i], NT) for i, c in zip(rows, cols)]
            for k, (i, c) in enumerate(zip(rows, cols)):
                p = jnp.exp(scores[k] - lse_ref[i])
                p = mask(k, p)
                ds = (p * (slopes[k] - delta_ref[i])).astype(BF16)
                dkvs[c] += mm(ds, q_ref[i]) + mm(p.astype(BF16), g_ext[i])
                dq_acc[i] += mm(kvs[c][:, :HEAD], ds, TN)

        if not lo:
            tri = lax.broadcasted_iota(jnp.int32, (blk, blk), 0) <= lane_iota((blk, blk))

            def diagonal(h, _):
                at = [h * WIDE_BACK + k for k in range(WIDE_BACK)]
                pair_terms(at, at, lambda k, p: jnp.where(tri, p, 0.0))
                return 0

            lax.fori_loop(0, ns // WIDE_BACK, diagonal, 0)

        def step(h, _):
            codes2 = [pairs[h * WIDE_BACK + 1 + k] for k in range(WIDE_BACK)]
            pair_terms(
                [c // 1024 for c in codes2],
                [c % 1024 for c in codes2],
                lambda k, p: jnp.where(h * WIDE_BACK + k < n, p, 0.0) if k else p,
            )
            return 0

        lax.fori_loop(0, (n + WIDE_BACK - 1) // WIDE_BACK, step, 0)
        if last:

            def finish(i, _):
                thin = dq_acc[i] * HEAD**-0.5
                wide = jnp.concatenate([thin, jnp.zeros_like(thin)], axis=0).T
                dq_ref[i] = wide.astype(BF16)
                return 0

            lax.fori_loop(0, ns, finish, 0)
        for b in range(nb):
            dkv_refs[b][...] = dkvs[b * ns : (b + 1) * ns].astype(BF16)

    return body


def attend_back_part(plan, blk, lo, hi, first, last, info, lists, q, lse, kvs, extra):
    ns, nb = len(plan.slots), hi - lo
    rows = sds((ns, blk, 2 * HEAD), BF16)
    outs = [rows] * nb + [sds((ns, HEAD, blk), F32)]
    if first:
        outs += [rows, sds((ns, 1, blk), F32)]
    if last:
        outs += [rows]
    pairs = 14 * nb
    return call(
        attend_back_body(plan, blk, lo, hi, first, last),
        "attend_back",
        [info, lists[lo, hi], q, lse] + list(kvs[lo:hi]) + list(extra),
        [SMEM] * 2 + [VMEM] * 2 + [ANY] * nb + [VMEM] * len(extra),
        outs,
        scratch=[
            pltpu.VMEM((nb * ns, blk, 2 * HEAD), BF16),
            pltpu.VMEM((nb * ns, blk, 2 * HEAD), F32),
            pltpu.SemaphoreType.DMA((nb,)),
        ],
        flops=pairs * 10 * blk * blk * 128 * 8,
        trans=pairs * blk * blk,
    )


Z_ORDER = (0, 2, 1, 3)


def mlp_body(plan, width, ff, blk, packed):
    nj, nw, nc = len(plan.peers), plan.n_wt, plan.n_ctx
    nq = ff // CHUNK

    def body(info, *refs):
        refs = list(refs)
        x_ref, teacher_ref, valid_ref, vec_ref, count_ref = refs[:5]
        att = refs[5 : 5 + nj]
        rest = refs[5 + nj :]
        nwt_in = 6 if packed else 3
        w_in, rest = rest[:nwt_in], rest[nwt_in:]
        lo_ref, sq_ref, g1_ref = rest[:3]
        gatt_refs, rest = rest[3 : 3 + nj], rest[3 + nj :]
        act_ref, gpre_ref, n2_ref, gb_ref, ga_ref, gv_ref = rest[:6]
        rest = rest[6:]
        if packed:
            wup, wdown, wout, meta, slope_ref, acc_ref, sem = rest
            copies = []
            here = info[0] % 2
            owners = [info[0] ^ m for m in plan.near(here)]
            owners += [info[0] ^ 1 ^ m for m in plan.near(1 - here)]
            sources = []
            for head, pair, tail in (w_in[:3], w_in[3:]):
                sources += [head, pair.at[0], pair.at[1], tail]
            for c, src in zip(owners, sources):
                for m in range(nw):
                    w = info[1] ^ Z_ORDER[m]
                    copies += [
                        pltpu.make_async_copy(
                            src.at[m, pl.ds(nq + 4, 1)], wout.at[w, pl.ds(c, 1)], sem.at[0]
                        ),
                        pltpu.make_async_copy(src.at[m, pl.ds(0, nq)], wup.at[:, w, c], sem.at[1]),
                        pltpu.make_async_copy(
                            src.at[m, pl.ds(nq, 4)], wdown.at[w, pl.ds(c * 4, 4)], sem.at[2]
                        ),
                        pltpu.make_async_copy(
                            src.at[m, pl.ds(nq + 5, 1)], meta.at[w, pl.ds(c, 1)], sem.at[3]
                        ),
                    ]
            for part in (0, 3, 1, 2):
                for cp in copies[part::4]:
                    cp.start()

            def arrived(*parts):
                for part in parts:
                    for cp in copies[part::4]:
                        cp.wait()

            arrived(0, 3)
            w_up = lambda q: wup[q].reshape(width, CHUNK)
            w_down = lambda q: wdown[q].reshape(CHUNK, width)
            out_rows = width // nw
            pair_rows = 2 * HEAD
            wout_flat = wout.reshape(width, width)
            w_out = lambda row: wout_flat[pl.ds(row, pair_rows), :]
            count = jnp.sum(meta[:, :, 0:1, 0:1].astype(F32))
        else:
            slope_ref, acc_ref = rest
            arrived = lambda *parts: None
            w_up = lambda q: w_in[0][q]
            w_down = lambda q: w_in[1][q]
            w_out = lambda row: w_in[2][pl.ds(row, 2 * HEAD), :]
            count = count_ref[0]
        vecs = vec_ref[...]
        gain, shift = vecs[2:3], vecs[3:4]
        rows = []
        for mc, mw in plan.peers:
            head = plan.head(info[0] ^ mc, info[1] ^ mw)
            rows.append(pl.multiple_of((head // 2) * (2 * HEAD), 2 * HEAD))
        mixed = mm(att[0][...], w_out(rows[0]))
        for j in range(1, nj):
            mixed = mixed + mm(att[j][...], w_out(rows[j]))
        res = mixed + x_ref[...].astype(F32)
        unit, inverse = norm_stats(res)
        n2 = (unit * gain + shift).astype(BF16)
        n2_ref[...] = n2
        arrived(1)
        for q in range(nq):
            if q == 0:
                first = mm(n2, w_up(q))
                arrived(2)
            pre = first if q == 0 else mm(n2, w_up(q))
            cdf = 0.5 * (1.0 + lax.erf(pre * 0.7071067811865476))
            pdf = jnp.exp(-0.5 * pre * pre) * 0.3989422804014327
            act = (pre * cdf).astype(BF16)
            slope_ref[q] = cdf + pre * pdf
            act_ref[q] = act
            if q == 0:
                acc_ref[...] = mm(act, w_down(q))
            else:
                acc_ref[...] += mm(act, w_down(q))
        two = acc_ref[...] + res
        lo_ref[...] = two.astype(BF16)
        distance = two - teacher_ref[...].astype(F32)
        valid = valid_ref[...].astype(F32)
        weighed = valid * distance
        square = jnp.sum(weighed * distance)
        first_row = lax.broadcasted_iota(jnp.int32, (8, 128), 0) == 0
        sq_ref[...] = jnp.where(first_row, square, count)
        g2 = (2.0 * LOSS_SCALE / (count * width)) * weighed
        gb = g2.astype(BF16)
        gb_ref[...] = gb
        for q in range(nq):
            gpre = (mm(gb, w_down(q), NT) * slope_ref[q]).astype(BF16)
            gpre_ref[q] = gpre
            if q == 0:
                acc_ref[...] = mm(gpre, w_up(q), NT)
            else:
                acc_ref[...] += mm(gpre, w_up(q), NT)
        gn2 = acc_ref[...]
        g1 = g2 + norm_back(gn2, unit, inverse, gain)
        g1_ref[...] = g1
        gv_ref[...] = jnp.concatenate(
            [
                jnp.sum(gn2 * unit, axis=0, keepdims=True),
                jnp.sum(gn2, axis=0, keepdims=True),
                jnp.zeros((6, width), F32),
            ],
            axis=0,
        )
        ga = g1.astype(BF16)
        ga_ref[...] = ga
        for j in range(nj):
            gatt_refs[j][...] = mm(ga, w_out(rows[j]), NT).astype(BF16)

    return body


def mlp_grads_body(plan, width, ff, blk, packed):
    nj, nw, nc = len(plan.peers), plan.n_wt, plan.n_ctx
    nq = ff // CHUNK

    def body(info, act_ref, gpre_ref, n2_ref, gb_ref, ga_ref, gv_ref, sq_ref, *refs):
        att, outs = refs[:nj], refs[nj:]
        if packed:
            outs, (ups, downs, attn, metas, sem) = outs[:2], outs[2:]
        n2, gb, ga = n2_ref[...], gb_ref[...], ga_ref[...]
        ctx, wt = info[0], info[1]
        rows_up = width // (nw * nc)

        def put(c, w, tile, value):
            plane = (c ^ ctx) // 2
            middle = (plane == 1) | (plane == 2)
            place = jnp.where(middle, 3 - plane, plane) if c % 2 else plane
            zed = w ^ wt
            zed = jnp.where((zed == 1) | (zed == 2), 3 - zed, zed)
            for k in (0, 1):

                @pl.when(ctx % 2 == k)
                def _():
                    target = outs[(c % 2) ^ k].at[place, zed, pl.ds(tile, value.shape[0])]
                    pltpu.make_async_copy(value, target, sem.at[0]).start()

        for q in range(nq):
            up = mm(n2, gpre_ref[q], TN).astype(BF16)
            down = mm(act_ref[q], gb, TN).astype(BF16)
            if packed:
                ups[q] = up.reshape(nw * nc, rows_up, CHUNK)
                downs[q] = down.reshape(nc * 4, TILE, width)
                for w in range(nw):
                    for c in range(nc):
                        put(c, w, q, ups.at[q, pl.ds(w * nc + c, 1)])
                for c in range(nc):
                    put(c, q, nq, downs.at[q, pl.ds(4 * c, 4)])
            else:
                outs[0][q] = up
                outs[1][q] = down
        for j, (mc, mw) in enumerate(plan.peers):
            head = plan.head(ctx ^ mc, wt ^ mw)
            part = mm(att[j][...], ga, TN).astype(BF16)
            if packed:
                attn[j] = part.reshape(2 * HEAD // TILE, TILE, width)
                for t in range(2 * HEAD // TILE):
                    put(t, head // 2, nq + 4, attn.at[j, pl.ds(t, 1)])
            else:
                row = pl.multiple_of((head // 2) * (2 * HEAD), 2 * HEAD)
                outs[2][pl.ds(row, 2 * HEAD), :] = part
        if packed:
            dev = ctx * nw + wt
            square = sq_ref[0:1, 0:1]
            high = square.astype(BF16).astype(F32)
            lane = lane_iota((1, CHUNK))
            n_dev = nw * nc
            line = jnp.where(lane == dev, high, 0.0) + jnp.where(
                lane == dev + n_dev, square - high, 0.0
            )
            for w in range(nw):
                per = width // nw
                vec = gv_ref[0:2, per * w : per * (w + 1)]
                vec = jnp.concatenate([vec, jnp.zeros((2, CHUNK - per), F32)], axis=1)
                tile = jnp.concatenate([line, vec, jnp.zeros((TILE - 3, CHUNK), F32)], axis=0)
                metas[w, 0] = tile.astype(BF16)
                for c in range(nc):
                    put(c, w, nq + 5, metas.at[w])
            for ref in outs:
                pltpu.make_async_copy(ref, ref, sem.at[0]).wait()

    return body


def head_grads_body(plan, blk, width, shard, nb):
    ns, nw, nj = len(plan.slots), plan.n_wt, len(plan.peers)

    def body(info, dq_ref, wh_ref, normed_ref, *refs):
        xs = refs[:ns]
        parts = refs[ns : ns + nb]
        outs = refs[ns + nb :]
        own_ref, sib_ref, dw_ref, acc = outs
        half = shard // 2
        weight = wh_ref[...]
        gsum = jnp.zeros((1, width), F32)
        ssum = jnp.zeros((1, width), F32)
        for s in range(ns):
            dkv = parts[0][s].astype(F32)
            for b in range(1, nb):
                dkv = dkv + parts[b][s].astype(F32)
            zero = jnp.zeros((blk, 2 * HEAD), F32)
            wide = pltpu.roll(jnp.concatenate([dkv, zero], axis=1), HEAD, 1)
            wide = wide + jnp.concatenate([dq_ref[s].astype(F32), zero], axis=1)
            gh = wide.astype(BF16)
            back = mm(gh, weight, NT)
            if s < nj:
                own_ref[s] = back.astype(BF16)
            else:
                sib_ref[s - nj] = back.astype(BF16)
            unit, _ = norm_stats(xs[s][:blk, :].astype(F32))
            gsum = gsum + jnp.sum(back * unit, axis=0, keepdims=True)
            ssum = ssum + jnp.sum(back, axis=0, keepdims=True)
            dw = mm(normed_ref[s], gh, TN)
            if s == 0:
                acc[...] = dw
            else:
                acc[...] += dw
        vecs = jnp.concatenate([gsum, ssum, jnp.zeros((6, width), F32)], axis=0).astype(BF16)
        rows = lax.broadcasted_iota(jnp.int32, (8, 4 * HEAD), 0)
        pick = jnp.where(lane_iota((8, 4 * HEAD)) == rows + 3 * HEAD, 1.0, 0.0).astype(BF16)
        acc[...] += mm(vecs, pick, TN)
        for m in range(nw):
            row = pl.multiple_of((info[1] ^ m) * shard, shard)
            block = acc[pl.ds(row, shard), :].astype(BF16)
            dw_ref[m, :, : 4 * HEAD] = block[:half]
            dw_ref[m, :, 4 * HEAD :] = block[half:]

    return body


def merge_body(nj, nw, blk):
    def body(own_ref, sib_ref, dw_ref, more_ref, *outs):
        for m in range(nw):
            dw = (dw_ref[m].astype(F32) + more_ref[m].astype(F32)).astype(BF16)
            if m < nj:
                rows = own_ref[m].astype(F32) + sib_ref[m].astype(F32)
                outs[m][:blk, :] = rows.astype(BF16)
                outs[m][blk:, :] = dw
            else:
                outs[m][...] = dw

    return body


def words_body(nj):
    def body(x_ref, vec_ref, g1_ref, *refs):
        parts, sibs, out_ref = refs[:nj], refs[nj : 2 * nj], refs[-1]
        up = parts[0][: x_ref.shape[0], :].astype(F32)
        for p in parts[1:]:
            up = up + p[: up.shape[0], :].astype(F32)
        unit, inverse = norm_stats(x_ref[...].astype(F32))
        out_ref[...] = g1_ref[...] + norm_back(up, unit, inverse, vec_ref[0:1, :])

    return body


def unpack_body(plan, width, ff):
    nq, nw, nc = ff // CHUNK, plan.n_wt, plan.n_ctx

    def body(info, sq_ref, own, sib, *outs):
        srcs = [r.at[n] for r in (own, sib) for n in range(nc // 2)]
        up_ref, down_ref, out_ref, loss_ref, gain_ref, shift_ref = outs
        here = info[0] % 2
        owners = [info[0] ^ m for m in plan.near(here)]
        owners += [info[0] ^ 1 ^ m for m in plan.near(1 - here)]
        for c, src in zip(owners, srcs):
            row = pl.multiple_of(c * TILE, TILE)
            for q in range(nq):
                up_ref[pl.ds(row, TILE), q * CHUNK : (q + 1) * CHUNK] = src[q].astype(F32)
            for t in range(4):
                down_ref[pl.ds(pl.multiple_of(c * 4 * TILE + t * TILE, TILE), TILE), :] = src[
                    nq + t
                ].astype(F32)
            out_ref[pl.ds(row, TILE), :] = src[nq + 4].astype(F32)
        meta = srcs[0][nq + 5].astype(F32)
        count = jnp.max(sq_ref[1:2, :], axis=1, keepdims=True)
        loss_ref[...] = jnp.sum(meta[0:1], axis=1, keepdims=True) / (count * width)
        gain_ref[...] = meta[1:2, : width // nw]
        shift_ref[...] = meta[2:3, : width // nw]

    return body


def head_out_body(plan, shard):
    nj, half = len(plan.peers), shard // 2

    def body(info, own_ref, sib_ref, out_ref, gain_ref, shift_ref):
        core = info[0] % 2
        rows = lax.broadcasted_iota(jnp.int32, (8, 4 * HEAD), 0)
        pick = jnp.where(lane_iota((8, 4 * HEAD)) == rows + 3 * HEAD, 1.0, 0.0)
        lane = lane_iota((half, 2 * HEAD))
        for side in (0, 1):
            at = slice(side * 4 * HEAD, (side + 1) * 4 * HEAD)
            here = slice(side * half, (side + 1) * half)
            total = jnp.zeros((half, 4 * HEAD), F32)
            for j, (mc, mw) in enumerate(plan.peers):
                head = plan.head(info[0] ^ mc, info[1] ^ mw)
                own = own_ref[j, :, at].astype(F32)
                sib = sib_ref[j, :, at].astype(F32)
                total = total + own + sib
                even = jnp.where(core == 0, own, sib)
                odd = jnp.where(core == 0, sib, own)
                turned = pltpu.roll(odd, 3 * HEAD, 1)
                mid = jnp.where(lane < HEAD, even[:, 2 * HEAD :], turned[:, 2 * HEAD :])
                col = pl.multiple_of((head // 2) * (6 * HEAD), 2 * HEAD)
                out_ref[here, pl.ds(col, 2 * HEAD)] = even[:, : 2 * HEAD]
                out_ref[here, pl.ds(col + 2 * HEAD, 2 * HEAD)] = mid
                out_ref[here, pl.ds(col + 4 * HEAD, 2 * HEAD)] = turned[:, : 2 * HEAD]
            both = lax.dot_general(
                pick, total, NT, precision=lax.Precision.HIGHEST, preferred_element_type=F32
            )
            gain_ref[:, here] = both[0:1]
            shift_ref[:, here] = both[1:2]

    return body


def last_body(plan, shard, nj, width, ff, n_more):
    def body(info, own_ref, sib_ref, x_ref, vec_ref, g1_ref, *refs):
        loads, refs = refs[:nj], refs[nj:]
        more, refs = refs[:n_more], refs[n_more:]
        words_ref, out_ref, gain_ref, shift_ref = refs[:4]
        words_body(nj)(x_ref, vec_ref, g1_ref, *loads, *loads, words_ref)
        head_out_body(plan, shard)(info, own_ref, sib_ref, out_ref, gain_ref, shift_ref)
        if n_more:
            unpack_body(plan, width, ff)(info, *more, *refs[4:])

    return body


def per_device(
    words,
    teacher,
    valid,
    lengths,
    deal,
    gain_attn,
    shift_attn,
    w_qkv,
    w_out,
    gain_mlp,
    shift_mlp,
    w_up,
    w_down,
):
    n_ctx, n_wt = lax.axis_size("ctx"), lax.axis_size("wt")
    plan = Plan(n_ctx, n_wt)
    ctx, wt = lax.axis_index("ctx"), lax.axis_index("wt")
    blk, width = words.shape
    shard = width // n_wt
    ff = w_up.shape[1]
    nq = ff // CHUNK
    nseq = lengths.shape[0]
    ns, nb, nj = len(plan.slots), len(plan.groups), len(plan.peers)
    packed = plan.square and width == CHUNK and width % (n_wt * n_ctx * TILE) == 0
    packed = packed and n_wt * CHUNK == ff and 2 * HEAD // TILE == n_ctx
    info = jnp.stack([ctx, wt]).astype(jnp.int32)
    codes = jnp.array([mc * n_wt + mw for mc, mw in plan.slots], jnp.int32)
    core = (1, 0)

    vecs_here = [v.reshape(1, shard) for v in (gain_attn, shift_attn, gain_mlp, shift_mlp)]
    load = call(
        pack_body(plan, shard, blk),
        "pack",
        [info, words, w_qkv, *vecs_here],
        [SMEM] + [VMEM] * 6,
        [sds((blk + shard // 2, width), BF16)] * n_wt,
    )
    loads = [load[0]] + [plan.swap(load[m], (0, m)) for m in range(1, n_wt)]
    sets = [(0, 1), (1, 3), (3, 4), (2, 4), (1, 2)] if plan.square else [(0, nb)]
    lists = call(
        lists_body(plan, blk, nseq, sets),
        "lists",
        [after(info, load[1]), deal, lengths, codes],
        [SMEM] * 4,
        [sds((ns * n_ctx * n_wt + WIDE + WIDE_BACK,), jnp.int32)] * len(sets),
        scratch=[pltpu.SMEM((n_ctx * n_wt,), jnp.int32)],
        out_specs=[SMEM] * len(sets),
    )
    lists = dict(zip(sets, lists))
    piece = info
    if packed:
        rows_up = width // (n_wt * n_ctx)
        up_piece = lax.dynamic_slice_in_dim(w_up, ctx * rows_up, rows_up, 0)
        up_piece = up_piece.reshape(rows_up, nq, CHUNK).transpose(1, 0, 2)
        down_piece = lax.dynamic_slice_in_dim(w_down, ctx * 4 * TILE, 4 * TILE, 0)
        out_piece = lax.dynamic_slice_in_dim(w_out, ctx * TILE, TILE, 0)
        count_here = jnp.sum(valid).astype(BF16)
        piece = jnp.concatenate(
            [
                up_piece,
                down_piece.reshape(4, TILE, CHUNK),
                out_piece[None],
                jnp.full((1, TILE, CHUNK), count_here, BF16),
            ],
            axis=0,
        )
    late = [loads[0], after(loads[1], lists[sets[0]], piece)] + loads[2:]
    xs = loads[:nj] + [plan.swap(x, core) for x in late[:nj]]

    q, kv, normed, w_head, vecs = call(
        project_body(plan, shard, blk),
        "project",
        [info] + xs + loads,
        [SMEM] + [VMEM] * (ns + n_wt),
        [
            sds((ns, blk, 2 * HEAD), BF16),
            sds((ns, blk, 2 * HEAD), BF16),
            sds((ns, blk, width), BF16),
            sds((width, 4 * HEAD), BF16),
            sds((8, width), F32),
        ],
        flops=2 * ns * blk * width * 4 * HEAD,
    )
    kvs = plan.gather_groups(kv)

    if packed:
        piece = after(piece, loads[2])
        two = jnp.stack([piece, plan.swap(piece, (0, 2))])
        two = after(two, kvs[1], kvs[2])
        near = plan.swap(two, (0, 1))
        count = jnp.zeros((1,), F32)
    else:
        up_full = lax.all_gather(w_up, "wt", axis=0, tiled=True)
        down_full = lax.all_gather(w_down, "wt", axis=0, tiled=True)
        out_full = lax.all_gather(w_out, "wt", axis=0, tiled=True)
        weights = [
            up_full.reshape(width, nq, CHUNK).transpose(1, 0, 2),
            down_full.reshape(nq, CHUNK, width),
            out_full,
        ]
        count = lax.psum(jnp.sum(valid).astype(F32), ("ctx", "wt")).reshape(1)

    state = []
    if not plan.square:
        state = attend_part(plan, blk, 0, nb, True, info, lists, q, kvs, state)
    else:
        state = attend_part(plan, blk, 0, 1, False, info, lists, q, kvs, state)
        if packed:
            stack = jnp.concatenate([two, near])
            stack = after(stack, kvs[3])
            kvs = kvs[:3] + [after(kvs[3], stack)]
        state = [after(state[0], kvs[3]), *state[1:]]
        state = attend_part(plan, blk, 1, 3, False, info, lists, q, kvs, state)
        if packed:
            one, side = plan.turn(stack, True), plan.turn(stack, False)
            stack_sib = plan.swap(stack, core)
        state = attend_part(plan, blk, 3, 4, True, info, lists, q, kvs, state)
    o, o_sib, of32, lse = state[3:]
    o_sib = plan.swap(o_sib, core)
    if packed:
        one = after(one, o_sib)
        last = plan.turn(one, False)
        pair = jnp.stack([one, side])
        weights = [stack, pair, last, stack_sib, plan.swap(pair, core)]
    mixed = o + o_sib
    att = [mixed[0]] + [plan.swap(mixed[j], plan.peers[j]) for j in range(1, nj)]
    if packed:
        weights += [plan.swap(after(last, *att[1:]), core)]

    mlp_in = [info, words, teacher, valid[:, None], vecs, count] + att + weights
    specs = [SMEM] + [VMEM] * 4 + [SMEM] + [VMEM] * nj
    specs += [ANY] * len(weights) if packed else [VMEM] * len(weights)
    scratch = [pltpu.VMEM((nq, blk, CHUNK), F32), pltpu.VMEM((blk, width), F32)]
    if packed:
        scratch = [
            pltpu.VMEM((nq, n_wt, n_ctx, TILE, CHUNK), BF16),
            pltpu.VMEM((n_wt, n_ctx * 4, TILE, CHUNK), BF16),
            pltpu.VMEM((n_wt, n_ctx, TILE, CHUNK), BF16),
            pltpu.VMEM((n_wt, n_ctx, TILE, CHUNK), BF16),
            *scratch,
            pltpu.SemaphoreType.DMA((4,)),
        ]
    layer_out, square, grad_one, *rest = call(
        mlp_body(plan, width, ff, blk, packed),
        "mlp",
        mlp_in,
        specs,
        [
            sds((blk, width), BF16),
            sds((8, 128), F32),
            sds((blk, width), F32),
            *[sds((blk, 2 * HEAD), BF16)] * nj,
            sds((nq, blk, CHUNK), BF16),
            sds((nq, blk, CHUNK), BF16),
            sds((blk, width), BF16),
            sds((blk, width), BF16),
            sds((blk, width), BF16),
            sds((8, width), F32),
        ],
        scratch=scratch,
        flops=8 * blk * width * ff,
        trans=2 * blk * ff,
    )
    gatt, (act, gpre, n2, gb, ga, gvec) = rest[:nj], rest[nj:]
    g_own = [gatt[0]] + [plan.swap(gatt[j], plan.peers[j]) for j in range(1, nj)]
    g_sib = plan.swap(jnp.stack(g_own), core)

    grads_in = [info, act, gpre, n2, gb, ga, gvec, square] + att
    if packed:
        grads_out = [sds((n_ctx // 2, n_wt, nq + 6, TILE, CHUNK), BF16)] * 2
        grads_scratch = [
            pltpu.VMEM((nq, n_wt * n_ctx, TILE, CHUNK), BF16),
            pltpu.VMEM((nq, n_ctx * 4, TILE, CHUNK), BF16),
            pltpu.VMEM((nj, n_ctx, TILE, CHUNK), BF16),
            pltpu.VMEM((n_wt, 1, TILE, CHUNK), BF16),
            pltpu.SemaphoreType.DMA((1,)),
        ]
    else:
        grads_out = [
            sds((nq, width, CHUNK), BF16),
            sds((nq, CHUNK, width), BF16),
            sds((width, width), BF16),
        ]
        grads_scratch = []
    weight_grads = call(
        mlp_grads_body(plan, width, ff, blk, packed),
        "mlp_grads",
        grads_in,
        [SMEM] + [VMEM] * (7 + nj),
        grads_out,
        scratch=grads_scratch,
        out_specs=[ANY if packed else VMEM] * len(grads_out),
        flops=4 * blk * width * ff,
    )

    extra = [of32] + g_own + [g_sib]
    if plan.square:
        if packed:
            g_all, g_core = weight_grads[0], plan.swap(weight_grads[1], core)
            g_far = (g_all[2:].astype(F32) + g_core[2:].astype(F32)).astype(BF16)
            extra = [after(of32, g_far)] + extra[1:]
            g_far = plan.turn(g_far, False)
        part = attend_back_part(plan, blk, 2, 4, True, False, info, lists, q, lse, kvs, extra)
        dkv2, dkv3, dq_part, g_ext, delta = part
        far = plan.turn(dkv3, False)
        dkv1, dq_part = attend_back_part(
            plan, blk, 1, 2, False, False, info, lists, q, lse, kvs, [g_ext, delta, dq_part]
        )
        far_two = plan.turn(after(dkv2, dkv1), False)
        mid = plan.turn((dkv1.astype(F32) + far.astype(F32)).astype(BF16), True)
        if packed:
            g_far = after(g_far, dkv1)
            g_mid = g_all[1].astype(F32) + g_core[1].astype(F32) + g_far[1].astype(F32)
            g_mid = g_mid.astype(BF16)
            dq_part = after(dq_part, g_mid)
            g_mid = plan.turn(g_mid, True)
        dkv0, _, dq = attend_back_part(
            plan, blk, 0, 1, False, True, info, lists, q, lse, kvs, [g_ext, delta, dq_part]
        )
        if packed:
            g_mid = after(g_mid, dkv0)
            g_near = g_all[0].astype(F32) + g_core[0].astype(F32) + g_far[0].astype(F32)
            g_near = (g_near + g_mid.astype(F32)).astype(BF16)
            g_other = plan.swap(g_near[2:], (0, 1))
        parts = [dkv0, far_two, mid]
    else:
        part = attend_back_part(plan, blk, 0, nb, True, True, info, lists, q, lse, kvs, extra)
        dq = part[-1]
        parts = [part[0]] + [plan.swap(part[b], plan.groups[b]) for b in range(1, nb)]

    head_outs = call(
        head_grads_body(plan, blk, width, shard, len(parts)),
        "head_grads",
        [info, dq, w_head, normed] + xs + parts,
        [SMEM] + [VMEM] * (3 + ns + len(parts)),
        [sds((nj, blk, width), BF16)] * 2 + [sds((n_wt, shard // 2, width), BF16)],
        scratch=[pltpu.VMEM((width, 4 * HEAD), F32)],
        flops=4 * ns * blk * width * 4 * HEAD,
    )
    own_rows, sib_rows, dw = head_outs
    if packed:
        g_two = (g_near[:2].astype(F32) + g_other.astype(F32)).astype(BF16)
        g_last = plan.swap(g_two[1], (0, 2))
    sib_rows = plan.swap(sib_rows, core)

    if plan.square:
        dw = (dw.astype(F32) + plan.turn(dw, True).astype(F32)).astype(BF16)
        dw_more = plan.turn(dw, False)
    else:
        step = CTX_HEADS
        while step < n_ctx:
            dw_more = plan.swap(dw, (step, 0))
            step *= 2
            if step < n_ctx:
                dw = (dw.astype(F32) + dw_more.astype(F32)).astype(BF16)
    load = call(
        merge_body(nj, n_wt, blk),
        "merge",
        [own_rows, sib_rows, dw, dw_more],
        [VMEM] * 4,
        [sds((blk + shard // 2, width), BF16)] * nj
        + [sds((shard // 2, width), BF16)] * (n_wt - nj),
    )
    loads = [load[0]] + [plan.swap(load[m], (0, m)) for m in range(1, n_wt)]
    if packed:
        g_last = after(g_last, load[0])
        final = (g_two[0].astype(F32) + g_last.astype(F32)).astype(BF16)
        finals = plan.gather_square(final)
        finals = jnp.stack(finals)
        finals = [finals, plan.swap(finals, core)]
    else:
        g_up, g_down, g_out = weight_grads
        g_up = g_up.transpose(1, 0, 2).reshape(width, ff)
        g_down = g_down.reshape(ff, width)

        def reduce_rows(g):
            part = lax.psum_scatter(g.astype(BF16), "wt", scatter_dimension=0, tiled=True)
            return lax.psum(part, "ctx").astype(F32)

        g_up, g_down, g_out = reduce_rows(g_up), reduce_rows(g_down), reduce_rows(g_out)
        both = lax.psum(gvec[:2], ("ctx", "wt"))
        both = lax.dynamic_slice_in_dim(both, wt * shard, shard, 1)
        g_gain, g_shift = both[0], both[1]
        loss = lax.psum(square[0, 0], ("ctx", "wt")) / (count[0] * width)
    own_heads = jnp.stack([x[blk:] for x in loads[:nj]])
    if n_wt > nj:
        own_heads = (own_heads.astype(F32) + jnp.stack(loads[nj:]).astype(F32)).astype(BF16)
    sib_heads = plan.swap(own_heads, core)
    more_in = [square, *finals] if packed else []
    more_out = []
    if packed:
        more_out = [
            sds((shard, ff), F32),
            sds((ff // n_wt, width), F32),
            sds((shard, width), F32),
            sds((1, 1), F32),
            sds((1, shard), F32),
            sds((1, shard), F32),
        ]
    grad_words, g_qkv, gain_one, shift_one, *more = call(
        last_body(plan, shard, nj, width, ff, len(more_in)),
        "last",
        [info, own_heads, sib_heads, words, vecs, grad_one] + loads[:nj] + more_in,
        [SMEM] + [VMEM] * (5 + nj + len(more_in)),
        [
            sds((blk, width), F32),
            sds((shard, 3 * width), F32),
            sds((1, shard), F32),
            sds((1, shard), F32),
        ]
        + more_out,
    )
    if packed:
        g_up, g_down, g_out, loss, g_gain, g_shift = more
        loss, g_gain, g_shift = loss[0, 0], g_gain.reshape(shard), g_shift.reshape(shard)
    return (
        layer_out,
        loss,
        grad_words,
        gain_one.reshape(shard),
        shift_one.reshape(shard),
        g_qkv,
        g_out,
        g_gain,
        g_shift,
        g_up,
        g_down,
    )


def solution(mesh):
    placed = (
        P(("ctx", "wt"), None),
        P(("ctx", "wt"), None),
        P(("ctx", "wt")),
        P(),
        P(),
        P("wt"),
        P("wt"),
        P("wt", None),
        P("wt", None),
        P("wt"),
        P("wt"),
        P("wt", None),
        P("wt", None),
    )
    return jax.shard_map(
        per_device,
        mesh=mesh,
        in_specs=placed,
        out_specs=(
            P(("ctx", "wt"), None),
            P(),
            P(("ctx", "wt"), None),
            P("wt"),
            P("wt"),
            P("wt", None),
            P("wt", None),
            P("wt"),
            P("wt"),
            P("wt", None),
            P("wt", None),
        ),
        check_vma=False,
    )
```

```python
import jax
import jax.numpy as jnp
from jax import lax
from jax.experimental import pallas as pl
from jax.experimental.pallas import tpu as pltpu
from jax.sharding import PartitionSpec as P

H = 8
HEAD = 64
EPS = 1e-05
LOSS_SCALE = 262144.0
CTX_HEADS = 2
WT_HEADS = 4
CHUNK = 512
TILE = 16
WIDE = 8
WIDE_BACK = 8
F32 = jnp.float32
BF16 = jnp.bfloat16
NEG = -1e30
NT = (((1,), (1,)), ((), ()))
TN = (((0,), (0,)), ((), ()))
NN = (((1,), (0,)), ((), ()))


def mm(a, b, dims=NN):
    return lax.dot_general(a, b, dims, preferred_element_type=F32)


def lane_iota(shape):
    return lax.broadcasted_iota(jnp.int32, shape, len(shape) - 1)


def norm_stats(values):
    center = values - jnp.mean(values, axis=-1, keepdims=True)
    inverse = lax.rsqrt(jnp.mean(center * center, axis=-1, keepdims=True) + EPS)
    return center * inverse, inverse


def norm_back(upstream, unit, inverse, gain):
    scaled = upstream * gain
    inner = jnp.mean(scaled * unit, axis=-1, keepdims=True)
    return inverse * (scaled - jnp.mean(scaled, axis=-1, keepdims=True) - unit * inner)


SMEM = pl.BlockSpec(memory_space=pltpu.SMEM)
VMEM = pl.BlockSpec(memory_space=pltpu.VMEM)
ANY = pl.BlockSpec(memory_space=pl.ANY)


def call(body, name, ins, in_specs, outs, scratch=(), flops=0, trans=0, out_specs=None):
    nbytes = sum(x.size * x.dtype.itemsize for x in list(ins) + list(outs))
    return pl.pallas_call(
        body,
        name=name,
        out_shape=list(outs),
        in_specs=in_specs,
        out_specs=out_specs or [VMEM] * len(outs),
        scratch_shapes=list(scratch),
        compiler_params=pltpu.CompilerParams(vmem_limit_bytes=58 * 1024 * 1024),
        cost_estimate=pl.CostEstimate(flops=flops, bytes_accessed=nbytes, transcendentals=trans),
    )(*ins)


def after(value, *earlier):
    return lax.optimization_barrier((value, *earlier))[0]


def sds(shape, dtype):
    return jax.ShapeDtypeStruct(shape, dtype)


class Plan:
    def __init__(self, n_ctx, n_wt):
        self.n_ctx, self.n_wt = n_ctx, n_wt
        ac, aw = CTX_HEADS, WT_HEADS
        assert ac * aw == H and n_ctx % ac == 0 and n_wt % aw == 0
        self.peers = [(mc, mw) for mw in range(aw) for mc in range(0, ac, 2)]
        self.slots = [(mc | k, mw) for k in (0, 1) for mc, mw in self.peers]
        self.groups = [(mc, mw) for mc in range(0, n_ctx, ac) for mw in range(0, n_wt, aw)]
        self.square = n_ctx == 8 and n_wt == aw

    def near(self, core):
        return [0, 2 + 2 * core, 4 - 2 * core, 6]

    def group_masks(self, core):
        return [(m, 0) for m in self.near(core)] if self.square else self.groups

    def head(self, ctx, wt):
        return (wt % WT_HEADS) * CTX_HEADS + ctx % CTX_HEADS

    def swap(self, x, mask):
        mc, mw = mask
        n = self.n_wt
        perm = [
            (c * n + w, (c ^ mc) * n + (w ^ mw)) for c in range(self.n_ctx) for w in range(n)
        ]
        return lax.ppermute(x, ("ctx", "wt"), perm)

    def turn(self, x, first):
        n = self.n_wt
        masks = (2, 4) if first else (4, 2)
        perm = [
            (c * n + w, (c ^ masks[c % 2]) * n + w) for c in range(self.n_ctx) for w in range(n)
        ]
        return lax.ppermute(x, ("ctx", "wt"), perm)

    def gather_square(self, x):
        one = self.turn(x, True)
        return [x, one, self.turn(x, False), self.turn(one, False)]

    def gather_groups(self, x):
        if self.square:
            return self.gather_square(x)
        return [x] + [self.swap(x, m) for m in self.groups[1:]]


def pack_body(plan, shard, blk):
    nw, half = plan.n_wt, shard // 2

    def body(info, words_ref, w_ref, *refs):
        vecs, outs = refs[:4], refs[4:]
        odd = (info[0] % 2) == 1
        rows = lax.broadcasted_iota(jnp.int32, (4, 4 * HEAD), 0)
        pick = jnp.where(lane_iota((4, 4 * HEAD)) == rows + 3 * HEAD, 1.0, 0.0).astype(BF16)
        stacked = jnp.concatenate([v[...].astype(F32) for v in vecs], axis=0).astype(BF16)
        vec = mm(stacked, pick, TN)
        lane = lane_iota((shard, 4 * HEAD))
        for m in range(nw):
            pair = plan.head(info[0], info[1] ^ m) // 2
            col = pl.multiple_of(pair * (6 * HEAD), 2 * HEAD)
            both = w_ref[:, pl.ds(col, 6 * HEAD)].astype(F32)
            turned = pltpu.roll(both, 3 * HEAD, 1)
            cols = jnp.where(odd, turned[:, : 4 * HEAD], both[:, : 4 * HEAD])
            cols = jnp.where(lane < 3 * HEAD, cols, vec).astype(BF16)
            outs[m][:blk, :] = words_ref[...]
            outs[m][blk:, : 4 * HEAD] = cols[:half]
            outs[m][blk:, 4 * HEAD :] = cols[half:]

    return body


def project_body(plan, shard, blk):
    ns, nw, half = len(plan.slots), plan.n_wt, shard // 2

    def body(info, *refs):
        xs, wps = refs[:ns], refs[ns : ns + nw]
        q_ref, kv_ref, normed_ref, wh_ref, vec_ref = refs[ns + nw :]
        wt = info[1]
        for m in range(nw):
            row = pl.multiple_of((wt ^ m) * shard, shard)
            wh_ref[pl.ds(row, half), :] = wps[m][blk:, : 4 * HEAD]
            wh_ref[pl.ds(row + half, half), :] = wps[m][blk:, 4 * HEAD :]
        weight = wh_ref[...]
        rows = lax.broadcasted_iota(jnp.int32, (8, 4 * HEAD), 0)
        pick = jnp.where(lane_iota((8, 4 * HEAD)) == rows + 3 * HEAD, 1.0, 0.0).astype(BF16)
        vecs = mm(pick, weight, NT)
        vec_ref[...] = vecs
        gain, shift = vecs[0:1], vecs[1:2]
        low = lane_iota((blk, 2 * HEAD)) < HEAD
        for s in range(ns):
            unit, _ = norm_stats(xs[s][:blk, :].astype(F32))
            normed = (unit * gain + shift).astype(BF16)
            normed_ref[s] = normed
            y = mm(normed, weight)
            q_ref[s] = (
                jnp.where(low, y[:, : 2 * HEAD], 0.0).astype(BF16).astype(F32) * HEAD**-0.5
            ).astype(BF16)
            kv_ref[s] = pltpu.roll(y, 3 * HEAD, 1)[:, : 2 * HEAD].astype(BF16)

    return body


def fill_slots(plan, info, deal, slot_of):
    for g, (gc, gw) in enumerate(plan.group_masks(info[0] % 2)):
        for s, (mc, mw) in enumerate(plan.slots):
            at = (info[0] ^ gc ^ mc) * plan.n_wt + (info[1] ^ gw ^ mw)
            slot_of[deal[at]] = g * len(plan.slots) + s


def slot_range(plan, info, deal, lengths, codes, i, blk, nseq):
    code = codes[i]
    here = deal[(info[0] ^ (code // plan.n_wt)) * plan.n_wt + (info[1] ^ (code % plan.n_wt))]
    first = jnp.int32(0)
    total = jnp.int32(0)
    for n in range(nseq):
        total = total + lengths[n]
        bound = total // blk
        first = jnp.where(bound <= here, bound, first)
    return first, here


def lists_body(plan, blk, nseq, sets):
    ns = len(plan.slots)

    def body(info, deal, lengths, codes, *refs):
        outs, slot_of = refs[:-1], refs[-1]
        fill_slots(plan, info, deal, slot_of)

        def one_block(i, counts):
            first, here = slot_range(plan, info, deal, lengths, codes, i, blk, nseq)

            def one_key(b, counts):
                slot = slot_of[b]
                more = []
                for out, n, (lo, hi) in zip(outs, counts, sets):
                    inside = (slot >= lo * ns) & (slot < hi * ns)
                    out[n] = i * 1024 + slot - lo * ns
                    more.append(n + inside.astype(jnp.int32))
                return tuple(more)

            return lax.fori_loop(first, here, one_key, counts)

        start = tuple(jnp.int32(1) for _ in sets)
        counts = lax.fori_loop(0, ns, one_block, start)
        for out, n in zip(outs, counts):
            spare = jnp.where(n > 1, out[jnp.maximum(n - 1, 1)], 0)
            for t in range(max(WIDE, WIDE_BACK) - 1):
                out[n + t] = spare
            out[0] = n - 1

    return body


def attend_body(plan, blk, lo, hi, last):
    ns, nb = len(plan.slots), hi - lo

    def body(info, pairs, q_ref, *refs):
        kv_refs, refs = refs[:nb], refs[nb:]
        if lo:
            olds, refs = refs[:3], refs[3:]
        (m_ref, l_ref, acc_ref), refs = refs[:3], refs[3:]
        if last:
            (o_ref, o_sib_ref, of_ref, lse_ref), refs = refs[:4], refs[4:]
        kvs, sem = refs
        copies = [
            pltpu.make_async_copy(ref, kvs.at[pl.ds(b * ns, ns)], sem.at[b])
            for b, ref in enumerate(kv_refs)
        ]
        for c in copies:
            c.start()
        n = pairs[0]
        if lo:
            for new, old in zip((m_ref, l_ref, acc_ref), olds):
                new[...] = old[...]
        for c in copies:
            c.wait()
        if not lo:
            tri = lax.broadcasted_iota(jnp.int32, (blk, blk), 0) <= lane_iota((blk, blk))

            def diagonal(h, _):
                scores = [mm(kvs[h * WIDE + k], q_ref[h * WIDE + k], NT) for k in range(WIDE)]
                for k in range(WIDE):
                    i = h * WIDE + k
                    s = jnp.where(tri, scores[k], NEG)
                    m = jnp.max(s, axis=0, keepdims=True)
                    p = jnp.exp(s - m)
                    m_ref[i] = m
                    l_ref[i] = jnp.sum(p, axis=0, keepdims=True)
                    acc_ref[i] = mm(kvs[i], p.astype(BF16), TN)
                return 0

            lax.fori_loop(0, ns // WIDE, diagonal, 0)

        def step(h, _):
            codes2 = [pairs[h * WIDE + 1 + k] for k in range(WIDE)]
            rows = [c // 1024 for c in codes2]
            cols = [c % 1024 for c in codes2]
            scores = [mm(kvs[cols[k]], q_ref[rows[k]], NT) for k in range(WIDE)]
            for k in range(1, WIDE):
                scores[k] = jnp.where(h * WIDE + k < n, scores[k], NEG)
            for k in range(WIDE):
                i, s = rows[k], scores[k]
                m_old = m_ref[i]
                m = jnp.maximum(m_old, jnp.max(s, axis=0, keepdims=True))
                p = jnp.exp(s - m)
                factor = jnp.exp(m_old - m)
                m_ref[i] = m
                l_ref[i] = l_ref[i] * factor + jnp.sum(p, axis=0, keepdims=True)
                acc_ref[i] = acc_ref[i] * factor + mm(kvs[cols[k]], p.astype(BF16), TN)
            return 0

        lax.fori_loop(0, (n + WIDE - 1) // WIDE, step, 0)
        if last:
            core = info[0] % 2

            def finish(i, _):
                total = l_ref[i]
                lse_ref[i] = m_ref[i] + jnp.log(total)
                out = acc_ref[i, HEAD:, :] / total
                zero = jnp.zeros_like(out)
                placed = jnp.concatenate(
                    [jnp.where(core == 0, out, zero), jnp.where(core == 1, out, zero)], axis=0
                )
                wide = placed.T
                of_ref[i] = wide

                @pl.when(i < ns // 2)
                def _():
                    o_ref[i] = wide.astype(BF16)

                @pl.when(i >= ns // 2)
                def _():
                    o_sib_ref[i - ns // 2] = wide.astype(BF16)

                return 0

            lax.fori_loop(0, ns, finish, 0)

    return body


def attend_part(plan, blk, lo, hi, last, info, lists, q, kvs, olds):
    ns, nb = len(plan.slots), hi - lo
    outs = [sds((ns, 1, blk), F32), sds((ns, 1, blk), F32), sds((ns, 2 * HEAD, blk), F32)]
    if last:
        outs += [
            sds((ns // 2, blk, 2 * HEAD), BF16),
            sds((ns // 2, blk, 2 * HEAD), BF16),
            sds((ns, blk, 2 * HEAD), F32),
            sds((ns, 1, blk), F32),
        ]
    pairs = 14 * nb
    return call(
        attend_body(plan, blk, lo, hi, last),
        "attend",
        [info, lists[lo, hi], q] + list(kvs[lo:hi]) + list(olds),
        [SMEM] * 2 + [VMEM] + [ANY] * nb + [VMEM] * len(olds),
        outs,
        scratch=[
            pltpu.VMEM((nb * ns, blk, 2 * HEAD), BF16),
            pltpu.SemaphoreType.DMA((nb,)),
        ],
        flops=pairs * 4 * blk * blk * 128 * 8,
        trans=pairs * blk * blk,
    )


def attend_back_body(plan, blk, lo, hi, first, last):
    ns, nb, nj = len(plan.slots), hi - lo, len(plan.peers)

    def body(info, pairs, q_ref, lse_ref, *refs):
        kv_refs, refs = refs[:nb], refs[nb:]
        if first:
            of_ref, g_refs, gs_ref, refs = refs[0], refs[1 : 1 + nj], refs[1 + nj], refs[2 + nj :]
        else:
            g_ext, delta_ref, old_dq, refs = refs[0], refs[1], refs[2], refs[3:]
        dkv_refs, refs = refs[:nb], refs[nb:]
        dq_acc, refs = refs[0], refs[1:]
        if first:
            g_ext, delta_ref, refs = refs[0], refs[1], refs[2:]
        if last:
            dq_ref, refs = refs[0], refs[1:]
        kvs, dkvs, sem = refs
        copies = [
            pltpu.make_async_copy(ref, kvs.at[pl.ds(b * ns, ns)], sem.at[b])
            for b, ref in enumerate(kv_refs)
        ]
        for c in copies:
            c.start()
        n = pairs[0]
        core = info[0] % 2
        high = lane_iota((blk, 2 * HEAD)) >= HEAD
        if first:
            own_half = (lane_iota((blk, 2 * HEAD)) // HEAD) == core
            for s in range(ns):
                g = (g_refs[s][...] if s < nj else gs_ref[s - nj]).astype(F32)
                g = jnp.where(own_half, g, 0.0)
                delta_ref[s] = jnp.sum((g * of_ref[s]).T, axis=0, keepdims=True)
                turned = pltpu.roll(g, HEAD, 1)
                g_ext[s] = jnp.where(high, jnp.where(core == 1, g, turned), 0.0).astype(BF16)
            dq_acc[...] = jnp.zeros_like(dq_acc)
        else:
            dq_acc[...] = old_dq[...]
        dkvs[...] = jnp.zeros_like(dkvs)
        for c in copies:
            c.wait()

        def pair_terms(rows, cols, mask):
            scores = [mm(kvs[c], q_ref[i], NT) for i, c in zip(rows, cols)]
            slopes = [mm(kvs[c], g_ext[i], NT) for i, c in zip(rows, cols)]
            for k, (i, c) in enumerate(zip(rows, cols)):
                p = jnp.exp(scores[k] - lse_ref[i])
                p = mask(k, p)
                ds = (p * (slopes[k] - delta_ref[i])).astype(BF16)
                dkvs[c] += mm(ds, q_ref[i]) + mm(p.astype(BF16), g_ext[i])
                dq_acc[i] += mm(kvs[c][:, :HEAD], ds, TN)

        if not lo:
            tri = lax.broadcasted_iota(jnp.int32, (blk, blk), 0) <= lane_iota((blk, blk))

            def diagonal(h, _):
                at = [h * WIDE_BACK + k for k in range(WIDE_BACK)]
                pair_terms(at, at, lambda k, p: jnp.where(tri, p, 0.0))
                return 0

            lax.fori_loop(0, ns // WIDE_BACK, diagonal, 0)

        def step(h, _):
            codes2 = [pairs[h * WIDE_BACK + 1 + k] for k in range(WIDE_BACK)]
            pair_terms(
                [c // 1024 for c in codes2],
                [c % 1024 for c in codes2],
                lambda k, p: jnp.where(h * WIDE_BACK + k < n, p, 0.0) if k else p,
            )
            return 0

        lax.fori_loop(0, (n + WIDE_BACK - 1) // WIDE_BACK, step, 0)
        if last:

            def finish(i, _):
                thin = dq_acc[i] * HEAD**-0.5
                wide = jnp.concatenate([thin, jnp.zeros_like(thin)], axis=0).T
                dq_ref[i] = wide.astype(BF16)
                return 0

            lax.fori_loop(0, ns, finish, 0)
        for b in range(nb):
            dkv_refs[b][...] = dkvs[b * ns : (b + 1) * ns].astype(BF16)

    return body


def attend_back_part(plan, blk, lo, hi, first, last, info, lists, q, lse, kvs, extra):
    ns, nb = len(plan.slots), hi - lo
    rows = sds((ns, blk, 2 * HEAD), BF16)
    outs = [rows] * nb + [sds((ns, HEAD, blk), F32)]
    if first:
        outs += [rows, sds((ns, 1, blk), F32)]
    if last:
        outs += [rows]
    pairs = 14 * nb
    return call(
        attend_back_body(plan, blk, lo, hi, first, last),
        "attend_back",
        [info, lists[lo, hi], q, lse] + list(kvs[lo:hi]) + list(extra),
        [SMEM] * 2 + [VMEM] * 2 + [ANY] * nb + [VMEM] * len(extra),
        outs,
        scratch=[
            pltpu.VMEM((nb * ns, blk, 2 * HEAD), BF16),
            pltpu.VMEM((nb * ns, blk, 2 * HEAD), F32),
            pltpu.SemaphoreType.DMA((nb,)),
        ],
        flops=pairs * 10 * blk * blk * 128 * 8,
        trans=pairs * blk * blk,
    )


Z_ORDER = (0, 2, 1, 3)


def mlp_body(plan, width, ff, blk, packed):
    nj, nw, nc = len(plan.peers), plan.n_wt, plan.n_ctx
    nq = ff // CHUNK

    def body(info, *refs):
        refs = list(refs)
        x_ref, teacher_ref, valid_ref, vec_ref, count_ref = refs[:5]
        att = refs[5 : 5 + nj]
        rest = refs[5 + nj :]
        nwt_in = 6 if packed else 3
        w_in, rest = rest[:nwt_in], rest[nwt_in:]
        lo_ref, sq_ref, g1_ref = rest[:3]
        gatt_refs, rest = rest[3 : 3 + nj], rest[3 + nj :]
        act_ref, gpre_ref, n2_ref, gb_ref, ga_ref, gv_ref = rest[:6]
        rest = rest[6:]
        if packed:
            wup, wdown, wout, meta, slope_ref, acc_ref, sem = rest
            copies = []
            here = info[0] % 2
            owners = [info[0] ^ m for m in plan.near(here)]
            owners += [info[0] ^ 1 ^ m for m in plan.near(1 - here)]
            sources = []
            for head, pair, tail in (w_in[:3], w_in[3:]):
                sources += [head, pair.at[0], pair.at[1], tail]
            for c, src in zip(owners, sources):
                for m in range(nw):
                    w = info[1] ^ Z_ORDER[m]
                    copies += [
                        pltpu.make_async_copy(
                            src.at[m, pl.ds(nq + 4, 1)], wout.at[w, pl.ds(c, 1)], sem.at[0]
                        ),
                        pltpu.make_async_copy(src.at[m, pl.ds(0, nq)], wup.at[:, w, c], sem.at[1]),
                        pltpu.make_async_copy(
                            src.at[m, pl.ds(nq, 4)], wdown.at[w, pl.ds(c * 4, 4)], sem.at[2]
                        ),
                        pltpu.make_async_copy(
                            src.at[m, pl.ds(nq + 5, 1)], meta.at[w, pl.ds(c, 1)], sem.at[3]
                        ),
                    ]
            for part in (0, 3, 1, 2):
                for cp in copies[part::4]:
                    cp.start()

            def arrived(*parts):
                for part in parts:
                    for cp in copies[part::4]:
                        cp.wait()

            arrived(0, 3)
            w_up = lambda q: wup[q].reshape(width, CHUNK)
            w_down = lambda q: wdown[q].reshape(CHUNK, width)
            out_rows = width // nw
            pair_rows = 2 * HEAD
            wout_flat = wout.reshape(width, width)
            w_out = lambda row: wout_flat[pl.ds(row, pair_rows), :]
            count = jnp.sum(meta[:, :, 0:1, 0:1].astype(F32))
        else:
            slope_ref, acc_ref = rest
            arrived = lambda *parts: None
            w_up = lambda q: w_in[0][q]
            w_down = lambda q: w_in[1][q]
            w_out = lambda row: w_in[2][pl.ds(row, 2 * HEAD), :]
            count = count_ref[0]
        vecs = vec_ref[...]
        gain, shift = vecs[2:3], vecs[3:4]
        rows = []
        for mc, mw in plan.peers:
            head = plan.head(info[0] ^ mc, info[1] ^ mw)
            rows.append(pl.multiple_of((head // 2) * (2 * HEAD), 2 * HEAD))
        mixed = mm(att[0][...], w_out(rows[0]))
        for j in range(1, nj):
            mixed = mixed + mm(att[j][...], w_out(rows[j]))
        res = mixed + x_ref[...].astype(F32)
        unit, inverse = norm_stats(res)
        n2 = (unit * gain + shift).astype(BF16)
        n2_ref[...] = n2
        arrived(1)
        for q in range(nq):
            if q == 0:
                first = mm(n2, w_up(q))
                arrived(2)
            pre = first if q == 0 else mm(n2, w_up(q))
            cdf = 0.5 * (1.0 + lax.erf(pre * 0.7071067811865476))
            pdf = jnp.exp(-0.5 * pre * pre) * 0.3989422804014327
            act = (pre * cdf).astype(BF16)
            slope_ref[q] = cdf + pre * pdf
            act_ref[q] = act
            if q == 0:
                acc_ref[...] = mm(act, w_down(q))
            else:
                acc_ref[...] += mm(act, w_down(q))
        two = acc_ref[...] + res
        lo_ref[...] = two.astype(BF16)
        distance = two - teacher_ref[...].astype(F32)
        valid = valid_ref[...].astype(F32)
        weighed = valid * distance
        square = jnp.sum(weighed * distance)
        first_row = lax.broadcasted_iota(jnp.int32, (8, 128), 0) == 0
        sq_ref[...] = jnp.where(first_row, square, count)
        g2 = (2.0 * LOSS_SCALE / (count * width)) * weighed
        gb = g2.astype(BF16)
        gb_ref[...] = gb
        for q in range(nq):
            gpre = (mm(gb, w_down(q), NT) * slope_ref[q]).astype(BF16)
            gpre_ref[q] = gpre
            if q == 0:
                acc_ref[...] = mm(gpre, w_up(q), NT)
            else:
                acc_ref[...] += mm(gpre, w_up(q), NT)
        gn2 = acc_ref[...]
        g1 = g2 + norm_back(gn2, unit, inverse, gain)
        g1_ref[...] = g1
        gv_ref[...] = jnp.concatenate(
            [
                jnp.sum(gn2 * unit, axis=0, keepdims=True),
                jnp.sum(gn2, axis=0, keepdims=True),
                jnp.zeros((6, width), F32),
            ],
            axis=0,
        )
        ga = g1.astype(BF16)
        ga_ref[...] = ga
        for j in range(nj):
            gatt_refs[j][...] = mm(ga, w_out(rows[j]), NT).astype(BF16)

    return body


def mlp_grads_body(plan, width, ff, blk, packed):
    nj, nw, nc = len(plan.peers), plan.n_wt, plan.n_ctx
    nq = ff // CHUNK

    def body(info, act_ref, gpre_ref, n2_ref, gb_ref, ga_ref, gv_ref, sq_ref, *refs):
        att, outs = refs[:nj], refs[nj:]
        if packed:
            outs, (ups, downs, attn, metas, sem) = outs[:2], outs[2:]
        n2, gb, ga = n2_ref[...], gb_ref[...], ga_ref[...]
        ctx, wt = info[0], info[1]
        rows_up = width // (nw * nc)

        def put(c, w, tile, value):
            plane = (c ^ ctx) // 2
            middle = (plane == 1) | (plane == 2)
            place = jnp.where(middle, 3 - plane, plane) if c % 2 else plane
            zed = w ^ wt
            zed = jnp.where((zed == 1) | (zed == 2), 3 - zed, zed)
            for k in (0, 1):

                @pl.when(ctx % 2 == k)
                def _():
                    target = outs[(c % 2) ^ k].at[place, zed, pl.ds(tile, value.shape[0])]
                    pltpu.make_async_copy(value, target, sem.at[0]).start()

        for q in range(nq):
            up = mm(n2, gpre_ref[q], TN).astype(BF16)
            down = mm(act_ref[q], gb, TN).astype(BF16)
            if packed:
                ups[q] = up.reshape(nw * nc, rows_up, CHUNK)
                downs[q] = down.reshape(nc * 4, TILE, width)
                for w in range(nw):
                    for c in range(nc):
                        put(c, w, q, ups.at[q, pl.ds(w * nc + c, 1)])
                for c in range(nc):
                    put(c, q, nq, downs.at[q, pl.ds(4 * c, 4)])
            else:
                outs[0][q] = up
                outs[1][q] = down
        for j, (mc, mw) in enumerate(plan.peers):
            head = plan.head(ctx ^ mc, wt ^ mw)
            part = mm(att[j][...], ga, TN).astype(BF16)
            if packed:
                attn[j] = part.reshape(2 * HEAD // TILE, TILE, width)
                for t in range(2 * HEAD // TILE):
                    put(t, head // 2, nq + 4, attn.at[j, pl.ds(t, 1)])
            else:
                row = pl.multiple_of((head // 2) * (2 * HEAD), 2 * HEAD)
                outs[2][pl.ds(row, 2 * HEAD), :] = part
        if packed:
            dev = ctx * nw + wt
            square = sq_ref[0:1, 0:1]
            high = square.astype(BF16).astype(F32)
            lane = lane_iota((1, CHUNK))
            n_dev = nw * nc
            line = jnp.where(lane == dev, high, 0.0) + jnp.where(
                lane == dev + n_dev, square - high, 0.0
            )
            for w in range(nw):
                per = width // nw
                vec = gv_ref[0:2, per * w : per * (w + 1)]
                vec = jnp.concatenate([vec, jnp.zeros((2, CHUNK - per), F32)], axis=1)
                tile = jnp.concatenate([line, vec, jnp.zeros((TILE - 3, CHUNK), F32)], axis=0)
                metas[w, 0] = tile.astype(BF16)
                for c in range(nc):
                    put(c, w, nq + 5, metas.at[w])
            for ref in outs:
                pltpu.make_async_copy(ref, ref, sem.at[0]).wait()

    return body


def head_grads_body(plan, blk, width, shard, nb):
    ns, nw, nj = len(plan.slots), plan.n_wt, len(plan.peers)

    def body(info, dq_ref, wh_ref, normed_ref, *refs):
        xs = refs[:ns]
        parts = refs[ns : ns + nb]
        outs = refs[ns + nb :]
        own_ref, sib_ref, dw_ref, acc = outs
        half = shard // 2
        weight = wh_ref[...]
        gsum = jnp.zeros((1, width), F32)
        ssum = jnp.zeros((1, width), F32)
        for s in range(ns):
            dkv = parts[0][s].astype(F32)
            for b in range(1, nb):
                dkv = dkv + parts[b][s].astype(F32)
            zero = jnp.zeros((blk, 2 * HEAD), F32)
            wide = pltpu.roll(jnp.concatenate([dkv, zero], axis=1), HEAD, 1)
            wide = wide + jnp.concatenate([dq_ref[s].astype(F32), zero], axis=1)
            gh = wide.astype(BF16)
            back = mm(gh, weight, NT)
            if s < nj:
                own_ref[s] = back.astype(BF16)
            else:
                sib_ref[s - nj] = back.astype(BF16)
            unit, _ = norm_stats(xs[s][:blk, :].astype(F32))
            gsum = gsum + jnp.sum(back * unit, axis=0, keepdims=True)
            ssum = ssum + jnp.sum(back, axis=0, keepdims=True)
            dw = mm(normed_ref[s], gh, TN)
            if s == 0:
                acc[...] = dw
            else:
                acc[...] += dw
        vecs = jnp.concatenate([gsum, ssum, jnp.zeros((6, width), F32)], axis=0).astype(BF16)
        rows = lax.broadcasted_iota(jnp.int32, (8, 4 * HEAD), 0)
        pick = jnp.where(lane_iota((8, 4 * HEAD)) == rows + 3 * HEAD, 1.0, 0.0).astype(BF16)
        acc[...] += mm(vecs, pick, TN)
        for m in range(nw):
            row = pl.multiple_of((info[1] ^ m) * shard, shard)
            block = acc[pl.ds(row, shard), :].astype(BF16)
            dw_ref[m, :, : 4 * HEAD] = block[:half]
            dw_ref[m, :, 4 * HEAD :] = block[half:]

    return body


def merge_body(nj, nw, blk):
    def body(own_ref, sib_ref, dw_ref, more_ref, *outs):
        for m in range(nw):
            dw = (dw_ref[m].astype(F32) + more_ref[m].astype(F32)).astype(BF16)
            if m < nj:
                rows = own_ref[m].astype(F32) + sib_ref[m].astype(F32)
                outs[m][:blk, :] = rows.astype(BF16)
                outs[m][blk:, :] = dw
            else:
                outs[m][...] = dw

    return body


def words_body(nj):
    def body(x_ref, vec_ref, g1_ref, *refs):
        parts, sibs, out_ref = refs[:nj], refs[nj : 2 * nj], refs[-1]
        up = parts[0][: x_ref.shape[0], :].astype(F32)
        for p in parts[1:]:
            up = up + p[: up.shape[0], :].astype(F32)
        unit, inverse = norm_stats(x_ref[...].astype(F32))
        out_ref[...] = g1_ref[...] + norm_back(up, unit, inverse, vec_ref[0:1, :])

    return body


def unpack_body(plan, width, ff):
    nq, nw, nc = ff // CHUNK, plan.n_wt, plan.n_ctx

    def body(info, sq_ref, own, sib, *outs):
        srcs = [r.at[n] for r in (own, sib) for n in range(nc // 2)]
        up_ref, down_ref, out_ref, loss_ref, gain_ref, shift_ref = outs
        here = info[0] % 2
        owners = [info[0] ^ m for m in plan.near(here)]
        owners += [info[0] ^ 1 ^ m for m in plan.near(1 - here)]
        for c, src in zip(owners, srcs):
            row = pl.multiple_of(c * TILE, TILE)
            for q in range(nq):
                up_ref[pl.ds(row, TILE), q * CHUNK : (q + 1) * CHUNK] = src[q].astype(F32)
            for t in range(4):
                down_ref[pl.ds(pl.multiple_of(c * 4 * TILE + t * TILE, TILE), TILE), :] = src[
                    nq + t
                ].astype(F32)
            out_ref[pl.ds(row, TILE), :] = src[nq + 4].astype(F32)
        meta = srcs[0][nq + 5].astype(F32)
        count = jnp.max(sq_ref[1:2, :], axis=1, keepdims=True)
        loss_ref[...] = jnp.sum(meta[0:1], axis=1, keepdims=True) / (count * width)
        gain_ref[...] = meta[1:2, : width // nw]
        shift_ref[...] = meta[2:3, : width // nw]

    return body


def head_out_body(plan, shard):
    nj, half = len(plan.peers), shard // 2

    def body(info, own_ref, sib_ref, out_ref, gain_ref, shift_ref):
        core = info[0] % 2
        rows = lax.broadcasted_iota(jnp.int32, (8, 4 * HEAD), 0)
        pick = jnp.where(lane_iota((8, 4 * HEAD)) == rows + 3 * HEAD, 1.0, 0.0)
        lane = lane_iota((half, 2 * HEAD))
        for side in (0, 1):
            at = slice(side * 4 * HEAD, (side + 1) * 4 * HEAD)
            here = slice(side * half, (side + 1) * half)
            total = jnp.zeros((half, 4 * HEAD), F32)
            for j, (mc, mw) in enumerate(plan.peers):
                head = plan.head(info[0] ^ mc, info[1] ^ mw)
                own = own_ref[j, :, at].astype(F32)
                sib = sib_ref[j, :, at].astype(F32)
                total = total + own + sib
                even = jnp.where(core == 0, own, sib)
                odd = jnp.where(core == 0, sib, own)
                turned = pltpu.roll(odd, 3 * HEAD, 1)
                mid = jnp.where(lane < HEAD, even[:, 2 * HEAD :], turned[:, 2 * HEAD :])
                col = pl.multiple_of((head // 2) * (6 * HEAD), 2 * HEAD)
                out_ref[here, pl.ds(col, 2 * HEAD)] = even[:, : 2 * HEAD]
                out_ref[here, pl.ds(col + 2 * HEAD, 2 * HEAD)] = mid
                out_ref[here, pl.ds(col + 4 * HEAD, 2 * HEAD)] = turned[:, : 2 * HEAD]
            both = lax.dot_general(
                pick, total, NT, precision=lax.Precision.HIGHEST, preferred_element_type=F32
            )
            gain_ref[:, here] = both[0:1]
            shift_ref[:, here] = both[1:2]

    return body


def last_body(plan, shard, nj, width, ff, n_more):
    def body(info, own_ref, sib_ref, x_ref, vec_ref, g1_ref, *refs):
        loads, refs = refs[:nj], refs[nj:]
        more, refs = refs[:n_more], refs[n_more:]
        words_ref, out_ref, gain_ref, shift_ref = refs[:4]
        words_body(nj)(x_ref, vec_ref, g1_ref, *loads, *loads, words_ref)
        head_out_body(plan, shard)(info, own_ref, sib_ref, out_ref, gain_ref, shift_ref)
        if n_more:
            unpack_body(plan, width, ff)(info, *more, *refs[4:])

    return body


def per_device(
    words,
    teacher,
    valid,
    lengths,
    deal,
    gain_attn,
    shift_attn,
    w_qkv,
    w_out,
    gain_mlp,
    shift_mlp,
    w_up,
    w_down,
):
    n_ctx, n_wt = lax.axis_size("ctx"), lax.axis_size("wt")
    plan = Plan(n_ctx, n_wt)
    ctx, wt = lax.axis_index("ctx"), lax.axis_index("wt")
    blk, width = words.shape
    shard = width // n_wt
    ff = w_up.shape[1]
    nq = ff // CHUNK
    nseq = lengths.shape[0]
    ns, nb, nj = len(plan.slots), len(plan.groups), len(plan.peers)
    packed = plan.square and width == CHUNK and width % (n_wt * n_ctx * TILE) == 0
    packed = packed and n_wt * CHUNK == ff and 2 * HEAD // TILE == n_ctx
    info = jnp.stack([ctx, wt]).astype(jnp.int32)
    codes = jnp.array([mc * n_wt + mw for mc, mw in plan.slots], jnp.int32)
    core = (1, 0)

    vecs_here = [v.reshape(1, shard) for v in (gain_attn, shift_attn, gain_mlp, shift_mlp)]
    load = call(
        pack_body(plan, shard, blk),
        "pack",
        [info, words, w_qkv, *vecs_here],
        [SMEM] + [VMEM] * 6,
        [sds((blk + shard // 2, width), BF16)] * n_wt,
    )
    loads = [load[0]] + [plan.swap(load[m], (0, m)) for m in range(1, n_wt)]
    sets = [(0, 1), (1, 3), (3, 4), (2, 4), (1, 2)] if plan.square else [(0, nb)]
    lists = call(
        lists_body(plan, blk, nseq, sets),
        "lists",
        [after(info, load[1]), deal, lengths, codes],
        [SMEM] * 4,
        [sds((ns * n_ctx * n_wt + WIDE + WIDE_BACK,), jnp.int32)] * len(sets),
        scratch=[pltpu.SMEM((n_ctx * n_wt,), jnp.int32)],
        out_specs=[SMEM] * len(sets),
    )
    lists = dict(zip(sets, lists))
    piece = info
    if packed:
        rows_up = width // (n_wt * n_ctx)
        up_piece = lax.dynamic_slice_in_dim(w_up, ctx * rows_up, rows_up, 0)
        up_piece = up_piece.reshape(rows_up, nq, CHUNK).transpose(1, 0, 2)
        down_piece = lax.dynamic_slice_in_dim(w_down, ctx * 4 * TILE, 4 * TILE, 0)
        out_piece = lax.dynamic_slice_in_dim(w_out, ctx * TILE, TILE, 0)
        count_here = jnp.sum(valid).astype(BF16)
        piece = jnp.concatenate(
            [
                up_piece,
                down_piece.reshape(4, TILE, CHUNK),
                out_piece[None],
                jnp.full((1, TILE, CHUNK), count_here, BF16),
            ],
            axis=0,
        )
    late = [loads[0], after(loads[1], lists[sets[0]], piece)] + loads[2:]
    xs = loads[:nj] + [plan.swap(x, core) for x in late[:nj]]

    q, kv, normed, w_head, vecs = call(
        project_body(plan, shard, blk),
        "project",
        [info] + xs + loads,
        [SMEM] + [VMEM] * (ns + n_wt),
        [
            sds((ns, blk, 2 * HEAD), BF16),
            sds((ns, blk, 2 * HEAD), BF16),
            sds((ns, blk, width), BF16),
            sds((width, 4 * HEAD), BF16),
            sds((8, width), F32),
        ],
        flops=2 * ns * blk * width * 4 * HEAD,
    )
    kvs = plan.gather_groups(kv)

    if packed:
        piece = after(piece, loads[2])
        two = jnp.stack([piece, plan.swap(piece, (0, 2))])
        two = after(two, kvs[1], kvs[2])
        near = plan.swap(two, (0, 1))
        count = jnp.zeros((1,), F32)
    else:
        up_full = lax.all_gather(w_up, "wt", axis=0, tiled=True)
        down_full = lax.all_gather(w_down, "wt", axis=0, tiled=True)
        out_full = lax.all_gather(w_out, "wt", axis=0, tiled=True)
        weights = [
            up_full.reshape(width, nq, CHUNK).transpose(1, 0, 2),
            down_full.reshape(nq, CHUNK, width),
            out_full,
        ]
        count = lax.psum(jnp.sum(valid).astype(F32), ("ctx", "wt")).reshape(1)

    state = []
    if not plan.square:
        state = attend_part(plan, blk, 0, nb, True, info, lists, q, kvs, state)
    else:
        state = attend_part(plan, blk, 0, 1, False, info, lists, q, kvs, state)
        if packed:
            stack = jnp.concatenate([two, near])
            stack = after(stack, kvs[3])
            kvs = kvs[:3] + [after(kvs[3], stack)]
        state = [after(state[0], kvs[3]), *state[1:]]
        state = attend_part(plan, blk, 1, 3, False, info, lists, q, kvs, state)
        if packed:
            one, side = plan.turn(stack, True), plan.turn(stack, False)
            stack_sib = plan.swap(stack, core)
        state = attend_part(plan, blk, 3, 4, True, info, lists, q, kvs, state)
    o, o_sib, of32, lse = state[3:]
    o_sib = plan.swap(o_sib, core)
    if packed:
        one = after(one, o_sib)
        last = plan.turn(one, False)
        pair = jnp.stack([one, side])
        weights = [stack, pair, last, stack_sib, plan.swap(pair, core)]
    mixed = o + o_sib
    att = [mixed[0]] + [plan.swap(mixed[j], plan.peers[j]) for j in range(1, nj)]
    if packed:
        weights += [plan.swap(after(last, *att[1:]), core)]

    mlp_in = [info, words, teacher, valid[:, None], vecs, count] + att + weights
    specs = [SMEM] + [VMEM] * 4 + [SMEM] + [VMEM] * nj
    specs += [ANY] * len(weights) if packed else [VMEM] * len(weights)
    scratch = [pltpu.VMEM((nq, blk, CHUNK), F32), pltpu.VMEM((blk, width), F32)]
    if packed:
        scratch = [
            pltpu.VMEM((nq, n_wt, n_ctx, TILE, CHUNK), BF16),
            pltpu.VMEM((n_wt, n_ctx * 4, TILE, CHUNK), BF16),
            pltpu.VMEM((n_wt, n_ctx, TILE, CHUNK), BF16),
            pltpu.VMEM((n_wt, n_ctx, TILE, CHUNK), BF16),
            *scratch,
            pltpu.SemaphoreType.DMA((4,)),
        ]
    layer_out, square, grad_one, *rest = call(
        mlp_body(plan, width, ff, blk, packed),
        "mlp",
        mlp_in,
        specs,
        [
            sds((blk, width), BF16),
            sds((8, 128), F32),
            sds((blk, width), F32),
            *[sds((blk, 2 * HEAD), BF16)] * nj,
            sds((nq, blk, CHUNK), BF16),
            sds((nq, blk, CHUNK), BF16),
            sds((blk, width), BF16),
            sds((blk, width), BF16),
            sds((blk, width), BF16),
            sds((8, width), F32),
        ],
        scratch=scratch,
        flops=8 * blk * width * ff,
        trans=2 * blk * ff,
    )
    gatt, (act, gpre, n2, gb, ga, gvec) = rest[:nj], rest[nj:]
    g_own = [gatt[0]] + [plan.swap(gatt[j], plan.peers[j]) for j in range(1, nj)]
    g_sib = plan.swap(jnp.stack(g_own), core)

    grads_in = [info, act, gpre, n2, gb, ga, gvec, square] + att
    if packed:
        grads_out = [sds((n_ctx // 2, n_wt, nq + 6, TILE, CHUNK), BF16)] * 2
        grads_scratch = [
            pltpu.VMEM((nq, n_wt * n_ctx, TILE, CHUNK), BF16),
            pltpu.VMEM((nq, n_ctx * 4, TILE, CHUNK), BF16),
            pltpu.VMEM((nj, n_ctx, TILE, CHUNK), BF16),
            pltpu.VMEM((n_wt, 1, TILE, CHUNK), BF16),
            pltpu.SemaphoreType.DMA((1,)),
        ]
    else:
        grads_out = [
            sds((nq, width, CHUNK), BF16),
            sds((nq, CHUNK, width), BF16),
            sds((width, width), BF16),
        ]
        grads_scratch = []
    weight_grads = call(
        mlp_grads_body(plan, width, ff, blk, packed),
        "mlp_grads",
        grads_in,
        [SMEM] + [VMEM] * (7 + nj),
        grads_out,
        scratch=grads_scratch,
        out_specs=[ANY if packed else VMEM] * len(grads_out),
        flops=4 * blk * width * ff,
    )

    extra = [of32] + g_own + [g_sib]
    if plan.square:
        if packed:
            g_all, g_core = weight_grads[0], plan.swap(weight_grads[1], core)
            g_far = (g_all[2:].astype(F32) + g_core[2:].astype(F32)).astype(BF16)
            extra = [after(of32, g_far)] + extra[1:]
            g_far = plan.turn(g_far, False)
        part = attend_back_part(plan, blk, 2, 4, True, False, info, lists, q, lse, kvs, extra)
        dkv2, dkv3, dq_part, g_ext, delta = part
        far = plan.turn(dkv3, False)
        dkv1, dq_part = attend_back_part(
            plan, blk, 1, 2, False, False, info, lists, q, lse, kvs, [g_ext, delta, dq_part]
        )
        far_two = plan.turn(after(dkv2, dkv1), False)
        mid = plan.turn((dkv1.astype(F32) + far.astype(F32)).astype(BF16), True)
        if packed:
            g_far = after(g_far, dkv1)
            g_mid = g_all[1].astype(F32) + g_core[1].astype(F32) + g_far[1].astype(F32)
            g_mid = g_mid.astype(BF16)
            dq_part = after(dq_part, g_mid)
            g_mid = plan.turn(g_mid, True)
        dkv0, _, dq = attend_back_part(
            plan, blk, 0, 1, False, True, info, lists, q, lse, kvs, [g_ext, delta, dq_part]
        )
        if packed:
            g_mid = after(g_mid, dkv0)
            g_near = g_all[0].astype(F32) + g_core[0].astype(F32) + g_far[0].astype(F32)
            g_near = (g_near + g_mid.astype(F32)).astype(BF16)
            g_other = plan.swap(g_near[2:], (0, 1))
        parts = [dkv0, far_two, mid]
    else:
        part = attend_back_part(plan, blk, 0, nb, True, True, info, lists, q, lse, kvs, extra)
        dq = part[-1]
        parts = [part[0]] + [plan.swap(part[b], plan.groups[b]) for b in range(1, nb)]

    head_outs = call(
        head_grads_body(plan, blk, width, shard, len(parts)),
        "head_grads",
        [info, dq, w_head, normed] + xs + parts,
        [SMEM] + [VMEM] * (3 + ns + len(parts)),
        [sds((nj, blk, width), BF16)] * 2 + [sds((n_wt, shard // 2, width), BF16)],
        scratch=[pltpu.VMEM((width, 4 * HEAD), F32)],
        flops=4 * ns * blk * width * 4 * HEAD,
    )
    own_rows, sib_rows, dw = head_outs
    if packed:
        g_two = (g_near[:2].astype(F32) + g_other.astype(F32)).astype(BF16)
        g_last = plan.swap(g_two[1], (0, 2))
    sib_rows = plan.swap(sib_rows, core)

    if plan.square:
        dw = (dw.astype(F32) + plan.turn(dw, True).astype(F32)).astype(BF16)
        dw_more = plan.turn(dw, False)
    else:
        step = CTX_HEADS
        while step < n_ctx:
            dw_more = plan.swap(dw, (step, 0))
            step *= 2
            if step < n_ctx:
                dw = (dw.astype(F32) + dw_more.astype(F32)).astype(BF16)
    load = call(
        merge_body(nj, n_wt, blk),
        "merge",
        [own_rows, sib_rows, dw, dw_more],
        [VMEM] * 4,
        [sds((blk + shard // 2, width), BF16)] * nj
        + [sds((shard // 2, width), BF16)] * (n_wt - nj),
    )
    loads = [load[0]] + [plan.swap(load[m], (0, m)) for m in range(1, n_wt)]
    if packed:
        g_last = after(g_last, load[0])
        final = (g_two[0].astype(F32) + g_last.astype(F32)).astype(BF16)
        finals = plan.gather_square(final)
        finals = jnp.stack(finals)
        finals = [finals, plan.swap(finals, core)]
    else:
        g_up, g_down, g_out = weight_grads
        g_up = g_up.transpose(1, 0, 2).reshape(width, ff)
        g_down = g_down.reshape(ff, width)

        def reduce_rows(g):
            part = lax.psum_scatter(g.astype(BF16), "wt", scatter_dimension=0, tiled=True)
            return lax.psum(part, "ctx").astype(F32)

        g_up, g_down, g_out = reduce_rows(g_up), reduce_rows(g_down), reduce_rows(g_out)
        both = lax.psum(gvec[:2], ("ctx", "wt"))
        both = lax.dynamic_slice_in_dim(both, wt * shard, shard, 1)
        g_gain, g_shift = both[0], both[1]
        loss = lax.psum(square[0, 0], ("ctx", "wt")) / (count[0] * width)
    own_heads = jnp.stack([x[blk:] for x in loads[:nj]])
    if n_wt > nj:
        own_heads = (own_heads.astype(F32) + jnp.stack(loads[nj:]).astype(F32)).astype(BF16)
    sib_heads = plan.swap(own_heads, core)
    more_in = [square, *finals] if packed else []
    more_out = []
    if packed:
        more_out = [
            sds((shard, ff), F32),
            sds((ff // n_wt, width), F32),
            sds((shard, width), F32),
            sds((1, 1), F32),
            sds((1, shard), F32),
            sds((1, shard), F32),
        ]
    grad_words, g_qkv, gain_one, shift_one, *more = call(
        last_body(plan, shard, nj, width, ff, len(more_in)),
        "last",
        [info, own_heads, sib_heads, words, vecs, grad_one] + loads[:nj] + more_in,
        [SMEM] + [VMEM] * (5 + nj + len(more_in)),
        [
            sds((blk, width), F32),
            sds((shard, 3 * width), F32),
            sds((1, shard), F32),
            sds((1, shard), F32),
        ]
        + more_out,
    )
    if packed:
        g_up, g_down, g_out, loss, g_gain, g_shift = more
        loss, g_gain, g_shift = loss[0, 0], g_gain.reshape(shard), g_shift.reshape(shard)
    return (
        layer_out,
        loss,
        grad_words,
        gain_one.reshape(shard),
        shift_one.reshape(shard),
        g_qkv,
        g_out,
        g_gain,
        g_shift,
        g_up,
        g_down,
    )


def solution(mesh):
    placed = (
        P(("ctx", "wt"), None),
        P(("ctx", "wt"), None),
        P(("ctx", "wt")),
        P(),
        P(),
        P("wt"),
        P("wt"),
        P("wt", None),
        P("wt", None),
        P("wt"),
        P("wt"),
        P("wt", None),
        P("wt", None),
    )
    return jax.shard_map(
        per_device,
        mesh=mesh,
        in_specs=placed,
        out_specs=(
            P(("ctx", "wt"), None),
            P(),
            P(("ctx", "wt"), None),
            P("wt"),
            P("wt"),
            P("wt", None),
            P("wt", None),
            P("wt"),
            P("wt"),
            P("wt", None),
            P("wt", None),
        ),
        check_vma=False,
    )
```
